32 devices in a mesh: dp: 4 (over x, core), expert: 8 (over z, y).
Axes of the slice: x: 2, y: 2, z: 4, core: 2. Of those that a mesh axis runs over, the one named last changes fastest.
Arguments:
- hidden_in: bfloat16 [8192, 2, 768], P(('dp', 'expert')), may hold values from -6 to 6
- cotangent: bfloat16 [8192, 2, 768], P(('dp', 'expert')), may hold values from -6 to 6
- gate_residual: float32 [8192, 2, 12], P(('dp', 'expert')), may hold values from -6 to 6
- routes: int32 [8192, 2, 2], P(('dp', 'expert')), may hold values from 0 to 11, all different within a row; in each aligned block of 512 rows (0 to 511, 512 to 1023, ..., all dimensions but the last counted through in order) at most 128 rows name the same one
- groups: int32 [32], P('dp'), may hold values from 0 to 0, as said below
- lengths: int32 [32], P('dp'), may hold values from 1 to 256, 6144 in all
- attn_gain: bfloat16 [768], P(('dp', 'expert')), may hold values from 0.5 to 1.5
- qkv_weight: bfloat16 [768, 2304], P(('dp', 'expert')), may hold values from -0.21875 to 0.21875
- out_weight: bfloat16 [768, 768], P(('dp', 'expert')), may hold values from -1.75 to 1.75
- ffn_gain: bfloat16 [768], P(('dp', 'expert')), may hold values from 0.5 to 1.5
- router_weight: bfloat16 [768, 12], P(('dp', 'expert')), may hold values from -0.21875 to 0.21875
- const_proj: bfloat16 [768, 4], P(('dp', 'expert')), may hold values from -0.21875 to 0.21875
- const_vec: bfloat16 [768, 2], P(('dp', 'expert')), may hold values from -6 to 6
- gate_weight: bfloat16 [768, 16384], P('dp', 'expert'), may hold values from -0.21875 to 0.21875
- up_weight: bfloat16 [768, 16384], P('dp', 'expert'), may hold values from -0.21875 to 0.21875
- down_weight: bfloat16 [768, 16384], P('dp', 'expert'), may hold values from -0.375 to 0.375
Outputs:
- output: bfloat16 [8192, 2, 768], P(('dp', 'expert'))
- grad_input: float32 [8192, 2, 768], P(('dp', 'expert'))
- grad_gate_residual: float32 [8192, 2, 12], P(('dp', 'expert'))
- grad_attn_gain: float32 [768], P(('dp', 'expert'))
- grad_qkv_weight: float32 [768, 2304], P(('dp', 'expert'))
- grad_out_weight: float32 [768, 768], P(('dp', 'expert'))
- grad_ffn_gain: float32 [768], P(('dp', 'expert'))
- grad_router_weight: float32 [768, 12], P(('dp', 'expert'))
- grad_const_proj: float32 [768, 4], P(('dp', 'expert'))
- grad_const_vec: float32 [768, 2], P(('dp', 'expert'))
- grad_gate_weight: float32 [768, 16384], P('dp', 'expert')
- grad_up_weight: float32 [768, 16384], P('dp', 'expert')
- grad_down_weight: float32 [768, 16384], P('dp', 'expert')
The draws below stay inside these ranges and needn't reach their ends.
Inputs may be any that keep to these rules, and one draw needn't show every extreme that they name: `routes`: among the 512 rows of one device (aligned blocks of 256 first-dimension indices), no number is named by more than 128 rows; each row names two different numbers; number 8 is the zero expert, 9 the copy expert, 10 and 11 the constant experts. `groups`: in each aligned block of 8 continuations (one index of dp) every prompt number is named by exactly 8 of them.
All inputs are finite; a program needn't handle non-finite values. No bound on the sum of `lengths` on one device may be relied on, other than what follows from the above.
Results may differ from the reference program's by a relative error of at most 0.022.
Values may be sent and summed in bfloat16 or wider, within the bound.
No kernel may reach another device: no remote copies, remote signals or barrier semaphores. Data moves between devices by JAX's collectives and lax.ppermute only.
A program may use at most 256 MiB of HBM per device.

```python
import math
from functools import partial
import jax
import jax.numpy as jnp
import numpy as np
from jax import lax

D = 768
HEADS = 12
HEAD_DIM = 64
FF = 2048
EXPERTS = 8
CONT_LEN = 256
CONT_PER = 8
GROUPS = 1
PROMPT = 2048
ROWS_DEV = 256
CAPACITY = 128
TOKS = 8192
CONTS_DP = 8
CONTS = 32
N_DP = 4


def draw_groups(key, part):
    block_count = CONTS // CONTS_DP
    key_list = jax.random.split(jax.random.fold_in(key, 17), block_count)

    def one_order(block_key):
        return jax.random.permutation(block_key, CONTS_DP)
    orders = jax.vmap(one_order)(key_list)
    return (orders // CONT_PER).astype(jnp.int32).reshape(CONTS)


def shard_levels(key, dims, cuts, least, top_value):
    level = 1.0
    for axis_at, blocks in cuts:
        draws = jax.random.uniform(jax.random.fold_in(jax.random.fold_in(key, 6), axis_at), (blocks,), jnp.float32, least / len(cuts), top_value / len(cuts))
        level = level * jnp.repeat(jnp.exp(draws), dims[axis_at] // blocks).reshape((-1,) + (1,) * (len(dims) - 1 - axis_at))
    return level


def length_profile(number_of, total, most, lean):
    weights = [(1 << 20) // math.isqrt(grade ** lean) + 1 for grade in range(2, number_of + 1)]
    rest, holding = total - most - (number_of - 1), [1] * (number_of - 1)
    while rest > 0:
        candidates = [i for i in range(number_of - 1) if holding[i] < most]
        whole, budget = sum([weights[i] for i in candidates]), rest
        for i in candidates:
            addition = min(most - holding[i], max(1, budget * weights[i] // whole), rest)
            holding[i] = holding[i] + addition
            rest = rest - addition
    return np.array([most] + holding)


def uneven_parts(key, number_of, total, most, lean):
    if number_of == 2:
        one = jax.random.randint(key, (), max(1, total - most), min(most, total - 1) + 1)
        return jnp.stack([one, total - one])
    sizes = jnp.asarray(length_profile(number_of, total, most, lean), jnp.int32)
    pairs = (number_of - 1) // 2
    giver, receiver = sizes[1:1 + 2 * pairs:2], sizes[2:2 + 2 * pairs:2]
    margin = jnp.minimum(giver - 1, most - receiver)
    shifted = jax.random.randint(jax.random.fold_in(key, 1), (pairs,), 0, 1 << 20) % (margin + 1)
    sizes = sizes.at[1:1 + 2 * pairs:2].set(giver - shifted).at[2:2 + 2 * pairs:2].set(receiver + shifted)
    return sizes[jax.random.permutation(jax.random.fold_in(key, 2), number_of)]


def shared_out(stream_key, own, number, rows, number_of, top, limit, slope):
    ranking = jax.random.permutation(stream_key, number_of)
    heavy_load, common = portions_of(number_of, rows * top, limit, slope, True), portions_of(number_of, rows * top, limit, slope, False)
    places = jnp.arange(number_of)

    def named(tallies, rotation):
        used = int((tallies > 0).sum())
        fixed = max(1, used // 4)
        shifted = fixed + (places - fixed + rotation * (used - fixed)) % max(1, number_of - fixed)
        return jnp.zeros((number_of,), jnp.int32).at[ranking[jnp.where(places < fixed, places, shifted)]].set(jnp.asarray(tallies, jnp.int32))

    tallies = jnp.where(number % 4 == 0, named(heavy_load, number // 4), named(common, number - number // 4 - 1))
    mixed = jax.random.permutation(jax.random.fold_in(own, 3), number_of)
    source_of, sink = mixed[0:number_of // 2 * 2:2], mixed[1:number_of // 2 * 2:2]
    margin = jnp.minimum(tallies[source_of] - 1, limit - tallies[sink]) // 2
    margin = jnp.where((source_of == ranking[0]) | (sink == ranking[0]) | (tallies[sink] == 0), 0, jnp.maximum(margin, 0))
    shifted = jax.random.randint(jax.random.fold_in(own, 4), (number_of // 2,), 0, 1 << 20) % (margin + 1)
    tallies = tallies.at[source_of].add(-shifted).at[sink].add(shifted)
    items = jnp.searchsorted(jnp.cumsum(tallies), jnp.arange(rows * top), side="right").astype(jnp.int32)
    listing = items.reshape(top, rows).T
    listing = listing[jax.random.permutation(jax.random.fold_in(own, 1), rows)]
    rotation = jax.random.randint(jax.random.fold_in(own, 2), (rows, 1), 0, top)
    return jnp.take_along_axis(listing, (jnp.arange(top)[None, :] + rotation) % top, axis=1)


def portions_of(count, total, reach, slope, full):
    portions = [(1 << 20) // math.isqrt(standing ** slope) + 1 for standing in range(1, count + 1)]
    largest = reach if full else min(reach, max(-(-total // count), total * portions[0] // sum(portions)))
    least = 1 if total - largest >= count - 1 else 0
    holding, rest = [largest] + [least] * (count - 1), total - largest - least * (count - 1)
    while rest > 0:
        candidates = [i for i in range(1, count) if holding[i] < largest] or [i for i in range(1, count) if holding[i] < reach]
        mass, left = sum([portions[i] for i in candidates]), rest
        for i in candidates:
            more = min(reach - holding[i], max(1, left * portions[i] // mass), rest)
            holding[i] = holding[i] + more
            rest = rest - more
    return np.array(holding)


def centred(stream_key, extent, width, most, cuts=(), kind=jnp.bfloat16):
    values = width * jax.random.normal(stream_key, extent, jnp.float32)
    if cuts:
        values = values * shard_levels(stream_key, extent, cuts, -0.22, 0.18)
    return jnp.clip(values, -most, most).astype(kind)


def setup_inputs(seed: int = 0) -> dict:
    splits = jax.random.split(jax.random.key(seed), 17)
    hidden_in = centred(splits[0], (TOKS, 2, D), 1.0, 6.0, ((0, 32),))
    cotangent = centred(splits[1], (TOKS, 2, D), 1.0, 6.0, ((0, 32),))
    gate_residual = centred(splits[2], (TOKS, 2, EXPERTS + 4), 1.0, 6.0, ((0, 32),), jnp.float32)
    routes_keys = jax.random.split(jax.random.fold_in(splits[3], 1), TOKS * 2 // (2 * ROWS_DEV))
    routes_turns = jax.random.permutation(jax.random.fold_in(splits[3], 3), TOKS * 2 // (2 * ROWS_DEV))
    routes = jax.vmap(lambda own, number: shared_out(jax.random.fold_in(splits[3], 2), own, number, 2 * ROWS_DEV, EXPERTS + 4, 2, CAPACITY, 1))(routes_keys, routes_turns).reshape((TOKS, 2, 2))
    groups = draw_groups(jax.random.fold_in(splits[16], 71), 0)
    lengths = uneven_parts(splits[5], CONTS, CONTS * CONT_LEN * 3 // 4, CONT_LEN, 1).astype(jnp.int32)
    attn_gain = jnp.clip(1.0 + 0.1 * jax.random.normal(splits[6], (D,), jnp.float32), 0.5, 1.5).astype(jnp.bfloat16)
    qkv_weight = centred(splits[7], (D, 3 * D), D ** -0.5, 0.21875, ((0, 32),))
    out_weight = centred(splits[8], (D, D), (D // 64) ** -0.5, 1.75, ((0, 32),))
    ffn_gain = jnp.clip(1.0 + 0.1 * jax.random.normal(splits[9], (D,), jnp.float32), 0.5, 1.5).astype(jnp.bfloat16)
    router_weight = centred(splits[10], (D, EXPERTS + 4), D ** -0.5, 0.21875, ((0, 32),))
    const_proj = centred(splits[11], (D, 4), D ** -0.5, 0.21875, ((0, 32),))
    const_vec = centred(splits[12], (D, 2), 1.0, 6.0, ((0, 32),))
    gate_weight = centred(splits[13], (D, EXPERTS * FF), D ** -0.5, 0.21875, ((0, 4), (1, 8)))
    up_weight = centred(splits[14], (D, EXPERTS * FF), D ** -0.5, 0.21875, ((0, 4), (1, 8)))
    down_weight = centred(splits[15], (D, EXPERTS * FF), (FF // 8) ** -0.5, 0.375, ((0, 4), (1, 8)))
    return dict(hidden_in=hidden_in, cotangent=cotangent, gate_residual=gate_residual, routes=routes, groups=groups, lengths=lengths, attn_gain=attn_gain, qkv_weight=qkv_weight, out_weight=out_weight, ffn_gain=ffn_gain, router_weight=router_weight, const_proj=const_proj, const_vec=const_vec, gate_weight=gate_weight, up_weight=up_weight, down_weight=down_weight)


@jax.custom_vjp
def low(v):
    return lax.optimization_barrier(v.astype(jnp.bfloat16)).astype(jnp.float32)

@jax.custom_vjp
def reduced_backward(v):
    return v

def low_keep(v):
    return (low(v), None)

def low_pass(kept, grad):
    return (grad,)

def back_keep(v):
    return (v, None)

def back_low(kept, grad):
    return (low(grad),)
low.defvjp(low_keep, low_pass)
reduced_backward.defvjp(back_keep, back_low)
epsilon = 1e-06
negative = -1e+30
top_precision = lax.Precision.HIGHEST

def rms_scale(value_matrix, gain):
    return value_matrix * lax.rsqrt(lax.optimization_barrier(jnp.mean(value_matrix * value_matrix, axis=-1, keepdims=True)) + epsilon) * gain

def rotate(value_matrix, position):
    half_width = value_matrix.shape[-1] // 2
    frequency = 10000.0 ** (-jnp.arange(half_width, dtype=jnp.float32) / half_width)
    angles = position[:, None, None] * frequency[None, None, :]
    cosine = jnp.cos(angles)
    sine_part = jnp.sin(angles)
    first_half = value_matrix[..., :half_width]
    second = value_matrix[..., half_width:]
    return jnp.concatenate([first_half * cosine - second * sine_part, first_half * sine_part + second * cosine], axis=-1)

def row_info(row_ids, kind_ids, length_table, prompt_table):
    matches = (row_ids // CONT_LEN)[:, None] == jnp.arange(length_table.shape[0], dtype=jnp.int32)[None, :]
    length = lax.optimization_barrier(jnp.sum(jnp.where(matches, length_table[None, :], 0), axis=1))
    prompt_of = lax.optimization_barrier(jnp.sum(jnp.where(matches, prompt_table[None, :], 0), axis=1))
    sequence = jnp.where(kind_ids == 0, row_ids // PROMPT, row_ids // CONT_LEN)
    placement = jnp.where(kind_ids == 0, row_ids % PROMPT, row_ids % CONT_LEN)
    return (kind_ids, sequence, placement, length, prompt_of)

def visible(query_info, key_info):
    query_prompt = query_info[0][:, None] == 0
    key_prompt = key_info[0][None, :] == 0
    same_seq = query_info[1][:, None] == key_info[1][None, :]
    causal = key_info[2][None, :] <= query_info[2][:, None]
    prompt_self = query_prompt & key_prompt & same_seq & causal
    to_prompt = ~query_prompt & key_prompt & (key_info[1][None, :] == query_info[4][:, None])
    live_key = key_info[2][None, :] < key_info[3][None, :]
    own_part = ~query_prompt & ~key_prompt & same_seq & causal & live_key
    return prompt_self | to_prompt | own_part

def mix_part(picked, normed, normed_low, router_w, proj_w, vec_w, residual_logits, expert_rows):
    logits = jnp.dot(normed_low, router_w, precision=top_precision) + residual_logits
    route_probs = jax.nn.softmax(logits, axis=-1)
    one_hot = (picked[:, :, None] == jnp.arange(route_probs.shape[-1], dtype=jnp.int32)[None, None, :]).astype(jnp.float32)
    mix_weight = lax.optimization_barrier(jnp.sum(route_probs[:, None, :] * one_hot, axis=-1))
    const_logits = jnp.dot(normed_low, proj_w, precision=top_precision).reshape(-1, 2, 2)
    const_mix = jax.nn.softmax(const_logits, axis=-1)
    const_out = const_mix[:, :, 0:1] * normed[:, None, :] + const_mix[:, :, 1:2] * jnp.transpose(vec_w)[None, :, :]
    copy_term = jnp.where(picked[:, :, None] == EXPERTS + 1, normed[:, None, :], 0.0)
    first_const = jnp.where(picked[:, :, None] == EXPERTS + 2, const_out[:, 0:1, :], 0.0)
    second_const = jnp.where(picked[:, :, None] == EXPERTS + 3, const_out[:, 1:2, :], 0.0)
    branch = expert_rows + copy_term + first_const + second_const
    return lax.optimization_barrier(jnp.sum(mix_weight[:, :, None] * branch, axis=1))

def attend_block(inputs):
    query_matrix, every_key, value_matrix, prompt_table, length_table = inputs
    token_count = query_matrix.shape[0]
    all_index = jnp.arange(token_count, dtype=jnp.int32)
    key_info = row_info(all_index // 2, all_index % 2, length_table, prompt_table)
    step_size = min(512, token_count)
    query_key_scale = float(HEAD_DIM) ** (-0.5)

    def query_part(first_row):
        query_index = first_row + jnp.arange(step_size, dtype=jnp.int32)
        query_info = row_info(query_index // 2, query_index % 2, length_table, prompt_table)
        block_of_queries = lax.dynamic_slice_in_dim(query_matrix, first_row, step_size, 0)
        score_matrix = reduced_backward(jnp.einsum('stc,atc->tsa', block_of_queries, every_key, precision=top_precision) * query_key_scale)
        score_matrix = jnp.where(visible(query_info, key_info)[None], score_matrix, negative)
        weight_matrix = low(jax.nn.softmax(score_matrix, axis=-1))
        return jnp.einsum('ezt,teu->zeu', weight_matrix, value_matrix, precision=top_precision)
    starts = jnp.arange(token_count // step_size, dtype=jnp.int32) * step_size
    return lax.map(jax.checkpoint(query_part), starts).reshape(token_count, HEADS, HEAD_DIM)

def expert_ffn(inputs):
    rows_in, gate_e, up_e, down_e = inputs
    gate_pre = reduced_backward(jnp.dot(rows_in, gate_e, precision=top_precision))
    up_pre = reduced_backward(jnp.dot(rows_in, up_e, precision=top_precision))
    activated = low(jax.nn.silu(gate_pre) * up_pre)
    return reduced_backward(jnp.dot(activated, jnp.transpose(down_e), precision=top_precision))

def forward(routes, groups, lengths, hidden_in, gate_residual, attn_gain, qkv_weight, out_weight, ffn_gain, router_weight, const_proj, const_vec, gate_weight, up_weight, down_weight):
    pair_all = 2 * TOKS
    x_flat = hidden_in.reshape(pair_all, D)
    rows_all = jnp.repeat(jnp.arange(TOKS, dtype=jnp.int32), 2)
    kinds_all = jnp.tile(jnp.arange(2, dtype=jnp.int32), TOKS)
    local_row = rows_all % (GROUPS * PROMPT)
    position = jnp.where(kinds_all == 0, local_row % PROMPT, PROMPT + local_row % CONT_LEN).astype(jnp.float32)
    normed_one = low(rms_scale(x_flat, attn_gain))
    qkv = reduced_backward(jnp.dot(normed_one, qkv_weight, precision=top_precision))
    query_matrix = low(rotate(qkv[:, :D].reshape(pair_all, HEADS, HEAD_DIM), position))
    every_key = low(rotate(qkv[:, D:2 * D].reshape(pair_all, HEADS, HEAD_DIM), position))
    value_matrix = low(qkv[:, 2 * D:].reshape(pair_all, HEADS, HEAD_DIM))
    span = 2 * GROUPS * PROMPT
    attended = lax.map(attend_block, (query_matrix.reshape(N_DP, span, HEADS, HEAD_DIM), every_key.reshape(N_DP, span, HEADS, HEAD_DIM), value_matrix.reshape(N_DP, span, HEADS, HEAD_DIM), groups.reshape(N_DP, CONTS_DP), lengths.reshape(N_DP, CONTS_DP)))
    attended = low(reduced_backward(attended.reshape(pair_all, D)))
    hidden = x_flat + reduced_backward(jnp.dot(attended, out_weight, precision=top_precision))
    normed_two = rms_scale(hidden, ffn_gain)
    normed_low = low(normed_two)
    block_count = TOKS // ROWS_DEV
    per_block = 4 * ROWS_DEV
    picked = routes.reshape(block_count, per_block)
    one_hot = (picked[:, :, None] == jnp.arange(EXPERTS + 4, dtype=jnp.int32)[None, None, :]).astype(jnp.int32)
    slot_index = lax.optimization_barrier(jnp.sum((jnp.cumsum(one_hot, axis=1) - one_hot) * one_hot, axis=2))
    bin_index = jnp.minimum(picked, EXPERTS)
    owner_id = jnp.broadcast_to(jnp.arange(block_count, dtype=jnp.int32)[:, None], (block_count, per_block))
    spread = jnp.repeat(normed_low.reshape(block_count, 2 * ROWS_DEV, D), 2, axis=1)
    buffer = jnp.zeros((block_count, EXPERTS + 1, CAPACITY, D), jnp.float32).at[owner_id, bin_index, slot_index].set(spread)
    grouped = jnp.transpose(buffer[:, :EXPERTS], (1, 0, 2, 3)).reshape(EXPERTS, block_count * CAPACITY, D)
    per_gate = jnp.transpose(gate_weight.reshape(D, EXPERTS, FF), (1, 0, 2))
    per_up = jnp.transpose(up_weight.reshape(D, EXPERTS, FF), (1, 0, 2))
    per_down = jnp.transpose(down_weight.reshape(D, EXPERTS, FF), (1, 0, 2))
    produced = lax.map(jax.checkpoint(expert_ffn), (grouped, per_gate, per_up, per_down))
    produced = jnp.transpose(produced.reshape(EXPERTS, block_count, CAPACITY, D), (1, 0, 2, 3))
    padded = jnp.concatenate([produced, jnp.zeros((block_count, 1, CAPACITY, D), jnp.float32)], axis=1)
    expert_rows = padded[owner_id, bin_index, slot_index].reshape(pair_all, 2, D)
    mixture = mix_part(routes.reshape(pair_all, 2), normed_two, normed_low, router_weight, const_proj, const_vec, gate_residual.reshape(pair_all, EXPERTS + 4), expert_rows)
    return (hidden + mixture).reshape(TOKS, 2, D)

def reference(hidden_in, cotangent, gate_residual, routes, groups, lengths, attn_gain, qkv_weight, out_weight, ffn_gain, router_weight, const_proj, const_vec, gate_weight, up_weight, down_weight):
    floats = [array.astype(jnp.float32) for array in (hidden_in, gate_residual, attn_gain, qkv_weight, out_weight, ffn_gain, router_weight, const_proj, const_vec, gate_weight, up_weight, down_weight)]
    output, pullback = jax.vjp(partial(forward, routes, groups, lengths), *floats)
    gradients = pullback(cotangent.astype(jnp.float32))
    return (output.astype(jnp.bfloat16), gradients[0], gradients[1], gradients[2], gradients[3], gradients[4], gradients[5], gradients[6], gradients[7], gradients[8], gradients[9], gradients[10], gradients[11])
```

```python
import functools

import jax
import jax.numpy as jnp
from jax import lax
from jax.experimental import pallas as pl
from jax.experimental.pallas import tpu as pltpu
from jax.sharding import PartitionSpec as P

D = 768
HEADS = 12
HEAD_DIM = 64
PAIRS = 6
EXPERTS = 8
CONT_LEN = 256
PROMPT = 2048
LANES = 128
EPS = 1e-06
NEG = -1e30
LOG2E = 1.4426950408889634
SCALE = float(HEAD_DIM) ** (-0.5)
LC = SCALE * LOG2E
F32 = jnp.float32
BF16 = jnp.bfloat16
ALL_AXES = ("dp", "expert")
VMEM_LIMIT = 60 * 1024 * 1024


def dot(a, b):
    return jnp.dot(a, b, preferred_element_type=F32)


def dot_nt(a, b):
    return lax.dot_general(a, b, (((1,), (1,)), ((), ())), preferred_element_type=F32)


def dot_tn(a, b):
    return lax.dot_general(a, b, (((0,), (0,)), ((), ())), preferred_element_type=F32)


def split_hi_lo(v):
    hi = v.astype(BF16)
    return hi, (v - hi.astype(F32)).astype(BF16)


def params(cost=None):
    return dict(
        compiler_params=pltpu.CompilerParams(vmem_limit_bytes=VMEM_LIMIT),
        cost_estimate=None if cost is None else pl.CostEstimate(
            flops=int(cost[0]), bytes_accessed=int(cost[1]), transcendentals=0
        ),
    )


def shape(dims, dtype):
    return jax.ShapeDtypeStruct(tuple(dims), dtype)


def spec(block, index):
    return pl.BlockSpec(tuple(block), index)


def whole(dims):
    return pl.BlockSpec(tuple(dims), lambda *_: (0,) * len(dims))


SMEM_SPEC = pl.BlockSpec(memory_space=pltpu.SMEM)


def partner(v):
    lane = lax.broadcasted_iota(jnp.int32, v.shape, 1)
    return jnp.where((lane & 63) < 32, pltpu.roll(v, 96, 1), pltpu.roll(v, 32, 1))


def qkv_body(x_ref, gain_ref, wq_ref, wk_ref, wv_ref, c_ref, s_ref, n_ref, q_ref, qt_ref, kv_ref):
    @pl.when(pl.program_id(0) == 0)
    def _():
        x = x_ref[...].astype(F32)
        scale = lax.rsqrt(jnp.mean(x * x, axis=-1, keepdims=True) + EPS)
        n_ref[...] = (x * scale * gain_ref[...]).astype(BF16)

    n = n_ref[...]
    cosine = c_ref[...]
    sine = s_ref[...]
    kv = dot(n, jnp.concatenate([wk_ref[...], wv_ref[...]], axis=1))
    k = kv[:, :LANES]
    kv_ref[:, :LANES] = (k * cosine + partner(k) * sine).astype(BF16)
    kv_ref[:, LANES:] = kv[:, LANES:].astype(BF16)
    q = dot(n, wq_ref[...])
    q = q * cosine + partner(q) * sine
    q_ref[...] = q.astype(BF16)
    qt_ref[...] = q.T.astype(BF16)


def qkv_call(x, gain, pack, cosine, sine):
    t = x.shape[0]
    return pl.pallas_call(
        qkv_body,
        grid=(PAIRS,),
        in_specs=[
            whole((t, D)),
            whole((1, D)),
            spec((D, LANES), lambda i: (0, i)),
            spec((D, LANES), lambda i: (0, PAIRS + i)),
            spec((D, LANES), lambda i: (0, 2 * PAIRS + i)),
            whole((t, LANES)),
            whole((t, LANES)),
        ],
        out_specs=[
            whole((t, D)),
            spec((t, LANES), lambda i: (0, i)),
            spec((LANES, t), lambda i: (i, 0)),
            spec((t, 2 * LANES), lambda i: (0, i)),
        ],
        out_shape=[
            shape((t, D), BF16),
            shape((t, D), BF16),
            shape((D, t), BF16),
            shape((t, 2 * D), BF16),
        ],
        name="qkv_rope",
        **params((2 * t * D * 3 * D, 6 * D * D)),
    )(x, gain, pack, pack, pack, cosine, sine)


def head_rows(v, h):
    row = lax.broadcasted_iota(jnp.int32, v.shape, 0)
    return jnp.where(row // HEAD_DIM == h, v, jnp.zeros_like(v))


def head_lanes(v, h):
    lane = lax.broadcasted_iota(jnp.int32, v.shape, 1)
    return jnp.where(lane // HEAD_DIM == h, v, jnp.zeros_like(v))


def attend_update(qz, kb, vt, lo, hi, mask, st_ref, a_ref, first):
    for h in range(2):
        s = dot(kb, qz[h][:, lo:hi])
        if mask is not None:
            s = jnp.where(mask, s, NEG)
        top = jnp.max(s, axis=0, keepdims=True)
        rows = slice(h * HEAD_DIM, (h + 1) * HEAD_DIM)
        if first:
            p = jnp.exp2((s - top) * LC)
            st_ref[h : h + 1, lo:hi] = top
            st_ref[2 + h : 3 + h, lo:hi] = jnp.sum(p, axis=0, keepdims=True)
            a_ref[rows, lo:hi] = dot(vt[rows], p.astype(BF16))
        else:
            old = st_ref[h : h + 1, lo:hi]
            new = jnp.maximum(old, top)
            alpha = jnp.exp2((old - new) * LC)
            p = jnp.exp2((s - new) * LC)
            st_ref[h : h + 1, lo:hi] = new
            st_ref[2 + h : 3 + h, lo:hi] = st_ref[2 + h : 3 + h, lo:hi] * alpha + jnp.sum(
                p, axis=0, keepdims=True
            )
            a_ref[rows, lo:hi] = a_ref[rows, lo:hi] * alpha + dot(vt[rows], p.astype(BF16))


def local_masks(sc_ref, r, keys, lo, hi):
    cpos = sc_ref[1]
    length = sc_ref[2]
    col = lo + lax.broadcasted_iota(jnp.int32, (r, hi - lo), 1)
    row = lax.broadcasted_iota(jnp.int32, (r, hi - lo), 0)
    own = (row <= col) | (col >= r)
    col = lo + lax.broadcasted_iota(jnp.int32, (keys, hi - lo), 1)
    row = lax.broadcasted_iota(jnp.int32, (keys, hi - lo), 0)
    cont = (col >= r) & (row <= cpos + col - r) & (row < length)
    return own, cont


def fwd_local_body(sc_ref, qt_ref, kv_ref, kvo_ref, st_ref, a_ref):
    t = qt_ref.shape[1]
    r = t // 2
    keys = kvo_ref.shape[0]
    qt = qt_ref[...]
    qz = [head_rows(qt, h) for h in range(2)]
    kb = kv_ref[:, :LANES]
    vt = kv_ref[:, LANES:].T
    kbo = kvo_ref[:, :LANES]
    vto = kvo_ref[:, LANES:].T
    st_ref[...] = jnp.zeros_like(st_ref)
    own, cont = local_masks(sc_ref, r, keys, 0, t)
    if r % LANES == 0:
        attend_update(qz, kb, vt, 0, r, own[:, :r], st_ref, a_ref, True)
        attend_update(qz, kb, vt, r, t, None, st_ref, a_ref, True)
        attend_update(qz, kbo, vto, r, t, cont[:, r:], st_ref, a_ref, False)
    else:
        attend_update(qz, kb, vt, 0, t, own, st_ref, a_ref, True)
        attend_update(qz, kbo, vto, 0, t, cont, st_ref, a_ref, False)


def fwd_remote_body(n, final, sc_ref, qt_ref, kv_ref, st_in, a_in, *outs):
    st_ref, a_ref = outs[0], outs[1]
    t = qt_ref.shape[1]
    r = t // 2
    me = sc_ref[0]
    qt = qt_ref[...]
    qz = [head_rows(qt, h) for h in range(2)]
    st_ref[...] = st_in[...]
    a_ref[...] = a_in[...]
    for j in range(n):
        block = sc_ref[3 + j]
        rows = slice(j * r, (j + 1) * r)

        def go(lo, mask):
            kb = kv_ref[rows, :LANES]
            vt = kv_ref[rows, LANES:].T
            attend_update(qz, kb, vt, lo, t, mask, st_ref, a_ref, False)

        if r % LANES == 0:

            @pl.when(block < me)
            def _():
                go(0, None)

            @pl.when(block > me)
            def _():
                go(r, None)

        else:

            @pl.when(block != me)
            def _():
                col = lax.broadcasted_iota(jnp.int32, (r, t), 1)
                go(0, (col >= r) | (block < me))

    if final:
        low_ref = outs[2]
        for h in range(2):
            rows = slice(h * HEAD_DIM, (h + 1) * HEAD_DIM)
            total = st_ref[2 + h : 3 + h, :]
            a_ref[rows, :] = a_ref[rows, :] / total
            st_ref[h : h + 1, :] = st_ref[h : h + 1, :] * LC + jnp.log2(total)
        low_ref[...] = a_ref[...].T.astype(BF16)


def fwd_local(sc, qt, kv_prompt, kv_own):
    t = qt.shape[1]
    keys = kv_own.shape[0]
    return pl.pallas_call(
        fwd_local_body,
        grid=(PAIRS,),
        in_specs=[
            SMEM_SPEC,
            spec((LANES, t), lambda i: (i, 0)),
            spec((t // 2, 2 * LANES), lambda i: (0, i)),
            spec((keys, 2 * LANES), lambda i: (0, i)),
        ],
        out_specs=[spec((8, t), lambda i: (i, 0)), spec((LANES, t), lambda i: (i, 0))],
        out_shape=[shape((8 * PAIRS, t), F32), shape((D, t), F32)],
        name="attend_local",
        **params((4 * 4 * t * keys * D, 4 * D * t)),
    )(sc, qt, kv_prompt, kv_own)


def fwd_remote(sc, qt, kv, st, acc, final):
    t = qt.shape[1]
    rows = kv.shape[0]
    out_specs = [spec((8, t), lambda i: (i, 0)), spec((LANES, t), lambda i: (i, 0))]
    out_shape = [shape((8 * PAIRS, t), F32), shape((D, t), F32)]
    if final:
        out_specs.append(spec((t, LANES), lambda i: (0, i)))
        out_shape.append(shape((t, D), BF16))
    return pl.pallas_call(
        functools.partial(fwd_remote_body, rows // (t // 2), final),
        grid=(PAIRS,),
        in_specs=[
            SMEM_SPEC,
            spec((LANES, t), lambda i: (i, 0)),
            spec((rows, 2 * LANES), lambda i: (0, i)),
            spec((8, t), lambda i: (i, 0)),
            spec((LANES, t), lambda i: (i, 0)),
        ],
        out_specs=out_specs,
        out_shape=out_shape,
        name="attend_remote",
        **params((4 * 4 * t * rows * D, 8 * D * t + 4 * D * rows)),
    )(sc, qt, kv, st, acc)


def back_block(ops, kb, vb, kt, lo, hi, mask, dq_ref):
    qz, qn, doz, don, lse, delta = ops
    dk = None
    dv = None
    for h in range(2):
        s = dot(kb, qz[h][:, lo:hi])
        dp = dot(vb, doz[h][:, lo:hi])
        p = jnp.exp2(s * LC - lse[h][:, lo:hi])
        if mask is not None:
            p = jnp.where(mask, p, 0.0)
        ds = (p * (dp - delta[h][:, lo:hi])).astype(BF16)
        dv_h = dot(p.astype(BF16), don[h][lo:hi])
        dk_h = dot(ds, qn[h][lo:hi])
        rows = slice(h * HEAD_DIM, (h + 1) * HEAD_DIM)
        dq_ref[rows, lo:hi] += dot(kt[rows], ds)
        dv = dv_h if dv is None else dv + dv_h
        dk = dk_h if dk is None else dk + dk_h
    return dk, dv


def back_operands(qt_ref, q_ref, dot_ref, do_ref, st_ref):
    qt, q, do_t, do = qt_ref[...], q_ref[...], dot_ref[...], do_ref[...]
    return (
        [head_rows(qt, h) for h in range(2)],
        [head_lanes(q, h) for h in range(2)],
        [head_rows(do_t, h) for h in range(2)],
        [head_lanes(do, h) for h in range(2)],
        [st_ref[h : h + 1, :] for h in range(2)],
        [st_ref[4 + h : 5 + h, :] for h in range(2)],
    )


def bwd_local_body(
    sc_ref, qt_ref, q_ref, dot_ref, do_ref, st_in, a_ref, kv_ref, kvo_ref,
    st_ref, dq_ref, dkv_ref, dkvo_ref,
):
    t = qt_ref.shape[1]
    r = t // 2
    keys = kvo_ref.shape[0]
    st_ref[...] = st_in[...]
    prod = a_ref[...] * dot_ref[...].astype(F32)
    for h in range(2):
        st_ref[4 + h : 5 + h, :] = jnp.sum(
            prod[h * HEAD_DIM : (h + 1) * HEAD_DIM], axis=0, keepdims=True
        )
    ops = back_operands(qt_ref, q_ref, dot_ref, do_ref, st_ref)
    dq_ref[...] = jnp.zeros_like(dq_ref)
    kb, vb = kv_ref[:, :LANES], kv_ref[:, LANES:]
    kbo, vbo = kvo_ref[:, :LANES], kvo_ref[:, LANES:]
    kt, kto = kb.T, kbo.T
    own, cont = local_masks(sc_ref, r, keys, 0, t)
    if r % LANES == 0:
        dk, dv = back_block(ops, kb, vb, kt, 0, r, own[:, :r], dq_ref)
        dk2, dv2 = back_block(ops, kb, vb, kt, r, t, None, dq_ref)
        dk, dv = dk + dk2, dv + dv2
        dko, dvo = back_block(ops, kbo, vbo, kto, r, t, cont[:, r:], dq_ref)
    else:
        dk, dv = back_block(ops, kb, vb, kt, 0, t, own, dq_ref)
        dko, dvo = back_block(ops, kbo, vbo, kto, 0, t, cont, dq_ref)
    dkv_ref[:, :LANES] = dk * SCALE
    dkv_ref[:, LANES:] = dv
    dkvo_ref[:, :LANES] = dko * SCALE
    dkvo_ref[:, LANES:] = dvo


def bwd_remote_body(
    n, final, sc_ref, qt_ref, q_ref, dot_ref, do_ref, st_ref, dq_in, kv_ref, dq_ref, dkv_ref, *outs
):
    t = qt_ref.shape[1]
    r = t // 2
    me = sc_ref[0]
    ops = back_operands(qt_ref, q_ref, dot_ref, do_ref, st_ref)
    dq_ref[...] = dq_in[...]
    for j in range(n):
        block = sc_ref[3 + j]
        rows = slice(j * r, (j + 1) * r)

        def go(lo, mask):
            kb, vb = kv_ref[rows, :LANES], kv_ref[rows, LANES:]
            dk, dv = back_block(ops, kb, vb, kb.T, lo, t, mask, dq_ref)
            dkv_ref[rows, :LANES] = (dk * SCALE).astype(BF16)
            dkv_ref[rows, LANES:] = dv.astype(BF16)

        @pl.when(block == me)
        def _():
            dkv_ref[rows, :] = jnp.zeros((r, 2 * LANES), BF16)

        if r % LANES == 0:

            @pl.when(block < me)
            def _():
                go(0, None)

            @pl.when(block > me)
            def _():
                go(r, None)

        else:

            @pl.when(block != me)
            def _():
                col = lax.broadcasted_iota(jnp.int32, (r, t), 1)
                go(0, (col >= r) | (block < me))

    if final:
        outs[0][...] = dq_ref[...].T * SCALE


def q_specs(t):
    return [
        spec((LANES, t), lambda i: (i, 0)),
        spec((t, LANES), lambda i: (0, i)),
        spec((LANES, t), lambda i: (i, 0)),
        spec((t, LANES), lambda i: (0, i)),
        spec((8, t), lambda i: (i, 0)),
    ]


def bwd_local(sc, qt, q, do_t, do, st, att_t, kv_prompt, kv_own):
    t = qt.shape[1]
    keys = kv_own.shape[0]
    return pl.pallas_call(
        bwd_local_body,
        grid=(PAIRS,),
        in_specs=[SMEM_SPEC]
        + q_specs(t)
        + [
            spec((LANES, t), lambda i: (i, 0)),
            spec((t // 2, 2 * LANES), lambda i: (0, i)),
            spec((keys, 2 * LANES), lambda i: (0, i)),
        ],
        out_specs=[
            spec((8, t), lambda i: (i, 0)),
            spec((LANES, t), lambda i: (i, 0)),
            spec((t // 2, 2 * LANES), lambda i: (0, i)),
            spec((keys, 2 * LANES), lambda i: (0, i)),
        ],
        out_shape=[
            shape((8 * PAIRS, t), F32),
            shape((D, t), F32),
            shape((t // 2, 2 * D), F32),
            shape((keys, 2 * D), F32),
        ],
        name="attend_back_local",
        **params((10 * 4 * t * keys * D, 16 * D * t)),
    )(sc, qt, q, do_t, do, st, att_t, kv_prompt, kv_own)


def bwd_remote(sc, qt, q, do_t, do, st, dq, kv, final):
    t = qt.shape[1]
    rows = kv.shape[0]
    out_specs = [spec((LANES, t), lambda i: (i, 0)), spec((rows, 2 * LANES), lambda i: (0, i))]
    out_shape = [shape((D, t), F32), shape((rows, 2 * D), BF16)]
    if final:
        out_specs.append(spec((t, LANES), lambda i: (0, i)))
        out_shape.append(shape((t, D), F32))
    return pl.pallas_call(
        functools.partial(bwd_remote_body, rows // (t // 2), final),
        grid=(PAIRS,),
        in_specs=[SMEM_SPEC]
        + q_specs(t)
        + [spec((LANES, t), lambda i: (i, 0)), spec((rows, 2 * LANES), lambda i: (0, i))],
        out_specs=out_specs,
        out_shape=out_shape,
        name="attend_back_remote",
        **params((10 * 4 * t * rows * D, 16 * D * t + 8 * D * rows)),
    )(sc, qt, q, do_t, do, st, dq, kv)


def route_body(
    x_ref, att_ref, ow_ref, sw_ref, gain_ref, res_ref, rt_ref, tc_ref, tr_ref,
    h_ref, n_ref, pr_ref, xs_ref, ms_ref,
):
    t = x_ref.shape[0]
    step = pl.program_id(0)

    @pl.when(step == 0)
    def _():
        hidden = x_ref[...].astype(F32) + dot(att_ref[...], ow_ref[...])
        h_ref[...] = hidden
        scale = lax.rsqrt(jnp.mean(hidden * hidden, axis=-1, keepdims=True) + EPS)
        low = (hidden * scale * gain_ref[...]).astype(BF16)
        n_ref[...] = low
        z = dot(low, sw_ref[...])
        lane = lax.broadcasted_iota(jnp.int32, (t, LANES), 1)
        is_route = lane < EXPERTS + 4
        logits = jnp.where(is_route, z + res_ref[...], NEG)
        ex = jnp.exp(logits - jnp.max(logits, axis=-1, keepdims=True))
        probs = ex / jnp.sum(ex, axis=-1, keepdims=True)
        out = probs
        first = EXPERTS + 4
        for k in range(2):
            l0 = z[:, first + 2 * k : first + 2 * k + 1]
            l1 = z[:, first + 2 * k + 1 : first + 2 * k + 2]
            top = jnp.maximum(l0, l1)
            e0 = jnp.exp(l0 - top)
            e1 = jnp.exp(l1 - top)
            den = e0 + e1
            out = jnp.where(lane == first + 2 * k, e0 / den, out)
            out = jnp.where(lane == first + 2 * k + 1, e1 / den, out)
        for j in range(2):
            mix = jnp.sum(jnp.where(lane == rt_ref[:, j : j + 1], probs, 0.0), axis=-1, keepdims=True)
            out = jnp.where(lane == 16 + j, mix, out)
        pr_ref[...] = out

    slots = xs_ref.shape[0]
    base = step * slots
    slot = base + lax.broadcasted_iota(jnp.int32, (slots, t), 0)
    pick = (slot == tr_ref[0:1, :]) | (slot == tr_ref[1:2, :])
    xs_ref[...] = dot(pick.astype(BF16), n_ref[...]).astype(BF16)
    slot = base + lax.broadcasted_iota(jnp.int32, (t, slots), 1)
    mixes = jnp.where(slot == tc_ref[:, 0:1], pr_ref[:, 16:17], 0.0) + jnp.where(
        slot == tc_ref[:, 1:2], pr_ref[:, 17:18], 0.0
    )
    ms_ref[...] = jnp.sum(mixes, axis=0, keepdims=True)


def route_call(x, att, ow, sw, gain, res, rt, tc, tr, slots):
    t = x.shape[0]
    part = min(slots, 256)
    return pl.pallas_call(
        route_body,
        grid=(slots // part,),
        in_specs=[
            whole((t, D)), whole((t, D)), whole((D, D)), whole((D, LANES)), whole((1, D)),
            whole((t, LANES)), whole((t, 2)), whole((t, 2)), whole((2, t)),
        ],
        out_specs=[
            whole((t, D)), whole((t, D)), whole((t, LANES)),
            spec((part, D), lambda i: (i, 0)),
            spec((1, part), lambda i: (0, i)),
        ],
        out_shape=[
            shape((t, D), F32), shape((t, D), BF16), shape((t, LANES), F32),
            shape((slots, D), BF16), shape((1, slots), F32),
        ],
        name="route_dispatch",
        **params((2 * t * D * D + 2 * slots * t * D, 8 * t * D)),
    )(x, att, ow, sw, gain, res, rt, tc, tr)


def expert_fwd_body(x_ref, w_ref, o_ref, acc_ref):
    step = pl.program_id(0)
    x = x_ref[...]
    wide = w_ref.shape[-1]
    wg = w_ref[:, 0].reshape(D, wide)
    wu = w_ref[:, 1].reshape(D, wide)
    wd = w_ref[:, 2].reshape(D, wide)
    gate = dot(x, wg)
    up = dot(x, wu)
    act = (gate / (1.0 + jnp.exp(-gate)) * up).astype(BF16)
    out = dot_nt(act, wd)

    @pl.when(step == 0)
    def _():
        acc_ref[...] = out

    @pl.when(step > 0)
    def _():
        acc_ref[...] += out

    @pl.when(step == pl.num_programs(0) - 1)
    def _():
        o_ref[...] = acc_ref[...].astype(BF16)


def expert_fwd(xr, w):
    rows = xr.shape[0]
    shards, _, per, wide = w.shape
    part = min(wide, 256)
    return pl.pallas_call(
        expert_fwd_body,
        grid=(wide // part,),
        in_specs=[whole((rows, D)), spec((shards, 3, per, part), lambda i: (0, 0, 0, i))],
        out_specs=whole((rows, D)),
        out_shape=shape((rows, D), BF16),
        scratch_shapes=[pltpu.VMEM((rows, D), F32)],
        name="expert_forward",
        **params((6 * rows * D * wide, 6 * D * wide)),
    )(xr, w)


def expert_bwd_body(x_ref, g_ref, m_ref, w_ref, gi_ref, dw_ref, acc_ref, xt_ref, gl_ref, gt_ref):
    step = pl.program_id(0)

    @pl.when(step == 0)
    def _():
        low = (g_ref[...].astype(F32) * m_ref[...]).astype(BF16)
        gl_ref[...] = low
        gt_ref[...] = low.T
        xt_ref[...] = x_ref[...].T

    x = x_ref[...]
    g = gl_ref[...]
    shards, _, per, wide = w_ref.shape
    wg = w_ref[:, 0].reshape(D, wide)
    wu = w_ref[:, 1].reshape(D, wide)
    wd = w_ref[:, 2].reshape(D, wide)
    gate = dot(x, wg)
    up = dot(x, wu)
    sig = 1.0 / (1.0 + jnp.exp(-gate))
    silu = gate * sig
    act = (silu * up).astype(BF16)
    ga = dot(g, wd)
    d_gate = (ga * up * sig * (1.0 + gate * (1.0 - sig))).astype(BF16)
    d_up = (ga * silu).astype(BF16)
    gi = dot_nt(d_gate, wg) + dot_nt(d_up, wu)

    @pl.when(step == 0)
    def _():
        acc_ref[...] = gi

    @pl.when(step > 0)
    def _():
        acc_ref[...] += gi

    xt = xt_ref[...]
    dw_ref[:, 0] = dot(xt, d_gate).astype(BF16).reshape(shards, per, wide)
    dw_ref[:, 1] = dot(xt, d_up).astype(BF16).reshape(shards, per, wide)
    dw_ref[:, 2] = dot(gt_ref[...], act).astype(BF16).reshape(shards, per, wide)

    @pl.when(step == pl.num_programs(0) - 1)
    def _():
        gi_ref[...] = acc_ref[...].astype(BF16)


def expert_bwd(xr, gr, mix, w):
    rows = xr.shape[0]
    shards, _, per, wide = w.shape
    part = min(wide, 256)
    wspec = spec((shards, 3, per, part), lambda i: (0, 0, 0, i))
    return pl.pallas_call(
        expert_bwd_body,
        grid=(wide // part,),
        in_specs=[whole((rows, D)), whole((rows, D)), whole((rows, 1)), wspec],
        out_specs=[whole((rows, D)), wspec],
        out_shape=[shape((rows, D), BF16), shape(w.shape, BF16)],
        scratch_shapes=[
            pltpu.VMEM((rows, D), F32),
            pltpu.VMEM((D, rows), BF16),
            pltpu.VMEM((rows, D), BF16),
            pltpu.VMEM((D, rows), BF16),
        ],
        name="expert_backward",
        **params((16 * rows * D * wide, 12 * D * wide)),
    )(xr, gr, mix, w)


def mix_body(
    h_ref, g_ref, pr_ref, rt_ref, tc_ref, ret_ref, n_ref, sw_ref, rows_ref,
    out_ref, gn_ref, gl_ref, gs_ref,
):
    t = h_ref.shape[0]
    slots = ret_ref.shape[0]
    hidden = h_ref[...]
    g16 = g_ref[...]
    g = g16.astype(F32)
    pr = pr_ref[...]
    scale = lax.rsqrt(jnp.mean(hidden * hidden, axis=-1, keepdims=True) + EPS)
    normed = hidden * scale * rows_ref[2:3, :]
    lane = lax.broadcasted_iota(jnp.int32, (t, LANES), 1)
    slot = lax.broadcasted_iota(jnp.int32, (t, slots), 1)
    first = EXPERTS + 4
    ret = ret_ref[...]
    c0 = [pr[:, first + 2 * k : first + 2 * k + 1] for k in range(2)]
    c1 = [pr[:, first + 2 * k + 1 : first + 2 * k + 2] for k in range(2)]
    total = hidden
    s = jnp.zeros((t, LANES), F32)
    coef = jnp.zeros((t, 1), F32)
    weight = [jnp.zeros((t, 1), F32) for _ in range(2)]
    for j in range(2):
        route = rt_ref[:, j : j + 1]
        mix = pr[:, 16 + j : 17 + j]
        branch = dot((slot == tc_ref[:, j : j + 1]).astype(BF16), ret)
        keep = jnp.where(route == EXPERTS + 1, 1.0, 0.0)
        for k in range(2):
            here = jnp.where(route == EXPERTS + 2 + k, 1.0, 0.0)
            keep = keep + here * c0[k]
            weight[k] = weight[k] + here * mix
            branch = branch + (here * c1[k]) * rows_ref[k : k + 1, :]
        branch = branch + keep * normed
        coef = coef + mix * keep
        total = total + mix * branch
        gp = jnp.sum(g * branch, axis=-1, keepdims=True)
        s = s + jnp.where(lane == route, gp, 0.0)
    out_ref[...] = total.astype(BF16)
    probs = jnp.where(lane < first, pr, 0.0)
    d_logits = probs * (s - jnp.sum(probs * s, axis=-1, keepdims=True))
    gl_ref[...] = d_logits
    dz = d_logits
    dvec = jnp.zeros((t, LANES), F32)
    g_dot_n = jnp.sum(g * normed, axis=-1, keepdims=True)
    for k in range(2):
        d0 = weight[k] * g_dot_n
        d1 = weight[k] * jnp.sum(g * rows_ref[k : k + 1, :], axis=-1, keepdims=True)
        mean = c0[k] * d0 + c1[k] * d1
        dz = jnp.where(lane == first + 2 * k, c0[k] * (d0 - mean), dz)
        dz = jnp.where(lane == first + 2 * k + 1, c1[k] * (d1 - mean), dz)
        dvec = jnp.where(lane == 16 + k, weight[k] * c1[k], dvec)
    hi, lo = split_hi_lo(dz)
    sw = sw_ref[...]
    gn_ref[...] = coef * g + (dot_nt(hi, sw) + dot_nt(lo, sw))
    nt = n_ref[...].T
    gt = g16.T
    vhi, vlo = split_hi_lo(dvec)
    gs = dot(nt, hi) + dot(nt, lo) + dot(gt, vhi) + dot(gt, vlo)

    @pl.when(pl.program_id(0) == 0)
    def _():
        gs_ref[...] = gs

    @pl.when(pl.program_id(0) > 0)
    def _():
        gs_ref[...] += gs


def mix_call(hidden, g, pr, rt, tc, ret, low, sw, rows):
    t = hidden.shape[0]
    half = t // 2
    slots = ret.shape[0]
    tile = spec((half, D), lambda i: (i, 0))
    lane_tile = spec((half, LANES), lambda i: (i, 0))
    pair = spec((half, 2), lambda i: (i, 0))
    return pl.pallas_call(
        mix_body,
        grid=(2,),
        in_specs=[
            tile, tile, lane_tile, pair, pair, whole((slots, D)), tile, whole((D, LANES)),
            whole((8, D)),
        ],
        out_specs=[tile, tile, lane_tile, whole((D, LANES))],
        out_shape=[
            shape((t, D), BF16), shape((t, D), F32), shape((t, LANES), F32), shape((D, LANES), F32),
        ],
        name="mixture",
        **params((4 * t * slots * D, 12 * t * D)),
    )(hidden, g, pr, rt, tc, ret, low, sw, rows)


def norm_back_body(
    h_ref, g_ref, gn_ref, tc_ref, ret_ref, rows_ref, ow_ref, att_ref,
    gh_ref, do_ref, dot_ref, gow_ref, gg_ref,
):
    t = h_ref.shape[0]
    slots = ret_ref.shape[0]
    hidden = h_ref[...]
    slot = lax.broadcasted_iota(jnp.int32, (t, slots), 1)
    pick = (slot == tc_ref[:, 0:1]) | (slot == tc_ref[:, 1:2])
    gn = gn_ref[...] + dot(pick.astype(BF16), ret_ref[...])
    q = lax.rsqrt(jnp.mean(hidden * hidden, axis=-1, keepdims=True) + EPS)
    u = gn * rows_ref[2:3, :]
    mean = jnp.mean(u * hidden, axis=-1, keepdims=True)
    gh = g_ref[...].astype(F32) + q * u - hidden * (q * q * q * mean)
    gh_ref[...] = gh
    gb = gh.astype(BF16)
    d_out = dot_nt(gb, ow_ref[...])
    do_ref[...] = d_out.astype(BF16)
    dot_ref[...] = d_out.T.astype(BF16)
    gow = dot(att_ref[...].T, gb)
    gain = jnp.sum(gn * hidden * q, axis=0, keepdims=True)

    @pl.when(pl.program_id(0) == 0)
    def _():
        gow_ref[...] = gow
        gg_ref[...] = jnp.broadcast_to(gain, gg_ref.shape)

    @pl.when(pl.program_id(0) > 0)
    def _():
        gow_ref[...] += gow
        gg_ref[...] += jnp.broadcast_to(gain, gg_ref.shape)


def norm_back_call(hidden, g, gn, tc, ret, rows, ow, att):
    t = hidden.shape[0]
    half = t // 2 if (t // 2) % LANES == 0 else t
    slots = ret.shape[0]
    tile = spec((half, D), lambda i: (i, 0))
    return pl.pallas_call(
        norm_back_body,
        grid=(t // half,),
        in_specs=[
            tile, tile, tile, spec((half, 2), lambda i: (i, 0)), whole((slots, D)), whole((8, D)),
            whole((D, D)), tile,
        ],
        out_specs=[tile, tile, spec((D, half), lambda i: (0, i)), whole((D, D)), whole((8, D))],
        out_shape=[
            shape((t, D), F32), shape((t, D), BF16), shape((D, t), BF16), shape((D, D), F32),
            shape((8, D), F32),
        ],
        name="norm_two_back",
        **params((2 * t * slots * D + 4 * t * D * D, 16 * t * D)),
    )(hidden, g, gn, tc, ret, rows, ow, att)


def qkv_back_body(
    x_ref, n_ref, dq_ref, dkv_ref, gh_ref, c_ref, s_ref, w_ref, gain_ref,
    gi_ref, gw_ref, gg_ref, gq_ref,
):
    cosine = c_ref[...]
    sine = s_ref[...]
    for i in range(PAIRS):
        cols = slice(i * LANES, (i + 1) * LANES)
        v = dq_ref[:, cols]
        gq_ref[:, cols] = (v * cosine - partner(v) * sine).astype(BF16)
        v = dkv_ref[:, 2 * i * LANES : (2 * i + 1) * LANES]
        gq_ref[:, D + i * LANES : D + (i + 1) * LANES] = (v * cosine - partner(v) * sine).astype(BF16)
        v = dkv_ref[:, (2 * i + 1) * LANES : (2 * i + 2) * LANES]
        gq_ref[:, 2 * D + i * LANES : 2 * D + (i + 1) * LANES] = v.astype(BF16)
    gq = gq_ref[...]
    gn = dot_nt(gq, w_ref[...])
    x = x_ref[...].astype(F32)
    q = lax.rsqrt(jnp.mean(x * x, axis=-1, keepdims=True) + EPS)
    u = gn * gain_ref[...]
    mean = jnp.mean(u * x, axis=-1, keepdims=True)
    gi_ref[...] = gh_ref[...] + q * u - x * (q * q * q * mean)
    gain = jnp.sum(gn * x * q, axis=0, keepdims=True)
    nt = n_ref[...].T
    start = pl.program_id(0) == 0
    for c in range(3):
        cols = slice(c * D, (c + 1) * D)
        gw = dot(nt, gq[:, cols])

        @pl.when(start)
        def _():
            gw_ref[:, cols] = gw

        @pl.when(jnp.logical_not(start))
        def _():
            gw_ref[:, cols] += gw

    @pl.when(start)
    def _():
        gg_ref[...] = jnp.broadcast_to(gain, gg_ref.shape)

    @pl.when(jnp.logical_not(start))
    def _():
        gg_ref[...] += jnp.broadcast_to(gain, gg_ref.shape)


def qkv_back_call(x, low, dq, dkv, gh, cosine, sine, pack, gain):
    t = x.shape[0]
    half = t // 2
    tile = spec((half, D), lambda i: (i, 0))
    lane_tile = spec((half, LANES), lambda i: (i, 0))
    return pl.pallas_call(
        qkv_back_body,
        grid=(2,),
        in_specs=[
            tile, tile, tile, spec((half, 2 * D), lambda i: (i, 0)), tile, lane_tile, lane_tile,
            whole((D, 3 * D)), whole((1, D)),
        ],
        out_specs=[tile, whole((D, 3 * D)), whole((8, D))],
        out_shape=[shape((t, D), F32), shape((D, 3 * D), F32), shape((8, D), F32)],
        scratch_shapes=[pltpu.VMEM((half, 3 * D), BF16)],
        name="qkv_back",
        **params((4 * t * D * 3 * D, 20 * t * D)),
    )(x, low, dq, dkv, gh, cosine, sine, pack, gain)


def rotation_tables(position):
    half = HEAD_DIM // 2
    frequency = 10000.0 ** (-jnp.arange(half, dtype=F32) / half)
    angles = position[:, None] * frequency[None, :]
    cosine, sine = jnp.cos(angles), jnp.sin(angles)
    return (
        jnp.concatenate([cosine] * 4, axis=1),
        jnp.concatenate([-sine, sine, -sine, sine], axis=1),
    )


def to_rows(array):
    return jnp.transpose(array, (1, 0, 2)).reshape(2 * array.shape[0], array.shape[2])


def from_rows(array):
    r = array.shape[0] // 2
    return jnp.transpose(array.reshape(2, r, array.shape[1]), (1, 0, 2))


def per_device(
    hidden_in, cotangent, gate_residual, routes, groups, lengths, attn_gain, qkv_weight, out_weight,
    ffn_gain, router_weight, const_proj, const_vec, gate_weight, up_weight, down_weight,
):
    del groups
    r = hidden_in.shape[0]
    t = 2 * r
    capacity = r // 2
    owners = lax.axis_size("expert")
    copies = owners // EXPERTS
    slots = EXPERTS * capacity
    me = lax.axis_index("expert")
    per_cont = max(CONT_LEN // r, 1)

    small = jnp.concatenate(
        [
            router_weight, const_proj, const_vec, attn_gain[:, None], ffn_gain[:, None],
            jnp.zeros((attn_gain.shape[0], LANES - 20), BF16),
        ],
        axis=1,
    )
    pack = lax.all_gather(
        jnp.concatenate([qkv_weight, out_weight, small], axis=1), ALL_AXES, axis=0, tiled=True
    )
    out_w = pack[:, 3 * D : 4 * D]
    small_w = pack[:, 4 * D :]
    small_rows = jnp.transpose(small_w[:, 16:24]).astype(F32)
    gain_one = small_rows[2:3]
    rows_two = jnp.concatenate([small_rows[0:2], small_rows[3:4], small_rows[3:8]], axis=0)
    gain_two = small_rows[3:4]

    index = jnp.arange(r, dtype=jnp.int32)
    row_ids = me * r + index
    position = jnp.concatenate([row_ids, PROMPT + row_ids % CONT_LEN]).astype(F32)
    cosine, sine = rotation_tables(position)
    cont = (me * r) // CONT_LEN
    length = lax.dynamic_slice(lengths, (cont,), (1,))
    header = jnp.stack([me, (me * r) % CONT_LEN]).astype(jnp.int32)
    header = jnp.concatenate([header, length.astype(jnp.int32)])
    sc = jnp.concatenate([header, jnp.arange(owners, dtype=jnp.int32)])

    picked = to_rows(routes)
    flat = jnp.transpose(picked).reshape(2 * t)
    hot = flat[:, None] == jnp.arange(EXPERTS, dtype=jnp.int32)[None, :]
    earlier = jnp.arange(2 * t)[:, None] > jnp.arange(2 * t)[None, :]
    before = jnp.dot(earlier.astype(BF16), hot.astype(BF16), preferred_element_type=F32)
    slot_index = jnp.sum(jnp.where(hot, before, 0.0), axis=1).astype(jnp.int32)
    target = jnp.where(flat < EXPERTS, flat * capacity + slot_index, -1)
    target_rows = target.reshape(2, t)
    target_cols = jnp.transpose(target_rows)

    def to_owners(rows):
        w = rows.shape[-1]
        shaped = rows.reshape(EXPERTS, 1, capacity, w)
        return jnp.broadcast_to(shaped, (EXPERTS, copies, capacity, w)).reshape(owners, capacity, w)

    def exchange(rows):
        got = lax.all_to_all(rows, "expert", split_axis=0, concat_axis=0, tiled=True)
        return got.reshape(owners * got.shape[1], got.shape[2])

    def from_owners(rows):
        got = exchange(rows.reshape(owners, capacity, D))
        if copies == 1:
            return got
        got = got.reshape(EXPERTS, copies, capacity, D).astype(F32)
        return jnp.sum(got, axis=1).reshape(slots, D).astype(BF16)

    x = to_rows(hidden_in)
    g = to_rows(cotangent)
    slot_ids = jnp.arange(slots, dtype=jnp.int32)[:, None]
    placement = (slot_ids == target_rows[0][None, :]) | (slot_ids == target_rows[1][None, :])
    g_send = jnp.dot(placement.astype(BF16), g, preferred_element_type=F32).astype(BF16)
    g_got = exchange(to_owners(g_send))

    low_one, q, q_t, kv = qkv_call(x, gain_one, pack, cosine, sine)
    kv_prompt = kv[:r]
    kv_all = lax.all_gather(kv_prompt, "expert", axis=0, tiled=True)
    if per_cont == 1:
        kv_own = kv[r:]
    else:
        cont_groups = [
            [c * per_cont + i for i in range(per_cont)] for c in range(owners // per_cont)
        ]
        kv_own = lax.all_gather(
            kv[r:], "expert", axis=0, tiled=True, axis_index_groups=cont_groups
        )
    weights = lax.all_gather(
        jnp.stack([gate_weight, up_weight, down_weight]), "dp", axis=0, tiled=False
    )
    st, acc = fwd_local(sc, q_t, kv_prompt, kv_own)
    st, att_t, att = fwd_remote(sc, q_t, kv_all, st, acc, True)

    res = jnp.pad(to_rows(gate_residual), ((0, 0), (0, LANES - EXPERTS - 4)))
    hidden, low_two, pr, x_send, mix_send = route_call(
        x, att, out_w, small_w, gain_two, res, picked, target_cols, target_rows, slots
    )
    x_got = exchange(to_owners(x_send))
    mix_got = lax.all_to_all(
        to_owners(mix_send.reshape(EXPERTS, capacity, 1)).reshape(owners, capacity),
        "expert", split_axis=0, concat_axis=0, tiled=True,
    ).reshape(owners * capacity, 1)
    out_back = from_owners(expert_fwd(x_got, weights))
    grad_in, grad_w = expert_bwd(x_got, g_got, mix_got, weights)
    in_back = from_owners(grad_in)
    output, gn, grad_logits, grad_small = mix_call(
        hidden, g, pr, picked, target_cols, out_back, low_two, small_w, rows_two
    )
    grad_expert = lax.psum_scatter(
        grad_w.reshape(-1, grad_w.shape[-1]), "dp", scatter_dimension=0, tiled=True
    ).astype(F32)
    gh, d_att, d_att_t, grad_ow, gg_two = norm_back_call(
        hidden, g, gn, target_cols, in_back, rows_two, out_w, att
    )

    st, dq_t, dkv_own_prompt, dkv_cont = bwd_local(
        sc, q_t, q, d_att_t, d_att, st, att_t, kv_prompt, kv_own
    )
    _, dkv_all, dq = bwd_remote(sc, q_t, q, d_att_t, d_att, st, dq_t, kv_all, True)
    dkv_prompt = lax.psum_scatter(dkv_all, "expert", scatter_dimension=0, tiled=True)
    if per_cont > 1:
        dkv_cont = lax.psum_scatter(
            dkv_cont, "expert", scatter_dimension=0, tiled=True, axis_index_groups=cont_groups
        )
    dkv = jnp.concatenate([dkv_prompt.astype(F32) + dkv_own_prompt, dkv_cont], axis=0)
    grad_input, grad_qkv, gg_one = qkv_back_call(
        x, low_one, dq, dkv, gh, cosine, sine, pack, gain_one
    )

    last = jnp.concatenate(
        [
            grad_small[:, :18], jnp.transpose(gg_one[0:1]), jnp.transpose(gg_two[0:1]),
            jnp.zeros((D, LANES - 20), F32),
        ],
        axis=1,
    )
    dense = lax.psum_scatter(
        jnp.concatenate([grad_qkv, grad_ow, last], axis=1).astype(BF16),
        ALL_AXES, scatter_dimension=0, tiled=True,
    ).astype(F32)
    tail = dense[:, 4 * D :]
    per = grad_expert.shape[0] // 3
    return (
        from_rows(output),
        from_rows(grad_input),
        from_rows(grad_logits)[:, :, : EXPERTS + 4],
        tail[:, 18],
        dense[:, : 3 * D],
        dense[:, 3 * D : 4 * D],
        tail[:, 19],
        tail[:, :12],
        tail[:, 12:16],
        tail[:, 16:18],
        grad_expert[:per],
        grad_expert[per : 2 * per],
        grad_expert[2 * per :],
    )


def solution(mesh):
    rows = P(ALL_AXES, None, None)
    flat = P(ALL_AXES)
    mat = P(ALL_AXES, None)
    expert = P("dp", "expert")
    in_specs = (
        rows, rows, rows, rows, P("dp"), P("dp"), flat, mat, mat, flat, mat, mat, mat,
        expert, expert, expert,
    )
    out_specs = (
        rows, rows, rows, flat, mat, mat, flat, mat, mat, mat, expert, expert, expert,
    )
    return jax.shard_map(
        per_device, mesh=mesh, in_specs=in_specs, out_specs=out_specs, check_vma=False
    )
```

```python
import functools

import jax
import jax.numpy as jnp
from jax import lax
from jax.experimental import pallas as pl
from jax.experimental.pallas import tpu as pltpu
from jax.sharding import PartitionSpec as P

D = 768
HEADS = 12
HEAD_DIM = 64
PAIRS = 6
EXPERTS = 8
CONT_LEN = 256
PROMPT = 2048
LANES = 128
EPS = 1e-06
NEG = -1e30
LOG2E = 1.4426950408889634
SCALE = float(HEAD_DIM) ** (-0.5)
LC = SCALE * LOG2E
F32 = jnp.float32
BF16 = jnp.bfloat16
ALL_AXES = ("dp", "expert")
VMEM_LIMIT = 60 * 1024 * 1024


def dot(a, b):
    return jnp.dot(a, b, preferred_element_type=F32)


def dot_nt(a, b):
    return lax.dot_general(a, b, (((1,), (1,)), ((), ())), preferred_element_type=F32)


def dot_tn(a, b):
    return lax.dot_general(a, b, (((0,), (0,)), ((), ())), preferred_element_type=F32)


def split_hi_lo(v):
    hi = v.astype(BF16)
    return hi, (v - hi.astype(F32)).astype(BF16)


def params(cost=None):
    return dict(
        compiler_params=pltpu.CompilerParams(vmem_limit_bytes=VMEM_LIMIT),
        cost_estimate=None if cost is None else pl.CostEstimate(
            flops=int(cost[0]), bytes_accessed=int(cost[1]), transcendentals=0
        ),
    )


def shape(dims, dtype):
    return jax.ShapeDtypeStruct(tuple(dims), dtype)


def spec(block, index):
    return pl.BlockSpec(tuple(block), index)


def whole(dims):
    return pl.BlockSpec(tuple(dims), lambda *_: (0,) * len(dims))


SMEM_SPEC = pl.BlockSpec(memory_space=pltpu.SMEM)


def partner(v):
    lane = lax.broadcasted_iota(jnp.int32, v.shape, 1)
    return jnp.where((lane & 63) < 32, pltpu.roll(v, 96, 1), pltpu.roll(v, 32, 1))


def qkv_body(x_ref, gain_ref, wq_ref, wk_ref, wv_ref, c_ref, s_ref, n_ref, q_ref, qt_ref, kv_ref):
    @pl.when(pl.program_id(0) == 0)
    def _():
        x = x_ref[...].astype(F32)
        scale = lax.rsqrt(jnp.mean(x * x, axis=-1, keepdims=True) + EPS)
        n_ref[...] = (x * scale * gain_ref[...]).astype(BF16)

    n = n_ref[...]
    cosine = c_ref[...]
    sine = s_ref[...]
    kv = dot(n, jnp.concatenate([wk_ref[...], wv_ref[...]], axis=1))
    k = kv[:, :LANES]
    kv_ref[:, :LANES] = (k * cosine + partner(k) * sine).astype(BF16)
    kv_ref[:, LANES:] = kv[:, LANES:].astype(BF16)
    q = dot(n, wq_ref[...])
    q = q * cosine + partner(q) * sine
    q_ref[...] = q.astype(BF16)
    qt_ref[...] = q.T.astype(BF16)


def qkv_call(x, gain, pack, cosine, sine):
    t = x.shape[0]
    return pl.pallas_call(
        qkv_body,
        grid=(PAIRS,),
        in_specs=[
            whole((t, D)),
            whole((1, D)),
            spec((D, LANES), lambda i: (0, i)),
            spec((D, LANES), lambda i: (0, PAIRS + i)),
            spec((D, LANES), lambda i: (0, 2 * PAIRS + i)),
            whole((t, LANES)),
            whole((t, LANES)),
        ],
        out_specs=[
            whole((t, D)),
            spec((t, LANES), lambda i: (0, i)),
            spec((LANES, t), lambda i: (i, 0)),
            spec((t, 2 * LANES), lambda i: (0, i)),
        ],
        out_shape=[
            shape((t, D), BF16),
            shape((t, D), BF16),
            shape((D, t), BF16),
            shape((t, 2 * D), BF16),
        ],
        name="qkv_rope",
        **params((2 * t * D * 3 * D, 6 * D * D)),
    )(x, gain, pack, pack, pack, cosine, sine)


def head_rows(v, h):
    row = lax.broadcasted_iota(jnp.int32, v.shape, 0)
    return jnp.where(row // HEAD_DIM == h, v, jnp.zeros_like(v))


def head_lanes(v, h):
    lane = lax.broadcasted_iota(jnp.int32, v.shape, 1)
    return jnp.where(lane // HEAD_DIM == h, v, jnp.zeros_like(v))


def attend_update(qz, kb, vt, lo, hi, mask, st_ref, a_ref, first):
    for h in range(2):
        s = dot(kb, qz[h][:, lo:hi])
        if mask is not None:
            s = jnp.where(mask, s, NEG)
        top = jnp.max(s, axis=0, keepdims=True)
        rows = slice(h * HEAD_DIM, (h + 1) * HEAD_DIM)
        if first:
            p = jnp.exp2((s - top) * LC)
            st_ref[h : h + 1, lo:hi] = top
            st_ref[2 + h : 3 + h, lo:hi] = jnp.sum(p, axis=0, keepdims=True)
            a_ref[rows, lo:hi] = dot(vt[rows], p.astype(BF16))
        else:
            old = st_ref[h : h + 1, lo:hi]
            new = jnp.maximum(old, top)
            alpha = jnp.exp2((old - new) * LC)
            p = jnp.exp2((s - new) * LC)
            st_ref[h : h + 1, lo:hi] = new
            st_ref[2 + h : 3 + h, lo:hi] = st_ref[2 + h : 3 + h, lo:hi] * alpha + jnp.sum(
                p, axis=0, keepdims=True
            )
            a_ref[rows, lo:hi] = a_ref[rows, lo:hi] * alpha + dot(vt[rows], p.astype(BF16))


def local_masks(sc_ref, r, keys, lo, hi):
    cpos = sc_ref[1]
    length = sc_ref[2]
    col = lo + lax.broadcasted_iota(jnp.int32, (r, hi - lo), 1)
    row = lax.broadcasted_iota(jnp.int32, (r, hi - lo), 0)
    own = (row <= col) | (col >= r)
    col = lo + lax.broadcasted_iota(jnp.int32, (keys, hi - lo), 1)
    row = lax.broadcasted_iota(jnp.int32, (keys, hi - lo), 0)
    cont = (col >= r) & (row <= cpos + col - r) & (row < length)
    return own, cont


def fwd_local_body(sc_ref, qt_ref, kv_ref, kvo_ref, st_ref, a_ref):
    t = qt_ref.shape[1]
    r = t // 2
    keys = kvo_ref.shape[0]
    qt = qt_ref[...]
    qz = [head_rows(qt, h) for h in range(2)]
    kb = kv_ref[:, :LANES]
    vt = kv_ref[:, LANES:].T
    kbo = kvo_ref[:, :LANES]
    vto = kvo_ref[:, LANES:].T
    st_ref[...] = jnp.zeros_like(st_ref)
    own, cont = local_masks(sc_ref, r, keys, 0, t)
    if r % LANES == 0:
        attend_update(qz, kb, vt, 0, r, own[:, :r], st_ref, a_ref, True)
        attend_update(qz, kb, vt, r, t, None, st_ref, a_ref, True)
        attend_update(qz, kbo, vto, r, t, cont[:, r:], st_ref, a_ref, False)
    else:
        attend_update(qz, kb, vt, 0, t, own, st_ref, a_ref, True)
        attend_update(qz, kbo, vto, 0, t, cont, st_ref, a_ref, False)


def halves_value(a_ref, b_ref):
    return jnp.where(pl.program_id(0) < PAIRS // 2, a_ref[...], b_ref[...])


def fwd_remote_body(offsets, count, halves, final, sc_ref, qt_ref, *refs):
    kv_refs, refs = refs[:count], refs[count:]
    st_in, a_in, st_ref, a_ref = refs[:4]
    t = qt_ref.shape[1]
    r = t // 2
    me = sc_ref[0]
    qt = qt_ref[...]
    qz = [head_rows(qt, h) for h in range(2)]
    st_ref[...] = st_in[...]
    a_ref[...] = a_in[...]
    for j, offset in enumerate(offsets):
        block = sc_ref[3 + offset]

        def go(lo, mask):
            if halves:
                kv = halves_value(*kv_refs)
            elif len(kv_refs) == len(offsets):
                kv = kv_refs[j][...]
            else:
                kv = kv_refs[0][j * r : (j + 1) * r, :]
            attend_update(qz, kv[:, :LANES], kv[:, LANES:].T, lo, t, mask, st_ref, a_ref, False)

        if r % LANES == 0:

            @pl.when(block < me)
            def _():
                go(0, None)

            @pl.when(block > me)
            def _():
                go(r, None)

        else:

            @pl.when(block != me)
            def _():
                col = lax.broadcasted_iota(jnp.int32, (r, t), 1)
                go(0, (col >= r) | (block < me))

    if final:
        low_ref = refs[4]
        for h in range(2):
            rows = slice(h * HEAD_DIM, (h + 1) * HEAD_DIM)
            total = st_ref[2 + h : 3 + h, :]
            a_ref[rows, :] = a_ref[rows, :] / total
            st_ref[h : h + 1, :] = st_ref[h : h + 1, :] * LC + jnp.log2(total)
        low_ref[...] = a_ref[...].T.astype(BF16)


def kv_specs(kvs, halves):
    if halves:
        r = kvs[0].shape[0]
        return [
            spec((r, 2 * LANES), lambda i: (0, jnp.minimum(i, PAIRS // 2 - 1))),
            spec((r, 2 * LANES), lambda i: (0, jnp.maximum(i - PAIRS // 2, 0))),
        ]
    return [spec((kv.shape[0], 2 * LANES), lambda i: (0, i)) for kv in kvs]


def fwd_local(sc, qt, kv_prompt, kv_own):
    t = qt.shape[1]
    keys = kv_own.shape[0]
    return pl.pallas_call(
        fwd_local_body,
        grid=(PAIRS,),
        in_specs=[
            SMEM_SPEC,
            spec((LANES, t), lambda i: (i, 0)),
            spec((t // 2, 2 * LANES), lambda i: (0, i)),
            spec((keys, 2 * LANES), lambda i: (0, i)),
        ],
        out_specs=[spec((8, t), lambda i: (i, 0)), spec((LANES, t), lambda i: (i, 0))],
        out_shape=[shape((8 * PAIRS, t), F32), shape((D, t), F32)],
        name="attend_local",
        **params((4 * 4 * t * keys * D, 4 * D * t)),
    )(sc, qt, kv_prompt, kv_own)


def fwd_remote(sc, qt, kvs, offsets, st, acc, halves=False, final=False):
    t = qt.shape[1]
    rows = len(offsets) * (t // 2)
    out_specs = [spec((8, t), lambda i: (i, 0)), spec((LANES, t), lambda i: (i, 0))]
    out_shape = [shape((8 * PAIRS, t), F32), shape((D, t), F32)]
    if final:
        out_specs.append(spec((t, LANES), lambda i: (0, i)))
        out_shape.append(shape((t, D), BF16))
    return pl.pallas_call(
        functools.partial(fwd_remote_body, tuple(offsets), len(kvs), halves, final),
        grid=(PAIRS,),
        in_specs=[SMEM_SPEC, spec((LANES, t), lambda i: (i, 0))]
        + kv_specs(kvs, halves)
        + [spec((8, t), lambda i: (i, 0)), spec((LANES, t), lambda i: (i, 0))],
        out_specs=out_specs,
        out_shape=out_shape,
        name="attend_remote",
        **params((4 * 4 * t * rows * D, 8 * D * t + 4 * D * rows)),
    )(sc, qt, *kvs, st, acc)


def back_block(ops, kb, vb, kt, lo, hi, mask, dq_ref):
    qz, qn, doz, don, lse, delta = ops
    dk = None
    dv = None
    for h in range(2):
        s = dot(kb, qz[h][:, lo:hi])
        dp = dot(vb, doz[h][:, lo:hi])
        p = jnp.exp2(s * LC - lse[h][:, lo:hi])
        if mask is not None:
            p = jnp.where(mask, p, 0.0)
        ds = (p * (dp - delta[h][:, lo:hi])).astype(BF16)
        dv_h = dot(p.astype(BF16), don[h][lo:hi])
        dk_h = dot(ds, qn[h][lo:hi])
        rows = slice(h * HEAD_DIM, (h + 1) * HEAD_DIM)
        dq_ref[rows, lo:hi] += dot(kt[rows], ds)
        dv = dv_h if dv is None else dv + dv_h
        dk = dk_h if dk is None else dk + dk_h
    return dk, dv


def back_operands(qt_ref, q_ref, dot_ref, do_ref, st_ref):
    qt, q, do_t, do = qt_ref[...], q_ref[...], dot_ref[...], do_ref[...]
    return (
        [head_rows(qt, h) for h in range(2)],
        [head_lanes(q, h) for h in range(2)],
        [head_rows(do_t, h) for h in range(2)],
        [head_lanes(do, h) for h in range(2)],
        [st_ref[h : h + 1, :] for h in range(2)],
        [st_ref[4 + h : 5 + h, :] for h in range(2)],
    )


def bwd_local_body(
    sc_ref, qt_ref, q_ref, dot_ref, do_ref, st_ref, dq_in, kv_ref, kvo_ref,
    out_ref, dkv_ref, dkvo_ref, dq_ref,
):
    t = qt_ref.shape[1]
    r = t // 2
    keys = kvo_ref.shape[0]
    ops = back_operands(qt_ref, q_ref, dot_ref, do_ref, st_ref)
    dq_ref[...] = dq_in[...]
    kb, vb = kv_ref[:, :LANES], kv_ref[:, LANES:]
    kbo, vbo = kvo_ref[:, :LANES], kvo_ref[:, LANES:]
    kt, kto = kb.T, kbo.T
    own, cont = local_masks(sc_ref, r, keys, 0, t)
    if r % LANES == 0:
        dk, dv = back_block(ops, kb, vb, kt, 0, r, own[:, :r], dq_ref)
        dk2, dv2 = back_block(ops, kb, vb, kt, r, t, None, dq_ref)
        dk, dv = dk + dk2, dv + dv2
        dko, dvo = back_block(ops, kbo, vbo, kto, r, t, cont[:, r:], dq_ref)
    else:
        dk, dv = back_block(ops, kb, vb, kt, 0, t, own, dq_ref)
        dko, dvo = back_block(ops, kbo, vbo, kto, 0, t, cont, dq_ref)
    dkv_ref[:, :LANES] = dk * SCALE
    dkv_ref[:, LANES:] = dv
    dkvo_ref[:, :LANES] = dko * SCALE
    dkvo_ref[:, LANES:] = dvo
    out_ref[...] = dq_ref[...].T * SCALE


def bwd_remote_body(
    offsets, count, halves, first, dtype, sc_ref, qt_ref, q_ref, dot_ref, do_ref, st_in, *refs
):
    t = qt_ref.shape[1]
    r = t // 2
    me = sc_ref[0]
    kv_refs, refs = refs[:count], refs[count:]
    src, refs = refs[0], refs[1:]
    dq_ref, refs = refs[0], refs[1:]
    out_refs, refs = refs[:count], refs[count:]
    if first:
        st_ref, refs = refs[0], refs[1:]
        st_ref[...] = st_in[...]
        prod = src[...] * dot_ref[...].astype(F32)
        for h in range(2):
            st_ref[4 + h : 5 + h, :] = jnp.sum(
                prod[h * HEAD_DIM : (h + 1) * HEAD_DIM], axis=0, keepdims=True
            )
        dq_ref[...] = jnp.zeros_like(dq_ref)
    else:
        st_ref = st_in
        dq_ref[...] = src[...]
    ops = back_operands(qt_ref, q_ref, dot_ref, do_ref, st_ref)
    split = len(offsets) != count and not halves

    def store(j, dk, dv):
        if halves:
            for part in range(2):

                @pl.when((pl.program_id(0) < PAIRS // 2) == (part == 0))
                def _():
                    out_refs[part][:, :LANES] = dk
                    out_refs[part][:, LANES:] = dv

        elif split:
            out_refs[0][j * r : (j + 1) * r, :LANES] = dk
            out_refs[0][j * r : (j + 1) * r, LANES:] = dv
        else:
            out_refs[j][:, :LANES] = dk
            out_refs[j][:, LANES:] = dv

    for j, offset in enumerate(offsets):
        block = sc_ref[3 + offset]

        def go(lo, mask):
            if halves:
                kv = halves_value(*kv_refs)
            elif split:
                kv = kv_refs[0][j * r : (j + 1) * r, :]
            else:
                kv = kv_refs[j][...]
            kb = kv[:, :LANES]
            dk, dv = back_block(ops, kb, kv[:, LANES:], kb.T, lo, t, mask, dq_ref)
            store(j, (dk * SCALE).astype(dtype), dv.astype(dtype))

        if split:

            @pl.when(block == me)
            def _():
                zero = jnp.zeros((r, LANES), dtype)
                store(j, zero, zero)

        if r % LANES == 0:

            @pl.when(block < me)
            def _():
                go(0, None)

            @pl.when(block > me)
            def _():
                go(r, None)

        else:

            @pl.when(block != me)
            def _():
                col = lax.broadcasted_iota(jnp.int32, (r, t), 1)
                go(0, (col >= r) | (block < me))


def q_specs(t):
    return [
        spec((LANES, t), lambda i: (i, 0)),
        spec((t, LANES), lambda i: (0, i)),
        spec((LANES, t), lambda i: (i, 0)),
        spec((t, LANES), lambda i: (0, i)),
        spec((8, t), lambda i: (i, 0)),
    ]


def bwd_local(sc, qt, q, do_t, do, st, dq, kv_prompt, kv_own):
    t = qt.shape[1]
    keys = kv_own.shape[0]
    return pl.pallas_call(
        bwd_local_body,
        grid=(PAIRS,),
        in_specs=[SMEM_SPEC]
        + q_specs(t)
        + [spec((LANES, t), lambda i: (i, 0))]
        + kv_specs((kv_prompt, kv_own), False),
        out_specs=[spec((t, LANES), lambda i: (0, i))] + kv_specs((kv_prompt, kv_own), False),
        out_shape=[
            shape((t, D), F32),
            shape((t // 2, 2 * D), F32),
            shape((keys, 2 * D), F32),
        ],
        scratch_shapes=[pltpu.VMEM((LANES, t), F32)],
        name="attend_back_local",
        **params((10 * 4 * t * keys * D, 16 * D * t)),
    )(sc, qt, q, do_t, do, st, dq, kv_prompt, kv_own)


def bwd_remote(
    sc, qt, q, do_t, do, st, src, kvs, offsets, halves=False, first=False, dtype=F32
):
    t = qt.shape[1]
    rows = len(offsets) * (t // 2)
    out_specs = [spec((LANES, t), lambda i: (i, 0))] + kv_specs(kvs, halves)
    out_shape = [shape((D, t), F32)] + [shape(kv.shape, dtype) for kv in kvs]
    if first:
        out_specs.append(spec((8, t), lambda i: (i, 0)))
        out_shape.append(shape((8 * PAIRS, t), F32))
    return pl.pallas_call(
        functools.partial(bwd_remote_body, tuple(offsets), len(kvs), halves, first, dtype),
        grid=(PAIRS,),
        in_specs=[SMEM_SPEC]
        + q_specs(t)
        + kv_specs(kvs, halves)
        + [spec((LANES, t), lambda i: (i, 0))],
        out_specs=out_specs,
        out_shape=out_shape,
        name="attend_back_remote",
        **params((10 * 4 * t * rows * D, 16 * D * t + 8 * D * rows)),
    )(sc, qt, q, do_t, do, st, *kvs, src)


def route_body(
    x_ref, att_ref, ow_ref, sw_ref, gain_ref, res_ref, rt_ref, tc_ref, tr_ref,
    h_ref, n_ref, pr_ref, xs_ref, ms_ref,
):
    t = x_ref.shape[0]
    step = pl.program_id(0)

    @pl.when(step == 0)
    def _():
        hidden = x_ref[...].astype(F32) + dot(att_ref[...], ow_ref[...])
        h_ref[...] = hidden
        scale = lax.rsqrt(jnp.mean(hidden * hidden, axis=-1, keepdims=True) + EPS)
        low = (hidden * scale * gain_ref[...]).astype(BF16)
        n_ref[...] = low
        z = dot(low, sw_ref[...])
        lane = lax.broadcasted_iota(jnp.int32, (t, LANES), 1)
        is_route = lane < EXPERTS + 4
        logits = jnp.where(is_route, z + res_ref[...], NEG)
        ex = jnp.exp(logits - jnp.max(logits, axis=-1, keepdims=True))
        probs = ex / jnp.sum(ex, axis=-1, keepdims=True)
        out = probs
        first = EXPERTS + 4
        for k in range(2):
            l0 = z[:, first + 2 * k : first + 2 * k + 1]
            l1 = z[:, first + 2 * k + 1 : first + 2 * k + 2]
            top = jnp.maximum(l0, l1)
            e0 = jnp.exp(l0 - top)
            e1 = jnp.exp(l1 - top)
            den = e0 + e1
            out = jnp.where(lane == first + 2 * k, e0 / den, out)
            out = jnp.where(lane == first + 2 * k + 1, e1 / den, out)
        for j in range(2):
            mix = jnp.sum(jnp.where(lane == rt_ref[:, j : j + 1], probs, 0.0), axis=-1, keepdims=True)
            out = jnp.where(lane == 16 + j, mix, out)
        pr_ref[...] = out

    slots = xs_ref.shape[0]
    base = step * slots
    slot = base + lax.broadcasted_iota(jnp.int32, (slots, t), 0)
    pick = (slot == tr_ref[0:1, :]) | (slot == tr_ref[1:2, :])
    xs_ref[...] = dot(pick.astype(BF16), n_ref[...]).astype(BF16)
    slot = base + lax.broadcasted_iota(jnp.int32, (t, slots), 1)
    mixes = jnp.where(slot == tc_ref[:, 0:1], pr_ref[:, 16:17], 0.0) + jnp.where(
        slot == tc_ref[:, 1:2], pr_ref[:, 17:18], 0.0
    )
    ms_ref[...] = jnp.sum(mixes, axis=0, keepdims=True)


def route_call(x, att, ow, sw, gain, res, rt, tc, tr, slots):
    t = x.shape[0]
    part = min(slots, 256)
    return pl.pallas_call(
        route_body,
        grid=(slots // part,),
        in_specs=[
            whole((t, D)), whole((t, D)), whole((D, D)), whole((D, LANES)), whole((1, D)),
            whole((t, LANES)), whole((t, 2)), whole((t, 2)), whole((2, t)),
        ],
        out_specs=[
            whole((t, D)), whole((t, D)), whole((t, LANES)),
            spec((part, D), lambda i: (i, 0)),
            spec((1, part), lambda i: (0, i)),
        ],
        out_shape=[
            shape((t, D), F32), shape((t, D), BF16), shape((t, LANES), F32),
            shape((slots, D), BF16), shape((1, slots), F32),
        ],
        name="route_dispatch",
        **params((2 * t * D * D + 2 * slots * t * D, 8 * t * D)),
    )(x, att, ow, sw, gain, res, rt, tc, tr)


def expert_fwd_body(x_ref, w_ref, o_ref, acc_ref):
    step = pl.program_id(0)
    x = x_ref[...]
    wide = w_ref.shape[-1]
    wg = w_ref[:, 0].reshape(D, wide)
    wu = w_ref[:, 1].reshape(D, wide)
    wd = w_ref[:, 2].reshape(D, wide)
    gate = dot(x, wg)
    up = dot(x, wu)
    act = (gate / (1.0 + jnp.exp(-gate)) * up).astype(BF16)
    out = dot_nt(act, wd)

    @pl.when(step == 0)
    def _():
        acc_ref[...] = out

    @pl.when(step > 0)
    def _():
        acc_ref[...] += out

    @pl.when(step == pl.num_programs(0) - 1)
    def _():
        o_ref[...] = acc_ref[...].astype(BF16)


def expert_fwd(xr, w):
    rows = xr.shape[0]
    shards, _, per, wide = w.shape
    part = min(wide, 256)
    return pl.pallas_call(
        expert_fwd_body,
        grid=(wide // part,),
        in_specs=[whole((rows, D)), spec((shards, 3, per, part), lambda i: (0, 0, 0, i))],
        out_specs=whole((rows, D)),
        out_shape=shape((rows, D), BF16),
        scratch_shapes=[pltpu.VMEM((rows, D), F32)],
        name="expert_forward",
        **params((6 * rows * D * wide, 6 * D * wide)),
    )(xr, w)


def expert_in_body(x_ref, g_ref, m_ref, w_ref, gi_ref, gl_ref, act_ref, dg_ref, du_ref, acc_ref):
    step = pl.program_id(0)

    @pl.when(step == 0)
    def _():
        gl_ref[...] = (g_ref[...].astype(F32) * m_ref[...]).astype(BF16)

    x = x_ref[...]
    g = gl_ref[...]
    wide = w_ref.shape[-1]
    wg = w_ref[:, 0].reshape(D, wide)
    wu = w_ref[:, 1].reshape(D, wide)
    wd = w_ref[:, 2].reshape(D, wide)
    gate = dot(x, wg)
    up = dot(x, wu)
    ga = dot(g, wd)
    sig = 1.0 / (1.0 + jnp.exp(-gate))
    silu = gate * sig
    act_ref[...] = (silu * up).astype(BF16)
    d_gate = (ga * up * sig * (1.0 + gate * (1.0 - sig))).astype(BF16)
    d_up = (ga * silu).astype(BF16)
    dg_ref[...] = d_gate
    du_ref[...] = d_up
    gi = dot_nt(d_gate, wg) + dot_nt(d_up, wu)

    @pl.when(step == 0)
    def _():
        acc_ref[...] = gi

    @pl.when(step > 0)
    def _():
        acc_ref[...] += gi

    @pl.when(step == pl.num_programs(0) - 1)
    def _():
        gi_ref[...] = acc_ref[...].astype(BF16)


def expert_in(xr, gr, mix, w):
    rows = xr.shape[0]
    shards, _, per, wide = w.shape
    part = min(wide, 256)
    tile = spec((rows, part), lambda i: (0, i))
    return pl.pallas_call(
        expert_in_body,
        grid=(wide // part,),
        in_specs=[
            whole((rows, D)), whole((rows, D)), whole((rows, 1)),
            spec((shards, 3, per, part), lambda i: (0, 0, 0, i)),
        ],
        out_specs=[whole((rows, D)), whole((rows, D)), tile, tile, tile],
        out_shape=[shape((rows, D), BF16)] * 2 + [shape((rows, wide), BF16)] * 3,
        scratch_shapes=[pltpu.VMEM((rows, D), F32)],
        name="expert_back_in",
        **params((10 * rows * D * wide, 12 * D * wide)),
    )(xr, gr, mix, w)


def expert_weights_body(x_ref, gl_ref, act_ref, dg_ref, du_ref, dw_ref, xt_ref, gt_ref):
    @pl.when(pl.program_id(0) == 0)
    def _():
        gt_ref[...] = gl_ref[...].T
        xt_ref[...] = x_ref[...].T

    shards, _, per, wide = dw_ref.shape
    xt = xt_ref[...]
    dw_ref[:, 0] = dot(xt, dg_ref[...]).astype(BF16).reshape(shards, per, wide)
    dw_ref[:, 1] = dot(xt, du_ref[...]).astype(BF16).reshape(shards, per, wide)
    dw_ref[:, 2] = dot(gt_ref[...], act_ref[...]).astype(BF16).reshape(shards, per, wide)


def expert_weights(xr, low, act, d_gate, d_up, dims):
    rows = xr.shape[0]
    shards, _, per, wide = dims
    part = min(wide, 256)
    tile = spec((rows, part), lambda i: (0, i))
    return pl.pallas_call(
        expert_weights_body,
        grid=(wide // part,),
        in_specs=[whole((rows, D)), whole((rows, D)), tile, tile, tile],
        out_specs=spec((shards, 3, per, part), lambda i: (0, 0, 0, i)),
        out_shape=shape(dims, BF16),
        scratch_shapes=[pltpu.VMEM((D, rows), BF16), pltpu.VMEM((D, rows), BF16)],
        name="expert_weight_grads",
        **params((6 * rows * D * wide, 12 * D * wide)),
    )(xr, low, act, d_gate, d_up)


def mix_body(
    h_ref, g_ref, pr_ref, rt_ref, tc_ref, ret_ref, n_ref, sw_ref, rows_ref,
    out_ref, gn_ref, gl_ref, gs_ref,
):
    t = h_ref.shape[0]
    slots = ret_ref.shape[0]
    hidden = h_ref[...]
    g16 = g_ref[...]
    g = g16.astype(F32)
    pr = pr_ref[...]
    scale = lax.rsqrt(jnp.mean(hidden * hidden, axis=-1, keepdims=True) + EPS)
    normed = hidden * scale * rows_ref[2:3, :]
    lane = lax.broadcasted_iota(jnp.int32, (t, LANES), 1)
    slot = lax.broadcasted_iota(jnp.int32, (t, slots), 1)
    first = EXPERTS + 4
    ret = ret_ref[...]
    c0 = [pr[:, first + 2 * k : first + 2 * k + 1] for k in range(2)]
    c1 = [pr[:, first + 2 * k + 1 : first + 2 * k + 2] for k in range(2)]
    total = hidden
    s = jnp.zeros((t, LANES), F32)
    coef = jnp.zeros((t, 1), F32)
    weight = [jnp.zeros((t, 1), F32) for _ in range(2)]
    for j in range(2):
        route = rt_ref[:, j : j + 1]
        mix = pr[:, 16 + j : 17 + j]
        branch = dot((slot == tc_ref[:, j : j + 1]).astype(BF16), ret)
        keep = jnp.where(route == EXPERTS + 1, 1.0, 0.0)
        for k in range(2):
            here = jnp.where(route == EXPERTS + 2 + k, 1.0, 0.0)
            keep = keep + here * c0[k]
            weight[k] = weight[k] + here * mix
            branch = branch + (here * c1[k]) * rows_ref[k : k + 1, :]
        branch = branch + keep * normed
        coef = coef + mix * keep
        total = total + mix * branch
        gp = jnp.sum(g * branch, axis=-1, keepdims=True)
        s = s + jnp.where(lane == route, gp, 0.0)
    out_ref[...] = total.astype(BF16)
    probs = jnp.where(lane < first, pr, 0.0)
    d_logits = probs * (s - jnp.sum(probs * s, axis=-1, keepdims=True))
    gl_ref[...] = d_logits
    dz = d_logits
    dvec = jnp.zeros((t, LANES), F32)
    g_dot_n = jnp.sum(g * normed, axis=-1, keepdims=True)
    for k in range(2):
        d0 = weight[k] * g_dot_n
        d1 = weight[k] * jnp.sum(g * rows_ref[k : k + 1, :], axis=-1, keepdims=True)
        mean = c0[k] * d0 + c1[k] * d1
        dz = jnp.where(lane == first + 2 * k, c0[k] * (d0 - mean), dz)
        dz = jnp.where(lane == first + 2 * k + 1, c1[k] * (d1 - mean), dz)
        dvec = jnp.where(lane == 16 + k, weight[k] * c1[k], dvec)
    hi, lo = split_hi_lo(dz)
    sw = sw_ref[...]
    gn_ref[...] = coef * g + (dot_nt(hi, sw) + dot_nt(lo, sw))
    nt = n_ref[...].T
    gt = g16.T
    vhi, vlo = split_hi_lo(dvec)
    gs = dot(nt, hi) + dot(nt, lo) + dot(gt, vhi) + dot(gt, vlo)

    @pl.when(pl.program_id(0) == 0)
    def _():
        gs_ref[...] = gs

    @pl.when(pl.program_id(0) > 0)
    def _():
        gs_ref[...] += gs


def mix_call(hidden, g, pr, rt, tc, ret, low, sw, rows):
    t = hidden.shape[0]
    half = t // 2
    slots = ret.shape[0]
    tile = spec((half, D), lambda i: (i, 0))
    lane_tile = spec((half, LANES), lambda i: (i, 0))
    pair = spec((half, 2), lambda i: (i, 0))
    return pl.pallas_call(
        mix_body,
        grid=(2,),
        in_specs=[
            tile, tile, lane_tile, pair, pair, whole((slots, D)), tile, whole((D, LANES)),
            whole((8, D)),
        ],
        out_specs=[tile, tile, lane_tile, whole((D, LANES))],
        out_shape=[
            shape((t, D), BF16), shape((t, D), F32), shape((t, LANES), F32), shape((D, LANES), F32),
        ],
        name="mixture",
        **params((4 * t * slots * D, 12 * t * D)),
    )(hidden, g, pr, rt, tc, ret, low, sw, rows)


def norm_back_body(
    h_ref, g_ref, gn_ref, tc_ref, ret_ref, rows_ref, ow_ref, att_ref,
    gh_ref, do_ref, dot_ref, gow_ref, gg_ref,
):
    t = h_ref.shape[0]
    slots = ret_ref.shape[0]
    hidden = h_ref[...]
    slot = lax.broadcasted_iota(jnp.int32, (t, slots), 1)
    pick = (slot == tc_ref[:, 0:1]) | (slot == tc_ref[:, 1:2])
    gn = gn_ref[...] + dot(pick.astype(BF16), ret_ref[...])
    q = lax.rsqrt(jnp.mean(hidden * hidden, axis=-1, keepdims=True) + EPS)
    u = gn * rows_ref[2:3, :]
    mean = jnp.mean(u * hidden, axis=-1, keepdims=True)
    gh = g_ref[...].astype(F32) + q * u - hidden * (q * q * q * mean)
    gh_ref[...] = gh
    gb = gh.astype(BF16)
    d_out = dot_nt(gb, ow_ref[...])
    do_ref[...] = d_out.astype(BF16)
    dot_ref[...] = d_out.T.astype(BF16)
    gow = dot(att_ref[...].T, gb)
    gain = jnp.sum(gn * hidden * q, axis=0, keepdims=True)

    @pl.when(pl.program_id(0) == 0)
    def _():
        gow_ref[...] = gow
        gg_ref[...] = jnp.broadcast_to(gain, gg_ref.shape)

    @pl.when(pl.program_id(0) > 0)
    def _():
        gow_ref[...] += gow
        gg_ref[...] += jnp.broadcast_to(gain, gg_ref.shape)


def norm_back_call(hidden, g, gn, tc, ret, rows, ow, att):
    t = hidden.shape[0]
    half = t // 2 if (t // 2) % LANES == 0 else t
    slots = ret.shape[0]
    tile = spec((half, D), lambda i: (i, 0))
    return pl.pallas_call(
        norm_back_body,
        grid=(t // half,),
        in_specs=[
            tile, tile, tile, spec((half, 2), lambda i: (i, 0)), whole((slots, D)), whole((8, D)),
            whole((D, D)), tile,
        ],
        out_specs=[tile, tile, spec((D, half), lambda i: (0, i)), whole((D, D)), whole((8, D))],
        out_shape=[
            shape((t, D), F32), shape((t, D), BF16), shape((D, t), BF16), shape((D, D), F32),
            shape((8, D), F32),
        ],
        name="norm_two_back",
        **params((2 * t * slots * D + 4 * t * D * D, 16 * t * D)),
    )(hidden, g, gn, tc, ret, rows, ow, att)


def store_grad(sc_ref, split, value, refs):
    if not split:
        refs[0][...] = value
        return
    send_ref, keep_ref = refs
    per = value.shape[0] // 4
    for core in range(2):

        @pl.when(sc_ref[11] == core)
        def _():
            for part in range(2):
                mine = (2 * part + core) * per
                other = (2 * part + 1 - core) * per
                send_ref[part] = value[other : other + per].astype(BF16)
                keep_ref[part] = value[mine : mine + per]


def grad_outs(split, width):
    block = 2 * LANES
    if not split:
        return [spec((D, block), lambda i: (0, i))], [shape((D, width), F32)]
    dims = (2, D // 4, width)
    tile = spec((2, D // 4, block), lambda i: (0, 0, i))
    return [tile, tile], [shape(dims, BF16), shape(dims, F32)]


def q_back_body(split, sc_ref, n_ref, dq_ref, c_ref, s_ref, w_ref, gn_ref, *refs):
    nt_ref = refs[-1]
    step = pl.program_id(0)

    @pl.when(step == 0)
    def _():
        nt_ref[...] = n_ref[...].T

    cosine = c_ref[...]
    sine = s_ref[...]
    v0 = dq_ref[:, :LANES]
    v1 = dq_ref[:, LANES:]
    gq = jnp.concatenate(
        [
            (v0 * cosine - partner(v0) * sine).astype(BF16),
            (v1 * cosine - partner(v1) * sine).astype(BF16),
        ],
        axis=1,
    )
    store_grad(sc_ref, split, dot(nt_ref[...], gq), refs[:-1])
    gn = dot_nt(gq, w_ref[...])

    @pl.when(step == 0)
    def _():
        gn_ref[...] = gn

    @pl.when(step > 0)
    def _():
        gn_ref[...] += gn


def q_back_call(sc, low, dq, cosine, sine, pack, split):
    t = low.shape[0]
    specs, shapes = grad_outs(split, D)
    return pl.pallas_call(
        functools.partial(q_back_body, split),
        grid=(PAIRS // 2,),
        in_specs=[
            SMEM_SPEC, whole((t, D)), spec((t, 2 * LANES), lambda i: (0, i)), whole((t, LANES)),
            whole((t, LANES)), spec((D, 2 * LANES), lambda i: (0, i)),
        ],
        out_specs=[whole((t, D))] + specs,
        out_shape=[shape((t, D), F32)] + shapes,
        scratch_shapes=[pltpu.VMEM((D, t), BF16)],
        name="q_back",
        **params((4 * t * D * D, 12 * t * D)),
    )(sc, low, dq, cosine, sine, pack)


def kv_back_body(
    split, count, sc_ref, x_ref, n_ref, gnq_ref, gh_ref, gain_ref, c_ref, s_ref, wk_ref, wv_ref,
    own_ref, cont_ref, *refs
):
    got_refs, refs = refs[:count], refs[count:]
    gi_ref, grads, (nt_ref, gn_ref) = refs[0], refs[1:-2], refs[-2:]
    step = pl.program_id(0)

    @pl.when(step == 0)
    def _():
        nt_ref[...] = n_ref[...].T
        gn_ref[...] = gnq_ref[...]

    own = own_ref[...]
    for got in got_refs:
        own = own + got[...].astype(F32)
    total = jnp.concatenate([own, cont_ref[...]], axis=0)
    k = total[:, :LANES]
    gk = (k * c_ref[...] - partner(k) * s_ref[...]).astype(BF16)
    gkv = jnp.concatenate([gk, total[:, LANES:].astype(BF16)], axis=1)
    store_grad(sc_ref, split, dot(nt_ref[...], gkv), grads)
    gn_ref[...] += dot_nt(gkv, jnp.concatenate([wk_ref[...], wv_ref[...]], axis=1))

    @pl.when(step == pl.num_programs(0) - 1)
    def _():
        gn = gn_ref[...]
        x = x_ref[...].astype(F32)
        q = lax.rsqrt(jnp.mean(x * x, axis=-1, keepdims=True) + EPS)
        u = gn * gain_ref[...]
        mean = jnp.mean(u * x, axis=-1, keepdims=True)
        gi_ref[...] = gh_ref[...] + q * u - x * (q * q * q * mean)


def kv_back_call(sc, x, low, gn, gh, gain, cosine, sine, pack, own, cont, got, split):
    t = x.shape[0]
    r = t // 2
    specs, shapes = grad_outs(split, 2 * D)
    wide = spec((r, 2 * LANES), lambda i: (0, i))
    return pl.pallas_call(
        functools.partial(kv_back_body, split, len(got)),
        grid=(PAIRS,),
        in_specs=[
            SMEM_SPEC, whole((t, D)), whole((t, D)), whole((t, D)), whole((t, D)), whole((1, D)),
            whole((t, LANES)), whole((t, LANES)),
            spec((D, LANES), lambda i: (0, PAIRS + i)),
            spec((D, LANES), lambda i: (0, 2 * PAIRS + i)),
            wide, wide,
        ]
        + [wide] * len(got),
        out_specs=[whole((t, D))] + specs,
        out_shape=[shape((t, D), F32)] + shapes,
        scratch_shapes=[pltpu.VMEM((D, t), BF16), pltpu.VMEM((t, D), F32)],
        name="kv_back",
        **params((8 * t * D * D, 24 * t * D)),
    )(sc, x, low, gn, gh, gain, cosine, sine, pack, pack, own, cont, *got)


def rotation_tables(position):
    half = HEAD_DIM // 2
    frequency = 10000.0 ** (-jnp.arange(half, dtype=F32) / half)
    angles = position[:, None] * frequency[None, :]
    cosine, sine = jnp.cos(angles), jnp.sin(angles)
    return (
        jnp.concatenate([cosine] * 4, axis=1),
        jnp.concatenate([-sine, sine, -sine, sine], axis=1),
    )


def to_rows(array):
    return jnp.transpose(array, (1, 0, 2)).reshape(2 * array.shape[0], array.shape[2])


def from_rows(array):
    r = array.shape[0] // 2
    return jnp.transpose(array.reshape(2, r, array.shape[1]), (1, 0, 2))


RING = (0, 2, 4, 6, 7, 5, 3, 1)


def ring_offsets():
    place = {e: i for i, e in enumerate(RING)}
    return [[RING[(place[e] + k) % 8] for k in range(8)] for e in range(8)]


def along_ring(array, step):
    pairs = [(RING[i], RING[(i + step) % 8]) for i in range(8)]
    return lax.ppermute(array, "expert", pairs)


def tie(*values):
    return lax.optimization_barrier(values)


def swap_core(array):
    return lax.ppermute(array, "dp", [(0, 1), (1, 0), (2, 3), (3, 2)])


def add_and_cross(keep, got):
    across = lax.axis_index("dp") // 2
    keep = keep + got.astype(F32)
    send = lax.dynamic_index_in_dim(keep, 1 - across, 0, keepdims=False).astype(BF16)
    mine = lax.dynamic_index_in_dim(keep, across, 0, keepdims=False)
    return mine, lax.ppermute(send, "dp", [(0, 2), (2, 0), (1, 3), (3, 1)])


def add_and_scatter(keep, got):
    keep = (keep + got.astype(F32)).astype(BF16)
    rows, w = keep.shape
    return lax.all_to_all(
        keep.reshape(8, rows // 8, w), "expert", split_axis=0, concat_axis=0, tiled=True
    )


def add_up(got):
    return jnp.sum(got.astype(F32), axis=0)


def scatter_all(array):
    return lax.psum_scatter(
        array.astype(BF16), ALL_AXES, scatter_dimension=0, tiled=True
    ).astype(F32)


def per_device(
    hidden_in, cotangent, gate_residual, routes, groups, lengths, attn_gain, qkv_weight, out_weight,
    ffn_gain, router_weight, const_proj, const_vec, gate_weight, up_weight, down_weight,
):
    del groups
    r = hidden_in.shape[0]
    t = 2 * r
    capacity = r // 2
    owners = lax.axis_size("expert")
    copies = owners // EXPERTS
    slots = EXPERTS * capacity
    me = lax.axis_index("expert")
    per_cont = max(CONT_LEN // r, 1)

    small = jnp.concatenate(
        [
            router_weight, const_proj, const_vec, attn_gain[:, None], ffn_gain[:, None],
            jnp.zeros((attn_gain.shape[0], LANES - 20), BF16),
        ],
        axis=1,
    )
    pack = lax.all_gather(
        jnp.concatenate([qkv_weight, out_weight, small], axis=1), ALL_AXES, axis=0, tiled=True
    )
    index = jnp.arange(r, dtype=jnp.int32)
    row_ids = me * r + index
    position = jnp.concatenate([row_ids, PROMPT + row_ids % CONT_LEN]).astype(F32)
    cosine, sine = rotation_tables(position)
    cont = (me * r) // CONT_LEN
    length = lax.dynamic_slice(lengths, (cont,), (1,))
    header = jnp.stack([me, (me * r) % CONT_LEN]).astype(jnp.int32)
    header = jnp.concatenate([header, length.astype(jnp.int32)])
    ring = owners == 8
    if ring:
        ids = lax.dynamic_index_in_dim(jnp.asarray(ring_offsets(), jnp.int32), me, 0, keepdims=False)
    else:
        ids = jnp.arange(owners, dtype=jnp.int32)
    sc = jnp.concatenate([header, ids, (lax.axis_index("dp") % 2).astype(jnp.int32)[None]])

    picked = to_rows(routes)
    flat = jnp.transpose(picked).reshape(2 * t)
    hot = flat[:, None] == jnp.arange(EXPERTS, dtype=jnp.int32)[None, :]
    earlier = jnp.arange(2 * t)[:, None] > jnp.arange(2 * t)[None, :]
    before = jnp.dot(earlier.astype(BF16), hot.astype(BF16), preferred_element_type=F32)
    slot_index = jnp.sum(jnp.where(hot, before, 0.0), axis=1).astype(jnp.int32)
    target = jnp.where(flat < EXPERTS, flat * capacity + slot_index, -1)
    target_rows = target.reshape(2, t)
    target_cols = jnp.transpose(target_rows)

    def to_owners(rows):
        w = rows.shape[-1]
        shaped = rows.reshape(EXPERTS, 1, capacity, w)
        return jnp.broadcast_to(shaped, (EXPERTS, copies, capacity, w)).reshape(owners, capacity, w)

    def exchange(rows):
        got = lax.all_to_all(rows, "expert", split_axis=0, concat_axis=0, tiled=True)
        return got.reshape(owners * got.shape[1], got.shape[2])

    def from_owners(rows):
        got = exchange(rows.reshape(owners, capacity, D))
        if copies == 1:
            return got
        got = got.reshape(EXPERTS, copies, capacity, D).astype(F32)
        return jnp.sum(got, axis=1).reshape(slots, D).astype(BF16)

    x = to_rows(hidden_in)
    g = to_rows(cotangent)
    slot_ids = jnp.arange(slots, dtype=jnp.int32)[:, None]
    placement = (slot_ids == target_rows[0][None, :]) | (slot_ids == target_rows[1][None, :])
    g_send = jnp.dot(placement.astype(BF16), g, preferred_element_type=F32).astype(BF16)
    g_got = exchange(to_owners(g_send))
    x, g_got = tie(x, g_got)
    out_w = pack[:, 3 * D : 4 * D]
    small_w = pack[:, 4 * D :]
    small_rows = jnp.transpose(small_w[:, 16:24]).astype(F32)
    gain_one = small_rows[2:3]
    rows_two = jnp.concatenate([small_rows[0:2], small_rows[3:4], small_rows[3:8]], axis=0)
    gain_two = small_rows[3:4]

    low_one, q, q_t, kv = qkv_call(x, gain_one, pack, cosine, sine)
    kv_prompt = kv[:r]
    if not ring:
        kv_all = lax.all_gather(kv_prompt, "expert", axis=0, tiled=True)
    if per_cont == 1:
        kv_own = kv[r:]
    else:
        cont_groups = [
            [c * per_cont + i for i in range(per_cont)] for c in range(owners // per_cont)
        ]
        kv_own = lax.all_gather(
            kv[r:], "expert", axis=0, tiled=True, axis_index_groups=cont_groups
        )
    weights = lax.all_gather(
        jnp.stack([gate_weight, up_weight, down_weight]), "dp", axis=0, tiled=False
    )
    if ring:
        right, left = [kv_prompt], [kv_prompt]
        for i in range(3):
            right.append(along_ring(right[i], 1))
            left.append(along_ring(left[i], -1))
            if i == 0:
                st, acc = fwd_local(sc, q_t, kv_prompt, kv_own)
            else:
                st, acc = fwd_remote(sc, q_t, (right[i], left[i]), (8 - i, i), st, acc)
            right[i + 1], left[i + 1], st = tie(right[i + 1], left[i + 1], st)
        far = [along_ring(right[3][:, :D], 1), along_ring(left[3][:, D:], -1)]
        st, acc = fwd_remote(sc, q_t, (right[3], left[3]), (5, 3), st, acc)
        st, att_t, att = fwd_remote(sc, q_t, far, (4,), st, acc, halves=True, final=True)
    else:
        st, acc = fwd_local(sc, q_t, kv_prompt, kv_own)
        st, att_t, att = fwd_remote(sc, q_t, (kv_all,), range(owners), st, acc, final=True)

    res = jnp.pad(to_rows(gate_residual), ((0, 0), (0, LANES - EXPERTS - 4)))
    hidden, low_two, pr, x_send, mix_send = route_call(
        x, att, out_w, small_w, gain_two, res, picked, target_cols, target_rows, slots
    )
    x_got = exchange(to_owners(x_send))
    x_got, mix_send = tie(x_got, mix_send)
    mix_got = lax.all_to_all(
        to_owners(mix_send.reshape(EXPERTS, capacity, 1)).reshape(owners, capacity),
        "expert", split_axis=0, concat_axis=0, tiled=True,
    ).reshape(owners * capacity, 1)
    out_back = from_owners(expert_fwd(x_got, weights))
    grad_in, g_low, act, d_gate, d_up = expert_in(x_got, g_got, mix_got, weights)
    in_back = from_owners(grad_in)
    output, gn, grad_logits, grad_small = mix_call(
        hidden, g, pr, picked, target_cols, out_back, low_two, small_w, rows_two
    )
    act, gn = tie(act, gn)
    grad_w = expert_weights(x_got, g_low, act, d_gate, d_up, weights.shape)
    grad_expert = lax.psum_scatter(
        grad_w.reshape(-1, grad_w.shape[-1]), "dp", scatter_dimension=0, tiled=True
    ).astype(F32)
    gh, d_att, d_att_t, grad_ow, gg_two = norm_back_call(
        hidden, g, gn, target_cols, in_back, rows_two, out_w, att
    )

    early = jnp.concatenate(
        [grad_ow, grad_small[:, :19], jnp.transpose(gg_two[0:1]), jnp.zeros((D, LANES - 20), F32)],
        axis=1,
    )
    back = (sc, q_t, q, d_att_t, d_att)
    if ring:
        parts = early.reshape(2, 2, D // 4, D + LANES)
        core = lax.axis_index("dp") % 2
        early_keep = lax.dynamic_index_in_dim(parts, core, 1, keepdims=False)
        early_got = swap_core(
            lax.dynamic_index_in_dim(parts, 1 - core, 1, keepdims=False).astype(BF16)
        )
        dq_t, send_r, send_l, st = bwd_remote(
            *back, st, att_t, far, (4,), halves=True, first=True, dtype=BF16
        )
        for i in range(3, 0, -1):
            got_r, got_l = along_ring(send_r, 1), along_ring(send_l, -1)
            dq_t, part_r, part_l = bwd_remote(
                *back, st, dq_t, (left[i], right[i]), (i, 8 - i)
            )
            got_r, got_l, part_r, part_l, dq_t, early_got = tie(
                got_r, got_l, part_r, part_l, dq_t, early_got
            )
            if i == 3:
                send_r = jnp.concatenate([part_r[:, :D] + got_r.astype(F32), part_r[:, D:]], axis=1)
                send_l = jnp.concatenate([part_l[:, :D], part_l[:, D:] + got_l.astype(F32)], axis=1)
                early_keep, early_got = add_and_cross(early_keep, early_got)
            else:
                send_r, send_l = part_r + got_r.astype(F32), part_l + got_l.astype(F32)
                if i == 2:
                    early_got = add_and_scatter(early_keep, early_got)
            send_r, send_l = send_r.astype(BF16), send_l.astype(BF16)
        send_r, send_l, dq_t = tie(send_r, send_l, dq_t)
        got = (along_ring(send_r, 1), along_ring(send_l, -1))
        dq, dkv_own, dkv_cont = bwd_local(*back, st, dq_t, kv_prompt, kv_own)
        early = add_up(early_got)
    else:
        dq_t, dkv_all, st = bwd_remote(
            *back, st, att_t, (kv_all,), range(owners), first=True, dtype=BF16
        )
        dq, dkv_own, dkv_cont = bwd_local(*back, st, dq_t, kv_prompt, kv_own)
        got = (lax.psum_scatter(dkv_all, "expert", scatter_dimension=0, tiled=True),)
        early = scatter_all(early)
    if per_cont > 1:
        dkv_cont = lax.psum_scatter(
            dkv_cont, "expert", scatter_dimension=0, tiled=True, axis_index_groups=cont_groups
        )
    gn_q, *grad_q = q_back_call(sc, low_one, dq, cosine, sine, pack, ring)
    if ring:
        keep_q, got_q = add_and_cross(grad_q[1], swap_core(grad_q[0]))
        keep_q, got_q, got_0, got_1 = tie(keep_q, got_q, *got)
        got = (got_0, got_1)
    grad_input, *grad_kv = kv_back_call(
        sc, x, low_one, gn_q, gh, gain_one, cosine, sine, pack, dkv_own, dkv_cont, got, ring
    )
    output, grad_input = from_rows(output), from_rows(grad_input)
    if ring:
        got_kv = swap_core(grad_kv[0])
        got_q = add_and_scatter(keep_q, got_q)
        keep_kv, got_kv = add_and_cross(grad_kv[1], got_kv)
        got_kv, grad_expert, output, grad_input = tie(got_kv, grad_expert, output, grad_input)
        late_q = add_up(got_q)
        late_kv = add_up(add_and_scatter(keep_kv, got_kv))
    else:
        late_q, late_kv = scatter_all(grad_q[0]), scatter_all(grad_kv[0])
    per = late_kv.shape[0]
    late_kv = jnp.transpose(late_kv.reshape(per, PAIRS, 2, LANES), (0, 2, 1, 3))
    late = jnp.concatenate([late_q, late_kv.reshape(per, 2 * D)], axis=1)
    grad_gain = jnp.sum(late * qkv_weight.astype(F32), axis=1) / attn_gain.astype(F32)
    tail = early[:, D:]
    per = grad_expert.shape[0] // 3
    return (
        output,
        grad_input,
        from_rows(grad_logits)[:, :, : EXPERTS + 4],
        grad_gain,
        late,
        early[:, :D],
        tail[:, 19],
        tail[:, :12],
        tail[:, 12:16],
        tail[:, 16:18],
        grad_expert[:per],
        grad_expert[per : 2 * per],
        grad_expert[2 * per :],
    )


def solution(mesh):
    rows = P(ALL_AXES, None, None)
    flat = P(ALL_AXES)
    mat = P(ALL_AXES, None)
    expert = P("dp", "expert")
    in_specs = (
        rows, rows, rows, rows, P("dp"), P("dp"), flat, mat, mat, flat, mat, mat, mat,
        expert, expert, expert,
    )
    out_specs = (
        rows, rows, rows, flat, mat, mat, flat, mat, mat, mat, expert, expert, expert,
    )
    return jax.shard_map(
        per_device, mesh=mesh, in_specs=in_specs, out_specs=out_specs, check_vma=False
    )
```

```python
import functools

import jax
import jax.numpy as jnp
from jax import lax
from jax.experimental import pallas as pl
from jax.experimental.pallas import tpu as pltpu
from jax.sharding import PartitionSpec as P


D = 768
HEAD_DIM = 64
PAIRS = 6
EXPERTS = 8
CONT_LEN = 256
PROMPT = 2048
LANES = 128
ROW_TILE = 512
EPS = 1e-06
NEG = -1e30
LOG2E = 1.4426950408889634
SCALE = float(HEAD_DIM) ** (-0.5)
LC = SCALE * LOG2E
F32 = jnp.float32
BF16 = jnp.bfloat16
ALL_AXES = ("dp", "expert")
VMEM_LIMIT = 60 * 1024 * 1024


def dot(a, b):
    return jnp.dot(a, b, preferred_element_type=F32)


def dot_nt(a, b):
    return lax.dot_general(a, b, (((1,), (1,)), ((), ())), preferred_element_type=F32)


def split_hi_lo(v):
    hi = v.astype(BF16)
    return hi, (v - hi.astype(F32)).astype(BF16)


def params(cost=None):
    return dict(
        compiler_params=pltpu.CompilerParams(vmem_limit_bytes=VMEM_LIMIT),
        cost_estimate=None if cost is None else pl.CostEstimate(
            flops=int(cost[0]), bytes_accessed=int(cost[1]), transcendentals=0
        ),
    )


def shape(dims, dtype):
    return jax.ShapeDtypeStruct(tuple(dims), dtype)


def spec(block, index):
    return pl.BlockSpec(tuple(block), index)


def whole(dims):
    return pl.BlockSpec(tuple(dims), lambda *_: (0,) * len(dims))


SMEM_SPEC = pl.BlockSpec(memory_space=pltpu.SMEM)


def partner(v):
    lane = lax.broadcasted_iota(jnp.int32, v.shape, 1)
    return jnp.where((lane & 63) < 32, pltpu.roll(v, 96, 1), pltpu.roll(v, 32, 1))


def qkv_body(x_ref, gain_ref, wq_ref, wk_ref, wv_ref, c_ref, s_ref, n_ref, q_ref, qt_ref, kvp_ref, kvc_ref):
    @pl.when(pl.program_id(0) == 0)
    def _():
        x = x_ref[...].astype(F32)
        scale = lax.rsqrt(jnp.mean(x * x, axis=-1, keepdims=True) + EPS)
        n_ref[...] = (x * scale * gain_ref[...]).astype(BF16)

    n = n_ref[...]
    cosine = c_ref[...]
    sine = s_ref[...]
    kv = dot(n, jnp.concatenate([wk_ref[...], wv_ref[...]], axis=1))
    k = kv[:, :LANES]
    k = (k * cosine + partner(k) * sine).astype(BF16)
    v = kv[:, LANES:].astype(BF16)
    r = k.shape[0] // 2
    kvp_ref[:, :LANES] = k[:r]
    kvp_ref[:, LANES:] = v[:r]
    kvc_ref[:, :LANES] = k[r:]
    kvc_ref[:, LANES:] = v[r:]
    q = dot(n, wq_ref[...])
    q = q * cosine + partner(q) * sine
    q_ref[...] = q.astype(BF16)
    qt_ref[...] = q.T.astype(BF16)


def qkv_call(x, gain, pack, cosine, sine):
    t = x.shape[0]
    return pl.pallas_call(
        qkv_body,
        grid=(PAIRS,),
        in_specs=[
            whole((t, D)),
            whole((1, D)),
            spec((D, LANES), lambda i: (0, i)),
            spec((D, LANES), lambda i: (0, PAIRS + i)),
            spec((D, LANES), lambda i: (0, 2 * PAIRS + i)),
            whole((t, LANES)),
            whole((t, LANES)),
        ],
        out_specs=[
            whole((t, D)),
            spec((t, LANES), lambda i: (0, i)),
            spec((LANES, t), lambda i: (i, 0)),
            spec((t // 2, 2 * LANES), lambda i: (0, i)),
            spec((t // 2, 2 * LANES), lambda i: (0, i)),
        ],
        out_shape=[
            shape((t, D), BF16),
            shape((t, D), BF16),
            shape((D, t), BF16),
            shape((t // 2, 2 * D), BF16),
            shape((t // 2, 2 * D), BF16),
        ],
        name="qkv_rope",
        **params((2 * t * D * 3 * D, 6 * D * D)),
    )(x, gain, pack, pack, pack, cosine, sine)


def head_rows(v, h):
    row = lax.broadcasted_iota(jnp.int32, v.shape, 0)
    return jnp.where(row // HEAD_DIM == h, v, jnp.zeros_like(v))


def head_lanes(v, h):
    lane = lax.broadcasted_iota(jnp.int32, v.shape, 1)
    return jnp.where(lane // HEAD_DIM == h, v, jnp.zeros_like(v))


def attend_update(qz, kb, vt, lo, hi, mask, st_ref, a_ref, first):
    for h in range(2):
        s = dot(kb, qz[h][:, lo:hi])
        if mask is not None:
            s = jnp.where(mask, s, NEG)
        top = jnp.max(s, axis=0, keepdims=True)
        rows = slice(h * HEAD_DIM, (h + 1) * HEAD_DIM)
        if first:
            p = jnp.exp2((s - top) * LC)
            st_ref[h : h + 1, lo:hi] = top
            st_ref[2 + h : 3 + h, lo:hi] = jnp.sum(p, axis=0, keepdims=True)
            a_ref[rows, lo:hi] = dot(vt[rows], p.astype(BF16))
        else:
            old = st_ref[h : h + 1, lo:hi]
            new = jnp.maximum(old, top)
            alpha = jnp.exp2((old - new) * LC)
            p = jnp.exp2((s - new) * LC)
            st_ref[h : h + 1, lo:hi] = new
            st_ref[2 + h : 3 + h, lo:hi] = st_ref[2 + h : 3 + h, lo:hi] * alpha + jnp.sum(
                p, axis=0, keepdims=True
            )
            a_ref[rows, lo:hi] = a_ref[rows, lo:hi] * alpha + dot(vt[rows], p.astype(BF16))


def local_masks(sc_ref, r, keys, lo, hi):
    cpos = sc_ref[1]
    length = sc_ref[2]
    col = lo + lax.broadcasted_iota(jnp.int32, (r, hi - lo), 1)
    row = lax.broadcasted_iota(jnp.int32, (r, hi - lo), 0)
    own = (row <= col) | (col >= r)
    col = lo + lax.broadcasted_iota(jnp.int32, (keys, hi - lo), 1)
    row = lax.broadcasted_iota(jnp.int32, (keys, hi - lo), 0)
    cont = (col >= r) & (row <= cpos + col - r) & (row < length)
    return own, cont


def fwd_local_body(sc_ref, qt_ref, kv_ref, kvo_ref, st_ref, a_ref):
    t = qt_ref.shape[1]
    r = t // 2
    keys = kvo_ref.shape[0]
    qt = qt_ref[...]
    qz = [head_rows(qt, h) for h in range(2)]
    kb = kv_ref[:, :LANES]
    vt = kv_ref[:, LANES:].T
    kbo = kvo_ref[:, :LANES]
    vto = kvo_ref[:, LANES:].T
    st_ref[...] = jnp.zeros_like(st_ref)
    own, cont = local_masks(sc_ref, r, keys, 0, t)
    if r % LANES == 0:
        attend_update(qz, kb, vt, 0, r, own[:, :r], st_ref, a_ref, True)
        attend_update(qz, kb, vt, r, t, None, st_ref, a_ref, True)
        attend_update(qz, kbo, vto, r, t, cont[:, r:], st_ref, a_ref, False)
    else:
        attend_update(qz, kb, vt, 0, t, own, st_ref, a_ref, True)
        attend_update(qz, kbo, vto, 0, t, cont, st_ref, a_ref, False)


def halves_value(a_ref, b_ref):
    return jnp.where(pl.program_id(0) < PAIRS // 2, a_ref[...], b_ref[...])


def fwd_remote_body(offsets, count, halves, final, sc_ref, qt_ref, *refs):
    kv_refs, refs = refs[:count], refs[count:]
    st_in, a_in, st_ref, a_ref = refs[:4]
    t = qt_ref.shape[1]
    r = t // 2
    me = sc_ref[0]
    qt = qt_ref[...]
    qz = [head_rows(qt, h) for h in range(2)]
    st_ref[...] = st_in[...]
    a_ref[...] = a_in[...]
    for j, offset in enumerate(offsets):
        block = sc_ref[3 + offset]

        def go(lo, hi, mask):
            if halves:
                kv = halves_value(*kv_refs)
            elif len(kv_refs) == len(offsets):
                kv = kv_refs[j][...]
            else:
                kv = kv_refs[0][j * r : (j + 1) * r, :]
            attend_update(qz, kv[:, :LANES], kv[:, LANES:].T, lo, hi, mask, st_ref, a_ref, False)

        if r % LANES == 0:
            if count != len(offsets) and not halves:
                pl.when(block != me)(lambda: go(r, t, None))
            else:
                go(r, t, None)

            @pl.when(block < me)
            def _():
                go(0, r, None)

        else:

            @pl.when(block != me)
            def _():
                col = lax.broadcasted_iota(jnp.int32, (r, t), 1)
                go(0, t, (col >= r) | (block < me))

    if final:
        low_ref = refs[4]
        for h in range(2):
            rows = slice(h * HEAD_DIM, (h + 1) * HEAD_DIM)
            total = st_ref[2 + h : 3 + h, :]
            a_ref[rows, :] = a_ref[rows, :] / total
            st_ref[h : h + 1, :] = st_ref[h : h + 1, :] * LC + jnp.log2(total)
        low_ref[...] = a_ref[...].T.astype(BF16)


def kv_specs(kvs, halves):
    if halves:
        r = kvs[0].shape[0]
        return [
            spec((r, 2 * LANES), lambda i: (0, jnp.minimum(i, PAIRS // 2 - 1))),
            spec((r, 2 * LANES), lambda i: (0, jnp.maximum(i - PAIRS // 2, 0))),
        ]
    return [spec((kv.shape[0], 2 * LANES), lambda i: (0, i)) for kv in kvs]


def fwd_local(sc, qt, kv_prompt, kv_own):
    t = qt.shape[1]
    keys = kv_own.shape[0]
    return pl.pallas_call(
        fwd_local_body,
        grid=(PAIRS,),
        in_specs=[
            SMEM_SPEC,
            spec((LANES, t), lambda i: (i, 0)),
            spec((t // 2, 2 * LANES), lambda i: (0, i)),
            spec((keys, 2 * LANES), lambda i: (0, i)),
        ],
        out_specs=[spec((8, t), lambda i: (i, 0)), spec((LANES, t), lambda i: (i, 0))],
        out_shape=[shape((8 * PAIRS, t), F32), shape((D, t), F32)],
        name="attend_local",
        **params((4 * 4 * t * keys * D, 4 * D * t)),
    )(sc, qt, kv_prompt, kv_own)


def fwd_remote(sc, qt, kvs, offsets, st, acc, halves=False, final=False):
    t = qt.shape[1]
    rows = len(offsets) * (t // 2)
    out_specs = [spec((8, t), lambda i: (i, 0)), spec((LANES, t), lambda i: (i, 0))]
    out_shape = [shape((8 * PAIRS, t), F32), shape((D, t), F32)]
    if final:
        out_specs.append(spec((t, LANES), lambda i: (0, i)))
        out_shape.append(shape((t, D), BF16))
    return pl.pallas_call(
        functools.partial(fwd_remote_body, tuple(offsets), len(kvs), halves, final),
        grid=(PAIRS,),
        in_specs=[SMEM_SPEC, spec((LANES, t), lambda i: (i, 0))]
        + kv_specs(kvs, halves)
        + [spec((8, t), lambda i: (i, 0)), spec((LANES, t), lambda i: (i, 0))],
        out_specs=out_specs,
        out_shape=out_shape,
        name="attend_remote",
        **params((4 * 4 * t * rows * D, 8 * D * t + 4 * D * rows)),
    )(sc, qt, *kvs, st, acc)


def back_block(ops, kb, vb, kt, lo, hi, mask, dq_ref):
    qz, qn, doz, don, lse, delta = ops
    dk = None
    dv = None
    for h in range(2):
        s = dot(kb, qz[h][:, lo:hi])
        dp = dot(vb, doz[h][:, lo:hi])
        p = jnp.exp2(s * LC - lse[h][:, lo:hi])
        if mask is not None:
            p = jnp.where(mask, p, 0.0)
        ds = (p * (dp - delta[h][:, lo:hi])).astype(BF16)
        dv_h = dot(p.astype(BF16), don[h][lo:hi])
        dk_h = dot(ds, qn[h][lo:hi])
        rows = slice(h * HEAD_DIM, (h + 1) * HEAD_DIM)
        dq_ref[rows, lo:hi] += dot(kt[rows], ds)
        dv = dv_h if dv is None else dv + dv_h
        dk = dk_h if dk is None else dk + dk_h
    return dk, dv


def back_operands(qt_ref, q_ref, dot_ref, do_ref, st_ref):
    qt, q, do_t, do = qt_ref[...], q_ref[...], dot_ref[...], do_ref[...]
    return (
        [head_rows(qt, h) for h in range(2)],
        [head_lanes(q, h) for h in range(2)],
        [head_rows(do_t, h) for h in range(2)],
        [head_lanes(do, h) for h in range(2)],
        [st_ref[h : h + 1, :] for h in range(2)],
        [st_ref[4 + h : 5 + h, :] for h in range(2)],
    )


def bwd_local_body(
    sc_ref, qt_ref, q_ref, dot_ref, do_ref, st_ref, dq_in, kv_ref, kvo_ref,
    out_ref, dkv_ref, dkvo_ref, dq_ref,
):
    t = qt_ref.shape[1]
    r = t // 2
    keys = kvo_ref.shape[0]
    ops = back_operands(qt_ref, q_ref, dot_ref, do_ref, st_ref)
    dq_ref[...] = dq_in[...]
    kb, vb = kv_ref[:, :LANES], kv_ref[:, LANES:]
    kbo, vbo = kvo_ref[:, :LANES], kvo_ref[:, LANES:]
    kt, kto = kb.T, kbo.T
    own, cont = local_masks(sc_ref, r, keys, 0, t)
    if r % LANES == 0:
        dk, dv = back_block(ops, kb, vb, kt, 0, r, own[:, :r], dq_ref)
        dk2, dv2 = back_block(ops, kb, vb, kt, r, t, None, dq_ref)
        dk, dv = dk + dk2, dv + dv2
        dko, dvo = back_block(ops, kbo, vbo, kto, r, t, cont[:, r:], dq_ref)
    else:
        dk, dv = back_block(ops, kb, vb, kt, 0, t, own, dq_ref)
        dko, dvo = back_block(ops, kbo, vbo, kto, 0, t, cont, dq_ref)
    dkv_ref[:, :LANES] = dk * SCALE
    dkv_ref[:, LANES:] = dv
    dkvo_ref[:, :LANES] = dko * SCALE
    dkvo_ref[:, LANES:] = dvo
    out_ref[...] = dq_ref[...].T * SCALE


def bwd_remote_body(
    offsets, count, halves, first, dtype, sc_ref, qt_ref, q_ref, dot_ref, do_ref, st_in, *refs
):
    t = qt_ref.shape[1]
    r = t // 2
    me = sc_ref[0]
    kv_refs, refs = refs[:count], refs[count:]
    src, refs = refs[0], refs[1:]
    dq_ref, refs = refs[0], refs[1:]
    out_refs, refs = refs[:count], refs[count:]
    sum_ref = refs[-1]
    if first:
        st_ref, refs = refs[0], refs[1:]
        st_ref[...] = st_in[...]
        prod = src[...] * dot_ref[...].astype(F32)
        for h in range(2):
            st_ref[4 + h : 5 + h, :] = jnp.sum(
                prod[h * HEAD_DIM : (h + 1) * HEAD_DIM], axis=0, keepdims=True
            )
        dq_ref[...] = jnp.zeros_like(dq_ref)
    else:
        st_ref = st_in
        dq_ref[...] = src[...]
    ops = back_operands(qt_ref, q_ref, dot_ref, do_ref, st_ref)
    split = len(offsets) != count and not halves

    def store(j, dk, dv):
        if halves:
            for part in range(2):

                @pl.when((pl.program_id(0) < PAIRS // 2) == (part == 0))
                def _():
                    out_refs[part][:, :LANES] = dk
                    out_refs[part][:, LANES:] = dv

        elif split:
            out_refs[0][j * r : (j + 1) * r, :LANES] = dk
            out_refs[0][j * r : (j + 1) * r, LANES:] = dv
        else:
            out_refs[j][:, :LANES] = dk
            out_refs[j][:, LANES:] = dv

    for j, offset in enumerate(offsets):
        block = sc_ref[3 + offset]

        def go(lo, hi, mask, add):
            if halves:
                kv = halves_value(*kv_refs)
            elif split:
                kv = kv_refs[0][j * r : (j + 1) * r, :]
            else:
                kv = kv_refs[j][...]
            kb = kv[:, :LANES]
            dk, dv = back_block(ops, kb, kv[:, LANES:], kb.T, lo, hi, mask, dq_ref)
            if add:
                dk, dv = dk + sum_ref[:, :LANES], dv + sum_ref[:, LANES:]
            sum_ref[:, :LANES] = dk
            sum_ref[:, LANES:] = dv

        if split:

            @pl.when(block == me)
            def _():
                sum_ref[...] = jnp.zeros_like(sum_ref)

        if r % LANES == 0:
            if split:
                pl.when(block != me)(lambda: go(r, t, None, False))
            else:
                go(r, t, None, False)

            @pl.when(block < me)
            def _():
                go(0, r, None, True)

        else:

            @pl.when(block != me)
            def _():
                col = lax.broadcasted_iota(jnp.int32, (r, t), 1)
                go(0, t, (col >= r) | (block < me), False)

        store(j, (sum_ref[:, :LANES] * SCALE).astype(dtype), sum_ref[:, LANES:].astype(dtype))


def q_specs(t):
    return [
        spec((LANES, t), lambda i: (i, 0)),
        spec((t, LANES), lambda i: (0, i)),
        spec((LANES, t), lambda i: (i, 0)),
        spec((t, LANES), lambda i: (0, i)),
        spec((8, t), lambda i: (i, 0)),
    ]


def bwd_local(sc, qt, q, do_t, do, st, dq, kv_prompt, kv_own):
    t = qt.shape[1]
    keys = kv_own.shape[0]
    return pl.pallas_call(
        bwd_local_body,
        grid=(PAIRS,),
        in_specs=[SMEM_SPEC]
        + q_specs(t)
        + [spec((LANES, t), lambda i: (i, 0))]
        + kv_specs((kv_prompt, kv_own), False),
        out_specs=[spec((t, LANES), lambda i: (0, i))] + kv_specs((kv_prompt, kv_own), False),
        out_shape=[
            shape((t, D), F32),
            shape((t // 2, 2 * D), F32),
            shape((keys, 2 * D), F32),
        ],
        scratch_shapes=[pltpu.VMEM((LANES, t), F32)],
        name="attend_back_local",
        **params((10 * 4 * t * keys * D, 16 * D * t)),
    )(sc, qt, q, do_t, do, st, dq, kv_prompt, kv_own)


def bwd_remote(
    sc, qt, q, do_t, do, st, src, kvs, offsets, halves=False, first=False, dtype=F32
):
    t = qt.shape[1]
    rows = len(offsets) * (t // 2)
    out_specs = [spec((LANES, t), lambda i: (i, 0))] + kv_specs(kvs, halves)
    out_shape = [shape((D, t), F32)] + [shape(kv.shape, dtype) for kv in kvs]
    if first:
        out_specs.append(spec((8, t), lambda i: (i, 0)))
        out_shape.append(shape((8 * PAIRS, t), F32))
    return pl.pallas_call(
        functools.partial(bwd_remote_body, tuple(offsets), len(kvs), halves, first, dtype),
        grid=(PAIRS,),
        in_specs=[SMEM_SPEC]
        + q_specs(t)
        + kv_specs(kvs, halves)
        + [spec((LANES, t), lambda i: (i, 0))],
        out_specs=out_specs,
        out_shape=out_shape,
        scratch_shapes=[pltpu.VMEM((t // 2, 2 * LANES), F32)],
        name="attend_back_remote",
        **params((10 * 4 * t * rows * D, 16 * D * t + 8 * D * rows)),
    )(sc, qt, q, do_t, do, st, *kvs, src)


def route_body(
    x_ref, att_ref, ow_ref, sw_ref, gain_ref, res_ref, rt_ref, tr_ref,
    h_ref, n_ref, pr_ref, xs_ref,
):
    t = x_ref.shape[0]
    step = pl.program_id(0)

    @pl.when(step == 0)
    def _():
        hidden = x_ref[...].astype(F32) + dot(att_ref[...], ow_ref[...])
        h_ref[...] = hidden
        scale = lax.rsqrt(jnp.mean(hidden * hidden, axis=-1, keepdims=True) + EPS)
        low = (hidden * scale * gain_ref[...]).astype(BF16)
        n_ref[...] = low
        z = dot(low, sw_ref[...])
        lane = lax.broadcasted_iota(jnp.int32, (t, LANES), 1)
        is_route = lane < EXPERTS + 4
        logits = jnp.where(is_route, z + res_ref[...], NEG)
        ex = jnp.exp(logits - jnp.max(logits, axis=-1, keepdims=True))
        probs = ex / jnp.sum(ex, axis=-1, keepdims=True)
        out = probs
        first = EXPERTS + 4
        for k in range(2):
            l0 = z[:, first + 2 * k : first + 2 * k + 1]
            l1 = z[:, first + 2 * k + 1 : first + 2 * k + 2]
            top = jnp.maximum(l0, l1)
            e0 = jnp.exp(l0 - top)
            e1 = jnp.exp(l1 - top)
            den = e0 + e1
            out = jnp.where(lane == first + 2 * k, e0 / den, out)
            out = jnp.where(lane == first + 2 * k + 1, e1 / den, out)
        for j in range(2):
            mix = jnp.sum(jnp.where(lane == rt_ref[:, j : j + 1], probs, 0.0), axis=-1, keepdims=True)
            out = jnp.where(lane == 16 + j, mix, out)
        pr_ref[...] = out

    slots = xs_ref.shape[0]
    base = step * slots
    slot = base + lax.broadcasted_iota(jnp.int32, (slots, t), 0)
    pick = (slot == tr_ref[0:1, :]) | (slot == tr_ref[1:2, :])
    xs_ref[...] = dot(pick.astype(BF16), n_ref[...]).astype(BF16)


def out_w_spec():
    return spec((D, D), lambda *_: (0, 3))


def small_w_spec():
    return spec((D, LANES), lambda *_: (0, 4 * D // LANES))


def grad_rows_body(g_ref, pr_ref, tr_ref, gs_ref, mg_ref):
    t = g_ref.shape[0]
    step = pl.program_id(0)

    @pl.when(step == 0)
    def _():
        g = g_ref[...].astype(F32)
        for j in range(2):
            mg_ref[j * t : (j + 1) * t, :] = (g * pr_ref[:, 16 + j : 17 + j]).astype(BF16)

    slots = gs_ref.shape[0]
    slot = step * slots + lax.broadcasted_iota(jnp.int32, (slots, t), 0)
    picks = [(slot == tr_ref[j : j + 1, :]).astype(BF16) for j in range(2)]
    gs_ref[...] = dot(jnp.concatenate(picks, axis=1), mg_ref[...]).astype(BF16)


def grad_rows_call(g, pr, tr, slots):
    t = g.shape[0]
    part = min(slots, 256)
    return pl.pallas_call(
        grad_rows_body,
        grid=(slots // part,),
        in_specs=[whole((t, D)), whole((t, LANES)), whole((2, t))],
        out_specs=spec((part, D), lambda i: (i, 0)),
        out_shape=shape((slots, D), BF16),
        scratch_shapes=[pltpu.VMEM((2 * t, D), BF16)],
        name="grad_rows",
        **params((4 * slots * t * D, 4 * t * D)),
    )(g, pr, tr)


def route_call(x, att, pack, gain, res, rt, tr, slots):
    t = x.shape[0]
    part = min(slots, 256)
    return pl.pallas_call(
        route_body,
        grid=(slots // part,),
        in_specs=[
            whole((t, D)), whole((t, D)), out_w_spec(), small_w_spec(), whole((1, D)),
            whole((t, LANES)), whole((t, 2)), whole((2, t)),
        ],
        out_specs=[
            whole((t, D)), whole((t, D)), whole((t, LANES)),
            spec((part, D), lambda i: (i, 0)),
        ],
        out_shape=[
            shape((t, D), F32), shape((t, D), BF16), shape((t, LANES), F32),
            shape((slots, D), BF16),
        ],
        name="route_dispatch",
        **params((2 * t * D * D + 2 * slots * t * D, 8 * t * D)),
    )(x, att, pack, pack, gain, res, rt, tr)


def expert_fwd_body(x_ref, w_ref, o_ref, acc_ref):
    step = pl.program_id(0)
    x = x_ref[...]
    wide = w_ref.shape[-1]
    wg = w_ref[:, 0].reshape(D, wide)
    wu = w_ref[:, 1].reshape(D, wide)
    wd = w_ref[:, 2].reshape(D, wide)
    gate = dot(x, wg)
    up = dot(x, wu)
    act = (gate / (1.0 + jnp.exp(-gate)) * up).astype(BF16)
    out = dot_nt(act, wd)

    @pl.when(step == 0)
    def _():
        acc_ref[...] = out

    @pl.when(step > 0)
    def _():
        acc_ref[...] += out

    @pl.when(step == pl.num_programs(0) - 1)
    def _():
        o_ref[...] = acc_ref[...].astype(BF16)


def expert_fwd(xr, w):
    rows = xr.shape[0]
    shards, _, per, wide = w.shape
    part = min(wide, 256)
    return pl.pallas_call(
        expert_fwd_body,
        grid=(wide // part,),
        in_specs=[whole((rows, D)), spec((shards, 3, per, part), lambda i: (0, 0, 0, i))],
        out_specs=whole((rows, D)),
        out_shape=shape((rows, D), BF16),
        scratch_shapes=[pltpu.VMEM((rows, D), F32)],
        name="expert_forward",
        **params((6 * rows * D * wide, 6 * D * wide)),
    )(xr, w)


def expert_in_body(x_ref, g_ref, w_ref, gi_ref, act_ref, dg_ref, du_ref, acc_ref):
    step = pl.program_id(0)
    wide = w_ref.shape[-1]
    wg = w_ref[:, 0].reshape(D, wide)
    wu = w_ref[:, 1].reshape(D, wide)
    wd = w_ref[:, 2].reshape(D, wide)

    @pl.loop(0, x_ref.shape[0] // ROW_TILE)
    def _(i):
        rows = pl.ds(pl.multiple_of(i * ROW_TILE, ROW_TILE), ROW_TILE)
        gate = dot(x_ref[rows, :], wg)
        up = dot(x_ref[rows, :], wu)
        ga = dot(g_ref[rows, :], wd)
        sig = 1.0 / (1.0 + jnp.exp(-gate))
        silu = gate * sig
        act_ref[rows, :] = (silu * up).astype(BF16)
        d_gate = (ga * up * sig * (1.0 + gate * (1.0 - sig))).astype(BF16)
        d_up = (ga * silu).astype(BF16)
        dg_ref[rows, :] = d_gate
        du_ref[rows, :] = d_up
        gi = dot_nt(d_gate, wg) + dot_nt(d_up, wu)

        @pl.when(step == 0)
        def _():
            acc_ref[rows, :] = gi

        @pl.when(step > 0)
        def _():
            acc_ref[rows, :] += gi

    @pl.when(step == pl.num_programs(0) - 1)
    def _():
        gi_ref[...] = acc_ref[...].astype(BF16)


def expert_in(xr, gr, w):
    rows = xr.shape[0]
    shards, _, per, wide = w.shape
    part = min(wide, 256)
    tile = spec((rows, part), lambda i: (0, i))
    return pl.pallas_call(
        expert_in_body,
        grid=(wide // part,),
        in_specs=[
            whole((rows, D)), whole((rows, D)),
            spec((shards, 3, per, part), lambda i: (0, 0, 0, i)),
        ],
        out_specs=[whole((rows, D)), tile, tile, tile],
        out_shape=[shape((rows, D), BF16)] + [shape((rows, wide), BF16)] * 3,
        scratch_shapes=[pltpu.VMEM((rows, D), F32)],
        name="expert_back_in",
        **params((10 * rows * D * wide, 12 * D * wide)),
    )(xr, gr, w)


def expert_weights_body(x_ref, gl_ref, act_ref, dg_ref, du_ref, dw_ref, xt_ref, gt_ref):
    @pl.when(pl.program_id(0) == 0)
    def _():
        gt_ref[...] = gl_ref[...].T
        xt_ref[...] = x_ref[...].T

    shards, _, per, wide = dw_ref.shape
    xt = xt_ref[...]
    dw_ref[:, 0] = dot(xt, dg_ref[...]).astype(BF16).reshape(shards, per, wide)
    dw_ref[:, 1] = dot(xt, du_ref[...]).astype(BF16).reshape(shards, per, wide)
    dw_ref[:, 2] = dot(gt_ref[...], act_ref[...]).astype(BF16).reshape(shards, per, wide)


def expert_weights(xr, low, act, d_gate, d_up, dims):
    rows = xr.shape[0]
    shards, _, per, wide = dims
    part = min(wide, 256)
    tile = spec((rows, part), lambda i: (0, i))
    return pl.pallas_call(
        expert_weights_body,
        grid=(wide // part,),
        in_specs=[whole((rows, D)), whole((rows, D)), tile, tile, tile],
        out_specs=spec((shards, 3, per, part), lambda i: (0, 0, 0, i)),
        out_shape=shape(dims, BF16),
        scratch_shapes=[pltpu.VMEM((D, rows), BF16), pltpu.VMEM((D, rows), BF16)],
        name="expert_weight_grads",
        **params((6 * rows * D * wide, 12 * D * wide)),
    )(xr, low, act, d_gate, d_up)


def mix_body(
    h_ref, g_ref, pr_ref, rt_ref, tc_ref, ret_ref, n_ref, sw_ref, rows_ref,
    out_ref, gn_ref, gl_ref, gs_ref,
):
    t = h_ref.shape[0]
    slots = ret_ref.shape[0]
    hidden = h_ref[...]
    g16 = g_ref[...]
    g = g16.astype(F32)
    pr = pr_ref[...]
    scale = lax.rsqrt(jnp.mean(hidden * hidden, axis=-1, keepdims=True) + EPS)
    normed = hidden * scale * rows_ref[2:3, :]
    lane = lax.broadcasted_iota(jnp.int32, (t, LANES), 1)
    slot = lax.broadcasted_iota(jnp.int32, (t, slots), 1)
    first = EXPERTS + 4
    ret = ret_ref[...]
    c0 = [pr[:, first + 2 * k : first + 2 * k + 1] for k in range(2)]
    c1 = [pr[:, first + 2 * k + 1 : first + 2 * k + 2] for k in range(2)]
    total = hidden
    s = jnp.zeros((t, LANES), F32)
    coef = jnp.zeros((t, 1), F32)
    weight = [jnp.zeros((t, 1), F32) for _ in range(2)]
    for j in range(2):
        route = rt_ref[:, j : j + 1]
        mix = pr[:, 16 + j : 17 + j]
        branch = dot((slot == tc_ref[:, j : j + 1]).astype(BF16), ret)
        keep = jnp.where(route == EXPERTS + 1, 1.0, 0.0)
        for k in range(2):
            here = jnp.where(route == EXPERTS + 2 + k, 1.0, 0.0)
            keep = keep + here * c0[k]
            weight[k] = weight[k] + here * mix
            branch = branch + (here * c1[k]) * rows_ref[k : k + 1, :]
        branch = branch + keep * normed
        coef = coef + mix * keep
        total = total + mix * branch
        gp = jnp.sum(g * branch, axis=-1, keepdims=True)
        s = s + jnp.where(lane == route, gp, 0.0)
    out_ref[...] = total.astype(BF16)
    probs = jnp.where(lane < first, pr, 0.0)
    d_logits = probs * (s - jnp.sum(probs * s, axis=-1, keepdims=True))
    gl_ref[...] = d_logits
    dz = d_logits
    dvec = jnp.zeros((t, LANES), F32)
    g_dot_n = jnp.sum(g * normed, axis=-1, keepdims=True)
    for k in range(2):
        d0 = weight[k] * g_dot_n
        d1 = weight[k] * jnp.sum(g * rows_ref[k : k + 1, :], axis=-1, keepdims=True)
        mean = c0[k] * d0 + c1[k] * d1
        dz = jnp.where(lane == first + 2 * k, c0[k] * (d0 - mean), dz)
        dz = jnp.where(lane == first + 2 * k + 1, c1[k] * (d1 - mean), dz)
        dvec = jnp.where(lane == 16 + k, weight[k] * c1[k], dvec)
    hi, lo = split_hi_lo(dz)
    sw = sw_ref[...]
    gn_ref[...] = coef * g + (dot_nt(hi, sw) + dot_nt(lo, sw))
    nt = n_ref[...].T
    gt = g16.T
    vhi, vlo = split_hi_lo(dvec)
    gs = dot(nt, hi) + dot(nt, lo) + dot(gt, vhi) + dot(gt, vlo)

    @pl.when(pl.program_id(0) == 0)
    def _():
        gs_ref[...] = gs

    @pl.when(pl.program_id(0) > 0)
    def _():
        gs_ref[...] += gs


def mix_call(hidden, g, pr, rt, tc, ret, low, pack, rows):
    t = hidden.shape[0]
    half = min(t, LANES)
    slots = ret.shape[0]
    tile = spec((half, D), lambda i: (i, 0))
    lane_tile = spec((half, LANES), lambda i: (i, 0))
    pair = spec((half, 2), lambda i: (i, 0))
    return pl.pallas_call(
        mix_body,
        grid=(t // half,),
        in_specs=[
            tile, tile, lane_tile, pair, pair, whole((slots, D)), tile, small_w_spec(),
            whole((8, D)),
        ],
        out_specs=[tile, tile, lane_tile, whole((D, LANES))],
        out_shape=[
            shape((t, D), BF16), shape((t, D), F32), shape((t, LANES), F32), shape((D, LANES), F32),
        ],
        name="mixture",
        **params((4 * t * slots * D, 12 * t * D)),
    )(hidden, g, pr, rt, tc, ret, low, pack, rows)


def norm_back_body(
    h_ref, g_ref, gn_ref, tc_ref, ret_ref, rows_ref, ow_ref, att_ref,
    gh_ref, do_ref, dot_ref, gow_ref, gg_ref,
):
    t = h_ref.shape[0]
    slots = ret_ref.shape[0]
    hidden = h_ref[...]
    slot = lax.broadcasted_iota(jnp.int32, (t, slots), 1)
    pick = (slot == tc_ref[:, 0:1]) | (slot == tc_ref[:, 1:2])
    gn = gn_ref[...] + dot(pick.astype(BF16), ret_ref[...])
    q = lax.rsqrt(jnp.mean(hidden * hidden, axis=-1, keepdims=True) + EPS)
    u = gn * rows_ref[2:3, :]
    mean = jnp.mean(u * hidden, axis=-1, keepdims=True)
    gh = g_ref[...].astype(F32) + q * u - hidden * (q * q * q * mean)
    gh_ref[...] = gh
    gb = gh.astype(BF16)
    d_out = dot_nt(gb, ow_ref[...])
    do_ref[...] = d_out.astype(BF16)
    dot_ref[...] = d_out.T.astype(BF16)
    gow = dot(att_ref[...].T, gb)
    gain = jnp.sum(gn * hidden * q, axis=0, keepdims=True)

    @pl.when(pl.program_id(0) == 0)
    def _():
        gow_ref[...] = gow
        gg_ref[...] = jnp.broadcast_to(gain, gg_ref.shape)

    @pl.when(pl.program_id(0) > 0)
    def _():
        gow_ref[...] += gow
        gg_ref[...] += jnp.broadcast_to(gain, gg_ref.shape)


def norm_back_call(hidden, g, gn, tc, ret, rows, pack, att):
    t = hidden.shape[0]
    half = t // 2 if (t // 2) % LANES == 0 else t
    slots = ret.shape[0]
    tile = spec((half, D), lambda i: (i, 0))
    return pl.pallas_call(
        norm_back_body,
        grid=(t // half,),
        in_specs=[
            tile, tile, tile, spec((half, 2), lambda i: (i, 0)), whole((slots, D)), whole((8, D)),
            out_w_spec(), tile,
        ],
        out_specs=[tile, tile, spec((D, half), lambda i: (0, i)), whole((D, D)), whole((8, D))],
        out_shape=[
            shape((t, D), F32), shape((t, D), BF16), shape((D, t), BF16), shape((D, D), F32),
            shape((8, D), F32),
        ],
        name="norm_two_back",
        **params((2 * t * slots * D + 4 * t * D * D, 16 * t * D)),
    )(hidden, g, gn, tc, ret, rows, pack, att)


def store_grad(sc_ref, split, value, refs):
    if not split:
        refs[0][...] = value
        return
    send_ref, keep_ref = refs
    per = value.shape[0] // 4
    for core in range(2):

        @pl.when(sc_ref[11] == core)
        def _():
            for part in range(2):
                mine = (2 * part + core) * per
                other = (2 * part + 1 - core) * per
                send_ref[part] = value[other : other + per].astype(BF16)
                keep_ref[part] = value[mine : mine + per]


def grad_outs(split, width):
    block = 2 * LANES
    if not split:
        return [spec((D, block), lambda i: (0, i))], [shape((D, width), F32)]
    dims = (2, D // 4, width)
    tile = spec((2, D // 4, block), lambda i: (0, 0, i))
    return [tile, tile], [shape(dims, BF16), shape(dims, F32)]


def q_back_body(split, sc_ref, n_ref, dq_ref, c_ref, s_ref, w_ref, gn_ref, *refs):
    nt_ref = refs[-1]
    step = pl.program_id(0)

    @pl.when(step == 0)
    def _():
        nt_ref[...] = n_ref[...].T

    cosine = c_ref[...]
    sine = s_ref[...]
    v0 = dq_ref[:, :LANES]
    v1 = dq_ref[:, LANES:]
    gq = jnp.concatenate(
        [
            (v0 * cosine - partner(v0) * sine).astype(BF16),
            (v1 * cosine - partner(v1) * sine).astype(BF16),
        ],
        axis=1,
    )
    store_grad(sc_ref, split, dot(nt_ref[...], gq), refs[:-1])
    gn = dot_nt(gq, w_ref[...])

    @pl.when(step == 0)
    def _():
        gn_ref[...] = gn

    @pl.when(step > 0)
    def _():
        gn_ref[...] += gn


def q_back_call(sc, low, dq, cosine, sine, pack, split):
    t = low.shape[0]
    specs, shapes = grad_outs(split, D)
    return pl.pallas_call(
        functools.partial(q_back_body, split),
        grid=(PAIRS // 2,),
        in_specs=[
            SMEM_SPEC, whole((t, D)), spec((t, 2 * LANES), lambda i: (0, i)), whole((t, LANES)),
            whole((t, LANES)), spec((D, 2 * LANES), lambda i: (0, i)),
        ],
        out_specs=[whole((t, D))] + specs,
        out_shape=[shape((t, D), F32)] + shapes,
        scratch_shapes=[pltpu.VMEM((D, t), BF16)],
        name="q_back",
        **params((4 * t * D * D, 12 * t * D)),
    )(sc, low, dq, cosine, sine, pack)


def kv_back_body(
    split, count, sc_ref, x_ref, n_ref, gnq_ref, gh_ref, gain_ref, c_ref, s_ref, wk_ref, wv_ref,
    own_ref, cont_ref, *refs
):
    got_refs, refs = refs[:count], refs[count:]
    gi_ref, grads, (nt_ref, gn_ref) = refs[0], refs[1:-2], refs[-2:]
    step = pl.program_id(0)

    @pl.when(step == 0)
    def _():
        nt_ref[...] = n_ref[...].T
        gn_ref[...] = gnq_ref[...]

    own = own_ref[...]
    for got in got_refs:
        own = own + got[...].astype(F32)
    total = jnp.concatenate([own, cont_ref[...]], axis=0)
    k = total[:, :LANES]
    gk = (k * c_ref[...] - partner(k) * s_ref[...]).astype(BF16)
    gkv = jnp.concatenate([gk, total[:, LANES:].astype(BF16)], axis=1)
    store_grad(sc_ref, split, dot(nt_ref[...], gkv), grads)
    gn_ref[...] += dot_nt(gkv, jnp.concatenate([wk_ref[...], wv_ref[...]], axis=1))

    @pl.when(step == pl.num_programs(0) - 1)
    def _():
        gn = gn_ref[...]
        x = x_ref[...].astype(F32)
        q = lax.rsqrt(jnp.mean(x * x, axis=-1, keepdims=True) + EPS)
        u = gn * gain_ref[...]
        mean = jnp.mean(u * x, axis=-1, keepdims=True)
        gi_ref[...] = gh_ref[...] + q * u - x * (q * q * q * mean)


def kv_back_call(sc, x, low, gn, gh, gain, cosine, sine, pack, own, cont, got, split):
    t = x.shape[0]
    r = t // 2
    specs, shapes = grad_outs(split, 2 * D)
    wide = spec((r, 2 * LANES), lambda i: (0, i))
    return pl.pallas_call(
        functools.partial(kv_back_body, split, len(got)),
        grid=(PAIRS,),
        in_specs=[
            SMEM_SPEC, whole((t, D)), whole((t, D)), whole((t, D)), whole((t, D)), whole((1, D)),
            whole((t, LANES)), whole((t, LANES)),
            spec((D, LANES), lambda i: (0, PAIRS + i)),
            spec((D, LANES), lambda i: (0, 2 * PAIRS + i)),
            wide, wide,
        ]
        + [wide] * len(got),
        out_specs=[whole((t, D))] + specs,
        out_shape=[shape((t, D), F32)] + shapes,
        scratch_shapes=[pltpu.VMEM((D, t), BF16), pltpu.VMEM((t, D), F32)],
        name="kv_back",
        **params((8 * t * D * D, 24 * t * D)),
    )(sc, x, low, gn, gh, gain, cosine, sine, pack, pack, own, cont, *got)


def rotation_tables(position):
    half = HEAD_DIM // 2
    frequency = 10000.0 ** (-jnp.arange(half, dtype=F32) / half)
    angles = position[:, None] * frequency[None, :]
    cosine, sine = jnp.cos(angles), jnp.sin(angles)
    return (
        jnp.concatenate([cosine] * 4, axis=1),
        jnp.concatenate([-sine, sine, -sine, sine], axis=1),
    )


def to_rows(array):
    return jnp.transpose(array, (1, 0, 2)).reshape(2 * array.shape[0], array.shape[2])


def from_rows(array):
    r = array.shape[0] // 2
    return jnp.transpose(array.reshape(2, r, array.shape[1]), (1, 0, 2))


RING = (0, 2, 4, 6, 7, 5, 3, 1)


def ring_offsets():
    place = {e: i for i, e in enumerate(RING)}
    return [[RING[(place[e] + k) % 8] for k in range(8)] for e in range(8)]


def along_ring(array, step):
    pairs = [(RING[i], RING[(i + step) % 8]) for i in range(8)]
    return lax.ppermute(array, "expert", pairs)


def tie(*values):
    return lax.optimization_barrier(values)


def swap_core(array):
    return lax.ppermute(array, "dp", [(0, 1), (1, 0), (2, 3), (3, 2)])


def add_and_cross(keep, got):
    across = lax.axis_index("dp") // 2
    keep = keep + got.astype(F32)
    send = lax.dynamic_index_in_dim(keep, 1 - across, 0, keepdims=False).astype(BF16)
    mine = lax.dynamic_index_in_dim(keep, across, 0, keepdims=False)
    return mine, lax.ppermute(send, "dp", [(0, 2), (2, 0), (1, 3), (3, 1)])


def add_and_scatter(keep, got):
    keep = (keep + got.astype(F32)).astype(BF16)
    rows, w = keep.shape
    return lax.all_to_all(
        keep.reshape(8, rows // 8, w), "expert", split_axis=0, concat_axis=0, tiled=True
    )


def add_up(got):
    return jnp.sum(got.astype(F32), axis=0)


def scatter_all(array):
    return lax.psum_scatter(
        array.astype(BF16), ALL_AXES, scatter_dimension=0, tiled=True
    ).astype(F32)


def per_device(
    hidden_in, cotangent, gate_residual, routes, groups, lengths, attn_gain, qkv_weight, out_weight,
    ffn_gain, router_weight, const_proj, const_vec, gate_weight, up_weight, down_weight,
):
    del groups
    r = hidden_in.shape[0]
    t = 2 * r
    capacity = r // 2
    owners = lax.axis_size("expert")
    copies = owners // EXPERTS
    slots = EXPERTS * capacity
    me = lax.axis_index("expert")
    per_cont = max(CONT_LEN // r, 1)

    small = jnp.concatenate(
        [
            router_weight, const_proj, const_vec, attn_gain[:, None], ffn_gain[:, None],
            jnp.zeros((attn_gain.shape[0], LANES - 20), BF16),
        ],
        axis=1,
    )
    pack = lax.all_gather(
        jnp.concatenate([qkv_weight, out_weight, small], axis=1), ALL_AXES, axis=0, tiled=True
    )
    index = jnp.arange(r, dtype=jnp.int32)
    row_ids = me * r + index
    position = jnp.concatenate([row_ids, PROMPT + row_ids % CONT_LEN]).astype(F32)
    cosine, sine = rotation_tables(position)
    cont = (me * r) // CONT_LEN
    length = lax.dynamic_slice(lengths, (cont,), (1,))
    header = jnp.stack([me, (me * r) % CONT_LEN]).astype(jnp.int32)
    header = jnp.concatenate([header, length.astype(jnp.int32)])
    ring = owners == 8
    if ring:
        ids = lax.dynamic_index_in_dim(jnp.asarray(ring_offsets(), jnp.int32), me, 0, keepdims=False)
    else:
        ids = jnp.arange(owners, dtype=jnp.int32)
    sc = jnp.concatenate([header, ids, (lax.axis_index("dp") % 2).astype(jnp.int32)[None]])

    picked = to_rows(routes)
    flat = jnp.transpose(picked).reshape(2 * t)
    hot = flat[:, None] == jnp.arange(EXPERTS, dtype=jnp.int32)[None, :]
    earlier = jnp.arange(2 * t)[:, None] > jnp.arange(2 * t)[None, :]
    before = jnp.dot(earlier.astype(BF16), hot.astype(BF16), preferred_element_type=F32)
    slot_index = jnp.sum(jnp.where(hot, before, 0.0), axis=1).astype(jnp.int32)
    target = jnp.where(flat < EXPERTS, flat * capacity + slot_index, -1)
    target_rows = target.reshape(2, t)
    target_cols = jnp.transpose(target_rows)

    def to_owners(rows):
        w = rows.shape[-1]
        shaped = rows.reshape(EXPERTS, 1, capacity, w)
        return jnp.broadcast_to(shaped, (EXPERTS, copies, capacity, w)).reshape(owners, capacity, w)

    def exchange(rows):
        got = lax.all_to_all(rows, "expert", split_axis=0, concat_axis=0, tiled=True)
        return got.reshape(owners * got.shape[1], got.shape[2])

    def from_owners(rows):
        got = exchange(rows.reshape(owners, capacity, D))
        if copies == 1:
            return got
        got = got.reshape(EXPERTS, copies, capacity, D).astype(F32)
        return jnp.sum(got, axis=1).reshape(slots, D).astype(BF16)

    x = to_rows(hidden_in)
    g = to_rows(cotangent)
    small_w = pack[:, 4 * D :]
    small_rows = jnp.transpose(small_w[:, 16:24]).astype(F32)
    gain_one = small_rows[2:3]
    rows_two = jnp.concatenate([small_rows[0:2], small_rows[3:4], small_rows[3:8]], axis=0)
    gain_two = small_rows[3:4]

    low_one, q, q_t, kv_prompt, kv_cont = qkv_call(x, gain_one, pack, cosine, sine)
    if not ring:
        kv_all = lax.all_gather(kv_prompt, "expert", axis=0, tiled=True)
    if per_cont == 1:
        kv_own = kv_cont
    else:
        cont_groups = [
            [c * per_cont + i for i in range(per_cont)] for c in range(owners // per_cont)
        ]
        kv_own = lax.all_gather(
            kv_cont, "expert", axis=0, tiled=True, axis_index_groups=cont_groups
        )
    weights = lax.all_gather(
        jnp.stack([gate_weight, up_weight, down_weight]), "dp", axis=0, tiled=False
    )
    if ring:
        right, left = [kv_prompt], [kv_prompt]
        for i in range(3):
            right.append(along_ring(right[i], 1))
            left.append(along_ring(left[i], -1))
            if i == 0:
                st, acc = fwd_local(sc, q_t, kv_prompt, kv_own)
            else:
                st, acc = fwd_remote(sc, q_t, (right[i], left[i]), (8 - i, i), st, acc)
            right[i + 1], left[i + 1], st = tie(right[i + 1], left[i + 1], st)
        far = [along_ring(right[3][:, :D], 1), along_ring(left[3][:, D:], -1)]
        st, acc = fwd_remote(sc, q_t, (right[3], left[3]), (5, 3), st, acc)
        st, att_t, att = fwd_remote(sc, q_t, far, (4,), st, acc, halves=True, final=True)
    else:
        st, acc = fwd_local(sc, q_t, kv_prompt, kv_own)
        st, att_t, att = fwd_remote(sc, q_t, (kv_all,), range(owners), st, acc, final=True)

    res = jnp.pad(to_rows(gate_residual), ((0, 0), (0, LANES - EXPERTS - 4)))
    hidden, low_two, pr, x_send = route_call(
        x, att, pack, gain_two, res, picked, target_rows, slots
    )
    x_got = exchange(to_owners(x_send))
    g_send = grad_rows_call(g, pr, target_rows, slots)
    x_got, g_send = tie(x_got, g_send)
    g_got = exchange(to_owners(g_send))
    expert_rows = expert_fwd(x_got, weights)
    out_back = from_owners(expert_rows)
    grad_in, act, d_gate, d_up = expert_in(x_got, g_got, weights)
    in_back = from_owners(grad_in)
    output, gn, grad_logits, grad_small = mix_call(
        hidden, g, pr, picked, target_cols, out_back, low_two, pack, rows_two
    )
    act, gn = tie(act, gn)
    grad_w = expert_weights(x_got, g_got, act, d_gate, d_up, weights.shape)
    grad_expert = lax.psum_scatter(
        grad_w.reshape(-1, grad_w.shape[-1]), "dp", scatter_dimension=0, tiled=True
    ).astype(F32)
    gh, d_att, d_att_t, grad_ow, gg_two = norm_back_call(
        hidden, g, gn, target_cols, in_back, rows_two, pack, att
    )

    early = jnp.concatenate(
        [grad_ow, grad_small[:, :19], jnp.transpose(gg_two[0:1]), jnp.zeros((D, LANES - 20), F32)],
        axis=1,
    )
    back = (sc, q_t, q, d_att_t, d_att)
    if ring:
        parts = early.reshape(2, 2, D // 4, D + LANES)
        core = lax.axis_index("dp") % 2
        early_keep = lax.dynamic_index_in_dim(parts, core, 1, keepdims=False)
        early_got = swap_core(
            lax.dynamic_index_in_dim(parts, 1 - core, 1, keepdims=False).astype(BF16)
        )
        dq_t, send_r, send_l, st = bwd_remote(
            *back, st, att_t, far, (4,), halves=True, first=True, dtype=BF16
        )
        for i in range(3, 0, -1):
            got_r, got_l = along_ring(send_r, 1), along_ring(send_l, -1)
            dq_t, part_r, part_l = bwd_remote(
                *back, st, dq_t, (left[i], right[i]), (i, 8 - i)
            )
            got_r, got_l, part_r, part_l, dq_t, early_got = tie(
                got_r, got_l, part_r, part_l, dq_t, early_got
            )
            if i == 3:
                send_r = jnp.concatenate([part_r[:, :D] + got_r.astype(F32), part_r[:, D:]], axis=1)
                send_l = jnp.concatenate([part_l[:, :D], part_l[:, D:] + got_l.astype(F32)], axis=1)
                early_keep, early_got = add_and_cross(early_keep, early_got)
            else:
                send_r, send_l = part_r + got_r.astype(F32), part_l + got_l.astype(F32)
            send_r, send_l = send_r.astype(BF16), send_l.astype(BF16)
        send_r, send_l, dq_t = tie(send_r, send_l, dq_t)
        got_r = along_ring(send_r, 1)
        got_l = along_ring(send_l, -1)
        got = (got_r, got_l)
        dq, dkv_own, dkv_cont = bwd_local(*back, st, dq_t, kv_prompt, kv_own)
    else:
        dq_t, dkv_all, st = bwd_remote(
            *back, st, att_t, (kv_all,), range(owners), first=True, dtype=BF16
        )
        dq, dkv_own, dkv_cont = bwd_local(*back, st, dq_t, kv_prompt, kv_own)
        got = (lax.psum_scatter(dkv_all, "expert", scatter_dimension=0, tiled=True),)
        early = scatter_all(early)
    if per_cont > 1:
        dkv_cont = lax.psum_scatter(
            dkv_cont, "expert", scatter_dimension=0, tiled=True, axis_index_groups=cont_groups
        )
    gn_q, *grad_q = q_back_call(sc, low_one, dq, cosine, sine, pack, ring)
    if ring:
        keep_q, got_q = add_and_cross(grad_q[1], swap_core(grad_q[0]))
        keep_q, got_q, got_0, got_1 = tie(keep_q, got_q, *got)
        got = (got_0, got_1)
    grad_input, *grad_kv = kv_back_call(
        sc, x, low_one, gn_q, gh, gain_one, cosine, sine, pack, dkv_own, dkv_cont, got, ring
    )
    output, grad_input = from_rows(output), from_rows(grad_input)
    if ring:
        got_kv = swap_core(grad_kv[0])
        got_q = add_and_scatter(
            jnp.concatenate([early_keep, keep_q], axis=1), jnp.concatenate([early_got, got_q], axis=1)
        )
        keep_kv, got_kv = add_and_cross(grad_kv[1], got_kv)
        got_kv, grad_expert, output, grad_input = tie(got_kv, grad_expert, output, grad_input)
        summed = add_up(got_q)
        early, late_q = summed[:, : D + LANES], summed[:, D + LANES :]
        late_kv = add_up(add_and_scatter(keep_kv, got_kv))
    else:
        late_q, late_kv = scatter_all(grad_q[0]), scatter_all(grad_kv[0])
    per = late_kv.shape[0]
    late_kv = jnp.transpose(late_kv.reshape(per, PAIRS, 2, LANES), (0, 2, 1, 3))
    late = jnp.concatenate([late_q, late_kv.reshape(per, 2 * D)], axis=1)
    grad_gain = jnp.sum(late * qkv_weight.astype(F32), axis=1) / attn_gain.astype(F32)
    tail = early[:, D:]
    per = grad_expert.shape[0] // 3
    return (
        output,
        grad_input,
        from_rows(grad_logits)[:, :, : EXPERTS + 4],
        grad_gain,
        late,
        early[:, :D],
        tail[:, 19],
        tail[:, :12],
        tail[:, 12:16],
        tail[:, 16:18],
        grad_expert[:per],
        grad_expert[per : 2 * per],
        grad_expert[2 * per :],
    )


def solution(mesh):
    rows = P(ALL_AXES, None, None)
    flat = P(ALL_AXES)
    mat = P(ALL_AXES, None)
    expert = P("dp", "expert")
    in_specs = (
        rows, rows, rows, rows, P("dp"), P("dp"), flat, mat, mat, flat, mat, mat, mat,
        expert, expert, expert,
    )
    out_specs = (
        rows, rows, rows, flat, mat, mat, flat, mat, mat, mat, expert, expert, expert,
    )

    return jax.shard_map(
        per_device, mesh=mesh, in_specs=in_specs, out_specs=out_specs, check_vma=False
    )
```

```python
import functools

import jax
import jax.numpy as jnp
from jax import lax
from jax.experimental import pallas as pl
from jax.experimental.pallas import tpu as pltpu
from jax.sharding import PartitionSpec as P


D = 768
HEAD_DIM = 64
PAIRS = 6
EXPERTS = 8
CONT_LEN = 256
PROMPT = 2048
LANES = 128
EPS = 1e-06
NEG = -1e30
LOG2E = 1.4426950408889634
SCALE = float(HEAD_DIM) ** (-0.5)
LC = SCALE * LOG2E
F32 = jnp.float32
BF16 = jnp.bfloat16
ALL_AXES = ("dp", "expert")
VMEM_LIMIT = 60 * 1024 * 1024


def dot(a, b):
    return jnp.dot(a, b, preferred_element_type=F32)


def dot_nt(a, b):
    return lax.dot_general(a, b, (((1,), (1,)), ((), ())), preferred_element_type=F32)


def split_hi_lo(v):
    hi = v.astype(BF16)
    return hi, (v - hi.astype(F32)).astype(BF16)


def params(cost=None):
    return dict(
        compiler_params=pltpu.CompilerParams(vmem_limit_bytes=VMEM_LIMIT),
        cost_estimate=None if cost is None else pl.CostEstimate(
            flops=int(cost[0]), bytes_accessed=int(cost[1]), transcendentals=0
        ),
    )


def shape(dims, dtype):
    return jax.ShapeDtypeStruct(tuple(dims), dtype)


def spec(block, index):
    return pl.BlockSpec(tuple(block), index)


def whole(dims):
    return pl.BlockSpec(tuple(dims), lambda *_: (0,) * len(dims))


SMEM_SPEC = pl.BlockSpec(memory_space=pltpu.SMEM)


def partner(v):
    lane = lax.broadcasted_iota(jnp.int32, v.shape, 1)
    return jnp.where((lane & 63) < 32, pltpu.roll(v, 96, 1), pltpu.roll(v, 32, 1))


def qkv_body(x_ref, gain_ref, wq_ref, wk_ref, wv_ref, c_ref, s_ref, n_ref, q_ref, qt_ref, kvp_ref, kvc_ref):
    @pl.when(pl.program_id(0) == 0)
    def _():
        x = x_ref[...].astype(F32)
        scale = lax.rsqrt(jnp.mean(x * x, axis=-1, keepdims=True) + EPS)
        n_ref[...] = (x * scale * gain_ref[...]).astype(BF16)

    n = n_ref[...]
    cosine = c_ref[...]
    sine = s_ref[...]
    kv = dot(n, jnp.concatenate([wk_ref[...], wv_ref[...]], axis=1))
    k = kv[:, :LANES]
    k = (k * cosine + partner(k) * sine).astype(BF16)
    v = kv[:, LANES:].astype(BF16)
    r = k.shape[0] // 2
    kvp_ref[:, :LANES] = k[:r]
    kvp_ref[:, LANES:] = v[:r]
    kvc_ref[:, :LANES] = k[r:]
    kvc_ref[:, LANES:] = v[r:]
    q = dot(n, wq_ref[...])
    q = q * cosine + partner(q) * sine
    q_ref[...] = q.astype(BF16)
    qt_ref[...] = q.T.astype(BF16)


def qkv_call(x, gain, pack, cosine, sine):
    t = x.shape[0]
    return pl.pallas_call(
        qkv_body,
        grid=(PAIRS,),
        in_specs=[
            whole((t, D)),
            whole((1, D)),
            spec((D, LANES), lambda i: (0, i)),
            spec((D, LANES), lambda i: (0, PAIRS + i)),
            spec((D, LANES), lambda i: (0, 2 * PAIRS + i)),
            whole((t, LANES)),
            whole((t, LANES)),
        ],
        out_specs=[
            whole((t, D)),
            spec((t, LANES), lambda i: (0, i)),
            spec((LANES, t), lambda i: (i, 0)),
            spec((t // 2, 2 * LANES), lambda i: (0, i)),
            spec((t // 2, 2 * LANES), lambda i: (0, i)),
        ],
        out_shape=[
            shape((t, D), BF16),
            shape((t, D), BF16),
            shape((D, t), BF16),
            shape((t // 2, 2 * D), BF16),
            shape((t // 2, 2 * D), BF16),
        ],
        name="qkv_rope",
        **params((2 * t * D * 3 * D, 6 * D * D)),
    )(x, gain, pack, pack, pack, cosine, sine)


def head_rows(v, h):
    row = lax.broadcasted_iota(jnp.int32, v.shape, 0)
    return jnp.where(row // HEAD_DIM == h, v, jnp.zeros_like(v))


def head_lanes(v, h):
    lane = lax.broadcasted_iota(jnp.int32, v.shape, 1)
    return jnp.where(lane // HEAD_DIM == h, v, jnp.zeros_like(v))


def attend_update(qz, kb, vt, lo, hi, mask, st_ref, a_ref, first):
    for h in range(2):
        s = dot(kb, qz[h][:, lo:hi])
        if mask is not None:
            s = jnp.where(mask, s, NEG)
        top = jnp.max(s, axis=0, keepdims=True)
        rows = slice(h * HEAD_DIM, (h + 1) * HEAD_DIM)
        if first:
            p = jnp.exp2((s - top) * LC)
            st_ref[h : h + 1, lo:hi] = top
            st_ref[2 + h : 3 + h, lo:hi] = jnp.sum(p, axis=0, keepdims=True)
            a_ref[rows, lo:hi] = dot(vt[rows], p.astype(BF16))
        else:
            old = st_ref[h : h + 1, lo:hi]
            new = jnp.maximum(old, top)
            alpha = jnp.exp2((old - new) * LC)
            p = jnp.exp2((s - new) * LC)
            st_ref[h : h + 1, lo:hi] = new
            st_ref[2 + h : 3 + h, lo:hi] = st_ref[2 + h : 3 + h, lo:hi] * alpha + jnp.sum(
                p, axis=0, keepdims=True
            )
            a_ref[rows, lo:hi] = a_ref[rows, lo:hi] * alpha + dot(vt[rows], p.astype(BF16))


def local_masks(sc_ref, r, keys, lo, hi):
    cpos = sc_ref[1]
    length = sc_ref[2]
    col = lo + lax.broadcasted_iota(jnp.int32, (r, hi - lo), 1)
    row = lax.broadcasted_iota(jnp.int32, (r, hi - lo), 0)
    own = (row <= col) | (col >= r)
    col = lo + lax.broadcasted_iota(jnp.int32, (keys, hi - lo), 1)
    row = lax.broadcasted_iota(jnp.int32, (keys, hi - lo), 0)
    cont = (col >= r) & (row <= cpos + col - r) & (row < length)
    return own, cont


def fwd_local_body(sc_ref, qt_ref, kv_ref, kvo_ref, st_ref, a_ref):
    t = qt_ref.shape[1]
    r = t // 2
    keys = kvo_ref.shape[0]
    qt = qt_ref[...]
    qz = [head_rows(qt, h) for h in range(2)]
    kb = kv_ref[:, :LANES]
    vt = kv_ref[:, LANES:].T
    kbo = kvo_ref[:, :LANES]
    vto = kvo_ref[:, LANES:].T
    st_ref[...] = jnp.zeros_like(st_ref)
    own, cont = local_masks(sc_ref, r, keys, 0, t)
    if r % LANES == 0:
        attend_update(qz, kb, vt, 0, r, own[:, :r], st_ref, a_ref, True)
        attend_update(qz, kb, vt, r, t, None, st_ref, a_ref, True)
        attend_update(qz, kbo, vto, r, t, cont[:, r:], st_ref, a_ref, False)
    else:
        attend_update(qz, kb, vt, 0, t, own, st_ref, a_ref, True)
        attend_update(qz, kbo, vto, 0, t, cont, st_ref, a_ref, False)


def halves_value(a_ref, b_ref):
    return jnp.where(pl.program_id(0) < PAIRS // 2, a_ref[...], b_ref[...])


def fwd_remote_body(offsets, count, halves, final, sc_ref, qt_ref, *refs):
    kv_refs, refs = refs[:count], refs[count:]
    st_in, a_in, st_ref, a_ref = refs[:4]
    t = qt_ref.shape[1]
    r = t // 2
    me = sc_ref[0]
    qt = qt_ref[...]
    qz = [head_rows(qt, h) for h in range(2)]
    st_ref[...] = st_in[...]
    a_ref[...] = a_in[...]
    for j, offset in enumerate(offsets):
        block = sc_ref[3 + offset]

        def go(lo, hi, mask):
            if halves:
                kv = halves_value(*kv_refs)
            elif len(kv_refs) == len(offsets):
                kv = kv_refs[j][...]
            else:
                kv = kv_refs[0][j * r : (j + 1) * r, :]
            attend_update(qz, kv[:, :LANES], kv[:, LANES:].T, lo, hi, mask, st_ref, a_ref, False)

        if r % LANES == 0:

            @pl.when(block < me)
            def _():
                go(0, t, None)

            @pl.when(block > me)
            def _():
                go(r, t, None)

        else:

            @pl.when(block != me)
            def _():
                col = lax.broadcasted_iota(jnp.int32, (r, t), 1)
                go(0, t, (col >= r) | (block < me))

    if final:
        low_ref = refs[4]
        for h in range(2):
            rows = slice(h * HEAD_DIM, (h + 1) * HEAD_DIM)
            total = st_ref[2 + h : 3 + h, :]
            a_ref[rows, :] = a_ref[rows, :] / total
            st_ref[h : h + 1, :] = st_ref[h : h + 1, :] * LC + jnp.log2(total)
        low_ref[...] = a_ref[...].T.astype(BF16)


def kv_specs(kvs, halves):
    if halves:
        r = kvs[0].shape[0]
        return [
            spec((r, 2 * LANES), lambda i: (0, jnp.minimum(i, PAIRS // 2 - 1))),
            spec((r, 2 * LANES), lambda i: (0, jnp.maximum(i - PAIRS // 2, 0))),
        ]
    return [spec((kv.shape[0], 2 * LANES), lambda i: (0, i)) for kv in kvs]


def fwd_local(sc, qt, kv_prompt, kv_own):
    t = qt.shape[1]
    keys = kv_own.shape[0]
    return pl.pallas_call(
        fwd_local_body,
        grid=(PAIRS,),
        in_specs=[
            SMEM_SPEC,
            spec((LANES, t), lambda i: (i, 0)),
            spec((t // 2, 2 * LANES), lambda i: (0, i)),
            spec((keys, 2 * LANES), lambda i: (0, i)),
        ],
        out_specs=[spec((8, t), lambda i: (i, 0)), spec((LANES, t), lambda i: (i, 0))],
        out_shape=[shape((8 * PAIRS, t), F32), shape((D, t), F32)],
        name="attend_local",
        **params((4 * 4 * t * keys * D, 4 * D * t)),
    )(sc, qt, kv_prompt, kv_own)


def fwd_remote(sc, qt, kvs, offsets, st, acc, halves=False, final=False):
    t = qt.shape[1]
    rows = len(offsets) * (t // 2)
    out_specs = [spec((8, t), lambda i: (i, 0)), spec((LANES, t), lambda i: (i, 0))]
    out_shape = [shape((8 * PAIRS, t), F32), shape((D, t), F32)]
    if final:
        out_specs.append(spec((t, LANES), lambda i: (0, i)))
        out_shape.append(shape((t, D), BF16))
    return pl.pallas_call(
        functools.partial(fwd_remote_body, tuple(offsets), len(kvs), halves, final),
        grid=(PAIRS,),
        in_specs=[SMEM_SPEC, spec((LANES, t), lambda i: (i, 0))]
        + kv_specs(kvs, halves)
        + [spec((8, t), lambda i: (i, 0)), spec((LANES, t), lambda i: (i, 0))],
        out_specs=out_specs,
        out_shape=out_shape,
        name="attend_remote",
        **params((4 * 4 * t * rows * D, 8 * D * t + 4 * D * rows)),
    )(sc, qt, *kvs, st, acc)


def back_block(ops, kb, vb, kt, lo, hi, mask, dq_ref):
    qz, qn, doz, don, lse, delta = ops
    dk = None
    dv = None
    for h in range(2):
        s = dot(kb, qz[h][:, lo:hi])
        dp = dot(vb, doz[h][:, lo:hi])
        p = jnp.exp2(s * LC - lse[h][:, lo:hi])
        if mask is not None:
            p = jnp.where(mask, p, 0.0)
        ds = (p * (dp - delta[h][:, lo:hi])).astype(BF16)
        dv_h = dot(p.astype(BF16), don[h][lo:hi])
        dk_h = dot(ds, qn[h][lo:hi])
        rows = slice(h * HEAD_DIM, (h + 1) * HEAD_DIM)
        dq_ref[rows, lo:hi] += dot(kt[rows], ds)
        dv = dv_h if dv is None else dv + dv_h
        dk = dk_h if dk is None else dk + dk_h
    return dk, dv


def back_operands(qt_ref, q_ref, dot_ref, do_ref, st_ref):
    qt, q, do_t, do = qt_ref[...], q_ref[...], dot_ref[...], do_ref[...]
    return (
        [head_rows(qt, h) for h in range(2)],
        [head_lanes(q, h) for h in range(2)],
        [head_rows(do_t, h) for h in range(2)],
        [head_lanes(do, h) for h in range(2)],
        [st_ref[h : h + 1, :] for h in range(2)],
        [st_ref[4 + h : 5 + h, :] for h in range(2)],
    )


def bwd_local_body(
    sc_ref, qt_ref, q_ref, dot_ref, do_ref, st_ref, dq_in, kv_ref, kvo_ref,
    out_ref, dkv_ref, dkvo_ref, dq_ref,
):
    t = qt_ref.shape[1]
    r = t // 2
    keys = kvo_ref.shape[0]
    ops = back_operands(qt_ref, q_ref, dot_ref, do_ref, st_ref)
    dq_ref[...] = dq_in[...]
    kb, vb = kv_ref[:, :LANES], kv_ref[:, LANES:]
    kbo, vbo = kvo_ref[:, :LANES], kvo_ref[:, LANES:]
    kt, kto = kb.T, kbo.T
    own, cont = local_masks(sc_ref, r, keys, 0, t)
    if r % LANES == 0:
        dk, dv = back_block(ops, kb, vb, kt, 0, r, own[:, :r], dq_ref)
        dk2, dv2 = back_block(ops, kb, vb, kt, r, t, None, dq_ref)
        dk, dv = dk + dk2, dv + dv2
        dko, dvo = back_block(ops, kbo, vbo, kto, r, t, cont[:, r:], dq_ref)
    else:
        dk, dv = back_block(ops, kb, vb, kt, 0, t, own, dq_ref)
        dko, dvo = back_block(ops, kbo, vbo, kto, 0, t, cont, dq_ref)
    dkv_ref[:, :LANES] = dk * SCALE
    dkv_ref[:, LANES:] = dv
    dkvo_ref[:, :LANES] = dko * SCALE
    dkvo_ref[:, LANES:] = dvo
    out_ref[...] = dq_ref[...].T * SCALE


def bwd_remote_body(
    offsets, count, halves, first, dtype, sc_ref, qt_ref, q_ref, dot_ref, do_ref, st_in, *refs
):
    t = qt_ref.shape[1]
    r = t // 2
    me = sc_ref[0]
    kv_refs, refs = refs[:count], refs[count:]
    src, refs = refs[0], refs[1:]
    dq_ref, refs = refs[0], refs[1:]
    out_refs, refs = refs[:count], refs[count:]
    if first:
        st_ref, refs = refs[0], refs[1:]
        st_ref[...] = st_in[...]
        prod = src[...] * dot_ref[...].astype(F32)
        for h in range(2):
            st_ref[4 + h : 5 + h, :] = jnp.sum(
                prod[h * HEAD_DIM : (h + 1) * HEAD_DIM], axis=0, keepdims=True
            )
        dq_ref[...] = jnp.zeros_like(dq_ref)
    else:
        st_ref = st_in
        dq_ref[...] = src[...]
    ops = back_operands(qt_ref, q_ref, dot_ref, do_ref, st_ref)
    split = len(offsets) != count and not halves

    def store(j, dk, dv):
        if halves:
            for part in range(2):

                @pl.when((pl.program_id(0) < PAIRS // 2) == (part == 0))
                def _():
                    out_refs[part][:, :LANES] = dk
                    out_refs[part][:, LANES:] = dv

        elif split:
            out_refs[0][j * r : (j + 1) * r, :LANES] = dk
            out_refs[0][j * r : (j + 1) * r, LANES:] = dv
        else:
            out_refs[j][:, :LANES] = dk
            out_refs[j][:, LANES:] = dv

    for j, offset in enumerate(offsets):
        block = sc_ref[3 + offset]

        def go(lo, mask):
            if halves:
                kv = halves_value(*kv_refs)
            elif split:
                kv = kv_refs[0][j * r : (j + 1) * r, :]
            else:
                kv = kv_refs[j][...]
            kb = kv[:, :LANES]
            dk, dv = back_block(ops, kb, kv[:, LANES:], kb.T, lo, t, mask, dq_ref)
            store(j, (dk * SCALE).astype(dtype), dv.astype(dtype))

        if split:

            @pl.when(block == me)
            def _():
                zero = jnp.zeros((r, LANES), dtype)
                store(j, zero, zero)

        if r % LANES == 0:

            @pl.when(block < me)
            def _():
                go(0, None)

            @pl.when(block > me)
            def _():
                go(r, None)

        else:

            @pl.when(block != me)
            def _():
                col = lax.broadcasted_iota(jnp.int32, (r, t), 1)
                go(0, (col >= r) | (block < me))


def ring_add_body(half, pr_ref, gr_ref, pl_ref, gl_ref, sr_ref, sl_ref):
    if not half:
        sr_ref[...] = (pr_ref[...] + gr_ref[...].astype(F32)).astype(BF16)
        sl_ref[...] = (pl_ref[...] + gl_ref[...].astype(F32)).astype(BF16)
        return
    sr_ref[:, :D] = (pr_ref[:, :D] + gr_ref[...].astype(F32)).astype(BF16)
    sr_ref[:, D:] = pr_ref[:, D:].astype(BF16)
    sl_ref[:, :D] = pl_ref[:, :D].astype(BF16)
    sl_ref[:, D:] = (pl_ref[:, D:] + gl_ref[...].astype(F32)).astype(BF16)


def ring_add(part_r, got_r, part_l, got_l):
    r = part_r.shape[0]
    part = r // 2
    half = got_r.shape[1] == D
    wide = spec((part, 2 * D), lambda i: (i, 0))
    got = spec((part, got_r.shape[1]), lambda i: (i, 0))
    return pl.pallas_call(
        functools.partial(ring_add_body, half),
        grid=(2,),
        in_specs=[wide, got, wide, got],
        out_specs=[wide, wide],
        out_shape=[shape((r, 2 * D), BF16)] * 2,
        name="ring_add",
        **params((4 * r * D, 16 * r * D)),
    )(part_r, got_r, part_l, got_l)


def q_specs(t):
    return [
        spec((LANES, t), lambda i: (i, 0)),
        spec((t, LANES), lambda i: (0, i)),
        spec((LANES, t), lambda i: (i, 0)),
        spec((t, LANES), lambda i: (0, i)),
        spec((8, t), lambda i: (i, 0)),
    ]


def bwd_local(sc, qt, q, do_t, do, st, dq, kv_prompt, kv_own):
    t = qt.shape[1]
    keys = kv_own.shape[0]
    return pl.pallas_call(
        bwd_local_body,
        grid=(PAIRS,),
        in_specs=[SMEM_SPEC]
        + q_specs(t)
        + [spec((LANES, t), lambda i: (i, 0))]
        + kv_specs((kv_prompt, kv_own), False),
        out_specs=[spec((t, LANES), lambda i: (0, i))] + kv_specs((kv_prompt, kv_own), False),
        out_shape=[
            shape((t, D), F32),
            shape((t // 2, 2 * D), F32),
            shape((keys, 2 * D), F32),
        ],
        scratch_shapes=[pltpu.VMEM((LANES, t), F32)],
        name="attend_back_local",
        **params((10 * 4 * t * keys * D, 16 * D * t)),
    )(sc, qt, q, do_t, do, st, dq, kv_prompt, kv_own)


def bwd_remote(
    sc, qt, q, do_t, do, st, src, kvs, offsets, halves=False, first=False, dtype=F32
):
    t = qt.shape[1]
    rows = len(offsets) * (t // 2)
    out_specs = [spec((LANES, t), lambda i: (i, 0))] + kv_specs(kvs, halves)
    out_shape = [shape((D, t), F32)] + [shape(kv.shape, dtype) for kv in kvs]
    if first:
        out_specs.append(spec((8, t), lambda i: (i, 0)))
        out_shape.append(shape((8 * PAIRS, t), F32))
    return pl.pallas_call(
        functools.partial(bwd_remote_body, tuple(offsets), len(kvs), halves, first, dtype),
        grid=(PAIRS,),
        in_specs=[SMEM_SPEC]
        + q_specs(t)
        + kv_specs(kvs, halves)
        + [spec((LANES, t), lambda i: (i, 0))],
        out_specs=out_specs,
        out_shape=out_shape,
        name="attend_back_remote",
        **params((10 * 4 * t * rows * D, 16 * D * t + 8 * D * rows)),
    )(sc, qt, q, do_t, do, st, *kvs, src)


def route_body(
    x_ref, att_ref, ow_ref, sw_ref, gain_ref, res_ref, rt_ref, tr_ref,
    h_ref, n_ref, pr_ref, xs_ref,
):
    t = x_ref.shape[0]
    step = pl.program_id(0)

    @pl.when(step == 0)
    def _():
        hidden = x_ref[...].astype(F32) + dot(att_ref[...], ow_ref[...])
        h_ref[...] = hidden
        scale = lax.rsqrt(jnp.mean(hidden * hidden, axis=-1, keepdims=True) + EPS)
        low = (hidden * scale * gain_ref[...]).astype(BF16)
        n_ref[...] = low
        z = dot(low, sw_ref[...])
        lane = lax.broadcasted_iota(jnp.int32, (t, LANES), 1)
        is_route = lane < EXPERTS + 4
        logits = jnp.where(is_route, z + res_ref[...], NEG)
        ex = jnp.exp(logits - jnp.max(logits, axis=-1, keepdims=True))
        probs = ex / jnp.sum(ex, axis=-1, keepdims=True)
        out = probs
        first = EXPERTS + 4
        for k in range(2):
            l0 = z[:, first + 2 * k : first + 2 * k + 1]
            l1 = z[:, first + 2 * k + 1 : first + 2 * k + 2]
            top = jnp.maximum(l0, l1)
            e0 = jnp.exp(l0 - top)
            e1 = jnp.exp(l1 - top)
            den = e0 + e1
            out = jnp.where(lane == first + 2 * k, e0 / den, out)
            out = jnp.where(lane == first + 2 * k + 1, e1 / den, out)
        for j in range(2):
            mix = jnp.sum(jnp.where(lane == rt_ref[:, j : j + 1], probs, 0.0), axis=-1, keepdims=True)
            out = jnp.where(lane == 16 + j, mix, out)
        pr_ref[...] = out

    slots = xs_ref.shape[0]
    base = step * slots
    slot = base + lax.broadcasted_iota(jnp.int32, (slots, t), 0)
    pick = (slot == tr_ref[0:1, :]) | (slot == tr_ref[1:2, :])
    xs_ref[...] = dot(pick.astype(BF16), n_ref[...]).astype(BF16)


def out_w_spec():
    return spec((D, D), lambda *_: (0, 3))


def small_w_spec():
    return spec((D, LANES), lambda *_: (0, 4 * D // LANES))


def grad_rows_body(g_ref, pr_ref, tr_ref, gs_ref, mg_ref):
    t = g_ref.shape[0]
    step = pl.program_id(0)

    @pl.when(step == 0)
    def _():
        g = g_ref[...].astype(F32)
        for j in range(2):
            mg_ref[j * t : (j + 1) * t, :] = (g * pr_ref[:, 16 + j : 17 + j]).astype(BF16)

    slots = gs_ref.shape[0]
    slot = step * slots + lax.broadcasted_iota(jnp.int32, (slots, t), 0)
    picks = [(slot == tr_ref[j : j + 1, :]).astype(BF16) for j in range(2)]
    gs_ref[...] = dot(jnp.concatenate(picks, axis=1), mg_ref[...]).astype(BF16)


def grad_rows_call(g, pr, tr, slots):
    t = g.shape[0]
    part = min(slots, 256)
    return pl.pallas_call(
        grad_rows_body,
        grid=(slots // part,),
        in_specs=[whole((t, D)), whole((t, LANES)), whole((2, t))],
        out_specs=spec((part, D), lambda i: (i, 0)),
        out_shape=shape((slots, D), BF16),
        scratch_shapes=[pltpu.VMEM((2 * t, D), BF16)],
        name="grad_rows",
        **params((4 * slots * t * D, 4 * t * D)),
    )(g, pr, tr)


def route_call(x, att, pack, gain, res, rt, tr, slots):
    t = x.shape[0]
    part = min(slots, 256)
    return pl.pallas_call(
        route_body,
        grid=(slots // part,),
        in_specs=[
            whole((t, D)), whole((t, D)), out_w_spec(), small_w_spec(), whole((1, D)),
            whole((t, LANES)), whole((t, 2)), whole((2, t)),
        ],
        out_specs=[
            whole((t, D)), whole((t, D)), whole((t, LANES)),
            spec((part, D), lambda i: (i, 0)),
        ],
        out_shape=[
            shape((t, D), F32), shape((t, D), BF16), shape((t, LANES), F32),
            shape((slots, D), BF16),
        ],
        name="route_dispatch",
        **params((2 * t * D * D + 2 * slots * t * D, 8 * t * D)),
    )(x, att, pack, pack, gain, res, rt, tr)


def expert_fwd_body(x_ref, w_ref, o_ref, gate_ref, up_ref, acc_ref):
    step = pl.program_id(0)
    x = x_ref[...]
    wide = w_ref.shape[-1]
    wg = w_ref[:, 0].reshape(D, wide)
    wu = w_ref[:, 1].reshape(D, wide)
    wd = w_ref[:, 2].reshape(D, wide)
    gate = dot(x, wg)
    up = dot(x, wu)
    gate_ref[...] = gate
    up_ref[...] = up
    act = (gate / (1.0 + jnp.exp(-gate)) * up).astype(BF16)
    out = dot_nt(act, wd)

    @pl.when(step == 0)
    def _():
        acc_ref[...] = out

    @pl.when(step > 0)
    def _():
        acc_ref[...] += out

    @pl.when(step == pl.num_programs(0) - 1)
    def _():
        o_ref[...] = acc_ref[...].astype(BF16)


def expert_fwd(xr, w):
    rows = xr.shape[0]
    shards, _, per, wide = w.shape
    part = min(wide, 256)
    return pl.pallas_call(
        expert_fwd_body,
        grid=(wide // part,),
        in_specs=[whole((rows, D)), spec((shards, 3, per, part), lambda i: (0, 0, 0, i))],
        out_specs=[whole((rows, D))] + [spec((rows, part), lambda i: (0, i))] * 2,
        out_shape=[shape((rows, D), BF16)] + [shape((rows, wide), F32)] * 2,
        scratch_shapes=[pltpu.VMEM((rows, D), F32)],
        name="expert_forward",
        **params((6 * rows * D * wide, 6 * D * wide)),
    )(xr, w)


def expert_in_body(gate_ref, up_ref, g_ref, w_ref, gi_ref, act_ref, dg_ref, du_ref, acc_ref):
    step = pl.program_id(0)
    wide = w_ref.shape[-1]
    wg = w_ref[:, 0].reshape(D, wide)
    wu = w_ref[:, 1].reshape(D, wide)
    wd = w_ref[:, 2].reshape(D, wide)
    gate = gate_ref[...]
    up = up_ref[...]
    ga = dot(g_ref[...], wd)
    sig = 1.0 / (1.0 + jnp.exp(-gate))
    silu = gate * sig
    act_ref[...] = (silu * up).astype(BF16)
    d_gate = (ga * up * sig * (1.0 + gate * (1.0 - sig))).astype(BF16)
    d_up = (ga * silu).astype(BF16)
    dg_ref[...] = d_gate
    du_ref[...] = d_up
    gi = dot_nt(
        jnp.concatenate([d_gate, d_up], axis=1), jnp.concatenate([wg, wu], axis=1)
    )

    @pl.when(step == 0)
    def _():
        acc_ref[...] = gi

    @pl.when(step > 0)
    def _():
        acc_ref[...] += gi

    @pl.when(step == pl.num_programs(0) - 1)
    def _():
        gi_ref[...] = acc_ref[...].astype(BF16)


def expert_in(gate, up, gr, w):
    rows = gr.shape[0]
    shards, _, per, wide = w.shape
    part = min(wide, 256)
    tile = spec((rows, part), lambda i: (0, i))
    return pl.pallas_call(
        expert_in_body,
        grid=(wide // part,),
        in_specs=[tile, tile, whole((rows, D)), spec((shards, 3, per, part), lambda i: (0, 0, 0, i))],
        out_specs=[whole((rows, D)), tile, tile, tile],
        out_shape=[shape((rows, D), BF16)] + [shape((rows, wide), BF16)] * 3,
        scratch_shapes=[pltpu.VMEM((rows, D), F32)],
        name="expert_back_in",
        **params((6 * rows * D * wide, 12 * D * wide)),
    )(gate, up, gr, w)


def expert_weights_body(x_ref, gl_ref, act_ref, dg_ref, du_ref, dw_ref, xt_ref, gt_ref):
    @pl.when(pl.program_id(0) == 0)
    def _():
        gt_ref[...] = gl_ref[...].T
        xt_ref[...] = x_ref[...].T

    shards, _, per, wide = dw_ref.shape
    xt = xt_ref[...]
    dw_ref[:, 0] = dot(xt, dg_ref[...]).astype(BF16).reshape(shards, per, wide)
    dw_ref[:, 1] = dot(xt, du_ref[...]).astype(BF16).reshape(shards, per, wide)
    dw_ref[:, 2] = dot(gt_ref[...], act_ref[...]).astype(BF16).reshape(shards, per, wide)


def expert_weights(xr, low, act, d_gate, d_up, dims):
    rows = xr.shape[0]
    shards, _, per, wide = dims
    part = min(wide, 256)
    tile = spec((rows, part), lambda i: (0, i))
    return pl.pallas_call(
        expert_weights_body,
        grid=(wide // part,),
        in_specs=[whole((rows, D)), whole((rows, D)), tile, tile, tile],
        out_specs=spec((shards, 3, per, part), lambda i: (0, 0, 0, i)),
        out_shape=shape(dims, BF16),
        scratch_shapes=[pltpu.VMEM((D, rows), BF16), pltpu.VMEM((D, rows), BF16)],
        name="expert_weight_grads",
        **params((6 * rows * D * wide, 12 * D * wide)),
    )(xr, low, act, d_gate, d_up)


def mix_body(
    h_ref, g_ref, pr_ref, rt_ref, tc_ref, ret_ref, n_ref, sw_ref, rows_ref,
    out_ref, gn_ref, gl_ref, gs_ref,
):
    t = h_ref.shape[0]
    slots = ret_ref.shape[0]
    hidden = h_ref[...]
    g16 = g_ref[...]
    g = g16.astype(F32)
    pr = pr_ref[...]
    scale = lax.rsqrt(jnp.mean(hidden * hidden, axis=-1, keepdims=True) + EPS)
    normed = hidden * scale * rows_ref[2:3, :]
    lane = lax.broadcasted_iota(jnp.int32, (t, LANES), 1)
    slot = lax.broadcasted_iota(jnp.int32, (t, slots), 1)
    first = EXPERTS + 4
    ret = ret_ref[...]
    c0 = [pr[:, first + 2 * k : first + 2 * k + 1] for k in range(2)]
    c1 = [pr[:, first + 2 * k + 1 : first + 2 * k + 2] for k in range(2)]
    total = hidden
    s = jnp.zeros((t, LANES), F32)
    coef = jnp.zeros((t, 1), F32)
    weight = [jnp.zeros((t, 1), F32) for _ in range(2)]
    for j in range(2):
        route = rt_ref[:, j : j + 1]
        mix = pr[:, 16 + j : 17 + j]
        branch = dot((slot == tc_ref[:, j : j + 1]).astype(BF16), ret)
        keep = jnp.where(route == EXPERTS + 1, 1.0, 0.0)
        for k in range(2):
            here = jnp.where(route == EXPERTS + 2 + k, 1.0, 0.0)
            keep = keep + here * c0[k]
            weight[k] = weight[k] + here * mix
            branch = branch + (here * c1[k]) * rows_ref[k : k + 1, :]
        branch = branch + keep * normed
        coef = coef + mix * keep
        total = total + mix * branch
        gp = jnp.sum(g * branch, axis=-1, keepdims=True)
        s = s + jnp.where(lane == route, gp, 0.0)
    out_ref[...] = total.astype(BF16)
    probs = jnp.where(lane < first, pr, 0.0)
    d_logits = probs * (s - jnp.sum(probs * s, axis=-1, keepdims=True))
    gl_ref[...] = d_logits
    dz = d_logits
    dvec = jnp.zeros((t, LANES), F32)
    g_dot_n = jnp.sum(g * normed, axis=-1, keepdims=True)
    for k in range(2):
        d0 = weight[k] * g_dot_n
        d1 = weight[k] * jnp.sum(g * rows_ref[k : k + 1, :], axis=-1, keepdims=True)
        mean = c0[k] * d0 + c1[k] * d1
        dz = jnp.where(lane == first + 2 * k, c0[k] * (d0 - mean), dz)
        dz = jnp.where(lane == first + 2 * k + 1, c1[k] * (d1 - mean), dz)
        dvec = jnp.where(lane == 16 + k, weight[k] * c1[k], dvec)
    hi, lo = split_hi_lo(dz)
    sw = sw_ref[...]
    gn_ref[...] = coef * g + (dot_nt(hi, sw) + dot_nt(lo, sw))
    nt = n_ref[...].T
    gt = g16.T
    vhi, vlo = split_hi_lo(dvec)
    gs = dot(nt, hi) + dot(nt, lo) + dot(gt, vhi) + dot(gt, vlo)

    @pl.when(pl.program_id(0) == 0)
    def _():
        gs_ref[...] = gs

    @pl.when(pl.program_id(0) > 0)
    def _():
        gs_ref[...] += gs


def mix_call(hidden, g, pr, rt, tc, ret, low, pack, rows):
    t = hidden.shape[0]
    half = min(t, LANES)
    slots = ret.shape[0]
    tile = spec((half, D), lambda i: (i, 0))
    lane_tile = spec((half, LANES), lambda i: (i, 0))
    pair = spec((half, 2), lambda i: (i, 0))
    return pl.pallas_call(
        mix_body,
        grid=(t // half,),
        in_specs=[
            tile, tile, lane_tile, pair, pair, whole((slots, D)), tile, small_w_spec(),
            whole((8, D)),
        ],
        out_specs=[tile, tile, lane_tile, whole((D, LANES))],
        out_shape=[
            shape((t, D), BF16), shape((t, D), F32), shape((t, LANES), F32), shape((D, LANES), F32),
        ],
        name="mixture",
        **params((4 * t * slots * D, 12 * t * D)),
    )(hidden, g, pr, rt, tc, ret, low, pack, rows)


def norm_back_body(
    h_ref, g_ref, gn_ref, tc_ref, ret_ref, rows_ref, ow_ref, att_ref,
    gh_ref, do_ref, dot_ref, gow_ref, gg_ref,
):
    t = h_ref.shape[0]
    slots = ret_ref.shape[0]
    hidden = h_ref[...]
    slot = lax.broadcasted_iota(jnp.int32, (t, slots), 1)
    pick = (slot == tc_ref[:, 0:1]) | (slot == tc_ref[:, 1:2])
    gn = gn_ref[...] + dot(pick.astype(BF16), ret_ref[...])
    q = lax.rsqrt(jnp.mean(hidden * hidden, axis=-1, keepdims=True) + EPS)
    u = gn * rows_ref[2:3, :]
    mean = jnp.mean(u * hidden, axis=-1, keepdims=True)
    gh = g_ref[...].astype(F32) + q * u - hidden * (q * q * q * mean)
    gh_ref[...] = gh
    gb = gh.astype(BF16)
    d_out = dot_nt(gb, ow_ref[...])
    do_ref[...] = d_out.astype(BF16)
    dot_ref[...] = d_out.T.astype(BF16)
    gow = dot(att_ref[...].T, gb)
    gain = jnp.sum(gn * hidden * q, axis=0, keepdims=True)

    @pl.when(pl.program_id(0) == 0)
    def _():
        gow_ref[...] = gow
        gg_ref[...] = jnp.broadcast_to(gain, gg_ref.shape)

    @pl.when(pl.program_id(0) > 0)
    def _():
        gow_ref[...] += gow
        gg_ref[...] += jnp.broadcast_to(gain, gg_ref.shape)


def norm_back_call(hidden, g, gn, tc, ret, rows, pack, att):
    t = hidden.shape[0]
    half = t // 2 if (t // 2) % LANES == 0 else t
    slots = ret.shape[0]
    tile = spec((half, D), lambda i: (i, 0))
    return pl.pallas_call(
        norm_back_body,
        grid=(t // half,),
        in_specs=[
            tile, tile, tile, spec((half, 2), lambda i: (i, 0)), whole((slots, D)), whole((8, D)),
            out_w_spec(), tile,
        ],
        out_specs=[tile, tile, spec((D, half), lambda i: (0, i)), whole((D, D)), whole((8, D))],
        out_shape=[
            shape((t, D), F32), shape((t, D), BF16), shape((D, t), BF16), shape((D, D), F32),
            shape((8, D), F32),
        ],
        name="norm_two_back",
        **params((2 * t * slots * D + 4 * t * D * D, 16 * t * D)),
    )(hidden, g, gn, tc, ret, rows, pack, att)


def store_grad(sc_ref, split, value, refs):
    if not split:
        refs[0][...] = value
        return
    send_ref, keep_ref = refs
    per = value.shape[0] // 4
    for core in range(2):

        @pl.when(sc_ref[11] == core)
        def _():
            for part in range(2):
                mine = (2 * part + core) * per
                other = (2 * part + 1 - core) * per
                send_ref[part] = value[other : other + per].astype(BF16)
                keep_ref[part] = value[mine : mine + per]


def grad_outs(split, width):
    block = 2 * LANES
    if not split:
        return [spec((D, block), lambda i: (0, i))], [shape((D, width), F32)]
    dims = (2, D // 4, width)
    tile = spec((2, D // 4, block), lambda i: (0, 0, i))
    return [tile, tile], [shape(dims, BF16), shape(dims, F32)]


def q_back_body(split, sc_ref, n_ref, dq_ref, c_ref, s_ref, w_ref, gn_ref, *refs):
    nt_ref = refs[-1]
    step = pl.program_id(0)

    @pl.when(step == 0)
    def _():
        nt_ref[...] = n_ref[...].T

    cosine = c_ref[...]
    sine = s_ref[...]
    v0 = dq_ref[:, :LANES]
    v1 = dq_ref[:, LANES:]
    gq = jnp.concatenate(
        [
            (v0 * cosine - partner(v0) * sine).astype(BF16),
            (v1 * cosine - partner(v1) * sine).astype(BF16),
        ],
        axis=1,
    )
    store_grad(sc_ref, split, dot(nt_ref[...], gq), refs[:-1])
    gn = dot_nt(gq, w_ref[...])

    @pl.when(step == 0)
    def _():
        gn_ref[...] = gn

    @pl.when(step > 0)
    def _():
        gn_ref[...] += gn


def q_back_call(sc, low, dq, cosine, sine, pack, split):
    t = low.shape[0]
    specs, shapes = grad_outs(split, D)
    return pl.pallas_call(
        functools.partial(q_back_body, split),
        grid=(PAIRS // 2,),
        in_specs=[
            SMEM_SPEC, whole((t, D)), spec((t, 2 * LANES), lambda i: (0, i)), whole((t, LANES)),
            whole((t, LANES)), spec((D, 2 * LANES), lambda i: (0, i)),
        ],
        out_specs=[whole((t, D))] + specs,
        out_shape=[shape((t, D), F32)] + shapes,
        scratch_shapes=[pltpu.VMEM((D, t), BF16)],
        name="q_back",
        **params((4 * t * D * D, 12 * t * D)),
    )(sc, low, dq, cosine, sine, pack)


def kv_back_body(
    split, count, sc_ref, x_ref, n_ref, gnq_ref, gh_ref, gain_ref, c_ref, s_ref, wk_ref, wv_ref,
    own_ref, cont_ref, *refs
):
    got_refs, refs = refs[:count], refs[count:]
    gi_ref, grads, (nt_ref, gn_ref) = refs[0], refs[1:-2], refs[-2:]
    step = pl.program_id(0)

    @pl.when(step == 0)
    def _():
        nt_ref[...] = n_ref[...].T
        gn_ref[...] = gnq_ref[...]

    own = own_ref[...]
    for got in got_refs:
        own = own + got[...].astype(F32)
    total = jnp.concatenate([own, cont_ref[...]], axis=0)
    k = total[:, :LANES]
    gk = (k * c_ref[...] - partner(k) * s_ref[...]).astype(BF16)
    gkv = jnp.concatenate([gk, total[:, LANES:].astype(BF16)], axis=1)
    store_grad(sc_ref, split, dot(nt_ref[...], gkv), grads)
    gn_ref[...] += dot_nt(gkv, jnp.concatenate([wk_ref[...], wv_ref[...]], axis=1))

    @pl.when(step == pl.num_programs(0) - 1)
    def _():
        gn = gn_ref[...]
        x = x_ref[...].astype(F32)
        q = lax.rsqrt(jnp.mean(x * x, axis=-1, keepdims=True) + EPS)
        u = gn * gain_ref[...]
        mean = jnp.mean(u * x, axis=-1, keepdims=True)
        gi_ref[...] = gh_ref[...] + q * u - x * (q * q * q * mean)


def kv_back_call(sc, x, low, gn, gh, gain, cosine, sine, pack, own, cont, got, split):
    t = x.shape[0]
    r = t // 2
    specs, shapes = grad_outs(split, 2 * D)
    wide = spec((r, 2 * LANES), lambda i: (0, i))
    return pl.pallas_call(
        functools.partial(kv_back_body, split, len(got)),
        grid=(PAIRS,),
        in_specs=[
            SMEM_SPEC, whole((t, D)), whole((t, D)), whole((t, D)), whole((t, D)), whole((1, D)),
            whole((t, LANES)), whole((t, LANES)),
            spec((D, LANES), lambda i: (0, PAIRS + i)),
            spec((D, LANES), lambda i: (0, 2 * PAIRS + i)),
            wide, wide,
        ]
        + [wide] * len(got),
        out_specs=[whole((t, D))] + specs,
        out_shape=[shape((t, D), F32)] + shapes,
        scratch_shapes=[pltpu.VMEM((D, t), BF16), pltpu.VMEM((t, D), F32)],
        name="kv_back",
        **params((8 * t * D * D, 24 * t * D)),
    )(sc, x, low, gn, gh, gain, cosine, sine, pack, pack, own, cont, *got)


def rotation_tables(position):
    half = HEAD_DIM // 2
    frequency = 10000.0 ** (-jnp.arange(half, dtype=F32) / half)
    angles = position[:, None] * frequency[None, :]
    cosine, sine = jnp.cos(angles), jnp.sin(angles)
    return (
        jnp.concatenate([cosine] * 4, axis=1),
        jnp.concatenate([-sine, sine, -sine, sine], axis=1),
    )


def to_rows(array):
    return jnp.transpose(array, (1, 0, 2)).reshape(2 * array.shape[0], array.shape[2])


def from_rows(array):
    r = array.shape[0] // 2
    return jnp.transpose(array.reshape(2, r, array.shape[1]), (1, 0, 2))


RING = (0, 2, 4, 6, 7, 5, 3, 1)


def ring_offsets():
    place = {e: i for i, e in enumerate(RING)}
    return [[RING[(place[e] + k) % 8] for k in range(8)] for e in range(8)]


def along_ring(array, step):
    pairs = [(RING[i], RING[(i + step) % 8]) for i in range(8)]
    return lax.ppermute(array, "expert", pairs)


def tie(*values):
    return lax.optimization_barrier(values)


def swap_core(array):
    return lax.ppermute(array, "dp", [(0, 1), (1, 0), (2, 3), (3, 2)])


def add_and_cross(keep, got):
    across = lax.axis_index("dp") // 2
    keep = keep + got.astype(F32)
    send = lax.dynamic_index_in_dim(keep, 1 - across, 0, keepdims=False).astype(BF16)
    mine = lax.dynamic_index_in_dim(keep, across, 0, keepdims=False)
    return mine, lax.ppermute(send, "dp", [(0, 2), (2, 0), (1, 3), (3, 1)])


def add_and_scatter(keep, got):
    keep = (keep + got.astype(F32)).astype(BF16)
    rows, w = keep.shape
    return lax.all_to_all(
        keep.reshape(8, rows // 8, w), "expert", split_axis=0, concat_axis=0, tiled=True
    )


def add_up(got):
    return jnp.sum(got.astype(F32), axis=0)


def scatter_all(array):
    return lax.psum_scatter(
        array.astype(BF16), ALL_AXES, scatter_dimension=0, tiled=True
    ).astype(F32)


def per_device(
    hidden_in, cotangent, gate_residual, routes, groups, lengths, attn_gain, qkv_weight, out_weight,
    ffn_gain, router_weight, const_proj, const_vec, gate_weight, up_weight, down_weight,
):
    del groups
    r = hidden_in.shape[0]
    t = 2 * r
    capacity = r // 2
    owners = lax.axis_size("expert")
    copies = owners // EXPERTS
    slots = EXPERTS * capacity
    me = lax.axis_index("expert")
    per_cont = max(CONT_LEN // r, 1)

    small = jnp.concatenate(
        [
            router_weight, const_proj, const_vec, attn_gain[:, None], ffn_gain[:, None],
            jnp.zeros((attn_gain.shape[0], LANES - 20), BF16),
        ],
        axis=1,
    )
    pack = lax.all_gather(
        jnp.concatenate([qkv_weight, out_weight, small], axis=1), ALL_AXES, axis=0, tiled=True
    )
    index = jnp.arange(r, dtype=jnp.int32)
    row_ids = me * r + index
    position = jnp.concatenate([row_ids, PROMPT + row_ids % CONT_LEN]).astype(F32)
    cosine, sine = rotation_tables(position)
    cont = (me * r) // CONT_LEN
    length = lax.dynamic_slice(lengths, (cont,), (1,))
    header = jnp.stack([me, (me * r) % CONT_LEN]).astype(jnp.int32)
    header = jnp.concatenate([header, length.astype(jnp.int32)])
    ring = owners == 8
    if ring:
        ids = lax.dynamic_index_in_dim(jnp.asarray(ring_offsets(), jnp.int32), me, 0, keepdims=False)
    else:
        ids = jnp.arange(owners, dtype=jnp.int32)
    sc = jnp.concatenate([header, ids, (lax.axis_index("dp") % 2).astype(jnp.int32)[None]])

    picked = to_rows(routes)
    flat = jnp.transpose(picked).reshape(2 * t)
    hot = flat[:, None] == jnp.arange(EXPERTS, dtype=jnp.int32)[None, :]
    earlier = jnp.arange(2 * t)[:, None] > jnp.arange(2 * t)[None, :]
    before = jnp.dot(earlier.astype(BF16), hot.astype(BF16), preferred_element_type=F32)
    slot_index = jnp.sum(jnp.where(hot, before, 0.0), axis=1).astype(jnp.int32)
    target = jnp.where(flat < EXPERTS, flat * capacity + slot_index, -1)
    target_rows = target.reshape(2, t)
    target_cols = jnp.transpose(target_rows)

    def to_owners(rows):
        w = rows.shape[-1]
        shaped = rows.reshape(EXPERTS, 1, capacity, w)
        return jnp.broadcast_to(shaped, (EXPERTS, copies, capacity, w)).reshape(owners, capacity, w)

    def exchange(rows):
        got = lax.all_to_all(rows, "expert", split_axis=0, concat_axis=0, tiled=True)
        return got.reshape(owners * got.shape[1], got.shape[2])

    def from_owners(rows):
        got = exchange(rows.reshape(owners, capacity, D))
        if copies == 1:
            return got
        got = got.reshape(EXPERTS, copies, capacity, D).astype(F32)
        return jnp.sum(got, axis=1).reshape(slots, D).astype(BF16)

    x = to_rows(hidden_in)
    g = to_rows(cotangent)
    small_w = pack[:, 4 * D :]
    small_rows = jnp.transpose(small_w[:, 16:24]).astype(F32)
    gain_one = small_rows[2:3]
    rows_two = jnp.concatenate([small_rows[0:2], small_rows[3:4], small_rows[3:8]], axis=0)
    gain_two = small_rows[3:4]

    low_one, q, q_t, kv_prompt, kv_cont = qkv_call(x, gain_one, pack, cosine, sine)
    if not ring:
        kv_all = lax.all_gather(kv_prompt, "expert", axis=0, tiled=True)
    if per_cont == 1:
        kv_own = kv_cont
    else:
        cont_groups = [
            [c * per_cont + i for i in range(per_cont)] for c in range(owners // per_cont)
        ]
        kv_own = lax.all_gather(
            kv_cont, "expert", axis=0, tiled=True, axis_index_groups=cont_groups
        )
    weights = lax.all_gather(
        jnp.stack([gate_weight, up_weight, down_weight]), "dp", axis=0, tiled=False
    )
    if ring:
        right, left = [kv_prompt], [kv_prompt]
        for i in range(3):
            right.append(along_ring(right[i], 1))
            left.append(along_ring(left[i], -1))
            if i == 0:
                st, acc = fwd_local(sc, q_t, kv_prompt, kv_own)
            else:
                st, acc = fwd_remote(sc, q_t, (right[i], left[i]), (8 - i, i), st, acc)
            right[i + 1], left[i + 1], st = tie(right[i + 1], left[i + 1], st)
        far = [along_ring(right[3][:, :D], 1), along_ring(left[3][:, D:], -1)]
        st, acc = fwd_remote(sc, q_t, (right[3], left[3]), (5, 3), st, acc)
        st, att_t, att = fwd_remote(sc, q_t, far, (4,), st, acc, halves=True, final=True)
    else:
        st, acc = fwd_local(sc, q_t, kv_prompt, kv_own)
        st, att_t, att = fwd_remote(sc, q_t, (kv_all,), range(owners), st, acc, final=True)

    res = jnp.pad(to_rows(gate_residual), ((0, 0), (0, LANES - EXPERTS - 4)))
    hidden, low_two, pr, x_send = route_call(
        x, att, pack, gain_two, res, picked, target_rows, slots
    )
    x_got = exchange(to_owners(x_send))
    g_send = grad_rows_call(g, pr, target_rows, slots)
    x_got, g_send = tie(x_got, g_send)
    g_got = exchange(to_owners(g_send))
    expert_rows, gate_pre, up_pre = expert_fwd(x_got, weights)
    out_back = from_owners(expert_rows)
    grad_in, act, d_gate, d_up = expert_in(gate_pre, up_pre, g_got, weights)
    in_back = from_owners(grad_in)
    output, gn, grad_logits, grad_small = mix_call(
        hidden, g, pr, picked, target_cols, out_back, low_two, pack, rows_two
    )
    act, gn = tie(act, gn)
    grad_w = expert_weights(x_got, g_got, act, d_gate, d_up, weights.shape)
    grad_expert = lax.psum_scatter(
        grad_w.reshape(-1, grad_w.shape[-1]), "dp", scatter_dimension=0, tiled=True
    )
    per = gate_weight.shape[0]
    grad_expert = [grad_expert[i * per : (i + 1) * per].astype(F32) for i in range(3)]
    gh, d_att, d_att_t, grad_ow, gg_two = norm_back_call(
        hidden, g, gn, target_cols, in_back, rows_two, pack, att
    )

    early = jnp.concatenate(
        [grad_ow, grad_small[:, :19], jnp.transpose(gg_two[0:1]), jnp.zeros((D, LANES - 20), F32)],
        axis=1,
    )
    back = (sc, q_t, q, d_att_t, d_att)
    if ring:
        parts = early.reshape(2, 2, D // 4, D + LANES)
        core = lax.axis_index("dp") % 2
        early_keep = lax.dynamic_index_in_dim(parts, core, 1, keepdims=False)
        early_got = swap_core(
            lax.dynamic_index_in_dim(parts, 1 - core, 1, keepdims=False).astype(BF16)
        )
        dq_t, send_r, send_l, st = bwd_remote(
            *back, st, att_t, far, (4,), halves=True, first=True, dtype=BF16
        )
        for i in range(3, 0, -1):
            got_r, got_l = along_ring(send_r, 1), along_ring(send_l, -1)
            dq_t, part_r, part_l = bwd_remote(
                *back, st, dq_t, (left[i], right[i]), (i, 8 - i)
            )
            got_r, got_l, part_r, part_l, dq_t, early_got = tie(
                got_r, got_l, part_r, part_l, dq_t, early_got
            )
            send_r, send_l = ring_add(part_r, got_r, part_l, got_l)
            if i == 3:
                early_keep, early_got = add_and_cross(early_keep, early_got)
        send_r, send_l, dq_t = tie(send_r, send_l, dq_t)
        got_r = along_ring(send_r, 1)
        got_l = along_ring(send_l, -1)
        got = (got_r, got_l)
        dq, dkv_own, dkv_cont = bwd_local(*back, st, dq_t, kv_prompt, kv_own)
    else:
        dq_t, dkv_all, st = bwd_remote(
            *back, st, att_t, (kv_all,), range(owners), first=True, dtype=BF16
        )
        dq, dkv_own, dkv_cont = bwd_local(*back, st, dq_t, kv_prompt, kv_own)
        got = (lax.psum_scatter(dkv_all, "expert", scatter_dimension=0, tiled=True),)
        early = scatter_all(early)
    if per_cont > 1:
        dkv_cont = lax.psum_scatter(
            dkv_cont, "expert", scatter_dimension=0, tiled=True, axis_index_groups=cont_groups
        )
    gn_q, *grad_q = q_back_call(sc, low_one, dq, cosine, sine, pack, ring)
    if ring:
        got_q = swap_core(grad_q[0])
        keep_q, got_q = add_and_cross(grad_q[1], got_q)
        keep_q, *got = tie(keep_q, *got)
    grad_input, *grad_kv = kv_back_call(
        sc, x, low_one, gn_q, gh, gain_one, cosine, sine, pack, dkv_own, dkv_cont, got, ring
    )
    output, grad_input = from_rows(output), from_rows(grad_input)
    if ring:
        got_kv = swap_core(grad_kv[0])
        keep_kv, got_kv = add_and_cross(grad_kv[1], got_kv)
        keep_kv, got_q, early_got = tie(keep_kv, got_q, early_got)
        got_q = add_and_scatter(
            jnp.concatenate([early_keep, keep_q], axis=1),
            jnp.concatenate([early_got, got_q], axis=1),
        )
        got_kv, output, grad_input, *grad_expert = tie(got_kv, output, grad_input, *grad_expert)
        summed = add_up(got_q)
        early, late_q = summed[:, : D + LANES], summed[:, D + LANES :]
        late_kv = add_up(add_and_scatter(keep_kv, got_kv))
    else:
        late_q, late_kv = scatter_all(grad_q[0]), scatter_all(grad_kv[0])
    per = late_kv.shape[0]
    late_kv = jnp.transpose(late_kv.reshape(per, PAIRS, 2, LANES), (0, 2, 1, 3))
    late = jnp.concatenate([late_q, late_kv.reshape(per, 2 * D)], axis=1)
    grad_gain = jnp.sum(late * qkv_weight.astype(F32), axis=1) / attn_gain.astype(F32)
    tail = early[:, D:]
    return (
        output,
        grad_input,
        from_rows(grad_logits)[:, :, : EXPERTS + 4],
        grad_gain,
        late,
        early[:, :D],
        tail[:, 19],
        tail[:, :12],
        tail[:, 12:16],
        tail[:, 16:18],
        grad_expert[0],
        grad_expert[1],
        grad_expert[2],
    )


def solution(mesh):
    rows = P(ALL_AXES, None, None)
    flat = P(ALL_AXES)
    mat = P(ALL_AXES, None)
    expert = P("dp", "expert")
    in_specs = (
        rows, rows, rows, rows, P("dp"), P("dp"), flat, mat, mat, flat, mat, mat, mat,
        expert, expert, expert,
    )
    out_specs = (
        rows, rows, rows, flat, mat, mat, flat, mat, mat, mat, expert, expert, expert,
    )

    return jax.shard_map(
        per_device, mesh=mesh, in_specs=in_specs, out_specs=out_specs, check_vma=False
    )
```

```python
import functools

import jax
import jax.numpy as jnp
from jax import lax
from jax.experimental import pallas as pl
from jax.experimental.pallas import tpu as pltpu
from jax.sharding import PartitionSpec as P


D = 768
HEAD_DIM = 64
PAIRS = 6
EXPERTS = 8
CONT_LEN = 256
PROMPT = 2048
LANES = 128
EPS = 1e-06
NEG = -1e30
LOG2E = 1.4426950408889634
SCALE = float(HEAD_DIM) ** (-0.5)
LC = SCALE * LOG2E
F32 = jnp.float32
BF16 = jnp.bfloat16
ALL_AXES = ("dp", "expert")
VMEM_LIMIT = 60 * 1024 * 1024


def dot(a, b):
    return jnp.dot(a, b, preferred_element_type=F32)


def dot_nt(a, b):
    return lax.dot_general(a, b, (((1,), (1,)), ((), ())), preferred_element_type=F32)


def split_hi_lo(v):
    hi = v.astype(BF16)
    return hi, (v - hi.astype(F32)).astype(BF16)


def params(cost=None):
    return dict(
        compiler_params=pltpu.CompilerParams(vmem_limit_bytes=VMEM_LIMIT),
        cost_estimate=None if cost is None else pl.CostEstimate(
            flops=int(cost[0]), bytes_accessed=int(cost[1]), transcendentals=0
        ),
    )


def shape(dims, dtype):
    return jax.ShapeDtypeStruct(tuple(dims), dtype)


def spec(block, index):
    return pl.BlockSpec(tuple(block), index)


def whole(dims):
    return pl.BlockSpec(tuple(dims), lambda *_: (0,) * len(dims))


SMEM_SPEC = pl.BlockSpec(memory_space=pltpu.SMEM)


def partner(v):
    lane = lax.broadcasted_iota(jnp.int32, v.shape, 1)
    return jnp.where((lane & 63) < 32, pltpu.roll(v, 96, 1), pltpu.roll(v, 32, 1))


def qkv_body(x_ref, gain_ref, wq_ref, wk_ref, wv_ref, c_ref, s_ref, n_ref, q_ref, qt_ref, kvp_ref, kvc_ref):
    @pl.when(pl.program_id(0) == 0)
    def _():
        x = x_ref[...].astype(F32)
        scale = lax.rsqrt(jnp.mean(x * x, axis=-1, keepdims=True) + EPS)
        n_ref[...] = (x * scale * gain_ref[...]).astype(BF16)

    n = n_ref[...]
    cosine = c_ref[...]
    sine = s_ref[...]
    kv = dot(n, jnp.concatenate([wk_ref[...], wv_ref[...]], axis=1))
    k = kv[:, :LANES]
    k = (k * cosine + partner(k) * sine).astype(BF16)
    v = kv[:, LANES:].astype(BF16)
    r = k.shape[0] // 2
    kvp_ref[:, :LANES] = k[:r]
    kvp_ref[:, LANES:] = v[:r]
    kvc_ref[:, :LANES] = k[r:]
    kvc_ref[:, LANES:] = v[r:]
    q = dot(n, wq_ref[...])
    q = q * cosine + partner(q) * sine
    q = q.astype(BF16)
    q_ref[...] = q
    qt_ref[...] = q.T


def qkv_call(x, gain, pack, cosine, sine):
    t = x.shape[0]
    return pl.pallas_call(
        qkv_body,
        grid=(PAIRS,),
        in_specs=[
            whole((t, D)),
            whole((1, D)),
            spec((D, LANES), lambda i: (0, i)),
            spec((D, LANES), lambda i: (0, PAIRS + i)),
            spec((D, LANES), lambda i: (0, 2 * PAIRS + i)),
            whole((t, LANES)),
            whole((t, LANES)),
        ],
        out_specs=[
            whole((t, D)),
            spec((t, LANES), lambda i: (0, i)),
            spec((LANES, t), lambda i: (i, 0)),
            spec((t // 2, 2 * LANES), lambda i: (0, i)),
            spec((t // 2, 2 * LANES), lambda i: (0, i)),
        ],
        out_shape=[
            shape((t, D), BF16),
            shape((t, D), BF16),
            shape((D, t), BF16),
            shape((t // 2, 2 * D), BF16),
            shape((t // 2, 2 * D), BF16),
        ],
        name="qkv_rope",
        **params((2 * t * D * 3 * D, 6 * D * D)),
    )(x, gain, pack, pack, pack, cosine, sine)


def head_rows(v, h):
    row = lax.broadcasted_iota(jnp.int32, v.shape, 0)
    return jnp.where(row // HEAD_DIM == h, v, jnp.zeros_like(v))


def head_lanes(v, h):
    lane = lax.broadcasted_iota(jnp.int32, v.shape, 1)
    return jnp.where(lane // HEAD_DIM == h, v, jnp.zeros_like(v))


def attend_update(qz, kb, vt, lo, hi, mask, st_ref, a_ref, first):
    for h in range(2):
        s = dot(kb, qz[h][:, lo:hi])
        if mask is not None:
            s = jnp.where(mask, s, NEG)
        top = jnp.max(s, axis=0, keepdims=True)
        rows = slice(h * HEAD_DIM, (h + 1) * HEAD_DIM)
        if first:
            p = jnp.exp2((s - top) * LC)
            st_ref[h : h + 1, lo:hi] = top
            st_ref[2 + h : 3 + h, lo:hi] = jnp.sum(p, axis=0, keepdims=True)
            a_ref[rows, lo:hi] = dot(vt[rows], p.astype(BF16))
        else:
            old = st_ref[h : h + 1, lo:hi]
            new = jnp.maximum(old, top)
            alpha = jnp.exp2((old - new) * LC)
            p = jnp.exp2((s - new) * LC)
            st_ref[h : h + 1, lo:hi] = new
            st_ref[2 + h : 3 + h, lo:hi] = st_ref[2 + h : 3 + h, lo:hi] * alpha + jnp.sum(
                p, axis=0, keepdims=True
            )
            a_ref[rows, lo:hi] = a_ref[rows, lo:hi] * alpha + dot(vt[rows], p.astype(BF16))


def local_masks(sc_ref, r, keys, lo, hi):
    cpos = sc_ref[1]
    length = sc_ref[2]
    col = lo + lax.broadcasted_iota(jnp.int32, (r, hi - lo), 1)
    row = lax.broadcasted_iota(jnp.int32, (r, hi - lo), 0)
    own = (row <= col) | (col >= r)
    col = lo + lax.broadcasted_iota(jnp.int32, (keys, hi - lo), 1)
    row = lax.broadcasted_iota(jnp.int32, (keys, hi - lo), 0)
    cont = (col >= r) & (row <= cpos + col - r) & (row < length)
    return own, cont


def fwd_local_body(sc_ref, qt_ref, kv_ref, kvo_ref, st_ref, a_ref):
    t = qt_ref.shape[1]
    r = t // 2
    keys = kvo_ref.shape[0]
    qt = qt_ref[...]
    qz = [head_rows(qt, h) for h in range(2)]
    kb = kv_ref[:, :LANES]
    vt = kv_ref[:, LANES:].T
    kbo = kvo_ref[:, :LANES]
    vto = kvo_ref[:, LANES:].T
    st_ref[...] = jnp.zeros_like(st_ref)
    own, cont = local_masks(sc_ref, r, keys, 0, t)
    attend_update(qz, kb, vt, 0, t, own, st_ref, a_ref, True)
    if r % LANES == 0:
        attend_update(qz, kbo, vto, r, t, cont[:, r:], st_ref, a_ref, False)
    else:
        attend_update(qz, kbo, vto, 0, t, cont, st_ref, a_ref, False)


def halves_value(a_ref, b_ref):
    return jnp.where(pl.program_id(0) < PAIRS // 2, a_ref[...], b_ref[...])


def fwd_remote_body(offsets, count, halves, final, sc_ref, qt_ref, *refs):
    kv_refs, refs = refs[:count], refs[count:]
    st_in, a_in, st_ref, a_ref = refs[:4]
    t = qt_ref.shape[1]
    r = t // 2
    me = sc_ref[0]
    qt = qt_ref[...]
    qz = [head_rows(qt, h) for h in range(2)]
    st_ref[...] = st_in[...]
    a_ref[...] = a_in[...]
    for j, offset in enumerate(offsets):
        block = sc_ref[3 + offset]

        def go(lo, hi, mask):
            if halves:
                kv = halves_value(*kv_refs)
            elif len(kv_refs) == len(offsets):
                kv = kv_refs[j][...]
            else:
                kv = kv_refs[0][j * r : (j + 1) * r, :]
            attend_update(qz, kv[:, :LANES], kv[:, LANES:].T, lo, hi, mask, st_ref, a_ref, False)

        if r % LANES == 0:

            @pl.when(block < me)
            def _():
                go(0, t, None)

            @pl.when(block > me)
            def _():
                go(r, t, None)

        else:

            @pl.when(block != me)
            def _():
                col = lax.broadcasted_iota(jnp.int32, (r, t), 1)
                go(0, t, (col >= r) | (block < me))

    if final:
        low_ref = refs[4]
        for h in range(2):
            rows = slice(h * HEAD_DIM, (h + 1) * HEAD_DIM)
            total = st_ref[2 + h : 3 + h, :]
            a_ref[rows, :] = a_ref[rows, :] / total
            st_ref[h : h + 1, :] = st_ref[h : h + 1, :] * LC + jnp.log2(total)
        low_ref[...] = a_ref[...].astype(BF16).T


def kv_specs(kvs, halves):
    if halves:
        r = kvs[0].shape[0]
        return [
            spec((r, 2 * LANES), lambda i: (0, jnp.minimum(i, PAIRS // 2 - 1))),
            spec((r, 2 * LANES), lambda i: (0, jnp.maximum(i - PAIRS // 2, 0))),
        ]
    return [spec((kv.shape[0], 2 * LANES), lambda i: (0, i)) for kv in kvs]


def fwd_local(sc, qt, kv_prompt, kv_own):
    t = qt.shape[1]
    keys = kv_own.shape[0]
    return pl.pallas_call(
        fwd_local_body,
        grid=(PAIRS,),
        in_specs=[
            SMEM_SPEC,
            spec((LANES, t), lambda i: (i, 0)),
            spec((t // 2, 2 * LANES), lambda i: (0, i)),
            spec((keys, 2 * LANES), lambda i: (0, i)),
        ],
        out_specs=[spec((8, t), lambda i: (i, 0)), spec((LANES, t), lambda i: (i, 0))],
        out_shape=[shape((8 * PAIRS, t), F32), shape((D, t), F32)],
        name="attend_local",
        **params((4 * 4 * t * keys * D, 4 * D * t)),
    )(sc, qt, kv_prompt, kv_own)


def fwd_remote(sc, qt, kvs, offsets, st, acc, halves=False, final=False):
    t = qt.shape[1]
    rows = len(offsets) * (t // 2)
    out_specs = [spec((8, t), lambda i: (i, 0)), spec((LANES, t), lambda i: (i, 0))]
    out_shape = [shape((8 * PAIRS, t), F32), shape((D, t), F32)]
    if final:
        out_specs.append(spec((t, LANES), lambda i: (0, i)))
        out_shape.append(shape((t, D), BF16))
    return pl.pallas_call(
        functools.partial(fwd_remote_body, tuple(offsets), len(kvs), halves, final),
        grid=(PAIRS,),
        in_specs=[SMEM_SPEC, spec((LANES, t), lambda i: (i, 0))]
        + kv_specs(kvs, halves)
        + [spec((8, t), lambda i: (i, 0)), spec((LANES, t), lambda i: (i, 0))],
        out_specs=out_specs,
        out_shape=out_shape,
        name="attend_remote",
        **params((4 * 4 * t * rows * D, 8 * D * t + 4 * D * rows)),
    )(sc, qt, *kvs, st, acc)


def back_block(ops, kb, vb, kt, lo, hi, mask, dq_ref):
    qz, qn, doz, don, lse, delta = ops
    dk = None
    dv = None
    for h in range(2):
        s = dot(kb, qz[h][:, lo:hi])
        dp = dot(vb, doz[h][:, lo:hi])
        p = jnp.exp2(s * LC - lse[h][:, lo:hi])
        if mask is not None:
            p = jnp.where(mask, p, 0.0)
        ds = (p * (dp - delta[h][:, lo:hi])).astype(BF16)
        dv_h = dot(p.astype(BF16), don[h][lo:hi])
        dk_h = dot(ds, qn[h][lo:hi])
        rows = slice(h * HEAD_DIM, (h + 1) * HEAD_DIM)
        dq_ref[rows, lo:hi] += dot(kt[rows], ds)
        dv = dv_h if dv is None else dv + dv_h
        dk = dk_h if dk is None else dk + dk_h
    return dk, dv


def back_operands(qt_ref, q_ref, dot_ref, do_ref, st_ref):
    qt, q, do_t, do = qt_ref[...], q_ref[...], dot_ref[...], do_ref[...]
    return (
        [head_rows(qt, h) for h in range(2)],
        [head_lanes(q, h) for h in range(2)],
        [head_rows(do_t, h) for h in range(2)],
        [head_lanes(do, h) for h in range(2)],
        [st_ref[h : h + 1, :] for h in range(2)],
        [st_ref[4 + h : 5 + h, :] for h in range(2)],
    )


def bwd_local_body(
    sc_ref, qt_ref, q_ref, dot_ref, do_ref, st_ref, dq_in, kv_ref, kvo_ref,
    out_ref, dkv_ref, dkvo_ref, dq_ref,
):
    t = qt_ref.shape[1]
    r = t // 2
    keys = kvo_ref.shape[0]
    ops = back_operands(qt_ref, q_ref, dot_ref, do_ref, st_ref)
    dq_ref[...] = dq_in[...]
    kb, vb = kv_ref[:, :LANES], kv_ref[:, LANES:]
    kbo, vbo = kvo_ref[:, :LANES], kvo_ref[:, LANES:]
    kt, kto = kb.T, kbo.T
    own, cont = local_masks(sc_ref, r, keys, 0, t)
    dk, dv = back_block(ops, kb, vb, kt, 0, t, own, dq_ref)
    if r % LANES == 0:
        dko, dvo = back_block(ops, kbo, vbo, kto, r, t, cont[:, r:], dq_ref)
    else:
        dko, dvo = back_block(ops, kbo, vbo, kto, 0, t, cont, dq_ref)
    dkv_ref[:, :LANES] = dk * SCALE
    dkv_ref[:, LANES:] = dv
    dkvo_ref[:, :LANES] = dko * SCALE
    dkvo_ref[:, LANES:] = dvo
    out_ref[...] = dq_ref[...].T * SCALE


def bwd_remote_body(
    offsets, count, halves, first, dtype, sc_ref, qt_ref, q_ref, dot_ref, do_ref, st_in, *refs
):
    t = qt_ref.shape[1]
    r = t // 2
    me = sc_ref[0]
    kv_refs, refs = refs[:count], refs[count:]
    src, refs = refs[0], refs[1:]
    dq_ref, refs = refs[0], refs[1:]
    out_refs, refs = refs[:count], refs[count:]
    if first:
        st_ref, refs = refs[0], refs[1:]
        st_ref[...] = st_in[...]
        prod = src[...] * dot_ref[...].astype(F32)
        for h in range(2):
            st_ref[4 + h : 5 + h, :] = jnp.sum(
                prod[h * HEAD_DIM : (h + 1) * HEAD_DIM], axis=0, keepdims=True
            )
        dq_ref[...] = jnp.zeros_like(dq_ref)
    else:
        st_ref = st_in
        dq_ref[...] = src[...]
    ops = back_operands(qt_ref, q_ref, dot_ref, do_ref, st_ref)
    split = len(offsets) != count and not halves

    def store(j, dk, dv):
        if halves:
            for part in range(2):

                @pl.when((pl.program_id(0) < PAIRS // 2) == (part == 0))
                def _():
                    out_refs[part][:, :LANES] = dk
                    out_refs[part][:, LANES:] = dv

        elif split:
            out_refs[0][j * r : (j + 1) * r, :LANES] = dk
            out_refs[0][j * r : (j + 1) * r, LANES:] = dv
        else:
            out_refs[j][:, :LANES] = dk
            out_refs[j][:, LANES:] = dv

    for j, offset in enumerate(offsets):
        block = sc_ref[3 + offset]

        def go(lo, mask):
            if halves:
                kv = halves_value(*kv_refs)
            elif split:
                kv = kv_refs[0][j * r : (j + 1) * r, :]
            else:
                kv = kv_refs[j][...]
            kb = kv[:, :LANES]
            dk, dv = back_block(ops, kb, kv[:, LANES:], kb.T, lo, t, mask, dq_ref)
            store(j, (dk * SCALE).astype(dtype), dv.astype(dtype))

        if split:

            @pl.when(block == me)
            def _():
                zero = jnp.zeros((r, LANES), dtype)
                store(j, zero, zero)

        if r % LANES == 0:

            @pl.when(block < me)
            def _():
                go(0, None)

            @pl.when(block > me)
            def _():
                go(r, None)

        else:

            @pl.when(block != me)
            def _():
                col = lax.broadcasted_iota(jnp.int32, (r, t), 1)
                go(0, (col >= r) | (block < me))


def add_low(a, b):
    return (a.astype(F32) + b.astype(F32)).astype(BF16)


def ring_add_body(half, pr_ref, gr_ref, pl_ref, gl_ref, sr_ref, sl_ref):
    if not half:
        sr_ref[...] = add_low(pr_ref[...], gr_ref[...])
        sl_ref[...] = add_low(pl_ref[...], gl_ref[...])
        return
    sr_ref[:, :D] = add_low(pr_ref[:, :D], gr_ref[...])
    sr_ref[:, D:] = pr_ref[:, D:]
    sl_ref[:, :D] = pl_ref[:, :D]
    sl_ref[:, D:] = add_low(pl_ref[:, D:], gl_ref[...])


def ring_add(part_r, got_r, part_l, got_l):
    r = part_r.shape[0]
    part = r // 2
    half = got_r.shape[1] == D
    wide = spec((part, 2 * D), lambda i: (i, 0))
    got = spec((part, got_r.shape[1]), lambda i: (i, 0))
    return pl.pallas_call(
        functools.partial(ring_add_body, half),
        grid=(2,),
        in_specs=[wide, got, wide, got],
        out_specs=[wide, wide],
        out_shape=[shape((r, 2 * D), BF16)] * 2,
        name="ring_add",
        **params((4 * r * D, 16 * r * D)),
    )(part_r, got_r, part_l, got_l)


def q_specs(t):
    return [
        spec((LANES, t), lambda i: (i, 0)),
        spec((t, LANES), lambda i: (0, i)),
        spec((LANES, t), lambda i: (i, 0)),
        spec((t, LANES), lambda i: (0, i)),
        spec((8, t), lambda i: (i, 0)),
    ]


def bwd_local(sc, qt, q, do_t, do, st, dq, kv_prompt, kv_own):
    t = qt.shape[1]
    keys = kv_own.shape[0]
    return pl.pallas_call(
        bwd_local_body,
        grid=(PAIRS,),
        in_specs=[SMEM_SPEC]
        + q_specs(t)
        + [spec((LANES, t), lambda i: (i, 0))]
        + kv_specs((kv_prompt, kv_own), False),
        out_specs=[spec((t, LANES), lambda i: (0, i))] + kv_specs((kv_prompt, kv_own), False),
        out_shape=[
            shape((t, D), F32),
            shape((t // 2, 2 * D), F32),
            shape((keys, 2 * D), F32),
        ],
        scratch_shapes=[pltpu.VMEM((LANES, t), F32)],
        name="attend_back_local",
        **params((10 * 4 * t * keys * D, 16 * D * t)),
    )(sc, qt, q, do_t, do, st, dq, kv_prompt, kv_own)


def bwd_remote(
    sc, qt, q, do_t, do, st, src, kvs, offsets, halves=False, first=False, dtype=F32
):
    t = qt.shape[1]
    rows = len(offsets) * (t // 2)
    out_specs = [spec((LANES, t), lambda i: (i, 0))] + kv_specs(kvs, halves)
    out_shape = [shape((D, t), F32)] + [shape(kv.shape, dtype) for kv in kvs]
    if first:
        out_specs.append(spec((8, t), lambda i: (i, 0)))
        out_shape.append(shape((8 * PAIRS, t), F32))
    return pl.pallas_call(
        functools.partial(bwd_remote_body, tuple(offsets), len(kvs), halves, first, dtype),
        grid=(PAIRS,),
        in_specs=[SMEM_SPEC]
        + q_specs(t)
        + kv_specs(kvs, halves)
        + [spec((LANES, t), lambda i: (i, 0))],
        out_specs=out_specs,
        out_shape=out_shape,
        name="attend_back_remote",
        **params((10 * 4 * t * rows * D, 16 * D * t + 8 * D * rows)),
    )(sc, qt, q, do_t, do, st, *kvs, src)


def route_body(
    x_ref, att_ref, ow_ref, sw_ref, gain_ref, res_ref, rt_ref, tr_ref,
    h_ref, n_ref, pr_ref, xs_ref,
):
    t = x_ref.shape[0]
    step = pl.program_id(0)

    @pl.when(step == 0)
    def _():
        hidden = x_ref[...].astype(F32) + dot(att_ref[...], ow_ref[...])
        h_ref[...] = hidden
        scale = lax.rsqrt(jnp.mean(hidden * hidden, axis=-1, keepdims=True) + EPS)
        low = (hidden * scale * gain_ref[...]).astype(BF16)
        n_ref[...] = low
        z = dot(low, sw_ref[...])
        lane = lax.broadcasted_iota(jnp.int32, (t, LANES), 1)
        is_route = lane < EXPERTS + 4
        logits = jnp.where(is_route, z + res_ref[...], NEG)
        ex = jnp.exp(logits - jnp.max(logits, axis=-1, keepdims=True))
        probs = ex / jnp.sum(ex, axis=-1, keepdims=True)
        out = probs
        first = EXPERTS + 4
        for k in range(2):
            l0 = z[:, first + 2 * k : first + 2 * k + 1]
            l1 = z[:, first + 2 * k + 1 : first + 2 * k + 2]
            top = jnp.maximum(l0, l1)
            e0 = jnp.exp(l0 - top)
            e1 = jnp.exp(l1 - top)
            den = e0 + e1
            out = jnp.where(lane == first + 2 * k, e0 / den, out)
            out = jnp.where(lane == first + 2 * k + 1, e1 / den, out)
        for j in range(2):
            mix = jnp.sum(jnp.where(lane == rt_ref[:, j : j + 1], probs, 0.0), axis=-1, keepdims=True)
            out = jnp.where(lane == 16 + j, mix, out)
        pr_ref[...] = out

    slots = xs_ref.shape[0]
    base = step * slots
    slot = base + lax.broadcasted_iota(jnp.int32, (slots, t), 0)
    pick = (slot == tr_ref[0:1, :]) | (slot == tr_ref[1:2, :])
    xs_ref[...] = dot(pick.astype(BF16), n_ref[...]).astype(BF16)


def out_w_spec():
    return spec((D, D), lambda *_: (0, 3))


def small_w_spec():
    return spec((D, LANES), lambda *_: (0, 4 * D // LANES))


def grad_rows_body(g_ref, pr_ref, tr_ref, gs_ref, mg_ref):
    t = g_ref.shape[0]
    step = pl.program_id(0)

    @pl.when(step == 0)
    def _():
        g = g_ref[...].astype(F32)
        for j in range(2):
            mg_ref[j * t : (j + 1) * t, :] = (g * pr_ref[:, 16 + j : 17 + j]).astype(BF16)

    slots = gs_ref.shape[0]
    slot = step * slots + lax.broadcasted_iota(jnp.int32, (slots, t), 0)
    picks = [(slot == tr_ref[j : j + 1, :]).astype(BF16) for j in range(2)]
    gs_ref[...] = dot(jnp.concatenate(picks, axis=1), mg_ref[...]).astype(BF16)


def grad_rows_call(g, pr, tr, slots):
    t = g.shape[0]
    part = min(slots, 256)
    return pl.pallas_call(
        grad_rows_body,
        grid=(slots // part,),
        in_specs=[whole((t, D)), whole((t, LANES)), whole((2, t))],
        out_specs=spec((part, D), lambda i: (i, 0)),
        out_shape=shape((slots, D), BF16),
        scratch_shapes=[pltpu.VMEM((2 * t, D), BF16)],
        name="grad_rows",
        **params((4 * slots * t * D, 4 * t * D)),
    )(g, pr, tr)


def route_call(x, att, pack, gain, res, rt, tr, slots):
    t = x.shape[0]
    part = min(slots, 256)
    return pl.pallas_call(
        route_body,
        grid=(slots // part,),
        in_specs=[
            whole((t, D)), whole((t, D)), out_w_spec(), small_w_spec(), whole((1, D)),
            whole((t, LANES)), whole((t, 2)), whole((2, t)),
        ],
        out_specs=[
            whole((t, D)), whole((t, D)), whole((t, LANES)),
            spec((part, D), lambda i: (i, 0)),
        ],
        out_shape=[
            shape((t, D), F32), shape((t, D), BF16), shape((t, LANES), F32),
            shape((slots, D), BF16),
        ],
        name="route_dispatch",
        **params((2 * t * D * D + 2 * slots * t * D, 8 * t * D)),
    )(x, att, pack, pack, gain, res, rt, tr)


def expert_fwd_body(x_ref, w_ref, o_ref, gate_ref, up_ref, acc_ref):
    step = pl.program_id(0)
    x = x_ref[...]
    wide = w_ref.shape[-1]
    wg = w_ref[:, 0].reshape(D, wide)
    wu = w_ref[:, 1].reshape(D, wide)
    wd = w_ref[:, 2].reshape(D, wide)
    gate = dot(x, wg)
    up = dot(x, wu)
    gate_ref[...] = gate
    up_ref[...] = up
    act = (gate / (1.0 + jnp.exp(-gate)) * up).astype(BF16)
    out = dot_nt(act, wd)

    @pl.when(step == 0)
    def _():
        acc_ref[...] = out

    @pl.when(step > 0)
    def _():
        acc_ref[...] += out

    @pl.when(step == pl.num_programs(0) - 1)
    def _():
        o_ref[...] = acc_ref[...].astype(BF16)


def expert_fwd(xr, w):
    rows = xr.shape[0]
    shards, _, per, wide = w.shape
    part = min(wide, 256)
    return pl.pallas_call(
        expert_fwd_body,
        grid=(wide // part,),
        in_specs=[whole((rows, D)), spec((shards, 3, per, part), lambda i: (0, 0, 0, i))],
        out_specs=[whole((rows, D))] + [spec((rows, part), lambda i: (0, i))] * 2,
        out_shape=[shape((rows, D), BF16)] + [shape((rows, wide), F32)] * 2,
        scratch_shapes=[pltpu.VMEM((rows, D), F32)],
        name="expert_forward",
        **params((6 * rows * D * wide, 6 * D * wide)),
    )(xr, w)


def expert_in_body(gate_ref, up_ref, g_ref, w_ref, gi_ref, act_ref, dg_ref, du_ref, acc_ref):
    step = pl.program_id(0)
    wide = w_ref.shape[-1]
    wg = w_ref[:, 0].reshape(D, wide)
    wu = w_ref[:, 1].reshape(D, wide)
    wd = w_ref[:, 2].reshape(D, wide)
    gate = gate_ref[...]
    up = up_ref[...]
    ga = dot(g_ref[...], wd)
    sig = 1.0 / (1.0 + jnp.exp(-gate))
    silu = gate * sig
    act_ref[...] = (silu * up).astype(BF16)
    d_gate = (ga * up * sig * (1.0 + gate * (1.0 - sig))).astype(BF16)
    d_up = (ga * silu).astype(BF16)
    dg_ref[...] = d_gate
    du_ref[...] = d_up
    gi = dot_nt(
        jnp.concatenate([d_gate, d_up], axis=1), jnp.concatenate([wg, wu], axis=1)
    )

    @pl.when(step == 0)
    def _():
        acc_ref[...] = gi

    @pl.when(step > 0)
    def _():
        acc_ref[...] += gi

    @pl.when(step == pl.num_programs(0) - 1)
    def _():
        gi_ref[...] = acc_ref[...].astype(BF16)


def expert_in(gate, up, gr, w):
    rows = gr.shape[0]
    shards, _, per, wide = w.shape
    part = min(wide, 256)
    tile = spec((rows, part), lambda i: (0, i))
    return pl.pallas_call(
        expert_in_body,
        grid=(wide // part,),
        in_specs=[tile, tile, whole((rows, D)), spec((shards, 3, per, part), lambda i: (0, 0, 0, i))],
        out_specs=[whole((rows, D)), tile, tile, tile],
        out_shape=[shape((rows, D), BF16)] + [shape((rows, wide), BF16)] * 3,
        scratch_shapes=[pltpu.VMEM((rows, D), F32)],
        name="expert_back_in",
        **params((6 * rows * D * wide, 12 * D * wide)),
    )(gate, up, gr, w)


def expert_weights_body(x_ref, gl_ref, act_ref, dg_ref, du_ref, dw_ref, xt_ref, gt_ref):
    @pl.when(pl.program_id(0) == 0)
    def _():
        gt_ref[...] = gl_ref[...].T
        xt_ref[...] = x_ref[...].T

    shards, _, per, wide = dw_ref.shape
    xt = xt_ref[...]
    dw_ref[:, 0] = dot(xt, dg_ref[...]).astype(BF16).reshape(shards, per, wide)
    dw_ref[:, 1] = dot(xt, du_ref[...]).astype(BF16).reshape(shards, per, wide)
    dw_ref[:, 2] = dot(gt_ref[...], act_ref[...]).astype(BF16).reshape(shards, per, wide)


def expert_weights(xr, low, act, d_gate, d_up, dims):
    rows = xr.shape[0]
    shards, _, per, wide = dims
    part = min(wide, 256)
    tile = spec((rows, part), lambda i: (0, i))
    return pl.pallas_call(
        expert_weights_body,
        grid=(wide // part,),
        in_specs=[whole((rows, D)), whole((rows, D)), tile, tile, tile],
        out_specs=spec((shards, 3, per, part), lambda i: (0, 0, 0, i)),
        out_shape=shape(dims, BF16),
        scratch_shapes=[pltpu.VMEM((D, rows), BF16), pltpu.VMEM((D, rows), BF16)],
        name="expert_weight_grads",
        **params((6 * rows * D * wide, 12 * D * wide)),
    )(xr, low, act, d_gate, d_up)


def mix_body(
    h_ref, g_ref, pr_ref, rt_ref, tc_ref, ret_ref, n_ref, sw_ref, rows_ref,
    out_ref, gn_ref, gl_ref, gs_ref,
):
    t = h_ref.shape[0]
    slots = ret_ref.shape[0]
    hidden = h_ref[...]
    g16 = g_ref[...]
    g = g16.astype(F32)
    pr = pr_ref[...]
    scale = lax.rsqrt(jnp.mean(hidden * hidden, axis=-1, keepdims=True) + EPS)
    normed = hidden * scale * rows_ref[2:3, :]
    lane = lax.broadcasted_iota(jnp.int32, (t, LANES), 1)
    slot = lax.broadcasted_iota(jnp.int32, (t, slots), 1)
    first = EXPERTS + 4
    ret = ret_ref[...]
    c0 = [pr[:, first + 2 * k : first + 2 * k + 1] for k in range(2)]
    c1 = [pr[:, first + 2 * k + 1 : first + 2 * k + 2] for k in range(2)]
    total = hidden
    s = jnp.zeros((t, LANES), F32)
    coef = jnp.zeros((t, 1), F32)
    weight = [jnp.zeros((t, 1), F32) for _ in range(2)]
    for j in range(2):
        route = rt_ref[:, j : j + 1]
        mix = pr[:, 16 + j : 17 + j]
        branch = dot((slot == tc_ref[:, j : j + 1]).astype(BF16), ret)
        keep = jnp.where(route == EXPERTS + 1, 1.0, 0.0)
        for k in range(2):
            here = jnp.where(route == EXPERTS + 2 + k, 1.0, 0.0)
            keep = keep + here * c0[k]
            weight[k] = weight[k] + here * mix
            branch = branch + (here * c1[k]) * rows_ref[k : k + 1, :]
        branch = branch + keep * normed
        coef = coef + mix * keep
        total = total + mix * branch
        gp = jnp.sum(g * branch, axis=-1, keepdims=True)
        s = s + jnp.where(lane == route, gp, 0.0)
    out_ref[...] = total.astype(BF16)
    probs = jnp.where(lane < first, pr, 0.0)
    d_logits = probs * (s - jnp.sum(probs * s, axis=-1, keepdims=True))
    gl_ref[...] = d_logits
    dz = d_logits
    dvec = jnp.zeros((t, LANES), F32)
    g_dot_n = jnp.sum(g * normed, axis=-1, keepdims=True)
    for k in range(2):
        d0 = weight[k] * g_dot_n
        d1 = weight[k] * jnp.sum(g * rows_ref[k : k + 1, :], axis=-1, keepdims=True)
        mean = c0[k] * d0 + c1[k] * d1
        dz = jnp.where(lane == first + 2 * k, c0[k] * (d0 - mean), dz)
        dz = jnp.where(lane == first + 2 * k + 1, c1[k] * (d1 - mean), dz)
        dvec = jnp.where(lane == 16 + k, weight[k] * c1[k], dvec)
    hi, lo = split_hi_lo(dz)
    sw = sw_ref[...]
    gn_ref[...] = coef * g + (dot_nt(hi, sw) + dot_nt(lo, sw))
    nt = n_ref[...].T
    gt = g16.T
    vhi, vlo = split_hi_lo(dvec)
    gs = dot(nt, hi) + dot(nt, lo) + dot(gt, vhi) + dot(gt, vlo)

    @pl.when(pl.program_id(0) == 0)
    def _():
        gs_ref[...] = gs

    @pl.when(pl.program_id(0) > 0)
    def _():
        gs_ref[...] += gs


def mix_call(hidden, g, pr, rt, tc, ret, low, pack, rows):
    t = hidden.shape[0]
    half = min(t, LANES)
    slots = ret.shape[0]
    tile = spec((half, D), lambda i: (i, 0))
    lane_tile = spec((half, LANES), lambda i: (i, 0))
    pair = spec((half, 2), lambda i: (i, 0))
    return pl.pallas_call(
        mix_body,
        grid=(t // half,),
        in_specs=[
            tile, tile, lane_tile, pair, pair, whole((slots, D)), tile, small_w_spec(),
            whole((8, D)),
        ],
        out_specs=[tile, tile, lane_tile, whole((D, LANES))],
        out_shape=[
            shape((t, D), BF16), shape((t, D), F32), shape((t, LANES), F32), shape((D, LANES), F32),
        ],
        name="mixture",
        **params((4 * t * slots * D, 12 * t * D)),
    )(hidden, g, pr, rt, tc, ret, low, pack, rows)


def norm_back_body(
    h_ref, g_ref, gn_ref, tc_ref, ret_ref, rows_ref, ow_ref, att_ref,
    gh_ref, do_ref, dot_ref, gow_ref, gg_ref,
):
    t = h_ref.shape[0]
    slots = ret_ref.shape[0]
    hidden = h_ref[...]
    slot = lax.broadcasted_iota(jnp.int32, (t, slots), 1)
    pick = (slot == tc_ref[:, 0:1]) | (slot == tc_ref[:, 1:2])
    gn = gn_ref[...] + dot(pick.astype(BF16), ret_ref[...])
    q = lax.rsqrt(jnp.mean(hidden * hidden, axis=-1, keepdims=True) + EPS)
    u = gn * rows_ref[2:3, :]
    mean = jnp.mean(u * hidden, axis=-1, keepdims=True)
    gh = g_ref[...].astype(F32) + q * u - hidden * (q * q * q * mean)
    gh_ref[...] = gh
    gb = gh.astype(BF16)
    d_out = dot_nt(gb, ow_ref[...]).astype(BF16)
    do_ref[...] = d_out
    dot_ref[...] = d_out.T
    gow = dot(att_ref[...].T, gb)
    gain = jnp.sum(gn * hidden * q, axis=0, keepdims=True)

    @pl.when(pl.program_id(0) == 0)
    def _():
        gow_ref[...] = gow
        gg_ref[...] = jnp.broadcast_to(gain, gg_ref.shape)

    @pl.when(pl.program_id(0) > 0)
    def _():
        gow_ref[...] += gow
        gg_ref[...] += jnp.broadcast_to(gain, gg_ref.shape)


def norm_back_call(hidden, g, gn, tc, ret, rows, pack, att):
    t = hidden.shape[0]
    half = t // 2 if (t // 2) % LANES == 0 else t
    slots = ret.shape[0]
    tile = spec((half, D), lambda i: (i, 0))
    return pl.pallas_call(
        norm_back_body,
        grid=(t // half,),
        in_specs=[
            tile, tile, tile, spec((half, 2), lambda i: (i, 0)), whole((slots, D)), whole((8, D)),
            out_w_spec(), tile,
        ],
        out_specs=[tile, tile, spec((D, half), lambda i: (0, i)), whole((D, D)), whole((8, D))],
        out_shape=[
            shape((t, D), F32), shape((t, D), BF16), shape((D, t), BF16), shape((D, D), F32),
            shape((8, D), F32),
        ],
        name="norm_two_back",
        **params((2 * t * slots * D + 4 * t * D * D, 16 * t * D)),
    )(hidden, g, gn, tc, ret, rows, pack, att)


def store_grad(sc_ref, split, value, refs):
    if not split:
        refs[0][...] = value
        return
    send_ref, keep_ref = refs
    per = value.shape[0] // 4
    for core in range(2):

        @pl.when(sc_ref[11] == core)
        def _():
            for part in range(2):
                mine = (2 * part + core) * per
                other = (2 * part + 1 - core) * per
                send_ref[part] = value[other : other + per].astype(BF16)
                keep_ref[part] = value[mine : mine + per]


def grad_outs(split, width):
    block = 2 * LANES
    if not split:
        return [spec((D, block), lambda i: (0, i))], [shape((D, width), F32)]
    dims = (2, D // 4, width)
    tile = spec((2, D // 4, block), lambda i: (0, 0, i))
    return [tile, tile], [shape(dims, BF16), shape(dims, F32)]


def q_back_body(split, sc_ref, n_ref, dq_ref, c_ref, s_ref, w_ref, gn_ref, nt_ref, *refs):
    step = pl.program_id(0)

    @pl.when(step == 0)
    def _():
        nt_ref[...] = n_ref[...].T

    cosine = c_ref[...]
    sine = s_ref[...]
    v0 = dq_ref[:, :LANES]
    v1 = dq_ref[:, LANES:]
    gq = jnp.concatenate(
        [
            (v0 * cosine - partner(v0) * sine).astype(BF16),
            (v1 * cosine - partner(v1) * sine).astype(BF16),
        ],
        axis=1,
    )
    store_grad(sc_ref, split, dot(nt_ref[...], gq), refs)
    gn = dot_nt(gq, w_ref[...])

    @pl.when(step == 0)
    def _():
        gn_ref[...] = gn

    @pl.when(step > 0)
    def _():
        gn_ref[...] += gn


def q_back_call(sc, low, dq, cosine, sine, pack, split):
    t = low.shape[0]
    specs, shapes = grad_outs(split, D)
    return pl.pallas_call(
        functools.partial(q_back_body, split),
        grid=(PAIRS // 2,),
        in_specs=[
            SMEM_SPEC, whole((t, D)), spec((t, 2 * LANES), lambda i: (0, i)), whole((t, LANES)),
            whole((t, LANES)), spec((D, 2 * LANES), lambda i: (0, i)),
        ],
        out_specs=[whole((t, D)), whole((D, t))] + specs,
        out_shape=[shape((t, D), F32), shape((D, t), BF16)] + shapes,
        name="q_back",
        **params((4 * t * D * D, 12 * t * D)),
    )(sc, low, dq, cosine, sine, pack)


def kv_back_body(
    split, count, sc_ref, x_ref, nt_ref, gnq_ref, gh_ref, gain_ref, c_ref, s_ref, wk_ref, wv_ref,
    own_ref, cont_ref, *refs
):
    got_refs, refs = refs[:count], refs[count:]
    gi_ref, grads, gn_ref = refs[0], refs[1:-1], refs[-1]
    step = pl.program_id(0)

    @pl.when(step == 0)
    def _():
        gn_ref[...] = gnq_ref[...]

    own = own_ref[...]
    for got in got_refs:
        own = own + got[...].astype(F32)
    total = jnp.concatenate([own, cont_ref[...]], axis=0)
    k = total[:, :LANES]
    gk = (k * c_ref[...] - partner(k) * s_ref[...]).astype(BF16)
    gkv = jnp.concatenate([gk, total[:, LANES:].astype(BF16)], axis=1)
    store_grad(sc_ref, split, dot(nt_ref[...], gkv), grads)
    gn_ref[...] += dot_nt(gkv, jnp.concatenate([wk_ref[...], wv_ref[...]], axis=1))

    @pl.when(step == pl.num_programs(0) - 1)
    def _():
        gn = gn_ref[...]
        x = x_ref[...].astype(F32)
        q = lax.rsqrt(jnp.mean(x * x, axis=-1, keepdims=True) + EPS)
        u = gn * gain_ref[...]
        mean = jnp.mean(u * x, axis=-1, keepdims=True)
        gi_ref[...] = gh_ref[...] + q * u - x * (q * q * q * mean)


def kv_back_call(sc, x, low_t, gn, gh, gain, cosine, sine, pack, own, cont, got, split):
    t = x.shape[0]
    r = t // 2
    specs, shapes = grad_outs(split, 2 * D)
    wide = spec((r, 2 * LANES), lambda i: (0, i))
    return pl.pallas_call(
        functools.partial(kv_back_body, split, len(got)),
        grid=(PAIRS,),
        in_specs=[
            SMEM_SPEC, whole((t, D)), whole((D, t)), whole((t, D)), whole((t, D)), whole((1, D)),
            whole((t, LANES)), whole((t, LANES)),
            spec((D, LANES), lambda i: (0, PAIRS + i)),
            spec((D, LANES), lambda i: (0, 2 * PAIRS + i)),
            wide, wide,
        ]
        + [wide] * len(got),
        out_specs=[whole((t, D))] + specs,
        out_shape=[shape((t, D), F32)] + shapes,
        scratch_shapes=[pltpu.VMEM((t, D), F32)],
        name="kv_back",
        **params((8 * t * D * D, 24 * t * D)),
    )(sc, x, low_t, gn, gh, gain, cosine, sine, pack, pack, own, cont, *got)


def rotation_tables(position):
    half = HEAD_DIM // 2
    frequency = 10000.0 ** (-jnp.arange(half, dtype=F32) / half)
    angles = position[:, None] * frequency[None, :]
    cosine, sine = jnp.cos(angles), jnp.sin(angles)
    return (
        jnp.concatenate([cosine] * 4, axis=1),
        jnp.concatenate([-sine, sine, -sine, sine], axis=1),
    )


def to_rows(array):
    return jnp.transpose(array, (1, 0, 2)).reshape(2 * array.shape[0], array.shape[2])


def from_rows(array):
    r = array.shape[0] // 2
    return jnp.transpose(array.reshape(2, r, array.shape[1]), (1, 0, 2))


RING = (0, 2, 4, 6, 7, 5, 3, 1)


def ring_offsets():
    place = {e: i for i, e in enumerate(RING)}
    return [[RING[(place[e] + k) % 8] for k in range(8)] for e in range(8)]


def along_ring(array, step):
    pairs = [(RING[i], RING[(i + step) % 8]) for i in range(8)]
    return lax.ppermute(array, "expert", pairs)


def tie(*values):
    return lax.optimization_barrier(values)


def swap_core(array):
    return lax.ppermute(array, "dp", [(0, 1), (1, 0), (2, 3), (3, 2)])


def add_and_cross(keep, got):
    across = lax.axis_index("dp") // 2
    keep = keep + got.astype(F32)
    send = lax.dynamic_index_in_dim(keep, 1 - across, 0, keepdims=False).astype(BF16)
    mine = lax.dynamic_index_in_dim(keep, across, 0, keepdims=False)
    return mine, lax.ppermute(send, "dp", [(0, 2), (2, 0), (1, 3), (3, 1)])


def add_and_scatter(keep, got):
    keep = (keep + got.astype(F32)).astype(BF16)
    rows, w = keep.shape
    return lax.all_to_all(
        keep.reshape(8, rows // 8, w), "expert", split_axis=0, concat_axis=0, tiled=True
    )


def add_up(got):
    return jnp.sum(got.astype(F32), axis=0)


def scatter_all(array):
    return lax.psum_scatter(
        array.astype(BF16), ALL_AXES, scatter_dimension=0, tiled=True
    ).astype(F32)


def per_device(
    hidden_in, cotangent, gate_residual, routes, groups, lengths, attn_gain, qkv_weight, out_weight,
    ffn_gain, router_weight, const_proj, const_vec, gate_weight, up_weight, down_weight,
):
    del groups
    r = hidden_in.shape[0]
    t = 2 * r
    capacity = r // 2
    owners = lax.axis_size("expert")
    copies = owners // EXPERTS
    slots = EXPERTS * capacity
    me = lax.axis_index("expert")
    per_cont = max(CONT_LEN // r, 1)

    small = jnp.concatenate(
        [
            router_weight, const_proj, const_vec, attn_gain[:, None], ffn_gain[:, None],
            jnp.zeros((attn_gain.shape[0], LANES - 20), BF16),
        ],
        axis=1,
    )
    pack = lax.all_gather(
        jnp.concatenate([qkv_weight, out_weight, small], axis=1), ALL_AXES, axis=0, tiled=True
    )
    index = jnp.arange(r, dtype=jnp.int32)
    row_ids = me * r + index
    position = jnp.concatenate([row_ids, PROMPT + row_ids % CONT_LEN]).astype(F32)
    cosine, sine = rotation_tables(position)
    cont = (me * r) // CONT_LEN
    length = lax.dynamic_slice(lengths, (cont,), (1,))
    header = jnp.stack([me, (me * r) % CONT_LEN]).astype(jnp.int32)
    header = jnp.concatenate([header, length.astype(jnp.int32)])
    ring = owners == 8
    if ring:
        ids = lax.dynamic_index_in_dim(jnp.asarray(ring_offsets(), jnp.int32), me, 0, keepdims=False)
    else:
        ids = jnp.arange(owners, dtype=jnp.int32)
    sc = jnp.concatenate([header, ids, (lax.axis_index("dp") % 2).astype(jnp.int32)[None]])

    picked = to_rows(routes)
    flat = jnp.transpose(picked).reshape(2 * t)
    hot = flat[:, None] == jnp.arange(EXPERTS, dtype=jnp.int32)[None, :]
    earlier = jnp.arange(2 * t)[:, None] > jnp.arange(2 * t)[None, :]
    before = jnp.dot(earlier.astype(BF16), hot.astype(BF16), preferred_element_type=F32)
    slot_index = jnp.sum(jnp.where(hot, before, 0.0), axis=1).astype(jnp.int32)
    target = jnp.where(flat < EXPERTS, flat * capacity + slot_index, -1)
    target_rows = target.reshape(2, t)
    target_cols = jnp.transpose(target_rows)

    def to_owners(rows):
        w = rows.shape[-1]
        shaped = rows.reshape(EXPERTS, 1, capacity, w)
        return jnp.broadcast_to(shaped, (EXPERTS, copies, capacity, w)).reshape(owners, capacity, w)

    def exchange(rows):
        got = lax.all_to_all(rows, "expert", split_axis=0, concat_axis=0, tiled=True)
        return got.reshape(owners * got.shape[1], got.shape[2])

    def from_owners(rows):
        got = exchange(rows.reshape(owners, capacity, D))
        if copies == 1:
            return got
        got = got.reshape(EXPERTS, copies, capacity, D).astype(F32)
        return jnp.sum(got, axis=1).reshape(slots, D).astype(BF16)

    x = to_rows(hidden_in)
    g = to_rows(cotangent)
    small_w = pack[:, 4 * D :]
    small_rows = jnp.transpose(small_w[:, 16:24]).astype(F32)
    gain_one = small_rows[2:3]
    rows_two = jnp.concatenate([small_rows[0:2], small_rows[3:4], small_rows[3:8]], axis=0)
    gain_two = small_rows[3:4]

    low_one, q, q_t, kv_prompt, kv_cont = qkv_call(x, gain_one, pack, cosine, sine)
    if not ring:
        kv_all = lax.all_gather(kv_prompt, "expert", axis=0, tiled=True)
    if per_cont == 1:
        kv_own = kv_cont
    else:
        cont_groups = [
            [c * per_cont + i for i in range(per_cont)] for c in range(owners // per_cont)
        ]
        kv_own = lax.all_gather(
            kv_cont, "expert", axis=0, tiled=True, axis_index_groups=cont_groups
        )
    weights = lax.all_gather(
        jnp.stack([gate_weight, up_weight, down_weight]), "dp", axis=0, tiled=False
    )
    if ring:
        right, left = [kv_prompt], [kv_prompt]
        for i in range(3):
            right.append(along_ring(right[i], 1))
            left.append(along_ring(left[i], -1))
            if i == 0:
                st, acc = fwd_local(sc, q_t, kv_prompt, kv_own)
            else:
                st, acc = fwd_remote(sc, q_t, (right[i], left[i]), (8 - i, i), st, acc)
            right[i + 1], left[i + 1], st = tie(right[i + 1], left[i + 1], st)
        far = [along_ring(right[3][:, :D], 1), along_ring(left[3][:, D:], -1)]
        st, acc = fwd_remote(sc, q_t, (right[3], left[3]), (5, 3), st, acc)
        st, att_t, att = fwd_remote(sc, q_t, far, (4,), st, acc, halves=True, final=True)
    else:
        st, acc = fwd_local(sc, q_t, kv_prompt, kv_own)
        st, att_t, att = fwd_remote(sc, q_t, (kv_all,), range(owners), st, acc, final=True)

    res = jnp.pad(to_rows(gate_residual), ((0, 0), (0, LANES - EXPERTS - 4)))
    hidden, low_two, pr, x_send = route_call(
        x, att, pack, gain_two, res, picked, target_rows, slots
    )
    x_got = exchange(to_owners(x_send))
    g_send = grad_rows_call(g, pr, target_rows, slots)
    x_got, g_send = tie(x_got, g_send)
    g_got = exchange(to_owners(g_send))
    expert_rows, gate_pre, up_pre = expert_fwd(x_got, weights)
    out_back = from_owners(expert_rows)
    grad_in, act, d_gate, d_up = expert_in(gate_pre, up_pre, g_got, weights)
    in_back = from_owners(grad_in)
    output, gn, grad_logits, grad_small = mix_call(
        hidden, g, pr, picked, target_cols, out_back, low_two, pack, rows_two
    )
    act, gn = tie(act, gn)
    grad_w = expert_weights(x_got, g_got, act, d_gate, d_up, weights.shape)
    grad_expert = lax.psum_scatter(
        grad_w.reshape(-1, grad_w.shape[-1]), "dp", scatter_dimension=0, tiled=True
    )
    per = gate_weight.shape[0]
    grad_expert = [grad_expert[i * per : (i + 1) * per].astype(F32) for i in range(3)]
    gh, d_att, d_att_t, grad_ow, gg_two = norm_back_call(
        hidden, g, gn, target_cols, in_back, rows_two, pack, att
    )

    early = jnp.concatenate(
        [grad_ow, grad_small[:, :19], jnp.transpose(gg_two[0:1]), jnp.zeros((D, LANES - 20), F32)],
        axis=1,
    )
    back = (sc, q_t, q, d_att_t, d_att)
    if ring:
        parts = early.reshape(2, 2, D // 4, D + LANES)
        core = lax.axis_index("dp") % 2
        early_keep = lax.dynamic_index_in_dim(parts, core, 1, keepdims=False)
        early_got = swap_core(
            lax.dynamic_index_in_dim(parts, 1 - core, 1, keepdims=False).astype(BF16)
        )
        dq_t, send_r, send_l, st = bwd_remote(
            *back, st, att_t, far, (4,), halves=True, first=True, dtype=BF16
        )
        for i in range(3, 0, -1):
            got_r, got_l = along_ring(send_r, 1), along_ring(send_l, -1)
            dq_t, part_r, part_l = bwd_remote(
                *back, st, dq_t, (left[i], right[i]), (i, 8 - i), dtype=BF16
            )
            got_r, got_l, part_r, part_l, dq_t, early_got = tie(
                got_r, got_l, part_r, part_l, dq_t, early_got
            )
            send_r, send_l = ring_add(part_r, got_r, part_l, got_l)
            if i == 3:
                early_keep, early_got = add_and_cross(early_keep, early_got)
        send_r, send_l, dq_t = tie(send_r, send_l, dq_t)
        got_r = along_ring(send_r, 1)
        got_l = along_ring(send_l, -1)
        got = (got_r, got_l)
        dq, dkv_own, dkv_cont = bwd_local(*back, st, dq_t, kv_prompt, kv_own)
    else:
        dq_t, dkv_all, st = bwd_remote(
            *back, st, att_t, (kv_all,), range(owners), first=True, dtype=BF16
        )
        dq, dkv_own, dkv_cont = bwd_local(*back, st, dq_t, kv_prompt, kv_own)
        got = (lax.psum_scatter(dkv_all, "expert", scatter_dimension=0, tiled=True),)
        early = scatter_all(early)
    if per_cont > 1:
        dkv_cont = lax.psum_scatter(
            dkv_cont, "expert", scatter_dimension=0, tiled=True, axis_index_groups=cont_groups
        )
    gn_q, low_one_t, *grad_q = q_back_call(sc, low_one, dq, cosine, sine, pack, ring)
    if ring:
        got_q = swap_core(grad_q[0])
        keep_q, got_q = add_and_cross(grad_q[1], got_q)
        keep_q, *got = tie(keep_q, *got)
    grad_input, *grad_kv = kv_back_call(
        sc, x, low_one_t, gn_q, gh, gain_one, cosine, sine, pack, dkv_own, dkv_cont, got, ring
    )
    output, grad_input = from_rows(output), from_rows(grad_input)
    if ring:
        got_kv = swap_core(grad_kv[0])
        keep_kv, got_kv = add_and_cross(grad_kv[1], got_kv)
        keep_kv, got_q, early_got = tie(keep_kv, got_q, early_got)
        got_q = add_and_scatter(
            jnp.concatenate([early_keep, keep_q], axis=1),
            jnp.concatenate([early_got, got_q], axis=1),
        )
        got_kv, output, grad_input, *grad_expert = tie(got_kv, output, grad_input, *grad_expert)
        summed = add_up(got_q)
        early, late_q = summed[:, : D + LANES], summed[:, D + LANES :]
        late_kv = add_up(add_and_scatter(keep_kv, got_kv))
    else:
        late_q, late_kv = scatter_all(grad_q[0]), scatter_all(grad_kv[0])
    per = late_kv.shape[0]
    late_kv = jnp.transpose(late_kv.reshape(per, PAIRS, 2, LANES), (0, 2, 1, 3))
    late = jnp.concatenate([late_q, late_kv.reshape(per, 2 * D)], axis=1)
    grad_gain = jnp.sum(late * qkv_weight.astype(F32), axis=1) / attn_gain.astype(F32)
    tail = early[:, D:]
    return (
        output,
        grad_input,
        from_rows(grad_logits)[:, :, : EXPERTS + 4],
        grad_gain,
        late,
        early[:, :D],
        tail[:, 19],
        tail[:, :12],
        tail[:, 12:16],
        tail[:, 16:18],
        grad_expert[0],
        grad_expert[1],
        grad_expert[2],
    )


def solution(mesh):
    rows = P(ALL_AXES, None, None)
    flat = P(ALL_AXES)
    mat = P(ALL_AXES, None)
    expert = P("dp", "expert")
    in_specs = (
        rows, rows, rows, rows, P("dp"), P("dp"), flat, mat, mat, flat, mat, mat, mat,
        expert, expert, expert,
    )
    out_specs = (
        rows, rows, rows, flat, mat, mat, flat, mat, mat, mat, expert, expert, expert,
    )

    return jax.shard_map(
        per_device, mesh=mesh, in_specs=in_specs, out_specs=out_specs, check_vma=False
    )
```

```python
import functools

import jax
import jax.numpy as jnp
from jax import lax
from jax.experimental import pallas as pl
from jax.experimental.pallas import tpu as pltpu
from jax.sharding import PartitionSpec as P


D = 768
HEAD_DIM = 64
PAIRS = 6
EXPERTS = 8
CONT_LEN = 256
PROMPT = 2048
LANES = 128
EPS = 1e-06
NEG = -1e30
LOG2E = 1.4426950408889634
SCALE = float(HEAD_DIM) ** (-0.5)
LC = SCALE * LOG2E
F32 = jnp.float32
BF16 = jnp.bfloat16
ALL_AXES = ("dp", "expert")
VMEM_LIMIT = 60 * 1024 * 1024


def dot(a, b):
    return jnp.dot(a, b, preferred_element_type=F32)


def dot_nt(a, b):
    return lax.dot_general(a, b, (((1,), (1,)), ((), ())), preferred_element_type=F32)


def split_hi_lo(v):
    hi = v.astype(BF16)
    return hi, (v - hi.astype(F32)).astype(BF16)


def params(cost=None):
    return dict(
        compiler_params=pltpu.CompilerParams(vmem_limit_bytes=VMEM_LIMIT),
        cost_estimate=None if cost is None else pl.CostEstimate(
            flops=int(cost[0]), bytes_accessed=int(cost[1]), transcendentals=0
        ),
    )


def shape(dims, dtype):
    return jax.ShapeDtypeStruct(tuple(dims), dtype)


def spec(block, index):
    return pl.BlockSpec(tuple(block), index)


def whole(dims):
    return pl.BlockSpec(tuple(dims), lambda *_: (0,) * len(dims))


SMEM_SPEC = pl.BlockSpec(memory_space=pltpu.SMEM)


def partner(v):
    lane = lax.broadcasted_iota(jnp.int32, v.shape, 1)
    return jnp.where((lane & 63) < 32, pltpu.roll(v, 96, 1), pltpu.roll(v, 32, 1))


def qkv_body(x_ref, gain_ref, wq_ref, wk_ref, wv_ref, c_ref, s_ref, n_ref, q_ref, qt_ref, kvp_ref, kvc_ref):
    @pl.when(pl.program_id(0) == 0)
    def _():
        x = x_ref[...].astype(F32)
        scale = lax.rsqrt(jnp.mean(x * x, axis=-1, keepdims=True) + EPS)
        n_ref[...] = (x * scale * gain_ref[...]).astype(BF16)

    n = n_ref[...]
    cosine = c_ref[...]
    sine = s_ref[...]
    kv = dot(n, jnp.concatenate([wk_ref[...], wv_ref[...]], axis=1))
    k = kv[:, :LANES]
    k = (k * cosine + partner(k) * sine).astype(BF16)
    v = kv[:, LANES:].astype(BF16)
    r = k.shape[0] // 2
    kvp_ref[:, :LANES] = k[:r]
    kvp_ref[:, LANES:] = v[:r]
    kvc_ref[:, :LANES] = k[r:]
    kvc_ref[:, LANES:] = v[r:]
    q = dot(n, wq_ref[...])
    q = q * cosine + partner(q) * sine
    q = q.astype(BF16)
    q_ref[...] = q
    qt_ref[...] = q.T


def qkv_call(x, gain, pack, cosine, sine):
    t = x.shape[0]
    return pl.pallas_call(
        qkv_body,
        grid=(PAIRS,),
        in_specs=[
            whole((t, D)),
            whole((1, D)),
            spec((D, LANES), lambda i: (0, i)),
            spec((D, LANES), lambda i: (0, PAIRS + i)),
            spec((D, LANES), lambda i: (0, 2 * PAIRS + i)),
            whole((t, LANES)),
            whole((t, LANES)),
        ],
        out_specs=[
            whole((t, D)),
            spec((t, LANES), lambda i: (0, i)),
            spec((LANES, t), lambda i: (i, 0)),
            spec((t // 2, 2 * LANES), lambda i: (0, i)),
            spec((t // 2, 2 * LANES), lambda i: (0, i)),
        ],
        out_shape=[
            shape((t, D), BF16),
            shape((t, D), BF16),
            shape((D, t), BF16),
            shape((t // 2, 2 * D), BF16),
            shape((t // 2, 2 * D), BF16),
        ],
        name="qkv_rope",
        **params((2 * t * D * 3 * D, 6 * D * D)),
    )(x, gain, pack, pack, pack, cosine, sine)


def head_rows(v, h):
    row = lax.broadcasted_iota(jnp.int32, v.shape, 0)
    return jnp.where(row // HEAD_DIM == h, v, jnp.zeros_like(v))


def head_lanes(v, h):
    lane = lax.broadcasted_iota(jnp.int32, v.shape, 1)
    return jnp.where(lane // HEAD_DIM == h, v, jnp.zeros_like(v))


def attend_update(qz, kb, vt, lo, hi, mask, st_ref, a_ref, first):
    for h in range(2):
        s = dot(kb, qz[h][:, lo:hi])
        if mask is not None:
            s = jnp.where(mask, s, NEG)
        top = jnp.max(s, axis=0, keepdims=True)
        rows = slice(h * HEAD_DIM, (h + 1) * HEAD_DIM)
        if first:
            p = jnp.exp2((s - top) * LC)
            st_ref[h : h + 1, lo:hi] = top
            st_ref[2 + h : 3 + h, lo:hi] = jnp.sum(p, axis=0, keepdims=True)
            a_ref[rows, lo:hi] = dot(vt[rows], p.astype(BF16))
        else:
            old = st_ref[h : h + 1, lo:hi]
            new = jnp.maximum(old, top)
            alpha = jnp.exp2((old - new) * LC)
            p = jnp.exp2((s - new) * LC)
            st_ref[h : h + 1, lo:hi] = new
            st_ref[2 + h : 3 + h, lo:hi] = st_ref[2 + h : 3 + h, lo:hi] * alpha + jnp.sum(
                p, axis=0, keepdims=True
            )
            a_ref[rows, lo:hi] = a_ref[rows, lo:hi] * alpha + dot(vt[rows], p.astype(BF16))


def local_masks(sc_ref, r, keys, lo, hi):
    cpos = sc_ref[1]
    length = sc_ref[2]
    col = lo + lax.broadcasted_iota(jnp.int32, (r, hi - lo), 1)
    row = lax.broadcasted_iota(jnp.int32, (r, hi - lo), 0)
    own = (row <= col) | (col >= r)
    col = lo + lax.broadcasted_iota(jnp.int32, (keys, hi - lo), 1)
    row = lax.broadcasted_iota(jnp.int32, (keys, hi - lo), 0)
    cont = (col >= r) & (row <= cpos + col - r) & (row < length)
    return own, cont


def fwd_local_body(sc_ref, qt_ref, kv_ref, kvo_ref, st_ref, a_ref):
    t = qt_ref.shape[1]
    r = t // 2
    keys = kvo_ref.shape[0]
    qt = qt_ref[...]
    qz = [head_rows(qt, h) for h in range(2)]
    kb = kv_ref[:, :LANES]
    vt = kv_ref[:, LANES:].T
    kbo = kvo_ref[:, :LANES]
    vto = kvo_ref[:, LANES:].T
    st_ref[...] = jnp.zeros_like(st_ref)
    own, cont = local_masks(sc_ref, r, keys, 0, t)
    attend_update(qz, kb, vt, 0, t, own, st_ref, a_ref, True)
    if r % LANES == 0:
        attend_update(qz, kbo, vto, r, t, cont[:, r:], st_ref, a_ref, False)
    else:
        attend_update(qz, kbo, vto, 0, t, cont, st_ref, a_ref, False)


def halves_value(a_ref, b_ref):
    return jnp.where(pl.program_id(0) < PAIRS // 2, a_ref[...], b_ref[...])


def fwd_remote_body(offsets, count, halves, final, sc_ref, qt_ref, *refs):
    kv_refs, refs = refs[:count], refs[count:]
    st_in, a_in, st_ref, a_ref = refs[:4]
    t = qt_ref.shape[1]
    r = t // 2
    me = sc_ref[0]
    qt = qt_ref[...]
    qz = [head_rows(qt, h) for h in range(2)]
    st_ref[...] = st_in[...]
    a_ref[...] = a_in[...]
    for j, offset in enumerate(offsets):
        block = sc_ref[3 + offset]

        def go(lo, hi, mask):
            if halves:
                kv = halves_value(*kv_refs)
            elif len(kv_refs) == len(offsets):
                kv = kv_refs[j][...]
            else:
                kv = kv_refs[0][j * r : (j + 1) * r, :]
            attend_update(qz, kv[:, :LANES], kv[:, LANES:].T, lo, hi, mask, st_ref, a_ref, False)

        if r % LANES == 0:

            @pl.when(block < me)
            def _():
                go(0, t, None)

            @pl.when(block > me)
            def _():
                go(r, t, None)

        else:

            @pl.when(block != me)
            def _():
                col = lax.broadcasted_iota(jnp.int32, (r, t), 1)
                go(0, t, (col >= r) | (block < me))

    if final:
        low_ref = refs[4]
        for h in range(2):
            rows = slice(h * HEAD_DIM, (h + 1) * HEAD_DIM)
            total = st_ref[2 + h : 3 + h, :]
            a_ref[rows, :] = a_ref[rows, :] / total
            st_ref[h : h + 1, :] = st_ref[h : h + 1, :] * LC + jnp.log2(total)
        low_ref[...] = a_ref[...].astype(BF16).T


def kv_specs(kvs, halves):
    if halves:
        r = kvs[0].shape[0]
        return [
            spec((r, 2 * LANES), lambda i: (0, jnp.minimum(i, PAIRS // 2 - 1))),
            spec((r, 2 * LANES), lambda i: (0, jnp.maximum(i - PAIRS // 2, 0))),
        ]
    return [spec((kv.shape[0], 2 * LANES), lambda i: (0, i)) for kv in kvs]


def fwd_local(sc, qt, kv_prompt, kv_own):
    t = qt.shape[1]
    keys = kv_own.shape[0]
    return pl.pallas_call(
        fwd_local_body,
        grid=(PAIRS,),
        in_specs=[
            SMEM_SPEC,
            spec((LANES, t), lambda i: (i, 0)),
            spec((t // 2, 2 * LANES), lambda i: (0, i)),
            spec((keys, 2 * LANES), lambda i: (0, i)),
        ],
        out_specs=[spec((8, t), lambda i: (i, 0)), spec((LANES, t), lambda i: (i, 0))],
        out_shape=[shape((8 * PAIRS, t), F32), shape((D, t), F32)],
        name="attend_local",
        **params((4 * 4 * t * keys * D, 4 * D * t)),
    )(sc, qt, kv_prompt, kv_own)


def fwd_remote(sc, qt, kvs, offsets, st, acc, halves=False, final=False):
    t = qt.shape[1]
    rows = len(offsets) * (t // 2)
    out_specs = [spec((8, t), lambda i: (i, 0)), spec((LANES, t), lambda i: (i, 0))]
    out_shape = [shape((8 * PAIRS, t), F32), shape((D, t), F32)]
    if final:
        out_specs.append(spec((t, LANES), lambda i: (0, i)))
        out_shape.append(shape((t, D), BF16))
    return pl.pallas_call(
        functools.partial(fwd_remote_body, tuple(offsets), len(kvs), halves, final),
        grid=(PAIRS,),
        in_specs=[SMEM_SPEC, spec((LANES, t), lambda i: (i, 0))]
        + kv_specs(kvs, halves)
        + [spec((8, t), lambda i: (i, 0)), spec((LANES, t), lambda i: (i, 0))],
        out_specs=out_specs,
        out_shape=out_shape,
        name="attend_remote",
        **params((4 * 4 * t * rows * D, 8 * D * t + 4 * D * rows)),
    )(sc, qt, *kvs, st, acc)


def back_block(ops, kb, vb, kt, lo, hi, mask, dq_ref):
    qz, qn, doz, don, lse, delta = ops
    dk = None
    dv = None
    for h in range(2):
        s = dot(kb, qz[h][:, lo:hi])
        dp = dot(vb, doz[h][:, lo:hi])
        p = jnp.exp2(s * LC - lse[h][:, lo:hi])
        if mask is not None:
            p = jnp.where(mask, p, 0.0)
        ds = (p * (dp - delta[h][:, lo:hi])).astype(BF16)
        dv_h = dot(p.astype(BF16), don[h][lo:hi])
        dk_h = dot(ds, qn[h][lo:hi])
        rows = slice(h * HEAD_DIM, (h + 1) * HEAD_DIM)
        dq_ref[rows, lo:hi] += dot(kt[rows], ds)
        dv = dv_h if dv is None else dv + dv_h
        dk = dk_h if dk is None else dk + dk_h
    return dk, dv


def back_operands(qt_ref, q_ref, dot_ref, do_ref, st_ref):
    qt, q, do_t, do = qt_ref[...], q_ref[...], dot_ref[...], do_ref[...]
    return (
        [head_rows(qt, h) for h in range(2)],
        [head_lanes(q, h) for h in range(2)],
        [head_rows(do_t, h) for h in range(2)],
        [head_lanes(do, h) for h in range(2)],
        [st_ref[h : h + 1, :] for h in range(2)],
        [st_ref[4 + h : 5 + h, :] for h in range(2)],
    )


def bwd_local_body(
    sc_ref, qt_ref, q_ref, dot_ref, do_ref, st_ref, dq_in, kv_ref, kvo_ref,
    out_ref, dkv_ref, dkvo_ref, dq_ref,
):
    t = qt_ref.shape[1]
    r = t // 2
    keys = kvo_ref.shape[0]
    ops = back_operands(qt_ref, q_ref, dot_ref, do_ref, st_ref)
    dq_ref[...] = dq_in[...]
    kb, vb = kv_ref[:, :LANES], kv_ref[:, LANES:]
    kbo, vbo = kvo_ref[:, :LANES], kvo_ref[:, LANES:]
    kt, kto = kb.T, kbo.T
    own, cont = local_masks(sc_ref, r, keys, 0, t)
    dk, dv = back_block(ops, kb, vb, kt, 0, t, own, dq_ref)
    if r % LANES == 0:
        dko, dvo = back_block(ops, kbo, vbo, kto, r, t, cont[:, r:], dq_ref)
    else:
        dko, dvo = back_block(ops, kbo, vbo, kto, 0, t, cont, dq_ref)
    dkv_ref[:, :LANES] = dk * SCALE
    dkv_ref[:, LANES:] = dv
    dkvo_ref[:, :LANES] = dko * SCALE
    dkvo_ref[:, LANES:] = dvo
    out_ref[...] = dq_ref[...].T * SCALE


def bwd_remote_body(
    offsets, count, halves, first, dtype, sc_ref, qt_ref, q_ref, dot_ref, do_ref, st_in, *refs
):
    t = qt_ref.shape[1]
    r = t // 2
    me = sc_ref[0]
    kv_refs, refs = refs[:count], refs[count:]
    src, refs = refs[0], refs[1:]
    dq_ref, refs = refs[0], refs[1:]
    out_refs, refs = refs[:count], refs[count:]
    if first:
        st_ref, refs = refs[0], refs[1:]
        st_ref[...] = st_in[...]
        prod = src[...] * dot_ref[...].astype(F32)
        for h in range(2):
            st_ref[4 + h : 5 + h, :] = jnp.sum(
                prod[h * HEAD_DIM : (h + 1) * HEAD_DIM], axis=0, keepdims=True
            )
        dq_ref[...] = jnp.zeros_like(dq_ref)
    else:
        st_ref = st_in
        dq_ref[...] = src[...]
    ops = back_operands(qt_ref, q_ref, dot_ref, do_ref, st_ref)
    split = len(offsets) != count and not halves

    def store(j, dk, dv):
        if halves:
            for part in range(2):

                @pl.when((pl.program_id(0) < PAIRS // 2) == (part == 0))
                def _():
                    out_refs[part][:, :LANES] = dk
                    out_refs[part][:, LANES:] = dv

        elif split:
            out_refs[0][j * r : (j + 1) * r, :LANES] = dk
            out_refs[0][j * r : (j + 1) * r, LANES:] = dv
        else:
            out_refs[j][:, :LANES] = dk
            out_refs[j][:, LANES:] = dv

    for j, offset in enumerate(offsets):
        block = sc_ref[3 + offset]

        def go(lo, mask):
            if halves:
                kv = halves_value(*kv_refs)
            elif split:
                kv = kv_refs[0][j * r : (j + 1) * r, :]
            else:
                kv = kv_refs[j][...]
            kb = kv[:, :LANES]
            dk, dv = back_block(ops, kb, kv[:, LANES:], kb.T, lo, t, mask, dq_ref)
            store(j, (dk * SCALE).astype(dtype), dv.astype(dtype))

        if split:

            @pl.when(block == me)
            def _():
                zero = jnp.zeros((r, LANES), dtype)
                store(j, zero, zero)

        if r % LANES == 0:

            @pl.when(block < me)
            def _():
                go(0, None)

            @pl.when(block > me)
            def _():
                go(r, None)

        else:

            @pl.when(block != me)
            def _():
                col = lax.broadcasted_iota(jnp.int32, (r, t), 1)
                go(0, (col >= r) | (block < me))


def add_low(a, b):
    return (a.astype(F32) + b.astype(F32)).astype(BF16)


def ring_add_body(half, pr_ref, gr_ref, pl_ref, gl_ref, sr_ref, sl_ref):
    if not half:
        sr_ref[...] = add_low(pr_ref[...], gr_ref[...])
        sl_ref[...] = add_low(pl_ref[...], gl_ref[...])
        return
    sr_ref[:, :D] = add_low(pr_ref[:, :D], gr_ref[...])
    sr_ref[:, D:] = pr_ref[:, D:]
    sl_ref[:, :D] = pl_ref[:, :D]
    sl_ref[:, D:] = add_low(pl_ref[:, D:], gl_ref[...])


def ring_add(part_r, got_r, part_l, got_l):
    r = part_r.shape[0]
    part = r // 2
    half = got_r.shape[1] == D
    wide = spec((part, 2 * D), lambda i: (i, 0))
    got = spec((part, got_r.shape[1]), lambda i: (i, 0))
    return pl.pallas_call(
        functools.partial(ring_add_body, half),
        grid=(2,),
        in_specs=[wide, got, wide, got],
        out_specs=[wide, wide],
        out_shape=[shape((r, 2 * D), BF16)] * 2,
        name="ring_add",
        **params((4 * r * D, 16 * r * D)),
    )(part_r, got_r, part_l, got_l)


def q_specs(t):
    return [
        spec((LANES, t), lambda i: (i, 0)),
        spec((t, LANES), lambda i: (0, i)),
        spec((LANES, t), lambda i: (i, 0)),
        spec((t, LANES), lambda i: (0, i)),
        spec((8, t), lambda i: (i, 0)),
    ]


def bwd_local(sc, qt, q, do_t, do, st, dq, kv_prompt, kv_own):
    t = qt.shape[1]
    keys = kv_own.shape[0]
    return pl.pallas_call(
        bwd_local_body,
        grid=(PAIRS,),
        in_specs=[SMEM_SPEC]
        + q_specs(t)
        + [spec((LANES, t), lambda i: (i, 0))]
        + kv_specs((kv_prompt, kv_own), False),
        out_specs=[spec((t, LANES), lambda i: (0, i))] + kv_specs((kv_prompt, kv_own), False),
        out_shape=[
            shape((t, D), F32),
            shape((t // 2, 2 * D), F32),
            shape((keys, 2 * D), F32),
        ],
        scratch_shapes=[pltpu.VMEM((LANES, t), F32)],
        name="attend_back_local",
        **params((10 * 4 * t * keys * D, 16 * D * t)),
    )(sc, qt, q, do_t, do, st, dq, kv_prompt, kv_own)


def bwd_remote(
    sc, qt, q, do_t, do, st, src, kvs, offsets, halves=False, first=False, dtype=F32
):
    t = qt.shape[1]
    rows = len(offsets) * (t // 2)
    out_specs = [spec((LANES, t), lambda i: (i, 0))] + kv_specs(kvs, halves)
    out_shape = [shape((D, t), F32)] + [shape(kv.shape, dtype) for kv in kvs]
    if first:
        out_specs.append(spec((8, t), lambda i: (i, 0)))
        out_shape.append(shape((8 * PAIRS, t), F32))
    return pl.pallas_call(
        functools.partial(bwd_remote_body, tuple(offsets), len(kvs), halves, first, dtype),
        grid=(PAIRS,),
        in_specs=[SMEM_SPEC]
        + q_specs(t)
        + kv_specs(kvs, halves)
        + [spec((LANES, t), lambda i: (i, 0))],
        out_specs=out_specs,
        out_shape=out_shape,
        name="attend_back_remote",
        **params((10 * 4 * t * rows * D, 16 * D * t + 8 * D * rows)),
    )(sc, qt, q, do_t, do, st, *kvs, src)


def route_body(
    x_ref, att_ref, ow_ref, sw_ref, gain_ref, res_ref, rt_ref, tr_ref,
    h_ref, n_ref, pr_ref, xs_ref,
):
    t = x_ref.shape[0]
    step = pl.program_id(0)

    @pl.when(step == 0)
    def _():
        hidden = x_ref[...].astype(F32) + dot(att_ref[...], ow_ref[...])
        h_ref[...] = hidden
        scale = lax.rsqrt(jnp.mean(hidden * hidden, axis=-1, keepdims=True) + EPS)
        low = (hidden * scale * gain_ref[...]).astype(BF16)
        n_ref[...] = low
        z = dot(low, sw_ref[...])
        lane = lax.broadcasted_iota(jnp.int32, (t, LANES), 1)
        is_route = lane < EXPERTS + 4
        logits = jnp.where(is_route, z + res_ref[...], NEG)
        ex = jnp.exp(logits - jnp.max(logits, axis=-1, keepdims=True))
        probs = ex / jnp.sum(ex, axis=-1, keepdims=True)
        out = probs
        first = EXPERTS + 4
        for k in range(2):
            l0 = z[:, first + 2 * k : first + 2 * k + 1]
            l1 = z[:, first + 2 * k + 1 : first + 2 * k + 2]
            top = jnp.maximum(l0, l1)
            e0 = jnp.exp(l0 - top)
            e1 = jnp.exp(l1 - top)
            den = e0 + e1
            out = jnp.where(lane == first + 2 * k, e0 / den, out)
            out = jnp.where(lane == first + 2 * k + 1, e1 / den, out)
        for j in range(2):
            mix = jnp.sum(jnp.where(lane == rt_ref[:, j : j + 1], probs, 0.0), axis=-1, keepdims=True)
            out = jnp.where(lane == 16 + j, mix, out)
        pr_ref[...] = out

    slots = xs_ref.shape[0]
    base = step * slots
    slot = base + lax.broadcasted_iota(jnp.int32, (slots, t), 0)
    pick = (slot == tr_ref[0:1, :]) | (slot == tr_ref[1:2, :])
    xs_ref[...] = dot(pick.astype(BF16), n_ref[...]).astype(BF16)


def out_w_spec():
    return spec((D, D), lambda *_: (0, 3))


def small_w_spec():
    return spec((D, LANES), lambda *_: (0, 4 * D // LANES))


def grad_rows_body(g_ref, pr_ref, tr_ref, gs_ref, mg_ref):
    t = g_ref.shape[0]
    step = pl.program_id(0)

    @pl.when(step == 0)
    def _():
        g = g_ref[...].astype(F32)
        for j in range(2):
            mg_ref[j * t : (j + 1) * t, :] = (g * pr_ref[:, 16 + j : 17 + j]).astype(BF16)

    slots = gs_ref.shape[0]
    slot = step * slots + lax.broadcasted_iota(jnp.int32, (slots, t), 0)
    picks = [(slot == tr_ref[j : j + 1, :]).astype(BF16) for j in range(2)]
    gs_ref[...] = dot(jnp.concatenate(picks, axis=1), mg_ref[...]).astype(BF16)


def grad_rows_call(g, pr, tr, slots):
    t = g.shape[0]
    part = min(slots, 256)
    return pl.pallas_call(
        grad_rows_body,
        grid=(slots // part,),
        in_specs=[whole((t, D)), whole((t, LANES)), whole((2, t))],
        out_specs=spec((part, D), lambda i: (i, 0)),
        out_shape=shape((slots, D), BF16),
        scratch_shapes=[pltpu.VMEM((2 * t, D), BF16)],
        name="grad_rows",
        **params((4 * slots * t * D, 4 * t * D)),
    )(g, pr, tr)


def route_call(x, att, pack, gain, res, rt, tr, slots):
    t = x.shape[0]
    part = min(slots, 256)
    return pl.pallas_call(
        route_body,
        grid=(slots // part,),
        in_specs=[
            whole((t, D)), whole((t, D)), out_w_spec(), small_w_spec(), whole((1, D)),
            whole((t, LANES)), whole((t, 2)), whole((2, t)),
        ],
        out_specs=[
            whole((t, D)), whole((t, D)), whole((t, LANES)),
            spec((part, D), lambda i: (i, 0)),
        ],
        out_shape=[
            shape((t, D), F32), shape((t, D), BF16), shape((t, LANES), F32),
            shape((slots, D), BF16),
        ],
        name="route_dispatch",
        **params((2 * t * D * D + 2 * slots * t * D, 8 * t * D)),
    )(x, att, pack, pack, gain, res, rt, tr)


def expert_fwd_body(blocks, sc_ref, x_ref, w_ref, gate_ref, up_ref, *refs):
    o_refs, acc_ref = refs[:-1], refs[-1]
    step = pl.program_id(0)
    x = x_ref[...]
    wide = w_ref.shape[-1]
    wg = w_ref[:, 0].reshape(D, wide)
    wu = w_ref[:, 1].reshape(D, wide)
    wd = w_ref[:, 2].reshape(D, wide)
    gate = dot(x, wg)
    up = dot(x, wu)
    gate_ref[...] = gate
    up_ref[...] = up
    act = (gate / (1.0 + jnp.exp(-gate)) * up).astype(BF16)
    out = dot_nt(act, wd)

    @pl.when(step == 0)
    def _():
        acc_ref[...] = out

    @pl.when(step > 0)
    def _():
        acc_ref[...] += out

    @pl.when(step == pl.num_programs(0) - 1)
    def _():
        if blocks == 1:
            o_refs[0][...] = acc_ref[...].astype(BF16)
        else:
            size = acc_ref.shape[0] // blocks
            for k in range(blocks):
                first = pl.multiple_of((sc_ref[0] ^ k) * size, size)
                o_refs[k][...] = acc_ref[pl.ds(first, size), :].astype(BF16)


def expert_fwd(sc, xr, w, blocks):
    rows = xr.shape[0]
    shards, _, per, wide = w.shape
    part = min(wide, 256)
    return pl.pallas_call(
        functools.partial(expert_fwd_body, blocks),
        grid=(wide // part,),
        in_specs=[
            SMEM_SPEC, whole((rows, D)), spec((shards, 3, per, part), lambda i: (0, 0, 0, i)),
        ],
        out_specs=[spec((rows, part), lambda i: (0, i))] * 2 + [whole((rows // blocks, D))] * blocks,
        out_shape=[shape((rows, wide), F32)] * 2 + [shape((rows // blocks, D), BF16)] * blocks,
        scratch_shapes=[pltpu.VMEM((rows, D), F32)],
        name="expert_forward",
        **params((6 * rows * D * wide, 6 * D * wide)),
    )(sc, xr, w)


def expert_in_body(gate_ref, up_ref, g_ref, w_ref, gi_ref, act_ref, dg_ref, du_ref, acc_ref):
    step = pl.program_id(0)
    wide = w_ref.shape[-1]
    wg = w_ref[:, 0].reshape(D, wide)
    wu = w_ref[:, 1].reshape(D, wide)
    wd = w_ref[:, 2].reshape(D, wide)
    gate = gate_ref[...]
    up = up_ref[...]
    ga = dot(g_ref[...], wd)
    sig = 1.0 / (1.0 + jnp.exp(-gate))
    silu = gate * sig
    act_ref[...] = (silu * up).astype(BF16)
    d_gate = (ga * up * sig * (1.0 + gate * (1.0 - sig))).astype(BF16)
    d_up = (ga * silu).astype(BF16)
    dg_ref[...] = d_gate
    du_ref[...] = d_up
    gi = dot_nt(
        jnp.concatenate([d_gate, d_up], axis=1), jnp.concatenate([wg, wu], axis=1)
    )

    @pl.when(step == 0)
    def _():
        acc_ref[...] = gi

    @pl.when(step > 0)
    def _():
        acc_ref[...] += gi

    @pl.when(step == pl.num_programs(0) - 1)
    def _():
        gi_ref[...] = acc_ref[...].astype(BF16)


def expert_in(gate, up, gr, w):
    rows = gr.shape[0]
    shards, _, per, wide = w.shape
    part = min(wide, 256)
    tile = spec((rows, part), lambda i: (0, i))
    return pl.pallas_call(
        expert_in_body,
        grid=(wide // part,),
        in_specs=[tile, tile, whole((rows, D)), spec((shards, 3, per, part), lambda i: (0, 0, 0, i))],
        out_specs=[whole((rows, D)), tile, tile, tile],
        out_shape=[shape((rows, D), BF16)] + [shape((rows, wide), BF16)] * 3,
        scratch_shapes=[pltpu.VMEM((rows, D), F32)],
        name="expert_back_in",
        **params((6 * rows * D * wide, 12 * D * wide)),
    )(gate, up, gr, w)


def expert_weights_body(x_ref, gl_ref, act_ref, dg_ref, du_ref, dw_ref, xt_ref, gt_ref):
    @pl.when(pl.program_id(0) == 0)
    def _():
        gt_ref[...] = gl_ref[...].T
        xt_ref[...] = x_ref[...].T

    shards, _, per, wide = dw_ref.shape
    xt = xt_ref[...]
    dw_ref[:, 0] = dot(xt, dg_ref[...]).astype(BF16).reshape(shards, per, wide)
    dw_ref[:, 1] = dot(xt, du_ref[...]).astype(BF16).reshape(shards, per, wide)
    dw_ref[:, 2] = dot(gt_ref[...], act_ref[...]).astype(BF16).reshape(shards, per, wide)


def expert_weights(xr, low, act, d_gate, d_up, dims):
    rows = xr.shape[0]
    shards, _, per, wide = dims
    part = min(wide, 256)
    tile = spec((rows, part), lambda i: (0, i))
    return pl.pallas_call(
        expert_weights_body,
        grid=(wide // part,),
        in_specs=[whole((rows, D)), whole((rows, D)), tile, tile, tile],
        out_specs=spec((shards, 3, per, part), lambda i: (0, 0, 0, i)),
        out_shape=shape(dims, BF16),
        scratch_shapes=[pltpu.VMEM((D, rows), BF16), pltpu.VMEM((D, rows), BF16)],
        name="expert_weight_grads",
        **params((6 * rows * D * wide, 12 * D * wide)),
    )(xr, low, act, d_gate, d_up)


def mix_body(h_ref, g_ref, pr_ref, rt_ref, tc_ref, n_ref, sw_ref, rows_ref, *refs):
    ret_refs, (out_ref, gn_ref, gl_ref, gs_ref) = refs[:-4], refs[-4:]
    t = h_ref.shape[0]
    slots = sum(ret_ref.shape[0] for ret_ref in ret_refs)
    hidden = h_ref[...]
    g16 = g_ref[...]
    g = g16.astype(F32)
    pr = pr_ref[...]
    scale = lax.rsqrt(jnp.mean(hidden * hidden, axis=-1, keepdims=True) + EPS)
    normed = hidden * scale * rows_ref[2:3, :]
    lane = lax.broadcasted_iota(jnp.int32, (t, LANES), 1)
    slot = lax.broadcasted_iota(jnp.int32, (t, slots), 1)
    first = EXPERTS + 4
    ret = jnp.concatenate([ret_ref[...] for ret_ref in ret_refs], axis=0)
    c0 = [pr[:, first + 2 * k : first + 2 * k + 1] for k in range(2)]
    c1 = [pr[:, first + 2 * k + 1 : first + 2 * k + 2] for k in range(2)]
    total = hidden
    s = jnp.zeros((t, LANES), F32)
    coef = jnp.zeros((t, 1), F32)
    weight = [jnp.zeros((t, 1), F32) for _ in range(2)]
    for j in range(2):
        route = rt_ref[:, j : j + 1]
        mix = pr[:, 16 + j : 17 + j]
        branch = dot((slot == tc_ref[:, j : j + 1]).astype(BF16), ret)
        keep = jnp.where(route == EXPERTS + 1, 1.0, 0.0)
        for k in range(2):
            here = jnp.where(route == EXPERTS + 2 + k, 1.0, 0.0)
            keep = keep + here * c0[k]
            weight[k] = weight[k] + here * mix
            branch = branch + (here * c1[k]) * rows_ref[k : k + 1, :]
        branch = branch + keep * normed
        coef = coef + mix * keep
        total = total + mix * branch
        gp = jnp.sum(g * branch, axis=-1, keepdims=True)
        s = s + jnp.where(lane == route, gp, 0.0)
    out_ref[...] = total.astype(BF16)
    probs = jnp.where(lane < first, pr, 0.0)
    d_logits = probs * (s - jnp.sum(probs * s, axis=-1, keepdims=True))
    gl_ref[...] = d_logits
    dz = d_logits
    dvec = jnp.zeros((t, LANES), F32)
    g_dot_n = jnp.sum(g * normed, axis=-1, keepdims=True)
    for k in range(2):
        d0 = weight[k] * g_dot_n
        d1 = weight[k] * jnp.sum(g * rows_ref[k : k + 1, :], axis=-1, keepdims=True)
        mean = c0[k] * d0 + c1[k] * d1
        dz = jnp.where(lane == first + 2 * k, c0[k] * (d0 - mean), dz)
        dz = jnp.where(lane == first + 2 * k + 1, c1[k] * (d1 - mean), dz)
        dvec = jnp.where(lane == 16 + k, weight[k] * c1[k], dvec)
    hi, lo = split_hi_lo(dz)
    sw = sw_ref[...]
    gn_ref[...] = coef * g + (dot_nt(hi, sw) + dot_nt(lo, sw))
    nt = n_ref[...].T
    gt = g16.T
    vhi, vlo = split_hi_lo(dvec)
    gs = dot(nt, hi) + dot(nt, lo) + dot(gt, vhi) + dot(gt, vlo)

    @pl.when(pl.program_id(0) == 0)
    def _():
        gs_ref[...] = gs

    @pl.when(pl.program_id(0) > 0)
    def _():
        gs_ref[...] += gs


def mix_call(hidden, g, pr, rt, tc, ret, low, pack, rows):
    t = hidden.shape[0]
    half = min(t, LANES)
    slots = sum(block.shape[0] for block in ret)
    tile = spec((half, D), lambda i: (i, 0))
    lane_tile = spec((half, LANES), lambda i: (i, 0))
    pair = spec((half, 2), lambda i: (i, 0))
    return pl.pallas_call(
        mix_body,
        grid=(t // half,),
        in_specs=[
            tile, tile, lane_tile, pair, pair, tile, small_w_spec(), whole((8, D)),
        ]
        + [whole(block.shape) for block in ret],
        out_specs=[tile, tile, lane_tile, whole((D, LANES))],
        out_shape=[
            shape((t, D), BF16), shape((t, D), F32), shape((t, LANES), F32), shape((D, LANES), F32),
        ],
        name="mixture",
        **params((4 * t * slots * D, 12 * t * D)),
    )(hidden, g, pr, rt, tc, low, pack, rows, *ret)


def norm_back_body(
    h_ref, g_ref, gn_ref, tc_ref, ret_ref, rows_ref, ow_ref, att_ref,
    gh_ref, do_ref, dot_ref, gow_ref, gg_ref,
):
    t = h_ref.shape[0]
    slots = ret_ref.shape[0]
    hidden = h_ref[...]
    slot = lax.broadcasted_iota(jnp.int32, (t, slots), 1)
    pick = (slot == tc_ref[:, 0:1]) | (slot == tc_ref[:, 1:2])
    gn = gn_ref[...] + dot(pick.astype(BF16), ret_ref[...])
    q = lax.rsqrt(jnp.mean(hidden * hidden, axis=-1, keepdims=True) + EPS)
    u = gn * rows_ref[2:3, :]
    mean = jnp.mean(u * hidden, axis=-1, keepdims=True)
    gh = g_ref[...].astype(F32) + q * u - hidden * (q * q * q * mean)
    gh_ref[...] = gh
    gb = gh.astype(BF16)
    d_out = dot_nt(gb, ow_ref[...]).astype(BF16)
    do_ref[...] = d_out
    dot_ref[...] = d_out.T
    gow = dot(att_ref[...].astype(BF16), gb)
    gain = jnp.sum(gn * hidden * q, axis=0, keepdims=True)

    @pl.when(pl.program_id(0) == 0)
    def _():
        gow_ref[...] = gow
        gg_ref[...] = jnp.broadcast_to(gain, gg_ref.shape)

    @pl.when(pl.program_id(0) > 0)
    def _():
        gow_ref[...] += gow
        gg_ref[...] += jnp.broadcast_to(gain, gg_ref.shape)


def norm_back_call(hidden, g, gn, tc, ret, rows, pack, att):
    t = hidden.shape[0]
    half = t // 2 if (t // 2) % LANES == 0 else t
    slots = ret.shape[0]
    tile = spec((half, D), lambda i: (i, 0))
    return pl.pallas_call(
        norm_back_body,
        grid=(t // half,),
        in_specs=[
            tile, tile, tile, spec((half, 2), lambda i: (i, 0)), whole((slots, D)), whole((8, D)),
            out_w_spec(), spec((D, half), lambda i: (0, i)),
        ],
        out_specs=[tile, tile, spec((D, half), lambda i: (0, i)), whole((D, D)), whole((8, D))],
        out_shape=[
            shape((t, D), F32), shape((t, D), BF16), shape((D, t), BF16), shape((D, D), F32),
            shape((8, D), F32),
        ],
        name="norm_two_back",
        **params((2 * t * slots * D + 4 * t * D * D, 16 * t * D)),
    )(hidden, g, gn, tc, ret, rows, pack, att)


def turn_body(x_ref, o_ref):
    o_ref[...] = x_ref[...].T


def turn(x):
    rows, wide = x.shape
    part = 256
    return pl.pallas_call(
        turn_body,
        grid=(wide // part,),
        in_specs=[spec((rows, part), lambda i: (0, i))],
        out_specs=spec((part, rows), lambda i: (i, 0)),
        out_shape=shape((wide, rows), x.dtype),
        name="turn",
        **params((rows * wide, 4 * rows * wide)),
    )(x)


def store_grad(sc_ref, split, value, refs):
    if not split:
        refs[0][...] = value
        return
    send_ref, keep_ref = refs
    per = value.shape[0] // 4
    for core in range(2):

        @pl.when(sc_ref[11] == core)
        def _():
            for part in range(2):
                mine = (2 * part + core) * per
                other = (2 * part + 1 - core) * per
                send_ref[part] = value[other : other + per].astype(BF16)
                keep_ref[part] = value[mine : mine + per]


def grad_outs(split, width):
    block = 2 * LANES
    if not split:
        return [spec((D, block), lambda i: (0, i))], [shape((D, width), F32)]
    dims = (2, D // 4, width)
    tile = spec((2, D // 4, block), lambda i: (0, 0, i))
    return [tile, tile], [shape(dims, BF16), shape(dims, F32)]


def q_back_body(split, sc_ref, nt_ref, dq_ref, c_ref, s_ref, w_ref, gn_ref, *refs):
    step = pl.program_id(0)
    cosine = c_ref[...]
    sine = s_ref[...]
    v0 = dq_ref[:, :LANES]
    v1 = dq_ref[:, LANES:]
    gq = jnp.concatenate(
        [
            (v0 * cosine - partner(v0) * sine).astype(BF16),
            (v1 * cosine - partner(v1) * sine).astype(BF16),
        ],
        axis=1,
    )
    store_grad(sc_ref, split, dot(nt_ref[...], gq), refs)
    gn = dot_nt(gq, w_ref[...])

    @pl.when(step == 0)
    def _():
        gn_ref[...] = gn

    @pl.when(step > 0)
    def _():
        gn_ref[...] += gn


def q_back_call(sc, low_t, dq, cosine, sine, pack, split):
    t = low_t.shape[1]
    specs, shapes = grad_outs(split, D)
    return pl.pallas_call(
        functools.partial(q_back_body, split),
        grid=(PAIRS // 2,),
        in_specs=[
            SMEM_SPEC, whole((D, t)), spec((t, 2 * LANES), lambda i: (0, i)), whole((t, LANES)),
            whole((t, LANES)), spec((D, 2 * LANES), lambda i: (0, i)),
        ],
        out_specs=[whole((t, D))] + specs,
        out_shape=[shape((t, D), F32)] + shapes,
        name="q_back",
        **params((4 * t * D * D, 12 * t * D)),
    )(sc, low_t, dq, cosine, sine, pack)


def kv_back_body(
    split, count, sc_ref, x_ref, nt_ref, gnq_ref, gh_ref, gain_ref, c_ref, s_ref, wk_ref, wv_ref,
    own_ref, cont_ref, *refs
):
    got_refs, refs = refs[:count], refs[count:]
    gi_ref, grads, gn_ref = refs[0], refs[1:-1], refs[-1]
    step = pl.program_id(0)

    @pl.when(step == 0)
    def _():
        gn_ref[...] = gnq_ref[...]

    own = own_ref[...]
    for got in got_refs:
        own = own + got[...].astype(F32)
    total = jnp.concatenate([own, cont_ref[...]], axis=0)
    k = total[:, :LANES]
    gk = (k * c_ref[...] - partner(k) * s_ref[...]).astype(BF16)
    gkv = jnp.concatenate([gk, total[:, LANES:].astype(BF16)], axis=1)
    store_grad(sc_ref, split, dot(nt_ref[...], gkv), grads)
    gn_ref[...] += dot_nt(gkv, jnp.concatenate([wk_ref[...], wv_ref[...]], axis=1))

    @pl.when(step == pl.num_programs(0) - 1)
    def _():
        gn = gn_ref[...]
        x = x_ref[...].astype(F32)
        q = lax.rsqrt(jnp.mean(x * x, axis=-1, keepdims=True) + EPS)
        u = gn * gain_ref[...]
        mean = jnp.mean(u * x, axis=-1, keepdims=True)
        gi_ref[...] = gh_ref[...] + q * u - x * (q * q * q * mean)


def kv_back_call(sc, x, low_t, gn, gh, gain, cosine, sine, pack, own, cont, got, split):
    t = x.shape[0]
    r = t // 2
    specs, shapes = grad_outs(split, 2 * D)
    wide = spec((r, 2 * LANES), lambda i: (0, i))
    return pl.pallas_call(
        functools.partial(kv_back_body, split, len(got)),
        grid=(PAIRS,),
        in_specs=[
            SMEM_SPEC, whole((t, D)), whole((D, t)), whole((t, D)), whole((t, D)), whole((1, D)),
            whole((t, LANES)), whole((t, LANES)),
            spec((D, LANES), lambda i: (0, PAIRS + i)),
            spec((D, LANES), lambda i: (0, 2 * PAIRS + i)),
            wide, wide,
        ]
        + [wide] * len(got),
        out_specs=[whole((t, D))] + specs,
        out_shape=[shape((t, D), F32)] + shapes,
        scratch_shapes=[pltpu.VMEM((t, D), F32)],
        name="kv_back",
        **params((8 * t * D * D, 24 * t * D)),
    )(sc, x, low_t, gn, gh, gain, cosine, sine, pack, pack, own, cont, *got)


def rotation_tables(position):
    half = HEAD_DIM // 2
    frequency = 10000.0 ** (-jnp.arange(half, dtype=F32) / half)
    angles = position[:, None] * frequency[None, :]
    cosine, sine = jnp.cos(angles), jnp.sin(angles)
    return (
        jnp.concatenate([cosine] * 4, axis=1),
        jnp.concatenate([-sine, sine, -sine, sine], axis=1),
    )


def to_rows(array):
    return jnp.transpose(array, (1, 0, 2)).reshape(2 * array.shape[0], array.shape[2])


def from_rows(array):
    r = array.shape[0] // 2
    return jnp.transpose(array.reshape(2, r, array.shape[1]), (1, 0, 2))


RING = (0, 2, 4, 6, 7, 5, 3, 1)


def ring_offsets():
    place = {e: i for i, e in enumerate(RING)}
    return [[RING[(place[e] + k) % 8] for k in range(8)] for e in range(8)]


def along_ring(array, step):
    pairs = [(RING[i], RING[(i + step) % 8]) for i in range(8)]
    return lax.ppermute(array, "expert", pairs)


def tie(*values):
    return lax.optimization_barrier(values)


def swap_core(array):
    return lax.ppermute(array, "dp", [(0, 1), (1, 0), (2, 3), (3, 2)])


def add_and_cross(keep, got):
    across = lax.axis_index("dp") // 2
    keep = keep + got.astype(F32)
    send = lax.dynamic_index_in_dim(keep, 1 - across, 0, keepdims=False).astype(BF16)
    mine = lax.dynamic_index_in_dim(keep, across, 0, keepdims=False)
    return mine, lax.ppermute(send, "dp", [(0, 2), (2, 0), (1, 3), (3, 1)])


def add_and_scatter(keep, got):
    keep = (keep + got.astype(F32)).astype(BF16)
    rows, w = keep.shape
    return lax.all_to_all(
        keep.reshape(8, rows // 8, w), "expert", split_axis=0, concat_axis=0, tiled=True
    )


def swap_blocks(blocks):
    out = [blocks[0]]
    for k in range(1, 8):
        out.append(lax.ppermute(blocks[k], "expert", [(e, e ^ k) for e in range(8)]))
    return out


def spread_body(sc_ref, keep_ref, got_ref, *refs):
    o_refs, sum_ref = refs[:-1], refs[-1]
    sum_ref[...] = keep_ref[...] + got_ref[...].astype(F32)
    size = sum_ref.shape[0] // 8
    for k in range(8):
        first = pl.multiple_of((sc_ref[0] ^ k) * size, size)
        o_refs[k][...] = sum_ref[pl.ds(first, size), :].astype(BF16)


def spread_call(sc, keep, got):
    rows, w = keep.shape
    part = w // 2
    tile = spec((rows, part), lambda i: (0, i))
    return pl.pallas_call(
        spread_body,
        grid=(2,),
        in_specs=[SMEM_SPEC, tile, tile],
        out_specs=[spec((rows // 8, part), lambda i: (0, i))] * 8,
        out_shape=[shape((rows // 8, w), BF16)] * 8,
        scratch_shapes=[pltpu.VMEM((rows, part), F32)],
        name="spread",
        **params((rows * w, 8 * rows * w)),
    )(sc, keep, got)


def add_up(got):
    return jnp.sum(got.astype(F32), axis=0)


def scatter_all(array):
    return lax.psum_scatter(
        array.astype(BF16), ALL_AXES, scatter_dimension=0, tiled=True
    ).astype(F32)


def per_device(
    hidden_in, cotangent, gate_residual, routes, groups, lengths, attn_gain, qkv_weight, out_weight,
    ffn_gain, router_weight, const_proj, const_vec, gate_weight, up_weight, down_weight,
):
    del groups
    r = hidden_in.shape[0]
    t = 2 * r
    capacity = r // 2
    owners = lax.axis_size("expert")
    copies = owners // EXPERTS
    slots = EXPERTS * capacity
    me = lax.axis_index("expert")
    per_cont = max(CONT_LEN // r, 1)

    small = jnp.concatenate(
        [
            router_weight, const_proj, const_vec, attn_gain[:, None], ffn_gain[:, None],
            jnp.zeros((attn_gain.shape[0], LANES - 20), BF16),
        ],
        axis=1,
    )
    pack = lax.all_gather(
        jnp.concatenate([qkv_weight, out_weight, small], axis=1), ALL_AXES, axis=0, tiled=True
    )
    index = jnp.arange(r, dtype=jnp.int32)
    row_ids = me * r + index
    position = jnp.concatenate([row_ids, PROMPT + row_ids % CONT_LEN]).astype(F32)
    cosine, sine = rotation_tables(position)
    cont = (me * r) // CONT_LEN
    length = lax.dynamic_slice(lengths, (cont,), (1,))
    header = jnp.stack([me, (me * r) % CONT_LEN]).astype(jnp.int32)
    header = jnp.concatenate([header, length.astype(jnp.int32)])
    ring = owners == 8
    if ring:
        ids = lax.dynamic_index_in_dim(jnp.asarray(ring_offsets(), jnp.int32), me, 0, keepdims=False)
    else:
        ids = jnp.arange(owners, dtype=jnp.int32)
    sc = jnp.concatenate([header, ids, (lax.axis_index("dp") % 2).astype(jnp.int32)[None]])

    picked = to_rows(routes)
    flat = jnp.transpose(picked).reshape(2 * t)
    hot = flat[:, None] == jnp.arange(EXPERTS, dtype=jnp.int32)[None, :]
    earlier = jnp.arange(2 * t)[:, None] > jnp.arange(2 * t)[None, :]
    before = jnp.dot(earlier.astype(BF16), hot.astype(BF16), preferred_element_type=F32)
    slot_index = jnp.sum(jnp.where(hot, before, 0.0), axis=1).astype(jnp.int32)
    target = jnp.where(flat < EXPERTS, flat * capacity + slot_index, -1)
    target_rows = target.reshape(2, t)
    target_cols = jnp.transpose(target_rows)

    def to_owners(rows):
        w = rows.shape[-1]
        shaped = rows.reshape(EXPERTS, 1, capacity, w)
        return jnp.broadcast_to(shaped, (EXPERTS, copies, capacity, w)).reshape(owners, capacity, w)

    def exchange(rows):
        got = lax.all_to_all(rows, "expert", split_axis=0, concat_axis=0, tiled=True)
        return got.reshape(owners * got.shape[1], got.shape[2])

    def from_owners(rows):
        got = exchange(rows.reshape(owners, capacity, D))
        if copies == 1:
            return got
        got = got.reshape(EXPERTS, copies, capacity, D).astype(F32)
        return jnp.sum(got, axis=1).reshape(slots, D).astype(BF16)

    x = to_rows(hidden_in)
    g = to_rows(cotangent)
    small_w = pack[:, 4 * D :]
    small_rows = jnp.transpose(small_w[:, 16:24]).astype(F32)
    gain_one = small_rows[2:3]
    rows_two = jnp.concatenate([small_rows[0:2], small_rows[3:4], small_rows[3:8]], axis=0)
    gain_two = small_rows[3:4]

    low_one, q, q_t, kv_prompt, kv_cont = qkv_call(x, gain_one, pack, cosine, sine)
    if not ring:
        kv_all = lax.all_gather(kv_prompt, "expert", axis=0, tiled=True)
    if per_cont == 1:
        kv_own = kv_cont
    else:
        cont_groups = [
            [c * per_cont + i for i in range(per_cont)] for c in range(owners // per_cont)
        ]
        kv_own = lax.all_gather(
            kv_cont, "expert", axis=0, tiled=True, axis_index_groups=cont_groups
        )
    weights = lax.all_gather(
        jnp.stack([gate_weight, up_weight, down_weight]), "dp", axis=0, tiled=False
    )
    if ring:
        right, left = [kv_prompt], [kv_prompt]
        for i in range(3):
            right.append(along_ring(right[i], 1))
            left.append(along_ring(left[i], -1))
            if i == 0:
                st, acc = fwd_local(sc, q_t, kv_prompt, kv_own)
            else:
                st, acc = fwd_remote(sc, q_t, (right[i], left[i]), (8 - i, i), st, acc)
            right[i + 1], left[i + 1], st = tie(right[i + 1], left[i + 1], st)
        far = [along_ring(right[3][:, :D], 1), along_ring(left[3][:, D:], -1)]
        st, acc = fwd_remote(sc, q_t, (right[3], left[3]), (5, 3), st, acc)
        st, att_t, att = fwd_remote(sc, q_t, far, (4,), st, acc, halves=True, final=True)
    else:
        st, acc = fwd_local(sc, q_t, kv_prompt, kv_own)
        st, att_t, att = fwd_remote(sc, q_t, (kv_all,), range(owners), st, acc, final=True)

    res = jnp.pad(to_rows(gate_residual), ((0, 0), (0, LANES - EXPERTS - 4)))
    hidden, low_two, pr, x_send = route_call(
        x, att, pack, gain_two, res, picked, target_rows, slots
    )
    x_got = exchange(to_owners(x_send))
    g_send = grad_rows_call(g, pr, target_rows, slots)
    low_one_t = turn(low_one)
    x_got, g_send = tie(x_got, g_send)
    g_got = exchange(to_owners(g_send))
    gate_pre, up_pre, *expert_rows = expert_fwd(sc, x_got, weights, 8 if ring else 1)
    if ring:
        out_back = swap_blocks(expert_rows)
        mix_target = jnp.where(flat < EXPERTS, (flat ^ me) * capacity + slot_index, -1)
        mix_cols = jnp.transpose(mix_target.reshape(2, t))
    else:
        out_back = [from_owners(expert_rows[0])]
        mix_cols = target_cols
    grad_in, act, d_gate, d_up = expert_in(gate_pre, up_pre, g_got, weights)
    in_back = from_owners(grad_in)
    output, gn, grad_logits, grad_small = mix_call(
        hidden, g, pr, picked, mix_cols, out_back, low_two, pack, rows_two
    )
    act, gn = tie(act, gn)
    grad_w = expert_weights(x_got, g_got, act, d_gate, d_up, weights.shape)
    grad_expert = lax.psum_scatter(
        grad_w.reshape(-1, grad_w.shape[-1]), "dp", scatter_dimension=0, tiled=True
    )
    per = gate_weight.shape[0]
    grad_expert = [grad_expert[i * per : (i + 1) * per].astype(F32) for i in range(3)]
    gh, d_att, d_att_t, grad_ow, gg_two = norm_back_call(
        hidden, g, gn, target_cols, in_back, rows_two, pack, att_t
    )

    early = jnp.concatenate(
        [grad_ow, grad_small[:, :19], jnp.transpose(gg_two[0:1]), jnp.zeros((D, LANES - 20), F32)],
        axis=1,
    )
    back = (sc, q_t, q, d_att_t, d_att)
    if ring:
        parts = early.reshape(2, 2, D // 4, D + LANES)
        core = lax.axis_index("dp") % 2
        early_keep = lax.dynamic_index_in_dim(parts, core, 1, keepdims=False)
        early_got = swap_core(
            lax.dynamic_index_in_dim(parts, 1 - core, 1, keepdims=False).astype(BF16)
        )
        dq_t, send_r, send_l, st = bwd_remote(
            *back, st, att_t, far, (4,), halves=True, first=True, dtype=BF16
        )
        for i in range(3, 0, -1):
            got_r, got_l = along_ring(send_r, 1), along_ring(send_l, -1)
            dq_t, part_r, part_l = bwd_remote(
                *back, st, dq_t, (left[i], right[i]), (i, 8 - i), dtype=BF16
            )
            got_r, got_l, part_r, part_l, dq_t, early_got = tie(
                got_r, got_l, part_r, part_l, dq_t, early_got
            )
            send_r, send_l = ring_add(part_r, got_r, part_l, got_l)
            if i == 3:
                early_keep, early_got = add_and_cross(early_keep, early_got)
        send_r, send_l, dq_t = tie(send_r, send_l, dq_t)
        got_r = along_ring(send_r, 1)
        got_l = along_ring(send_l, -1)
        got = (got_r, got_l)
        dq, dkv_own, dkv_cont = bwd_local(*back, st, dq_t, kv_prompt, kv_own)
    else:
        dq_t, dkv_all, st = bwd_remote(
            *back, st, att_t, (kv_all,), range(owners), first=True, dtype=BF16
        )
        dq, dkv_own, dkv_cont = bwd_local(*back, st, dq_t, kv_prompt, kv_own)
        got = (lax.psum_scatter(dkv_all, "expert", scatter_dimension=0, tiled=True),)
        early = scatter_all(early)
    if per_cont > 1:
        dkv_cont = lax.psum_scatter(
            dkv_cont, "expert", scatter_dimension=0, tiled=True, axis_index_groups=cont_groups
        )
    gn_q, *grad_q = q_back_call(sc, low_one_t, dq, cosine, sine, pack, ring)
    if ring:
        got_q = swap_core(grad_q[0])
        keep_q, got_q = add_and_cross(grad_q[1], got_q)
        keep_q, *got = tie(keep_q, *got)
    grad_input, *grad_kv = kv_back_call(
        sc, x, low_one_t, gn_q, gh, gain_one, cosine, sine, pack, dkv_own, dkv_cont, got, ring
    )
    output, grad_input = from_rows(output), from_rows(grad_input)
    if ring:
        got_kv = swap_core(grad_kv[0])
        keep_kv, got_kv = add_and_cross(grad_kv[1], got_kv)
        keep_kv, got_q, early_got = tie(keep_kv, got_q, early_got)
        got_q = add_and_scatter(
            jnp.concatenate([early_keep, keep_q], axis=1),
            jnp.concatenate([early_got, got_q], axis=1),
        )
        got_kv, output, grad_input, *grad_expert = tie(got_kv, output, grad_input, *grad_expert)
        summed = add_up(got_q)
        early, late_q = summed[:, : D + LANES], summed[:, D + LANES :]
        blocks = swap_blocks(spread_call(sc, keep_kv, got_kv))
        late_kv = blocks[0].astype(F32)
        for block in blocks[1:]:
            late_kv = late_kv + block.astype(F32)
    else:
        late_q, late_kv = scatter_all(grad_q[0]), scatter_all(grad_kv[0])
    per = late_kv.shape[0]
    late_kv = jnp.transpose(late_kv.reshape(per, PAIRS, 2, LANES), (0, 2, 1, 3))
    late = jnp.concatenate([late_q, late_kv.reshape(per, 2 * D)], axis=1)
    grad_gain = jnp.sum(late * qkv_weight.astype(F32), axis=1) / attn_gain.astype(F32)
    tail = early[:, D:]
    return (
        output,
        grad_input,
        from_rows(grad_logits)[:, :, : EXPERTS + 4],
        grad_gain,
        late,
        early[:, :D],
        tail[:, 19],
        tail[:, :12],
        tail[:, 12:16],
        tail[:, 16:18],
        grad_expert[0],
        grad_expert[1],
        grad_expert[2],
    )


def solution(mesh):
    rows = P(ALL_AXES, None, None)
    flat = P(ALL_AXES)
    mat = P(ALL_AXES, None)
    expert = P("dp", "expert")
    in_specs = (
        rows, rows, rows, rows, P("dp"), P("dp"), flat, mat, mat, flat, mat, mat, mat,
        expert, expert, expert,
    )
    out_specs = (
        rows, rows, rows, flat, mat, mat, flat, mat, mat, mat, expert, expert, expert,
    )

    return jax.shard_map(
        per_device, mesh=mesh, in_specs=in_specs, out_specs=out_specs, check_vma=False
    )
```

```python
import functools

import jax
import jax.numpy as jnp
from jax import lax
from jax.experimental import pallas as pl
from jax.experimental.pallas import tpu as pltpu
from jax.sharding import PartitionSpec as P


D = 768
HEAD_DIM = 64
PAIRS = 6
EXPERTS = 8
CONT_LEN = 256
PROMPT = 2048
LANES = 128
EPS = 1e-06
NEG = -1e30
LOG2E = 1.4426950408889634
SCALE = float(HEAD_DIM) ** (-0.5)
LC = SCALE * LOG2E
F32 = jnp.float32
BF16 = jnp.bfloat16
ALL_AXES = ("dp", "expert")
VMEM_SMALL = 24 * 1024 * 1024
VMEM_LARGE = 44 * 1024 * 1024


def dot(a, b):
    return jnp.dot(a, b, preferred_element_type=F32)


def dot_nt(a, b):
    return lax.dot_general(a, b, (((1,), (1,)), ((), ())), preferred_element_type=F32)


def split_hi_lo(v):
    hi = v.astype(BF16)
    return hi, (v - hi.astype(F32)).astype(BF16)


def params(cost=None, limit=VMEM_SMALL):
    return dict(
        compiler_params=pltpu.CompilerParams(vmem_limit_bytes=limit),
        cost_estimate=None if cost is None else pl.CostEstimate(
            flops=int(cost[0]), bytes_accessed=int(cost[1]), transcendentals=0
        ),
    )


def shape(dims, dtype):
    return jax.ShapeDtypeStruct(tuple(dims), dtype)


def spec(block, index):
    return pl.BlockSpec(tuple(block), index)


def whole(dims):
    return pl.BlockSpec(tuple(dims), lambda *_: (0,) * len(dims))


SMEM_SPEC = pl.BlockSpec(memory_space=pltpu.SMEM)


def partner(v):
    lane = lax.broadcasted_iota(jnp.int32, v.shape, 1)
    return jnp.where((lane & 63) < 32, pltpu.roll(v, 96, 1), pltpu.roll(v, 32, 1))


def qkv_body(x_ref, gain_ref, wq_ref, wk_ref, wv_ref, c_ref, s_ref, n_ref, q_ref, qt_ref, kvp_ref, kvc_ref):
    @pl.when(pl.program_id(0) == 0)
    def _():
        x = x_ref[...].astype(F32)
        scale = lax.rsqrt(jnp.mean(x * x, axis=-1, keepdims=True) + EPS)
        n_ref[...] = (x * scale * gain_ref[...]).astype(BF16)

    n = n_ref[...]
    cosine = c_ref[...]
    sine = s_ref[...]
    kv = dot(n, jnp.concatenate([wk_ref[...], wv_ref[...]], axis=1))
    k = kv[:, :LANES]
    k = (k * cosine + partner(k) * sine).astype(BF16)
    v = kv[:, LANES:].astype(BF16)
    r = k.shape[0] // 2
    kvp_ref[:, :LANES] = k[:r]
    kvp_ref[:, LANES:] = v[:r]
    kvc_ref[:, :LANES] = k[r:]
    kvc_ref[:, LANES:] = v[r:]
    q = dot(n, wq_ref[...])
    q = q * cosine + partner(q) * sine
    q = q.astype(BF16)
    q_ref[...] = q
    qt_ref[...] = q.T


def qkv_call(x, gain, pack, cosine, sine):
    t = x.shape[0]
    return pl.pallas_call(
        qkv_body,
        grid=(PAIRS,),
        in_specs=[
            whole((t, D)),
            whole((1, D)),
            spec((D, LANES), lambda i: (0, i)),
            spec((D, LANES), lambda i: (0, PAIRS + i)),
            spec((D, LANES), lambda i: (0, 2 * PAIRS + i)),
            whole((t, LANES)),
            whole((t, LANES)),
        ],
        out_specs=[
            whole((t, D)),
            spec((t, LANES), lambda i: (0, i)),
            spec((LANES, t), lambda i: (i, 0)),
            spec((t // 2, 2 * LANES), lambda i: (0, i)),
            spec((t // 2, 2 * LANES), lambda i: (0, i)),
        ],
        out_shape=[
            shape((t, D), BF16),
            shape((t, D), BF16),
            shape((D, t), BF16),
            shape((t // 2, 2 * D), BF16),
            shape((t // 2, 2 * D), BF16),
        ],
        name="qkv_rope",
        **params((2 * t * D * 3 * D, 6 * D * D)),
    )(x, gain, pack, pack, pack, cosine, sine)


def head_rows(v, h):
    row = lax.broadcasted_iota(jnp.int32, v.shape, 0)
    return jnp.where(row // HEAD_DIM == h, v, jnp.zeros_like(v))


def head_lanes(v, h):
    lane = lax.broadcasted_iota(jnp.int32, v.shape, 1)
    return jnp.where(lane // HEAD_DIM == h, v, jnp.zeros_like(v))


def attend_update(qz, kb, vt, lo, hi, mask, st_ref, a_ref, first):
    for h in range(2):
        s = dot(kb, qz[h][:, lo:hi])
        if mask is not None:
            s = jnp.where(mask, s, NEG)
        top = jnp.max(s, axis=0, keepdims=True)
        rows = slice(h * HEAD_DIM, (h + 1) * HEAD_DIM)
        if first:
            p = jnp.exp2((s - top) * LC)
            st_ref[h : h + 1, lo:hi] = top
            st_ref[2 + h : 3 + h, lo:hi] = jnp.sum(p, axis=0, keepdims=True)
            a_ref[rows, lo:hi] = dot(vt[rows], p.astype(BF16))
        else:
            old = st_ref[h : h + 1, lo:hi]
            new = jnp.maximum(old, top)
            alpha = jnp.exp2((old - new) * LC)
            p = jnp.exp2((s - new) * LC)
            st_ref[h : h + 1, lo:hi] = new
            st_ref[2 + h : 3 + h, lo:hi] = st_ref[2 + h : 3 + h, lo:hi] * alpha + jnp.sum(
                p, axis=0, keepdims=True
            )
            a_ref[rows, lo:hi] = a_ref[rows, lo:hi] * alpha + dot(vt[rows], p.astype(BF16))


def local_masks(sc_ref, r, keys, lo, hi):
    cpos = sc_ref[1]
    length = sc_ref[2]
    col = lo + lax.broadcasted_iota(jnp.int32, (r, hi - lo), 1)
    row = lax.broadcasted_iota(jnp.int32, (r, hi - lo), 0)
    own = (row <= col) | (col >= r)
    col = lo + lax.broadcasted_iota(jnp.int32, (keys, hi - lo), 1)
    row = lax.broadcasted_iota(jnp.int32, (keys, hi - lo), 0)
    cont = (col >= r) & (row <= cpos + col - r) & (row < length)
    return own, cont


def fwd_local_body(sc_ref, qt_ref, kv_ref, kvo_ref, st_ref, a_ref):
    t = qt_ref.shape[1]
    r = t // 2
    keys = kvo_ref.shape[0]
    qt = qt_ref[...]
    qz = [head_rows(qt, h) for h in range(2)]
    kb = kv_ref[:, :LANES]
    vt = kv_ref[:, LANES:].T
    kbo = kvo_ref[:, :LANES]
    vto = kvo_ref[:, LANES:].T
    st_ref[...] = jnp.zeros_like(st_ref)
    own, cont = local_masks(sc_ref, r, keys, 0, t)
    attend_update(qz, kb, vt, 0, t, own, st_ref, a_ref, True)
    if r % LANES == 0:
        attend_update(qz, kbo, vto, r, t, cont[:, r:], st_ref, a_ref, False)
    else:
        attend_update(qz, kbo, vto, 0, t, cont, st_ref, a_ref, False)


def halves_value(a_ref, b_ref):
    return jnp.where(pl.program_id(0) < PAIRS // 2, a_ref[...], b_ref[...])


def fwd_remote_body(offsets, count, halves, final, sc_ref, qt_ref, *refs):
    kv_refs, refs = refs[:count], refs[count:]
    st_in, a_in, st_ref, a_ref = refs[:4]
    t = qt_ref.shape[1]
    r = t // 2
    me = sc_ref[0]
    qt = qt_ref[...]
    qz = [head_rows(qt, h) for h in range(2)]
    st_ref[...] = st_in[...]
    a_ref[...] = a_in[...]
    for j, offset in enumerate(offsets):
        block = sc_ref[3 + offset]

        def go(lo, hi, mask):
            if halves:
                kv = halves_value(*kv_refs)
            elif len(kv_refs) == len(offsets):
                kv = kv_refs[j][...]
            else:
                kv = kv_refs[0][j * r : (j + 1) * r, :]
            attend_update(qz, kv[:, :LANES], kv[:, LANES:].T, lo, hi, mask, st_ref, a_ref, False)

        if r % LANES == 0:

            @pl.when(block < me)
            def _():
                go(0, t, None)

            @pl.when(block > me)
            def _():
                go(r, t, None)

        else:

            @pl.when(block != me)
            def _():
                col = lax.broadcasted_iota(jnp.int32, (r, t), 1)
                go(0, t, (col >= r) | (block < me))

    if final:
        low_ref = refs[4]
        for h in range(2):
            rows = slice(h * HEAD_DIM, (h + 1) * HEAD_DIM)
            total = st_ref[2 + h : 3 + h, :]
            a_ref[rows, :] = a_ref[rows, :] / total
            st_ref[h : h + 1, :] = st_ref[h : h + 1, :] * LC + jnp.log2(total)
        low_ref[...] = a_ref[...].astype(BF16).T


def kv_specs(kvs, halves):
    if halves:
        r = kvs[0].shape[0]
        return [
            spec((r, 2 * LANES), lambda i: (0, jnp.minimum(i, PAIRS // 2 - 1))),
            spec((r, 2 * LANES), lambda i: (0, jnp.maximum(i - PAIRS // 2, 0))),
        ]
    return [spec((kv.shape[0], 2 * LANES), lambda i: (0, i)) for kv in kvs]


def fwd_local(sc, qt, kv_prompt, kv_own):
    t = qt.shape[1]
    keys = kv_own.shape[0]
    return pl.pallas_call(
        fwd_local_body,
        grid=(PAIRS,),
        in_specs=[
            SMEM_SPEC,
            spec((LANES, t), lambda i: (i, 0)),
            spec((t // 2, 2 * LANES), lambda i: (0, i)),
            spec((keys, 2 * LANES), lambda i: (0, i)),
        ],
        out_specs=[spec((8, t), lambda i: (i, 0)), spec((LANES, t), lambda i: (i, 0))],
        out_shape=[shape((8 * PAIRS, t), F32), shape((D, t), F32)],
        name="attend_local",
        **params((4 * 4 * t * keys * D, 4 * D * t)),
    )(sc, qt, kv_prompt, kv_own)


def fwd_remote(sc, qt, kvs, offsets, st, acc, halves=False, final=False):
    t = qt.shape[1]
    rows = len(offsets) * (t // 2)
    out_specs = [spec((8, t), lambda i: (i, 0)), spec((LANES, t), lambda i: (i, 0))]
    out_shape = [shape((8 * PAIRS, t), F32), shape((D, t), F32)]
    if final:
        out_specs.append(spec((t, LANES), lambda i: (0, i)))
        out_shape.append(shape((t, D), BF16))
    return pl.pallas_call(
        functools.partial(fwd_remote_body, tuple(offsets), len(kvs), halves, final),
        grid=(PAIRS,),
        in_specs=[SMEM_SPEC, spec((LANES, t), lambda i: (i, 0))]
        + kv_specs(kvs, halves)
        + [spec((8, t), lambda i: (i, 0)), spec((LANES, t), lambda i: (i, 0))],
        out_specs=out_specs,
        out_shape=out_shape,
        name="attend_remote",
        **params((4 * 4 * t * rows * D, 8 * D * t + 4 * D * rows)),
    )(sc, qt, *kvs, st, acc)


def back_block(ops, kb, vb, kt, lo, hi, mask, dq_ref):
    qz, qn, doz, don, lse, delta = ops
    dk = None
    dv = None
    for h in range(2):
        s = dot(kb, qz[h][:, lo:hi])
        dp = dot(vb, doz[h][:, lo:hi])
        p = jnp.exp2(s * LC - lse[h][:, lo:hi])
        if mask is not None:
            p = jnp.where(mask, p, 0.0)
        ds = (p * (dp - delta[h][:, lo:hi])).astype(BF16)
        dv_h = dot(p.astype(BF16), don[h][lo:hi])
        dk_h = dot(ds, qn[h][lo:hi])
        rows = slice(h * HEAD_DIM, (h + 1) * HEAD_DIM)
        dq_ref[rows, lo:hi] += dot(kt[rows], ds)
        dv = dv_h if dv is None else dv + dv_h
        dk = dk_h if dk is None else dk + dk_h
    return dk, dv


def back_operands(qt_ref, q_ref, dot_ref, do_ref, st_ref):
    qt, q, do_t, do = qt_ref[...], q_ref[...], dot_ref[...], do_ref[...]
    return (
        [head_rows(qt, h) for h in range(2)],
        [head_lanes(q, h) for h in range(2)],
        [head_rows(do_t, h) for h in range(2)],
        [head_lanes(do, h) for h in range(2)],
        [st_ref[h : h + 1, :] for h in range(2)],
        [st_ref[4 + h : 5 + h, :] for h in range(2)],
    )


def bwd_local_body(
    sc_ref, qt_ref, q_ref, dot_ref, do_ref, st_ref, dq_in, kv_ref, kvo_ref,
    out_ref, dkv_ref, dkvo_ref, dq_ref,
):
    t = qt_ref.shape[1]
    r = t // 2
    keys = kvo_ref.shape[0]
    ops = back_operands(qt_ref, q_ref, dot_ref, do_ref, st_ref)
    dq_ref[...] = dq_in[...]
    kb, vb = kv_ref[:, :LANES], kv_ref[:, LANES:]
    kbo, vbo = kvo_ref[:, :LANES], kvo_ref[:, LANES:]
    kt, kto = kb.T, kbo.T
    own, cont = local_masks(sc_ref, r, keys, 0, t)
    dk, dv = back_block(ops, kb, vb, kt, 0, t, own, dq_ref)
    if r % LANES == 0:
        dko, dvo = back_block(ops, kbo, vbo, kto, r, t, cont[:, r:], dq_ref)
    else:
        dko, dvo = back_block(ops, kbo, vbo, kto, 0, t, cont, dq_ref)
    dkv_ref[:, :LANES] = dk * SCALE
    dkv_ref[:, LANES:] = dv
    dkvo_ref[:, :LANES] = dko * SCALE
    dkvo_ref[:, LANES:] = dvo
    out_ref[...] = dq_ref[...].T * SCALE


def bwd_remote_body(
    offsets, count, halves, first, dtype, sc_ref, qt_ref, q_ref, dot_ref, do_ref, st_in, *refs
):
    t = qt_ref.shape[1]
    r = t // 2
    me = sc_ref[0]
    kv_refs, refs = refs[:count], refs[count:]
    src, refs = refs[0], refs[1:]
    dq_ref, refs = refs[0], refs[1:]
    out_refs, refs = refs[:count], refs[count:]
    if first:
        st_ref, refs = refs[0], refs[1:]
        st_ref[...] = st_in[...]
        prod = src[...] * dot_ref[...].astype(F32)
        for h in range(2):
            st_ref[4 + h : 5 + h, :] = jnp.sum(
                prod[h * HEAD_DIM : (h + 1) * HEAD_DIM], axis=0, keepdims=True
            )
        dq_ref[...] = jnp.zeros_like(dq_ref)
    else:
        st_ref = st_in
        dq_ref[...] = src[...]
    ops = back_operands(qt_ref, q_ref, dot_ref, do_ref, st_ref)
    split = len(offsets) != count and not halves

    def store(j, dk, dv):
        if halves:
            for part in range(2):

                @pl.when((pl.program_id(0) < PAIRS // 2) == (part == 0))
                def _():
                    out_refs[part][:, :LANES] = dk
                    out_refs[part][:, LANES:] = dv

        elif split:
            out_refs[0][j * r : (j + 1) * r, :LANES] = dk
            out_refs[0][j * r : (j + 1) * r, LANES:] = dv
        else:
            out_refs[j][:, :LANES] = dk
            out_refs[j][:, LANES:] = dv

    for j, offset in enumerate(offsets):
        block = sc_ref[3 + offset]

        def go(lo, mask):
            if halves:
                kv = halves_value(*kv_refs)
            elif split:
                kv = kv_refs[0][j * r : (j + 1) * r, :]
            else:
                kv = kv_refs[j][...]
            kb = kv[:, :LANES]
            dk, dv = back_block(ops, kb, kv[:, LANES:], kb.T, lo, t, mask, dq_ref)
            store(j, (dk * SCALE).astype(dtype), dv.astype(dtype))

        if split:

            @pl.when(block == me)
            def _():
                zero = jnp.zeros((r, LANES), dtype)
                store(j, zero, zero)

        if r % LANES == 0:

            @pl.when(block < me)
            def _():
                go(0, None)

            @pl.when(block > me)
            def _():
                go(r, None)

        else:

            @pl.when(block != me)
            def _():
                col = lax.broadcasted_iota(jnp.int32, (r, t), 1)
                go(0, (col >= r) | (block < me))


def add_low(a, b):
    return (a.astype(F32) + b.astype(F32)).astype(BF16)


def ring_add_body(half, pr_ref, gr_ref, pl_ref, gl_ref, sr_ref, sl_ref):
    if not half:
        sr_ref[...] = add_low(pr_ref[...], gr_ref[...])
        sl_ref[...] = add_low(pl_ref[...], gl_ref[...])
        return
    sr_ref[:, :D] = add_low(pr_ref[:, :D], gr_ref[...])
    sr_ref[:, D:] = pr_ref[:, D:]
    sl_ref[:, :D] = pl_ref[:, :D]
    sl_ref[:, D:] = add_low(pl_ref[:, D:], gl_ref[...])


def ring_add(part_r, got_r, part_l, got_l):
    r = part_r.shape[0]
    part = r // 2
    half = got_r.shape[1] == D
    wide = spec((part, 2 * D), lambda i: (i, 0))
    got = spec((part, got_r.shape[1]), lambda i: (i, 0))
    return pl.pallas_call(
        functools.partial(ring_add_body, half),
        grid=(2,),
        in_specs=[wide, got, wide, got],
        out_specs=[wide, wide],
        out_shape=[shape((r, 2 * D), BF16)] * 2,
        name="ring_add",
        **params((4 * r * D, 16 * r * D)),
    )(part_r, got_r, part_l, got_l)


def q_specs(t):
    return [
        spec((LANES, t), lambda i: (i, 0)),
        spec((t, LANES), lambda i: (0, i)),
        spec((LANES, t), lambda i: (i, 0)),
        spec((t, LANES), lambda i: (0, i)),
        spec((8, t), lambda i: (i, 0)),
    ]


def bwd_local(sc, qt, q, do_t, do, st, dq, kv_prompt, kv_own):
    t = qt.shape[1]
    keys = kv_own.shape[0]
    return pl.pallas_call(
        bwd_local_body,
        grid=(PAIRS,),
        in_specs=[SMEM_SPEC]
        + q_specs(t)
        + [spec((LANES, t), lambda i: (i, 0))]
        + kv_specs((kv_prompt, kv_own), False),
        out_specs=[spec((t, LANES), lambda i: (0, i))] + kv_specs((kv_prompt, kv_own), False),
        out_shape=[
            shape((t, D), F32),
            shape((t // 2, 2 * D), F32),
            shape((keys, 2 * D), F32),
        ],
        scratch_shapes=[pltpu.VMEM((LANES, t), F32)],
        name="attend_back_local",
        **params((10 * 4 * t * keys * D, 16 * D * t)),
    )(sc, qt, q, do_t, do, st, dq, kv_prompt, kv_own)


def bwd_remote(
    sc, qt, q, do_t, do, st, src, kvs, offsets, halves=False, first=False, dtype=F32
):
    t = qt.shape[1]
    rows = len(offsets) * (t // 2)
    out_specs = [spec((LANES, t), lambda i: (i, 0))] + kv_specs(kvs, halves)
    out_shape = [shape((D, t), F32)] + [shape(kv.shape, dtype) for kv in kvs]
    if first:
        out_specs.append(spec((8, t), lambda i: (i, 0)))
        out_shape.append(shape((8 * PAIRS, t), F32))
    return pl.pallas_call(
        functools.partial(bwd_remote_body, tuple(offsets), len(kvs), halves, first, dtype),
        grid=(PAIRS,),
        in_specs=[SMEM_SPEC]
        + q_specs(t)
        + kv_specs(kvs, halves)
        + [spec((LANES, t), lambda i: (i, 0))],
        out_specs=out_specs,
        out_shape=out_shape,
        name="attend_back_remote",
        **params((10 * 4 * t * rows * D, 16 * D * t + 8 * D * rows)),
    )(sc, qt, q, do_t, do, st, *kvs, src)


def route_body(
    x_ref, att_ref, ow_ref, sw_ref, gain_ref, res_ref, rt_ref, tr_ref,
    h_ref, n_ref, pr_ref, xs_ref,
):
    t = x_ref.shape[0]
    step = pl.program_id(0)

    @pl.when(step == 0)
    def _():
        hidden = x_ref[...].astype(F32) + dot(att_ref[...], ow_ref[...])
        h_ref[...] = hidden
        scale = lax.rsqrt(jnp.mean(hidden * hidden, axis=-1, keepdims=True) + EPS)
        low = (hidden * scale * gain_ref[...]).astype(BF16)
        n_ref[...] = low
        z = dot(low, sw_ref[...])
        lane = lax.broadcasted_iota(jnp.int32, (t, LANES), 1)
        is_route = lane < EXPERTS + 4
        logits = jnp.where(is_route, z + res_ref[...], NEG)
        ex = jnp.exp(logits - jnp.max(logits, axis=-1, keepdims=True))
        probs = ex / jnp.sum(ex, axis=-1, keepdims=True)
        out = probs
        first = EXPERTS + 4
        for k in range(2):
            l0 = z[:, first + 2 * k : first + 2 * k + 1]
            l1 = z[:, first + 2 * k + 1 : first + 2 * k + 2]
            top = jnp.maximum(l0, l1)
            e0 = jnp.exp(l0 - top)
            e1 = jnp.exp(l1 - top)
            den = e0 + e1
            out = jnp.where(lane == first + 2 * k, e0 / den, out)
            out = jnp.where(lane == first + 2 * k + 1, e1 / den, out)
        for j in range(2):
            mix = jnp.sum(jnp.where(lane == rt_ref[:, j : j + 1], probs, 0.0), axis=-1, keepdims=True)
            out = jnp.where(lane == 16 + j, mix, out)
        pr_ref[...] = out

    slots = xs_ref.shape[0]
    base = step * slots
    slot = base + lax.broadcasted_iota(jnp.int32, (slots, t), 0)
    pick = (slot == tr_ref[0:1, :]) | (slot == tr_ref[1:2, :])
    xs_ref[...] = dot(pick.astype(BF16), n_ref[...]).astype(BF16)


def out_w_spec():
    return spec((D, D), lambda *_: (0, 3))


def small_w_spec():
    return spec((D, LANES), lambda *_: (0, 4 * D // LANES))


def grad_rows_body(g_ref, pr_ref, tr_ref, gs_ref, mg_ref):
    t = g_ref.shape[0]
    step = pl.program_id(0)

    @pl.when(step == 0)
    def _():
        g = g_ref[...].astype(F32)
        for j in range(2):
            mg_ref[j * t : (j + 1) * t, :] = (g * pr_ref[:, 16 + j : 17 + j]).astype(BF16)

    slots = gs_ref.shape[0]
    slot = step * slots + lax.broadcasted_iota(jnp.int32, (slots, t), 0)
    picks = [(slot == tr_ref[j : j + 1, :]).astype(BF16) for j in range(2)]
    gs_ref[...] = dot(jnp.concatenate(picks, axis=1), mg_ref[...]).astype(BF16)


def grad_rows_call(g, pr, tr, slots):
    t = g.shape[0]
    part = min(slots, 256)
    return pl.pallas_call(
        grad_rows_body,
        grid=(slots // part,),
        in_specs=[whole((t, D)), whole((t, LANES)), whole((2, t))],
        out_specs=spec((part, D), lambda i: (i, 0)),
        out_shape=shape((slots, D), BF16),
        scratch_shapes=[pltpu.VMEM((2 * t, D), BF16)],
        name="grad_rows",
        **params((4 * slots * t * D, 4 * t * D)),
    )(g, pr, tr)


def route_call(x, att, pack, gain, res, rt, tr, slots):
    t = x.shape[0]
    part = min(slots, 256)
    return pl.pallas_call(
        route_body,
        grid=(slots // part,),
        in_specs=[
            whole((t, D)), whole((t, D)), out_w_spec(), small_w_spec(), whole((1, D)),
            whole((t, LANES)), whole((t, 2)), whole((2, t)),
        ],
        out_specs=[
            whole((t, D)), whole((t, D)), whole((t, LANES)),
            spec((part, D), lambda i: (i, 0)),
        ],
        out_shape=[
            shape((t, D), F32), shape((t, D), BF16), shape((t, LANES), F32),
            shape((slots, D), BF16),
        ],
        name="route_dispatch",
        **params((2 * t * D * D + 2 * slots * t * D, 8 * t * D)),
    )(x, att, pack, pack, gain, res, rt, tr)


def expert_fwd_body(x_ref, w_ref, o_ref, gate_ref, up_ref, acc_ref):
    step = pl.program_id(0)
    x = x_ref[...]
    wide = w_ref.shape[-1]
    wg = w_ref[:, 0].reshape(D, wide)
    wu = w_ref[:, 1].reshape(D, wide)
    wd = w_ref[:, 2].reshape(D, wide)
    gate = dot(x, wg)
    up = dot(x, wu)
    gate_ref[...] = gate
    up_ref[...] = up
    act = (gate / (1.0 + jnp.exp(-gate)) * up).astype(BF16)
    out = dot_nt(act, wd)

    @pl.when(step == 0)
    def _():
        acc_ref[...] = out

    @pl.when(step > 0)
    def _():
        acc_ref[...] += out

    @pl.when(step == pl.num_programs(0) - 1)
    def _():
        o_ref[...] = acc_ref[...].astype(BF16)


def expert_fwd(xr, w):
    rows = xr.shape[0]
    shards, _, per, wide = w.shape
    part = min(wide, 256)
    return pl.pallas_call(
        expert_fwd_body,
        grid=(wide // part,),
        in_specs=[whole((rows, D)), spec((shards, 3, per, part), lambda i: (0, 0, 0, i))],
        out_specs=[whole((rows, D))] + [spec((rows, part), lambda i: (0, i))] * 2,
        out_shape=[shape((rows, D), BF16)] + [shape((rows, wide), F32)] * 2,
        scratch_shapes=[pltpu.VMEM((rows, D), F32)],
        name="expert_forward",
        **params((6 * rows * D * wide, 6 * D * wide), VMEM_LARGE),
    )(xr, w)


def expert_in_body(gate_ref, up_ref, g_ref, w_ref, gi_ref, act_ref, dg_ref, du_ref, acc_ref):
    step = pl.program_id(0)
    wide = w_ref.shape[-1]
    wg = w_ref[:, 0].reshape(D, wide)
    wu = w_ref[:, 1].reshape(D, wide)
    wd = w_ref[:, 2].reshape(D, wide)
    gate = gate_ref[...]
    up = up_ref[...]
    ga = dot(g_ref[...], wd)
    sig = 1.0 / (1.0 + jnp.exp(-gate))
    silu = gate * sig
    act_ref[...] = (silu * up).astype(BF16)
    d_gate = (ga * up * sig * (1.0 + gate * (1.0 - sig))).astype(BF16)
    d_up = (ga * silu).astype(BF16)
    dg_ref[...] = d_gate
    du_ref[...] = d_up
    gi = dot_nt(
        jnp.concatenate([d_gate, d_up], axis=1), jnp.concatenate([wg, wu], axis=1)
    )

    @pl.when(step == 0)
    def _():
        acc_ref[...] = gi

    @pl.when(step > 0)
    def _():
        acc_ref[...] += gi

    @pl.when(step == pl.num_programs(0) - 1)
    def _():
        gi_ref[...] = acc_ref[...].astype(BF16)


def expert_in(gate, up, gr, w):
    rows = gr.shape[0]
    shards, _, per, wide = w.shape
    part = min(wide, 256)
    tile = spec((rows, part), lambda i: (0, i))
    return pl.pallas_call(
        expert_in_body,
        grid=(wide // part,),
        in_specs=[tile, tile, whole((rows, D)), spec((shards, 3, per, part), lambda i: (0, 0, 0, i))],
        out_specs=[whole((rows, D)), tile, tile, tile],
        out_shape=[shape((rows, D), BF16)] + [shape((rows, wide), BF16)] * 3,
        scratch_shapes=[pltpu.VMEM((rows, D), F32)],
        name="expert_back_in",
        **params((6 * rows * D * wide, 12 * D * wide), VMEM_LARGE),
    )(gate, up, gr, w)


def expert_weights_body(x_ref, gl_ref, act_ref, dg_ref, du_ref, dw_ref, xt_ref, gt_ref):
    @pl.when(pl.program_id(0) == 0)
    def _():
        gt_ref[...] = gl_ref[...].T
        xt_ref[...] = x_ref[...].T

    shards, _, per, wide = dw_ref.shape
    xt = xt_ref[...]
    dw_ref[:, 0] = dot(xt, dg_ref[...]).astype(BF16).reshape(shards, per, wide)
    dw_ref[:, 1] = dot(xt, du_ref[...]).astype(BF16).reshape(shards, per, wide)
    dw_ref[:, 2] = dot(gt_ref[...], act_ref[...]).astype(BF16).reshape(shards, per, wide)


def expert_weights(xr, low, act, d_gate, d_up, dims):
    rows = xr.shape[0]
    shards, _, per, wide = dims
    part = min(wide, 256)
    tile = spec((rows, part), lambda i: (0, i))
    return pl.pallas_call(
        expert_weights_body,
        grid=(wide // part,),
        in_specs=[whole((rows, D)), whole((rows, D)), tile, tile, tile],
        out_specs=spec((shards, 3, per, part), lambda i: (0, 0, 0, i)),
        out_shape=shape(dims, BF16),
        scratch_shapes=[pltpu.VMEM((D, rows), BF16), pltpu.VMEM((D, rows), BF16)],
        name="expert_weight_grads",
        **params((6 * rows * D * wide, 12 * D * wide), VMEM_LARGE),
    )(xr, low, act, d_gate, d_up)


def mix_body(
    h_ref, g_ref, pr_ref, rt_ref, tc_ref, ret_ref, n_ref, sw_ref, rows_ref,
    out_ref, gn_ref, gl_ref, gs_ref,
):
    t = h_ref.shape[0]
    slots = ret_ref.shape[0]
    hidden = h_ref[...]
    g16 = g_ref[...]
    g = g16.astype(F32)
    pr = pr_ref[...]
    scale = lax.rsqrt(jnp.mean(hidden * hidden, axis=-1, keepdims=True) + EPS)
    normed = hidden * scale * rows_ref[2:3, :]
    lane = lax.broadcasted_iota(jnp.int32, (t, LANES), 1)
    slot = lax.broadcasted_iota(jnp.int32, (t, slots), 1)
    first = EXPERTS + 4
    ret = ret_ref[...]
    c0 = [pr[:, first + 2 * k : first + 2 * k + 1] for k in range(2)]
    c1 = [pr[:, first + 2 * k + 1 : first + 2 * k + 2] for k in range(2)]
    total = hidden
    s = jnp.zeros((t, LANES), F32)
    coef = jnp.zeros((t, 1), F32)
    weight = [jnp.zeros((t, 1), F32) for _ in range(2)]
    for j in range(2):
        route = rt_ref[:, j : j + 1]
        mix = pr[:, 16 + j : 17 + j]
        branch = dot((slot == tc_ref[:, j : j + 1]).astype(BF16), ret)
        keep = jnp.where(route == EXPERTS + 1, 1.0, 0.0)
        for k in range(2):
            here = jnp.where(route == EXPERTS + 2 + k, 1.0, 0.0)
            keep = keep + here * c0[k]
            weight[k] = weight[k] + here * mix
            branch = branch + (here * c1[k]) * rows_ref[k : k + 1, :]
        branch = branch + keep * normed
        coef = coef + mix * keep
        total = total + mix * branch
        gp = jnp.sum(g * branch, axis=-1, keepdims=True)
        s = s + jnp.where(lane == route, gp, 0.0)
    out_ref[...] = total.astype(BF16)
    probs = jnp.where(lane < first, pr, 0.0)
    d_logits = probs * (s - jnp.sum(probs * s, axis=-1, keepdims=True))
    gl_ref[...] = d_logits
    dz = d_logits
    dvec = jnp.zeros((t, LANES), F32)
    g_dot_n = jnp.sum(g * normed, axis=-1, keepdims=True)
    for k in range(2):
        d0 = weight[k] * g_dot_n
        d1 = weight[k] * jnp.sum(g * rows_ref[k : k + 1, :], axis=-1, keepdims=True)
        mean = c0[k] * d0 + c1[k] * d1
        dz = jnp.where(lane == first + 2 * k, c0[k] * (d0 - mean), dz)
        dz = jnp.where(lane == first + 2 * k + 1, c1[k] * (d1 - mean), dz)
        dvec = jnp.where(lane == 16 + k, weight[k] * c1[k], dvec)
    hi, lo = split_hi_lo(dz)
    sw = sw_ref[...]
    gn_ref[...] = coef * g + (dot_nt(hi, sw) + dot_nt(lo, sw))
    nt = n_ref[...].T
    gt = g16.T
    vhi, vlo = split_hi_lo(dvec)
    gs = dot(nt, hi) + dot(nt, lo) + dot(gt, vhi) + dot(gt, vlo)

    @pl.when(pl.program_id(0) == 0)
    def _():
        gs_ref[...] = gs

    @pl.when(pl.program_id(0) > 0)
    def _():
        gs_ref[...] += gs


def mix_call(hidden, g, pr, rt, tc, ret, low, pack, rows):
    t = hidden.shape[0]
    half = min(t, LANES)
    slots = ret.shape[0]
    tile = spec((half, D), lambda i: (i, 0))
    lane_tile = spec((half, LANES), lambda i: (i, 0))
    pair = spec((half, 2), lambda i: (i, 0))
    return pl.pallas_call(
        mix_body,
        grid=(t // half,),
        in_specs=[
            tile, tile, lane_tile, pair, pair, whole((slots, D)), tile, small_w_spec(),
            whole((8, D)),
        ],
        out_specs=[tile, tile, lane_tile, whole((D, LANES))],
        out_shape=[
            shape((t, D), BF16), shape((t, D), F32), shape((t, LANES), F32), shape((D, LANES), F32),
        ],
        name="mixture",
        **params((4 * t * slots * D, 12 * t * D)),
    )(hidden, g, pr, rt, tc, ret, low, pack, rows)


def norm_back_body(
    h_ref, g_ref, gn_ref, tc_ref, ret_ref, rows_ref, ow_ref, att_ref,
    gh_ref, do_ref, dot_ref, gow_ref, gg_ref,
):
    t = h_ref.shape[0]
    slots = ret_ref.shape[0]
    hidden = h_ref[...]
    slot = lax.broadcasted_iota(jnp.int32, (t, slots), 1)
    pick = (slot == tc_ref[:, 0:1]) | (slot == tc_ref[:, 1:2])
    gn = gn_ref[...] + dot(pick.astype(BF16), ret_ref[...])
    q = lax.rsqrt(jnp.mean(hidden * hidden, axis=-1, keepdims=True) + EPS)
    u = gn * rows_ref[2:3, :]
    mean = jnp.mean(u * hidden, axis=-1, keepdims=True)
    gh = g_ref[...].astype(F32) + q * u - hidden * (q * q * q * mean)
    gh_ref[...] = gh
    gb = gh.astype(BF16)
    d_out = dot_nt(gb, ow_ref[...]).astype(BF16)
    do_ref[...] = d_out
    dot_ref[...] = d_out.T
    gow = dot(att_ref[...].T, gb)
    gain = jnp.sum(gn * hidden * q, axis=0, keepdims=True)

    @pl.when(pl.program_id(0) == 0)
    def _():
        gow_ref[...] = gow
        gg_ref[...] = jnp.broadcast_to(gain, gg_ref.shape)

    @pl.when(pl.program_id(0) > 0)
    def _():
        gow_ref[...] += gow
        gg_ref[...] += jnp.broadcast_to(gain, gg_ref.shape)


def norm_back_call(hidden, g, gn, tc, ret, rows, pack, att):
    t = hidden.shape[0]
    half = t // 2 if (t // 2) % LANES == 0 else t
    slots = ret.shape[0]
    tile = spec((half, D), lambda i: (i, 0))
    return pl.pallas_call(
        norm_back_body,
        grid=(t // half,),
        in_specs=[
            tile, tile, tile, spec((half, 2), lambda i: (i, 0)), whole((slots, D)), whole((8, D)),
            out_w_spec(), tile,
        ],
        out_specs=[tile, tile, spec((D, half), lambda i: (0, i)), whole((D, D)), whole((8, D))],
        out_shape=[
            shape((t, D), F32), shape((t, D), BF16), shape((D, t), BF16), shape((D, D), F32),
            shape((8, D), F32),
        ],
        name="norm_two_back",
        **params((2 * t * slots * D + 4 * t * D * D, 16 * t * D)),
    )(hidden, g, gn, tc, ret, rows, pack, att)


def turn_body(x_ref, o_ref):
    o_ref[...] = x_ref[...].T


def turn(x):
    rows, wide = x.shape
    part = 256
    return pl.pallas_call(
        turn_body,
        grid=(wide // part,),
        in_specs=[spec((rows, part), lambda i: (0, i))],
        out_specs=spec((part, rows), lambda i: (i, 0)),
        out_shape=shape((wide, rows), x.dtype),
        name="turn",
        **params((rows * wide, 4 * rows * wide)),
    )(x)


def store_grad(sc_ref, split, value, refs):
    if not split:
        refs[0][...] = value
        return
    send_ref, keep_ref = refs
    per = value.shape[0] // 4
    for core in range(2):

        @pl.when(sc_ref[11] == core)
        def _():
            for part in range(2):
                mine = (2 * part + core) * per
                other = (2 * part + 1 - core) * per
                send_ref[part] = value[other : other + per].astype(BF16)
                keep_ref[part] = value[mine : mine + per]


def grad_outs(split, width):
    block = 2 * LANES
    if not split:
        return [spec((D, block), lambda i: (0, i))], [shape((D, width), F32)]
    dims = (2, D // 4, width)
    tile = spec((2, D // 4, block), lambda i: (0, 0, i))
    return [tile, tile], [shape(dims, BF16), shape(dims, F32)]


def q_back_body(split, sc_ref, nt_ref, dq_ref, c_ref, s_ref, w_ref, gn_ref, *refs):
    step = pl.program_id(0)
    cosine = c_ref[...]
    sine = s_ref[...]
    v0 = dq_ref[:, :LANES]
    v1 = dq_ref[:, LANES:]
    gq = jnp.concatenate(
        [
            (v0 * cosine - partner(v0) * sine).astype(BF16),
            (v1 * cosine - partner(v1) * sine).astype(BF16),
        ],
        axis=1,
    )
    store_grad(sc_ref, split, dot(nt_ref[...], gq), refs)
    gn = dot_nt(gq, w_ref[...])

    @pl.when(step == 0)
    def _():
        gn_ref[...] = gn

    @pl.when(step > 0)
    def _():
        gn_ref[...] += gn


def q_back_call(sc, low_t, dq, cosine, sine, pack, split):
    t = low_t.shape[1]
    specs, shapes = grad_outs(split, D)
    return pl.pallas_call(
        functools.partial(q_back_body, split),
        grid=(PAIRS // 2,),
        in_specs=[
            SMEM_SPEC, whole((D, t)), spec((t, 2 * LANES), lambda i: (0, i)), whole((t, LANES)),
            whole((t, LANES)), spec((D, 2 * LANES), lambda i: (0, i)),
        ],
        out_specs=[whole((t, D))] + specs,
        out_shape=[shape((t, D), F32)] + shapes,
        name="q_back",
        **params((4 * t * D * D, 12 * t * D)),
    )(sc, low_t, dq, cosine, sine, pack)


def kv_back_body(
    split, count, sc_ref, x_ref, nt_ref, gnq_ref, gh_ref, gain_ref, c_ref, s_ref, wk_ref, wv_ref,
    own_ref, cont_ref, *refs
):
    got_refs, refs = refs[:count], refs[count:]
    gi_ref, grads, gn_ref = refs[0], refs[1:-1], refs[-1]
    step = pl.program_id(0)

    @pl.when(step == 0)
    def _():
        gn_ref[...] = gnq_ref[...]

    own = own_ref[...]
    for got in got_refs:
        own = own + got[...].astype(F32)
    total = jnp.concatenate([own, cont_ref[...]], axis=0)
    k = total[:, :LANES]
    gk = (k * c_ref[...] - partner(k) * s_ref[...]).astype(BF16)
    gkv = jnp.concatenate([gk, total[:, LANES:].astype(BF16)], axis=1)
    store_grad(sc_ref, split, dot(nt_ref[...], gkv), grads)
    gn_ref[...] += dot_nt(gkv, jnp.concatenate([wk_ref[...], wv_ref[...]], axis=1))

    @pl.when(step == pl.num_programs(0) - 1)
    def _():
        gn = gn_ref[...]
        x = x_ref[...].astype(F32)
        q = lax.rsqrt(jnp.mean(x * x, axis=-1, keepdims=True) + EPS)
        u = gn * gain_ref[...]
        mean = jnp.mean(u * x, axis=-1, keepdims=True)
        gi_ref[...] = gh_ref[...] + q * u - x * (q * q * q * mean)


def kv_back_call(sc, x, low_t, gn, gh, gain, cosine, sine, pack, own, cont, got, split):
    t = x.shape[0]
    r = t // 2
    specs, shapes = grad_outs(split, 2 * D)
    wide = spec((r, 2 * LANES), lambda i: (0, i))
    return pl.pallas_call(
        functools.partial(kv_back_body, split, len(got)),
        grid=(PAIRS,),
        in_specs=[
            SMEM_SPEC, whole((t, D)), whole((D, t)), whole((t, D)), whole((t, D)), whole((1, D)),
            whole((t, LANES)), whole((t, LANES)),
            spec((D, LANES), lambda i: (0, PAIRS + i)),
            spec((D, LANES), lambda i: (0, 2 * PAIRS + i)),
            wide, wide,
        ]
        + [wide] * len(got),
        out_specs=[whole((t, D))] + specs,
        out_shape=[shape((t, D), F32)] + shapes,
        scratch_shapes=[pltpu.VMEM((t, D), F32)],
        name="kv_back",
        **params((8 * t * D * D, 24 * t * D)),
    )(sc, x, low_t, gn, gh, gain, cosine, sine, pack, pack, own, cont, *got)


def rotation_tables(position):
    half = HEAD_DIM // 2
    frequency = 10000.0 ** (-jnp.arange(half, dtype=F32) / half)
    angles = position[:, None] * frequency[None, :]
    cosine, sine = jnp.cos(angles), jnp.sin(angles)
    return (
        jnp.concatenate([cosine] * 4, axis=1),
        jnp.concatenate([-sine, sine, -sine, sine], axis=1),
    )


def to_rows(array):
    return jnp.transpose(array, (1, 0, 2)).reshape(2 * array.shape[0], array.shape[2])


def from_rows(array):
    r = array.shape[0] // 2
    return jnp.transpose(array.reshape(2, r, array.shape[1]), (1, 0, 2))


RING = (0, 2, 4, 6, 7, 5, 3, 1)


def ring_offsets():
    place = {e: i for i, e in enumerate(RING)}
    return [[RING[(place[e] + k) % 8] for k in range(8)] for e in range(8)]


def along_ring(array, step):
    pairs = [(RING[i], RING[(i + step) % 8]) for i in range(8)]
    return lax.ppermute(array, "expert", pairs)


def tie(*values):
    return lax.optimization_barrier(values)


def swap_core(array):
    return lax.ppermute(array, "dp", [(0, 1), (1, 0), (2, 3), (3, 2)])


def add_and_cross(keep, got):
    across = lax.axis_index("dp") // 2
    keep = keep + got.astype(F32)
    send = lax.dynamic_index_in_dim(keep, 1 - across, 0, keepdims=False).astype(BF16)
    mine = lax.dynamic_index_in_dim(keep, across, 0, keepdims=False)
    return mine, lax.ppermute(send, "dp", [(0, 2), (2, 0), (1, 3), (3, 1)])


def add_and_scatter(keep, got):
    keep = (keep + got.astype(F32)).astype(BF16)
    rows, w = keep.shape
    return lax.all_to_all(
        keep.reshape(8, rows // 8, w), "expert", split_axis=0, concat_axis=0, tiled=True
    )


def add_up(got):
    return jnp.sum(got.astype(F32), axis=0)


def scatter_all(array):
    return lax.psum_scatter(
        array.astype(BF16), ALL_AXES, scatter_dimension=0, tiled=True
    ).astype(F32)


def per_device(
    hidden_in, cotangent, gate_residual, routes, groups, lengths, attn_gain, qkv_weight, out_weight,
    ffn_gain, router_weight, const_proj, const_vec, gate_weight, up_weight, down_weight,
):
    del groups
    r = hidden_in.shape[0]
    t = 2 * r
    capacity = r // 2
    owners = lax.axis_size("expert")
    copies = owners // EXPERTS
    slots = EXPERTS * capacity
    me = lax.axis_index("expert")
    per_cont = max(CONT_LEN // r, 1)

    small = jnp.concatenate(
        [
            router_weight, const_proj, const_vec, attn_gain[:, None], ffn_gain[:, None],
            jnp.zeros((attn_gain.shape[0], LANES - 20), BF16),
        ],
        axis=1,
    )
    pack = lax.all_gather(
        jnp.concatenate([qkv_weight, out_weight, small], axis=1), ALL_AXES, axis=0, tiled=True
    )
    index = jnp.arange(r, dtype=jnp.int32)
    row_ids = me * r + index
    position = jnp.concatenate([row_ids, PROMPT + row_ids % CONT_LEN]).astype(F32)
    cosine, sine = rotation_tables(position)
    cont = (me * r) // CONT_LEN
    length = lax.dynamic_slice(lengths, (cont,), (1,))
    header = jnp.stack([me, (me * r) % CONT_LEN]).astype(jnp.int32)
    header = jnp.concatenate([header, length.astype(jnp.int32)])
    ring = owners == 8
    if ring:
        ids = lax.dynamic_index_in_dim(jnp.asarray(ring_offsets(), jnp.int32), me, 0, keepdims=False)
    else:
        ids = jnp.arange(owners, dtype=jnp.int32)
    sc = jnp.concatenate([header, ids, (lax.axis_index("dp") % 2).astype(jnp.int32)[None]])

    picked = to_rows(routes)
    flat = jnp.transpose(picked).reshape(2 * t)
    hot = flat[:, None] == jnp.arange(EXPERTS, dtype=jnp.int32)[None, :]
    earlier = jnp.arange(2 * t)[:, None] > jnp.arange(2 * t)[None, :]
    before = jnp.dot(earlier.astype(BF16), hot.astype(BF16), preferred_element_type=F32)
    slot_index = jnp.sum(jnp.where(hot, before, 0.0), axis=1).astype(jnp.int32)
    target = jnp.where(flat < EXPERTS, flat * capacity + slot_index, -1)
    target_rows = target.reshape(2, t)
    target_cols = jnp.transpose(target_rows)

    def to_owners(rows):
        w = rows.shape[-1]
        shaped = rows.reshape(EXPERTS, 1, capacity, w)
        return jnp.broadcast_to(shaped, (EXPERTS, copies, capacity, w)).reshape(owners, capacity, w)

    def exchange(rows):
        got = lax.all_to_all(rows, "expert", split_axis=0, concat_axis=0, tiled=True)
        return got.reshape(owners * got.shape[1], got.shape[2])

    def from_owners(rows):
        got = exchange(rows.reshape(owners, capacity, D))
        if copies == 1:
            return got
        got = got.reshape(EXPERTS, copies, capacity, D).astype(F32)
        return jnp.sum(got, axis=1).reshape(slots, D).astype(BF16)

    x = to_rows(hidden_in)
    g = to_rows(cotangent)
    small_w = pack[:, 4 * D :]
    small_rows = jnp.transpose(small_w[:, 16:24]).astype(F32)
    gain_one = small_rows[2:3]
    rows_two = jnp.concatenate([small_rows[0:2], small_rows[3:4], small_rows[3:8]], axis=0)
    gain_two = small_rows[3:4]

    low_one, q, q_t, kv_prompt, kv_cont = qkv_call(x, gain_one, pack, cosine, sine)
    if not ring:
        kv_all = lax.all_gather(kv_prompt, "expert", axis=0, tiled=True)
    if per_cont == 1:
        kv_own = kv_cont
    else:
        cont_groups = [
            [c * per_cont + i for i in range(per_cont)] for c in range(owners // per_cont)
        ]
        kv_own = lax.all_gather(
            kv_cont, "expert", axis=0, tiled=True, axis_index_groups=cont_groups
        )
    weights = lax.all_gather(
        jnp.stack([gate_weight, up_weight, down_weight]), "dp", axis=0, tiled=False
    )
    if ring:
        right, left = [kv_prompt], [kv_prompt]
        for i in range(3):
            right.append(along_ring(right[i], 1))
            left.append(along_ring(left[i], -1))
            if i == 0:
                st, acc = fwd_local(sc, q_t, kv_prompt, kv_own)
            else:
                st, acc = fwd_remote(sc, q_t, (right[i], left[i]), (8 - i, i), st, acc)
            right[i + 1], left[i + 1], st = tie(right[i + 1], left[i + 1], st)
        far = [along_ring(right[3][:, :D], 1), along_ring(left[3][:, D:], -1)]
        st, acc = fwd_remote(sc, q_t, (right[3], left[3]), (5, 3), st, acc)
        st, att_t, att = fwd_remote(sc, q_t, far, (4,), st, acc, halves=True, final=True)
    else:
        st, acc = fwd_local(sc, q_t, kv_prompt, kv_own)
        st, att_t, att = fwd_remote(sc, q_t, (kv_all,), range(owners), st, acc, final=True)

    res = jnp.pad(to_rows(gate_residual), ((0, 0), (0, LANES - EXPERTS - 4)))
    hidden, low_two, pr, x_send = route_call(
        x, att, pack, gain_two, res, picked, target_rows, slots
    )
    x_got = exchange(to_owners(x_send))
    g_send = grad_rows_call(g, pr, target_rows, slots)
    low_one_t = turn(low_one)
    x_got, g_send = tie(x_got, g_send)
    g_got = exchange(to_owners(g_send))
    expert_rows, gate_pre, up_pre = expert_fwd(x_got, weights)
    out_back = from_owners(expert_rows)
    grad_in, act, d_gate, d_up = expert_in(gate_pre, up_pre, g_got, weights)
    in_back = from_owners(grad_in)
    output, gn, grad_logits, grad_small = mix_call(
        hidden, g, pr, picked, target_cols, out_back, low_two, pack, rows_two
    )
    act, gn = tie(act, gn)
    grad_w = expert_weights(x_got, g_got, act, d_gate, d_up, weights.shape)
    grad_expert = lax.psum_scatter(
        grad_w.reshape(-1, grad_w.shape[-1]), "dp", scatter_dimension=0, tiled=True
    )
    per = gate_weight.shape[0]
    grad_expert = [grad_expert[i * per : (i + 1) * per].astype(F32) for i in range(3)]
    gh, d_att, d_att_t, grad_ow, gg_two = norm_back_call(
        hidden, g, gn, target_cols, in_back, rows_two, pack, att
    )

    early = jnp.concatenate(
        [grad_ow, grad_small[:, :19], jnp.transpose(gg_two[0:1]), jnp.zeros((D, LANES - 20), F32)],
        axis=1,
    )
    back = (sc, q_t, q, d_att_t, d_att)
    if ring:
        parts = early.reshape(2, 2, D // 4, D + LANES)
        core = lax.axis_index("dp") % 2
        early_keep = lax.dynamic_index_in_dim(parts, core, 1, keepdims=False)
        early_got = swap_core(
            lax.dynamic_index_in_dim(parts, 1 - core, 1, keepdims=False).astype(BF16)
        )
        dq_t, send_r, send_l, st = bwd_remote(
            *back, st, att_t, far, (4,), halves=True, first=True, dtype=BF16
        )
        for i in range(3, 0, -1):
            got_r, got_l = along_ring(send_r, 1), along_ring(send_l, -1)
            dq_t, part_r, part_l = bwd_remote(
                *back, st, dq_t, (left[i], right[i]), (i, 8 - i), dtype=BF16
            )
            got_r, got_l, part_r, part_l, dq_t, early_got = tie(
                got_r, got_l, part_r, part_l, dq_t, early_got
            )
            send_r, send_l = ring_add(part_r, got_r, part_l, got_l)
            if i == 3:
                early_keep, early_got = add_and_cross(early_keep, early_got)
        send_r, send_l, dq_t = tie(send_r, send_l, dq_t)
        got_r = along_ring(send_r, 1)
        got_l = along_ring(send_l, -1)
        got = (got_r, got_l)
        dq, dkv_own, dkv_cont = bwd_local(*back, st, dq_t, kv_prompt, kv_own)
    else:
        dq_t, dkv_all, st = bwd_remote(
            *back, st, att_t, (kv_all,), range(owners), first=True, dtype=BF16
        )
        dq, dkv_own, dkv_cont = bwd_local(*back, st, dq_t, kv_prompt, kv_own)
        got = (lax.psum_scatter(dkv_all, "expert", scatter_dimension=0, tiled=True),)
        early = scatter_all(early)
    if per_cont > 1:
        dkv_cont = lax.psum_scatter(
            dkv_cont, "expert", scatter_dimension=0, tiled=True, axis_index_groups=cont_groups
        )
    gn_q, *grad_q = q_back_call(sc, low_one_t, dq, cosine, sine, pack, ring)
    if ring:
        got_q = swap_core(grad_q[0])
        keep_q, got_q = add_and_cross(grad_q[1], got_q)
        keep_q, *got = tie(keep_q, *got)
    grad_input, *grad_kv = kv_back_call(
        sc, x, low_one_t, gn_q, gh, gain_one, cosine, sine, pack, dkv_own, dkv_cont, got, ring
    )
    output, grad_input = from_rows(output), from_rows(grad_input)
    if ring:
        got_kv = swap_core(grad_kv[0])
        keep_kv, got_kv = add_and_cross(grad_kv[1], got_kv)
        keep_kv, got_q, early_got = tie(keep_kv, got_q, early_got)
        got_q = add_and_scatter(
            jnp.concatenate([early_keep, keep_q], axis=1),
            jnp.concatenate([early_got, got_q], axis=1),
        )
        got_kv, output, grad_input, *grad_expert = tie(got_kv, output, grad_input, *grad_expert)
        summed = add_up(got_q)
        early, late_q = summed[:, : D + LANES], summed[:, D + LANES :]
        late_kv = add_up(add_and_scatter(keep_kv, got_kv))
    else:
        late_q, late_kv = scatter_all(grad_q[0]), scatter_all(grad_kv[0])
    per = late_kv.shape[0]
    late_kv = jnp.transpose(late_kv.reshape(per, PAIRS, 2, LANES), (0, 2, 1, 3))
    late = jnp.concatenate([late_q, late_kv.reshape(per, 2 * D)], axis=1)
    grad_gain = jnp.sum(late * qkv_weight.astype(F32), axis=1) / attn_gain.astype(F32)
    tail = early[:, D:]
    return (
        output,
        grad_input,
        from_rows(grad_logits)[:, :, : EXPERTS + 4],
        grad_gain,
        late,
        early[:, :D],
        tail[:, 19],
        tail[:, :12],
        tail[:, 12:16],
        tail[:, 16:18],
        grad_expert[0],
        grad_expert[1],
        grad_expert[2],
    )


def solution(mesh):
    rows = P(ALL_AXES, None, None)
    flat = P(ALL_AXES)
    mat = P(ALL_AXES, None)
    expert = P("dp", "expert")
    in_specs = (
        rows, rows, rows, rows, P("dp"), P("dp"), flat, mat, mat, flat, mat, mat, mat,
        expert, expert, expert,
    )
    out_specs = (
        rows, rows, rows, flat, mat, mat, flat, mat, mat, mat, expert, expert, expert,
    )

    return jax.shard_map(
        per_device, mesh=mesh, in_specs=in_specs, out_specs=out_specs, check_vma=False
    )
```

```python
import functools

import jax
import jax.numpy as jnp
from jax import lax
from jax.experimental import pallas as pl
from jax.experimental.pallas import tpu as pltpu
from jax.sharding import PartitionSpec as P


D = 768
HEAD_DIM = 64
PAIRS = 6
EXPERTS = 8
CONT_LEN = 256
PROMPT = 2048
LANES = 128
EPS = 1e-06
NEG = -1e30
LOG2E = 1.4426950408889634
SCALE = float(HEAD_DIM) ** (-0.5)
LC = SCALE * LOG2E
F32 = jnp.float32
BF16 = jnp.bfloat16
ALL_AXES = ("dp", "expert")
VMEM_SMALL = 24 * 1024 * 1024
VMEM_LARGE = 60 * 1024 * 1024


def dot(a, b):
    return jnp.dot(a, b, preferred_element_type=F32)


def dot_nt(a, b):
    return lax.dot_general(a, b, (((1,), (1,)), ((), ())), preferred_element_type=F32)


def split_hi_lo(v):
    hi = v.astype(BF16)
    return hi, (v - hi.astype(F32)).astype(BF16)


def params(cost=None, limit=VMEM_LARGE):
    return dict(
        compiler_params=pltpu.CompilerParams(vmem_limit_bytes=limit),
        cost_estimate=None if cost is None else pl.CostEstimate(
            flops=int(cost[0]), bytes_accessed=int(cost[1]), transcendentals=0
        ),
    )


def shape(dims, dtype):
    return jax.ShapeDtypeStruct(tuple(dims), dtype)


def spec(block, index):
    return pl.BlockSpec(tuple(block), index)


def whole(dims):
    return pl.BlockSpec(tuple(dims), lambda *_: (0,) * len(dims))


SMEM_SPEC = pl.BlockSpec(memory_space=pltpu.SMEM)


def partner(v):
    lane = lax.broadcasted_iota(jnp.int32, v.shape, 1)
    return jnp.where((lane & 63) < 32, pltpu.roll(v, 96, 1), pltpu.roll(v, 32, 1))


def qkv_body(x_ref, gain_ref, wq_ref, wk_ref, wv_ref, c_ref, s_ref, n_ref, q_ref, qt_ref, kvp_ref, kvc_ref):
    @pl.when(pl.program_id(0) == 0)
    def _():
        x = x_ref[...].astype(F32)
        scale = lax.rsqrt(jnp.mean(x * x, axis=-1, keepdims=True) + EPS)
        n_ref[...] = (x * scale * gain_ref[...]).astype(BF16)

    n = n_ref[...]
    cosine = c_ref[...]
    sine = s_ref[...]
    kv = dot(n, jnp.concatenate([wk_ref[...], wv_ref[...]], axis=1))
    k = kv[:, :LANES]
    k = (k * cosine + partner(k) * sine).astype(BF16)
    v = kv[:, LANES:].astype(BF16)
    r = k.shape[0] // 2
    kvp_ref[:, :LANES] = k[:r]
    kvp_ref[:, LANES:] = v[:r]
    kvc_ref[:, :LANES] = k[r:]
    kvc_ref[:, LANES:] = v[r:]
    q = dot(n, wq_ref[...])
    q = q * cosine + partner(q) * sine
    q = q.astype(BF16)
    q_ref[...] = q
    qt_ref[...] = q.T


def qkv_call(x, gain, pack, cosine, sine):
    t = x.shape[0]
    return pl.pallas_call(
        qkv_body,
        grid=(PAIRS,),
        in_specs=[
            whole((t, D)),
            whole((1, D)),
            spec((D, LANES), lambda i: (0, i)),
            spec((D, LANES), lambda i: (0, PAIRS + i)),
            spec((D, LANES), lambda i: (0, 2 * PAIRS + i)),
            whole((t, LANES)),
            whole((t, LANES)),
        ],
        out_specs=[
            whole((t, D)),
            spec((t, LANES), lambda i: (0, i)),
            spec((LANES, t), lambda i: (i, 0)),
            spec((t // 2, 2 * LANES), lambda i: (0, i)),
            spec((t // 2, 2 * LANES), lambda i: (0, i)),
        ],
        out_shape=[
            shape((t, D), BF16),
            shape((t, D), BF16),
            shape((D, t), BF16),
            shape((t // 2, 2 * D), BF16),
            shape((t // 2, 2 * D), BF16),
        ],
        name="qkv_rope",
        **params((2 * t * D * 3 * D, 6 * D * D)),
    )(x, gain, pack, pack, pack, cosine, sine)


def head_rows(v, h):
    row = lax.broadcasted_iota(jnp.int32, v.shape, 0)
    return jnp.where(row // HEAD_DIM == h, v, jnp.zeros_like(v))


def head_lanes(v, h):
    lane = lax.broadcasted_iota(jnp.int32, v.shape, 1)
    return jnp.where(lane // HEAD_DIM == h, v, jnp.zeros_like(v))


def attend_update(qz, kb, vt, lo, hi, mask, st_ref, a_ref, first):
    for h in range(2):
        s = dot(kb, qz[h][:, lo:hi])
        if mask is not None:
            s = jnp.where(mask, s, NEG)
        top = jnp.max(s, axis=0, keepdims=True)
        rows = slice(h * HEAD_DIM, (h + 1) * HEAD_DIM)
        if first:
            p = jnp.exp2((s - top) * LC)
            st_ref[h : h + 1, lo:hi] = top
            st_ref[2 + h : 3 + h, lo:hi] = jnp.sum(p, axis=0, keepdims=True)
            a_ref[rows, lo:hi] = dot(vt[rows], p.astype(BF16))
        else:
            old = st_ref[h : h + 1, lo:hi]
            new = jnp.maximum(old, top)
            alpha = jnp.exp2((old - new) * LC)
            p = jnp.exp2((s - new) * LC)
            st_ref[h : h + 1, lo:hi] = new
            st_ref[2 + h : 3 + h, lo:hi] = st_ref[2 + h : 3 + h, lo:hi] * alpha + jnp.sum(
                p, axis=0, keepdims=True
            )
            a_ref[rows, lo:hi] = a_ref[rows, lo:hi] * alpha + dot(vt[rows], p.astype(BF16))


def local_masks(sc_ref, r, keys, lo, hi):
    cpos = sc_ref[1]
    length = sc_ref[2]
    col = lo + lax.broadcasted_iota(jnp.int32, (r, hi - lo), 1)
    row = lax.broadcasted_iota(jnp.int32, (r, hi - lo), 0)
    own = (row <= col) | (col >= r)
    col = lo + lax.broadcasted_iota(jnp.int32, (keys, hi - lo), 1)
    row = lax.broadcasted_iota(jnp.int32, (keys, hi - lo), 0)
    cont = (col >= r) & (row <= cpos + col - r) & (row < length)
    return own, cont


def fwd_local_body(sc_ref, qt_ref, kv_ref, kvo_ref, st_ref, a_ref):
    t = qt_ref.shape[1]
    r = t // 2
    keys = kvo_ref.shape[0]
    qt = qt_ref[...]
    qz = [head_rows(qt, h) for h in range(2)]
    kb = kv_ref[:, :LANES]
    vt = kv_ref[:, LANES:].T
    kbo = kvo_ref[:, :LANES]
    vto = kvo_ref[:, LANES:].T
    st_ref[...] = jnp.zeros_like(st_ref)
    own, cont = local_masks(sc_ref, r, keys, 0, t)
    attend_update(qz, kb, vt, 0, t, own, st_ref, a_ref, True)
    if r % LANES == 0:
        attend_update(qz, kbo, vto, r, t, cont[:, r:], st_ref, a_ref, False)
    else:
        attend_update(qz, kbo, vto, 0, t, cont, st_ref, a_ref, False)


def halves_value(a_ref, b_ref):
    return jnp.where(pl.program_id(0) < PAIRS // 2, a_ref[...], b_ref[...])


def fwd_remote_body(offsets, count, halves, final, sc_ref, qt_ref, *refs):
    kv_refs, refs = refs[:count], refs[count:]
    st_in, a_in, st_ref, a_ref = refs[:4]
    t = qt_ref.shape[1]
    r = t // 2
    me = sc_ref[0]
    qt = qt_ref[...]
    qz = [head_rows(qt, h) for h in range(2)]
    st_ref[...] = st_in[...]
    a_ref[...] = a_in[...]
    for j, offset in enumerate(offsets):
        block = sc_ref[3 + offset]

        def go(lo, hi, mask):
            if halves:
                kv = halves_value(*kv_refs)
            elif len(kv_refs) == len(offsets):
                kv = kv_refs[j][...]
            else:
                kv = kv_refs[0][j * r : (j + 1) * r, :]
            attend_update(qz, kv[:, :LANES], kv[:, LANES:].T, lo, hi, mask, st_ref, a_ref, False)

        if r % LANES == 0:

            @pl.when(block < me)
            def _():
                go(0, t, None)

            @pl.when(block > me)
            def _():
                go(r, t, None)

        else:

            @pl.when(block != me)
            def _():
                col = lax.broadcasted_iota(jnp.int32, (r, t), 1)
                go(0, t, (col >= r) | (block < me))

    if final:
        low_ref = refs[4]
        for h in range(2):
            rows = slice(h * HEAD_DIM, (h + 1) * HEAD_DIM)
            total = st_ref[2 + h : 3 + h, :]
            a_ref[rows, :] = a_ref[rows, :] / total
            st_ref[h : h + 1, :] = st_ref[h : h + 1, :] * LC + jnp.log2(total)
        low_ref[...] = a_ref[...].astype(BF16).T


def kv_specs(kvs, halves):
    if halves:
        r = kvs[0].shape[0]
        return [
            spec((r, 2 * LANES), lambda i: (0, jnp.minimum(i, PAIRS // 2 - 1))),
            spec((r, 2 * LANES), lambda i: (0, jnp.maximum(i - PAIRS // 2, 0))),
        ]
    return [spec((kv.shape[0], 2 * LANES), lambda i: (0, i)) for kv in kvs]


def fwd_local(sc, qt, kv_prompt, kv_own):
    t = qt.shape[1]
    keys = kv_own.shape[0]
    return pl.pallas_call(
        fwd_local_body,
        grid=(PAIRS,),
        in_specs=[
            SMEM_SPEC,
            spec((LANES, t), lambda i: (i, 0)),
            spec((t // 2, 2 * LANES), lambda i: (0, i)),
            spec((keys, 2 * LANES), lambda i: (0, i)),
        ],
        out_specs=[spec((8, t), lambda i: (i, 0)), spec((LANES, t), lambda i: (i, 0))],
        out_shape=[shape((8 * PAIRS, t), F32), shape((D, t), F32)],
        name="attend_local",
        **params((4 * 4 * t * keys * D, 4 * D * t)),
    )(sc, qt, kv_prompt, kv_own)


def fwd_remote(sc, qt, kvs, offsets, st, acc, halves=False, final=False):
    t = qt.shape[1]
    rows = len(offsets) * (t // 2)
    out_specs = [spec((8, t), lambda i: (i, 0)), spec((LANES, t), lambda i: (i, 0))]
    out_shape = [shape((8 * PAIRS, t), F32), shape((D, t), F32)]
    if final:
        out_specs.append(spec((t, LANES), lambda i: (0, i)))
        out_shape.append(shape((t, D), BF16))
    return pl.pallas_call(
        functools.partial(fwd_remote_body, tuple(offsets), len(kvs), halves, final),
        grid=(PAIRS,),
        in_specs=[SMEM_SPEC, spec((LANES, t), lambda i: (i, 0))]
        + kv_specs(kvs, halves)
        + [spec((8, t), lambda i: (i, 0)), spec((LANES, t), lambda i: (i, 0))],
        out_specs=out_specs,
        out_shape=out_shape,
        name="attend_remote",
        **params((4 * 4 * t * rows * D, 8 * D * t + 4 * D * rows)),
    )(sc, qt, *kvs, st, acc)


def back_block(ops, kb, vb, kt, lo, hi, mask, dq_ref):
    qz, qn, doz, don, lse, delta = ops
    dk = None
    dv = None
    for h in range(2):
        s = dot(kb, qz[h][:, lo:hi])
        dp = dot(vb, doz[h][:, lo:hi])
        p = jnp.exp2(s * LC - lse[h][:, lo:hi])
        if mask is not None:
            p = jnp.where(mask, p, 0.0)
        ds = (p * (dp - delta[h][:, lo:hi])).astype(BF16)
        dv_h = dot(p.astype(BF16), don[h][lo:hi])
        dk_h = dot(ds, qn[h][lo:hi])
        rows = slice(h * HEAD_DIM, (h + 1) * HEAD_DIM)
        dq_ref[rows, lo:hi] += dot(kt[rows], ds)
        dv = dv_h if dv is None else dv + dv_h
        dk = dk_h if dk is None else dk + dk_h
    return dk, dv


def back_operands(qt_ref, q_ref, dot_ref, do_ref, st_ref):
    qt, q, do_t, do = qt_ref[...], q_ref[...], dot_ref[...], do_ref[...]
    return (
        [head_rows(qt, h) for h in range(2)],
        [head_lanes(q, h) for h in range(2)],
        [head_rows(do_t, h) for h in range(2)],
        [head_lanes(do, h) for h in range(2)],
        [st_ref[h : h + 1, :] for h in range(2)],
        [st_ref[4 + h : 5 + h, :] for h in range(2)],
    )


def bwd_local_body(
    sc_ref, qt_ref, q_ref, dot_ref, do_ref, st_ref, dq_in, kv_ref, kvo_ref,
    out_ref, dkv_ref, dkvo_ref, dq_ref,
):
    t = qt_ref.shape[1]
    r = t // 2
    keys = kvo_ref.shape[0]
    ops = back_operands(qt_ref, q_ref, dot_ref, do_ref, st_ref)
    dq_ref[...] = dq_in[...]
    kb, vb = kv_ref[:, :LANES], kv_ref[:, LANES:]
    kbo, vbo = kvo_ref[:, :LANES], kvo_ref[:, LANES:]
    kt, kto = kb.T, kbo.T
    own, cont = local_masks(sc_ref, r, keys, 0, t)
    dk, dv = back_block(ops, kb, vb, kt, 0, t, own, dq_ref)
    if r % LANES == 0:
        dko, dvo = back_block(ops, kbo, vbo, kto, r, t, cont[:, r:], dq_ref)
    else:
        dko, dvo = back_block(ops, kbo, vbo, kto, 0, t, cont, dq_ref)
    dkv_ref[:, :LANES] = dk * SCALE
    dkv_ref[:, LANES:] = dv
    dkvo_ref[:, :LANES] = dko * SCALE
    dkvo_ref[:, LANES:] = dvo
    out_ref[...] = dq_ref[...].T * SCALE


def bwd_remote_body(
    offsets, count, halves, first, dtype, sc_ref, qt_ref, q_ref, dot_ref, do_ref, st_in, *refs
):
    t = qt_ref.shape[1]
    r = t // 2
    me = sc_ref[0]
    kv_refs, refs = refs[:count], refs[count:]
    src, refs = refs[0], refs[1:]
    dq_ref, refs = refs[0], refs[1:]
    out_refs, refs = refs[:count], refs[count:]
    if first:
        st_ref, refs = refs[0], refs[1:]
        st_ref[...] = st_in[...]
        prod = src[...] * dot_ref[...].astype(F32)
        for h in range(2):
            st_ref[4 + h : 5 + h, :] = jnp.sum(
                prod[h * HEAD_DIM : (h + 1) * HEAD_DIM], axis=0, keepdims=True
            )
        dq_ref[...] = jnp.zeros_like(dq_ref)
    else:
        st_ref = st_in
        dq_ref[...] = src[...]
    ops = back_operands(qt_ref, q_ref, dot_ref, do_ref, st_ref)
    split = len(offsets) != count and not halves

    def store(j, dk, dv):
        if halves:
            for part in range(2):

                @pl.when((pl.program_id(0) < PAIRS // 2) == (part == 0))
                def _():
                    out_refs[part][:, :LANES] = dk
                    out_refs[part][:, LANES:] = dv

        elif split:
            out_refs[0][j * r : (j + 1) * r, :LANES] = dk
            out_refs[0][j * r : (j + 1) * r, LANES:] = dv
        else:
            out_refs[j][:, :LANES] = dk
            out_refs[j][:, LANES:] = dv

    for j, offset in enumerate(offsets):
        block = sc_ref[3 + offset]

        def go(lo, mask):
            if halves:
                kv = halves_value(*kv_refs)
            elif split:
                kv = kv_refs[0][j * r : (j + 1) * r, :]
            else:
                kv = kv_refs[j][...]
            kb = kv[:, :LANES]
            dk, dv = back_block(ops, kb, kv[:, LANES:], kb.T, lo, t, mask, dq_ref)
            store(j, (dk * SCALE).astype(dtype), dv.astype(dtype))

        if split:

            @pl.when(block == me)
            def _():
                zero = jnp.zeros((r, LANES), dtype)
                store(j, zero, zero)

        if r % LANES == 0:

            @pl.when(block < me)
            def _():
                go(0, None)

            @pl.when(block > me)
            def _():
                go(r, None)

        else:

            @pl.when(block != me)
            def _():
                col = lax.broadcasted_iota(jnp.int32, (r, t), 1)
                go(0, (col >= r) | (block < me))


def add_low(a, b):
    return (a.astype(F32) + b.astype(F32)).astype(BF16)


def ring_add_body(half, pr_ref, gr_ref, pl_ref, gl_ref, sr_ref, sl_ref):
    if not half:
        sr_ref[...] = add_low(pr_ref[...], gr_ref[...])
        sl_ref[...] = add_low(pl_ref[...], gl_ref[...])
        return
    sr_ref[:, :D] = add_low(pr_ref[:, :D], gr_ref[...])
    sr_ref[:, D:] = pr_ref[:, D:]
    sl_ref[:, :D] = pl_ref[:, :D]
    sl_ref[:, D:] = add_low(pl_ref[:, D:], gl_ref[...])


def ring_add(part_r, got_r, part_l, got_l):
    r = part_r.shape[0]
    part = r // 2
    half = got_r.shape[1] == D
    wide = spec((part, 2 * D), lambda i: (i, 0))
    got = spec((part, got_r.shape[1]), lambda i: (i, 0))
    return pl.pallas_call(
        functools.partial(ring_add_body, half),
        grid=(2,),
        in_specs=[wide, got, wide, got],
        out_specs=[wide, wide],
        out_shape=[shape((r, 2 * D), BF16)] * 2,
        name="ring_add",
        **params((4 * r * D, 16 * r * D)),
    )(part_r, got_r, part_l, got_l)


def q_specs(t):
    return [
        spec((LANES, t), lambda i: (i, 0)),
        spec((t, LANES), lambda i: (0, i)),
        spec((LANES, t), lambda i: (i, 0)),
        spec((t, LANES), lambda i: (0, i)),
        spec((8, t), lambda i: (i, 0)),
    ]


def bwd_local(sc, qt, q, do_t, do, st, dq, kv_prompt, kv_own):
    t = qt.shape[1]
    keys = kv_own.shape[0]
    return pl.pallas_call(
        bwd_local_body,
        grid=(PAIRS,),
        in_specs=[SMEM_SPEC]
        + q_specs(t)
        + [spec((LANES, t), lambda i: (i, 0))]
        + kv_specs((kv_prompt, kv_own), False),
        out_specs=[spec((t, LANES), lambda i: (0, i))] + kv_specs((kv_prompt, kv_own), False),
        out_shape=[
            shape((t, D), F32),
            shape((t // 2, 2 * D), F32),
            shape((keys, 2 * D), F32),
        ],
        scratch_shapes=[pltpu.VMEM((LANES, t), F32)],
        name="attend_back_local",
        **params((10 * 4 * t * keys * D, 16 * D * t)),
    )(sc, qt, q, do_t, do, st, dq, kv_prompt, kv_own)


def bwd_remote(
    sc, qt, q, do_t, do, st, src, kvs, offsets, halves=False, first=False, dtype=F32
):
    t = qt.shape[1]
    rows = len(offsets) * (t // 2)
    out_specs = [spec((LANES, t), lambda i: (i, 0))] + kv_specs(kvs, halves)
    out_shape = [shape((D, t), F32)] + [shape(kv.shape, dtype) for kv in kvs]
    if first:
        out_specs.append(spec((8, t), lambda i: (i, 0)))
        out_shape.append(shape((8 * PAIRS, t), F32))
    return pl.pallas_call(
        functools.partial(bwd_remote_body, tuple(offsets), len(kvs), halves, first, dtype),
        grid=(PAIRS,),
        in_specs=[SMEM_SPEC]
        + q_specs(t)
        + kv_specs(kvs, halves)
        + [spec((LANES, t), lambda i: (i, 0))],
        out_specs=out_specs,
        out_shape=out_shape,
        name="attend_back_remote",
        **params((10 * 4 * t * rows * D, 16 * D * t + 8 * D * rows)),
    )(sc, qt, q, do_t, do, st, *kvs, src)


def route_body(
    x_ref, att_ref, ow_ref, sw_ref, gain_ref, res_ref, rt_ref, tr_ref,
    h_ref, n_ref, pr_ref, xs_ref,
):
    t = x_ref.shape[0]
    step = pl.program_id(0)

    @pl.when(step == 0)
    def _():
        hidden = x_ref[...].astype(F32) + dot(att_ref[...], ow_ref[...])
        h_ref[...] = hidden
        scale = lax.rsqrt(jnp.mean(hidden * hidden, axis=-1, keepdims=True) + EPS)
        low = (hidden * scale * gain_ref[...]).astype(BF16)
        n_ref[...] = low
        z = dot(low, sw_ref[...])
        lane = lax.broadcasted_iota(jnp.int32, (t, LANES), 1)
        is_route = lane < EXPERTS + 4
        logits = jnp.where(is_route, z + res_ref[...], NEG)
        ex = jnp.exp(logits - jnp.max(logits, axis=-1, keepdims=True))
        probs = ex / jnp.sum(ex, axis=-1, keepdims=True)
        out = probs
        first = EXPERTS + 4
        for k in range(2):
            l0 = z[:, first + 2 * k : first + 2 * k + 1]
            l1 = z[:, first + 2 * k + 1 : first + 2 * k + 2]
            top = jnp.maximum(l0, l1)
            e0 = jnp.exp(l0 - top)
            e1 = jnp.exp(l1 - top)
            den = e0 + e1
            out = jnp.where(lane == first + 2 * k, e0 / den, out)
            out = jnp.where(lane == first + 2 * k + 1, e1 / den, out)
        for j in range(2):
            mix = jnp.sum(jnp.where(lane == rt_ref[:, j : j + 1], probs, 0.0), axis=-1, keepdims=True)
            out = jnp.where(lane == 16 + j, mix, out)
        pr_ref[...] = out

    slots = xs_ref.shape[0]
    base = step * slots
    slot = base + lax.broadcasted_iota(jnp.int32, (slots, t), 0)
    pick = (slot == tr_ref[0:1, :]) | (slot == tr_ref[1:2, :])
    xs_ref[...] = dot(pick.astype(BF16), n_ref[...]).astype(BF16)


def grad_rows_body(g_ref, pr_ref, tr_ref, gs_ref, mg_ref):
    t = g_ref.shape[0]
    step = pl.program_id(0)

    @pl.when(step == 0)
    def _():
        g = g_ref[...].astype(F32)
        for j in range(2):
            mg_ref[j * t : (j + 1) * t, :] = (g * pr_ref[:, 16 + j : 17 + j]).astype(BF16)

    slots = gs_ref.shape[0]
    slot = step * slots + lax.broadcasted_iota(jnp.int32, (slots, t), 0)
    picks = [(slot == tr_ref[j : j + 1, :]).astype(BF16) for j in range(2)]
    gs_ref[...] = dot(jnp.concatenate(picks, axis=1), mg_ref[...]).astype(BF16)


def grad_rows_call(g, pr, tr, slots):
    t = g.shape[0]
    part = min(slots, 256)
    return pl.pallas_call(
        grad_rows_body,
        grid=(slots // part,),
        in_specs=[whole((t, D)), whole((t, LANES)), whole((2, t))],
        out_specs=spec((part, D), lambda i: (i, 0)),
        out_shape=shape((slots, D), BF16),
        scratch_shapes=[pltpu.VMEM((2 * t, D), BF16)],
        name="grad_rows",
        **params((4 * slots * t * D, 4 * t * D)),
    )(g, pr, tr)


def route_call(x, att, ow, sw, gain, res, rt, tr, slots):
    t = x.shape[0]
    part = min(slots, 256)
    return pl.pallas_call(
        route_body,
        grid=(slots // part,),
        in_specs=[
            whole((t, D)), whole((t, D)), whole((D, D)), whole((D, LANES)), whole((1, D)),
            whole((t, LANES)), whole((t, 2)), whole((2, t)),
        ],
        out_specs=[
            whole((t, D)), whole((t, D)), whole((t, LANES)),
            spec((part, D), lambda i: (i, 0)),
        ],
        out_shape=[
            shape((t, D), F32), shape((t, D), BF16), shape((t, LANES), F32),
            shape((slots, D), BF16),
        ],
        name="route_dispatch",
        **params((2 * t * D * D + 2 * slots * t * D, 8 * t * D), VMEM_SMALL),
    )(x, att, ow, sw, gain, res, rt, tr)


def expert_fwd_body(x_ref, w_ref, o_ref, gate_ref, up_ref, acc_ref):
    step = pl.program_id(0)
    x = x_ref[...]
    wide = w_ref.shape[-1]
    wg = w_ref[:, 0].reshape(D, wide)
    wu = w_ref[:, 1].reshape(D, wide)
    wd = w_ref[:, 2].reshape(D, wide)
    gate = dot(x, wg)
    up = dot(x, wu)
    gate_ref[...] = gate
    up_ref[...] = up
    act = (gate / (1.0 + jnp.exp(-gate)) * up).astype(BF16)
    out = dot_nt(act, wd)

    @pl.when(step == 0)
    def _():
        acc_ref[...] = out

    @pl.when(step > 0)
    def _():
        acc_ref[...] += out

    @pl.when(step == pl.num_programs(0) - 1)
    def _():
        o_ref[...] = acc_ref[...].astype(BF16)


def expert_fwd(xr, w):
    rows = xr.shape[0]
    shards, _, per, wide = w.shape
    part = min(wide, 256)
    return pl.pallas_call(
        expert_fwd_body,
        grid=(wide // part,),
        in_specs=[whole((rows, D)), spec((shards, 3, per, part), lambda i: (0, 0, 0, i))],
        out_specs=[whole((rows, D))] + [spec((rows, part), lambda i: (0, i))] * 2,
        out_shape=[shape((rows, D), BF16)] + [shape((rows, wide), F32)] * 2,
        scratch_shapes=[pltpu.VMEM((rows, D), F32)],
        name="expert_forward",
        **params((6 * rows * D * wide, 6 * D * wide)),
    )(xr, w)


def expert_in_body(gate_ref, up_ref, g_ref, w_ref, gi_ref, act_ref, dg_ref, du_ref, acc_ref):
    step = pl.program_id(0)
    wide = w_ref.shape[-1]
    wg = w_ref[:, 0].reshape(D, wide)
    wu = w_ref[:, 1].reshape(D, wide)
    wd = w_ref[:, 2].reshape(D, wide)
    gate = gate_ref[...]
    up = up_ref[...]
    ga = dot(g_ref[...], wd)
    sig = 1.0 / (1.0 + jnp.exp(-gate))
    silu = gate * sig
    act_ref[...] = (silu * up).astype(BF16)
    d_gate = (ga * up * sig * (1.0 + gate * (1.0 - sig))).astype(BF16)
    d_up = (ga * silu).astype(BF16)
    dg_ref[...] = d_gate
    du_ref[...] = d_up
    gi = dot_nt(
        jnp.concatenate([d_gate, d_up], axis=1), jnp.concatenate([wg, wu], axis=1)
    )

    @pl.when(step == 0)
    def _():
        acc_ref[...] = gi

    @pl.when(step > 0)
    def _():
        acc_ref[...] += gi

    @pl.when(step == pl.num_programs(0) - 1)
    def _():
        gi_ref[...] = acc_ref[...].astype(BF16)


def expert_in(gate, up, gr, w):
    rows = gr.shape[0]
    shards, _, per, wide = w.shape
    part = min(wide, 256)
    tile = spec((rows, part), lambda i: (0, i))
    return pl.pallas_call(
        expert_in_body,
        grid=(wide // part,),
        in_specs=[tile, tile, whole((rows, D)), spec((shards, 3, per, part), lambda i: (0, 0, 0, i))],
        out_specs=[whole((rows, D)), tile, tile, tile],
        out_shape=[shape((rows, D), BF16)] + [shape((rows, wide), BF16)] * 3,
        scratch_shapes=[pltpu.VMEM((rows, D), F32)],
        name="expert_back_in",
        **params((6 * rows * D * wide, 12 * D * wide)),
    )(gate, up, gr, w)


def expert_weights_body(x_ref, gl_ref, act_ref, dg_ref, du_ref, dw_ref, xt_ref, gt_ref):
    @pl.when(pl.program_id(0) == 0)
    def _():
        gt_ref[...] = gl_ref[...].T
        xt_ref[...] = x_ref[...].T

    shards, _, per, wide = dw_ref.shape
    xt = xt_ref[...]
    dw_ref[:, 0] = dot(xt, dg_ref[...]).astype(BF16).reshape(shards, per, wide)
    dw_ref[:, 1] = dot(xt, du_ref[...]).astype(BF16).reshape(shards, per, wide)
    dw_ref[:, 2] = dot(gt_ref[...], act_ref[...]).astype(BF16).reshape(shards, per, wide)


def expert_weights(xr, low, act, d_gate, d_up, dims):
    rows = xr.shape[0]
    shards, _, per, wide = dims
    part = min(wide, 256)
    tile = spec((rows, part), lambda i: (0, i))
    return pl.pallas_call(
        expert_weights_body,
        grid=(wide // part,),
        in_specs=[whole((rows, D)), whole((rows, D)), tile, tile, tile],
        out_specs=spec((shards, 3, per, part), lambda i: (0, 0, 0, i)),
        out_shape=shape(dims, BF16),
        scratch_shapes=[pltpu.VMEM((D, rows), BF16), pltpu.VMEM((D, rows), BF16)],
        name="expert_weight_grads",
        **params((6 * rows * D * wide, 12 * D * wide)),
    )(xr, low, act, d_gate, d_up)


def mix_body(
    h_ref, g_ref, pr_ref, rt_ref, tc_ref, ret_ref, n_ref, sw_ref, rows_ref,
    out_ref, gn_ref, gl_ref, gs_ref,
):
    t = h_ref.shape[0]
    slots = ret_ref.shape[0]
    hidden = h_ref[...]
    g16 = g_ref[...]
    g = g16.astype(F32)
    pr = pr_ref[...]
    scale = lax.rsqrt(jnp.mean(hidden * hidden, axis=-1, keepdims=True) + EPS)
    normed = hidden * scale * rows_ref[2:3, :]
    lane = lax.broadcasted_iota(jnp.int32, (t, LANES), 1)
    slot = lax.broadcasted_iota(jnp.int32, (t, slots), 1)
    first = EXPERTS + 4
    ret = ret_ref[...]
    c0 = [pr[:, first + 2 * k : first + 2 * k + 1] for k in range(2)]
    c1 = [pr[:, first + 2 * k + 1 : first + 2 * k + 2] for k in range(2)]
    total = hidden
    s = jnp.zeros((t, LANES), F32)
    coef = jnp.zeros((t, 1), F32)
    weight = [jnp.zeros((t, 1), F32) for _ in range(2)]
    for j in range(2):
        route = rt_ref[:, j : j + 1]
        mix = pr[:, 16 + j : 17 + j]
        branch = dot((slot == tc_ref[:, j : j + 1]).astype(BF16), ret)
        keep = jnp.where(route == EXPERTS + 1, 1.0, 0.0)
        for k in range(2):
            here = jnp.where(route == EXPERTS + 2 + k, 1.0, 0.0)
            keep = keep + here * c0[k]
            weight[k] = weight[k] + here * mix
            branch = branch + (here * c1[k]) * rows_ref[k : k + 1, :]
        branch = branch + keep * normed
        coef = coef + mix * keep
        total = total + mix * branch
        gp = jnp.sum(g * branch, axis=-1, keepdims=True)
        s = s + jnp.where(lane == route, gp, 0.0)
    out_ref[...] = total.astype(BF16)
    probs = jnp.where(lane < first, pr, 0.0)
    d_logits = probs * (s - jnp.sum(probs * s, axis=-1, keepdims=True))
    gl_ref[...] = d_logits
    dz = d_logits
    dvec = jnp.zeros((t, LANES), F32)
    g_dot_n = jnp.sum(g * normed, axis=-1, keepdims=True)
    for k in range(2):
        d0 = weight[k] * g_dot_n
        d1 = weight[k] * jnp.sum(g * rows_ref[k : k + 1, :], axis=-1, keepdims=True)
        mean = c0[k] * d0 + c1[k] * d1
        dz = jnp.where(lane == first + 2 * k, c0[k] * (d0 - mean), dz)
        dz = jnp.where(lane == first + 2 * k + 1, c1[k] * (d1 - mean), dz)
        dvec = jnp.where(lane == 16 + k, weight[k] * c1[k], dvec)
    hi, lo = split_hi_lo(dz)
    sw = sw_ref[...]
    gn_ref[...] = coef * g + (dot_nt(hi, sw) + dot_nt(lo, sw))
    nt = n_ref[...].T
    gt = g16.T
    vhi, vlo = split_hi_lo(dvec)
    gs = dot(nt, hi) + dot(nt, lo) + dot(gt, vhi) + dot(gt, vlo)

    @pl.when(pl.program_id(0) == 0)
    def _():
        gs_ref[...] = gs

    @pl.when(pl.program_id(0) > 0)
    def _():
        gs_ref[...] += gs


def mix_call(hidden, g, pr, rt, tc, ret, low, sw, rows):
    t = hidden.shape[0]
    half = min(t, LANES)
    slots = ret.shape[0]
    tile = spec((half, D), lambda i: (i, 0))
    lane_tile = spec((half, LANES), lambda i: (i, 0))
    pair = spec((half, 2), lambda i: (i, 0))
    return pl.pallas_call(
        mix_body,
        grid=(t // half,),
        in_specs=[
            tile, tile, lane_tile, pair, pair, whole((slots, D)), tile, whole((D, LANES)),
            whole((8, D)),
        ],
        out_specs=[tile, tile, lane_tile, whole((D, LANES))],
        out_shape=[
            shape((t, D), BF16), shape((t, D), F32), shape((t, LANES), F32), shape((D, LANES), F32),
        ],
        name="mixture",
        **params((4 * t * slots * D, 12 * t * D)),
    )(hidden, g, pr, rt, tc, ret, low, sw, rows)


def norm_back_body(
    h_ref, g_ref, gn_ref, tc_ref, ret_ref, rows_ref, ow_ref, att_ref,
    gh_ref, do_ref, dot_ref, gow_ref, gg_ref,
):
    t = h_ref.shape[0]
    slots = ret_ref.shape[0]
    hidden = h_ref[...]
    slot = lax.broadcasted_iota(jnp.int32, (t, slots), 1)
    pick = (slot == tc_ref[:, 0:1]) | (slot == tc_ref[:, 1:2])
    gn = gn_ref[...] + dot(pick.astype(BF16), ret_ref[...])
    q = lax.rsqrt(jnp.mean(hidden * hidden, axis=-1, keepdims=True) + EPS)
    u = gn * rows_ref[2:3, :]
    mean = jnp.mean(u * hidden, axis=-1, keepdims=True)
    gh = g_ref[...].astype(F32) + q * u - hidden * (q * q * q * mean)
    gh_ref[...] = gh
    gb = gh.astype(BF16)
    d_out = dot_nt(gb, ow_ref[...]).astype(BF16)
    do_ref[...] = d_out
    dot_ref[...] = d_out.T
    gow = dot(att_ref[...].T, gb)
    gain = jnp.sum(gn * hidden * q, axis=0, keepdims=True)

    @pl.when(pl.program_id(0) == 0)
    def _():
        gow_ref[...] = gow
        gg_ref[...] = jnp.broadcast_to(gain, gg_ref.shape)

    @pl.when(pl.program_id(0) > 0)
    def _():
        gow_ref[...] += gow
        gg_ref[...] += jnp.broadcast_to(gain, gg_ref.shape)


def norm_back_call(hidden, g, gn, tc, ret, rows, ow, att):
    t = hidden.shape[0]
    half = t // 2 if (t // 2) % LANES == 0 else t
    slots = ret.shape[0]
    tile = spec((half, D), lambda i: (i, 0))
    return pl.pallas_call(
        norm_back_body,
        grid=(t // half,),
        in_specs=[
            tile, tile, tile, spec((half, 2), lambda i: (i, 0)), whole((slots, D)), whole((8, D)),
            whole((D, D)), tile,
        ],
        out_specs=[tile, tile, spec((D, half), lambda i: (0, i)), whole((D, D)), whole((8, D))],
        out_shape=[
            shape((t, D), F32), shape((t, D), BF16), shape((D, t), BF16), shape((D, D), F32),
            shape((8, D), F32),
        ],
        name="norm_two_back",
        **params((2 * t * slots * D + 4 * t * D * D, 16 * t * D), VMEM_SMALL),
    )(hidden, g, gn, tc, ret, rows, ow, att)


def turn_body(x_ref, o_ref):
    o_ref[...] = x_ref[...].T


def turn(x):
    rows, wide = x.shape
    part = 256
    return pl.pallas_call(
        turn_body,
        grid=(wide // part,),
        in_specs=[spec((rows, part), lambda i: (0, i))],
        out_specs=spec((part, rows), lambda i: (i, 0)),
        out_shape=shape((wide, rows), x.dtype),
        name="turn",
        **params((rows * wide, 4 * rows * wide)),
    )(x)


def store_grad(sc_ref, split, value, refs):
    if not split:
        refs[0][...] = value
        return
    send_ref, keep_ref = refs
    per = value.shape[0] // 4
    for core in range(2):

        @pl.when(sc_ref[11] == core)
        def _():
            for part in range(2):
                mine = (2 * part + core) * per
                other = (2 * part + 1 - core) * per
                send_ref[part] = value[other : other + per].astype(BF16)
                keep_ref[part] = value[mine : mine + per]


def grad_outs(split, width):
    block = 2 * LANES
    if not split:
        return [spec((D, block), lambda i: (0, i))], [shape((D, width), F32)]
    dims = (2, D // 4, width)
    tile = spec((2, D // 4, block), lambda i: (0, 0, i))
    return [tile, tile], [shape(dims, BF16), shape(dims, F32)]


def q_back_body(split, sc_ref, nt_ref, dq_ref, c_ref, s_ref, w_ref, gn_ref, *refs):
    step = pl.program_id(0)
    cosine = c_ref[...]
    sine = s_ref[...]
    v0 = dq_ref[:, :LANES]
    v1 = dq_ref[:, LANES:]
    gq = jnp.concatenate(
        [
            (v0 * cosine - partner(v0) * sine).astype(BF16),
            (v1 * cosine - partner(v1) * sine).astype(BF16),
        ],
        axis=1,
    )
    store_grad(sc_ref, split, dot(nt_ref[...], gq), refs)
    gn = dot_nt(gq, w_ref[...])

    @pl.when(step == 0)
    def _():
        gn_ref[...] = gn

    @pl.when(step > 0)
    def _():
        gn_ref[...] += gn


def q_back_call(sc, low_t, dq, cosine, sine, pack, split):
    t = low_t.shape[1]
    specs, shapes = grad_outs(split, D)
    return pl.pallas_call(
        functools.partial(q_back_body, split),
        grid=(PAIRS // 2,),
        in_specs=[
            SMEM_SPEC, whole((D, t)), spec((t, 2 * LANES), lambda i: (0, i)), whole((t, LANES)),
            whole((t, LANES)), spec((D, 2 * LANES), lambda i: (0, i)),
        ],
        out_specs=[whole((t, D))] + specs,
        out_shape=[shape((t, D), F32)] + shapes,
        name="q_back",
        **params((4 * t * D * D, 12 * t * D)),
    )(sc, low_t, dq, cosine, sine, pack)


def kv_back_body(
    split, count, sc_ref, x_ref, nt_ref, gnq_ref, gh_ref, gain_ref, c_ref, s_ref, wk_ref, wv_ref,
    own_ref, cont_ref, *refs
):
    got_refs, refs = refs[:count], refs[count:]
    gi_ref, grads, gn_ref = refs[0], refs[1:-1], refs[-1]
    step = pl.program_id(0)

    @pl.when(step == 0)
    def _():
        gn_ref[...] = gnq_ref[...]

    own = own_ref[...]
    for got in got_refs:
        own = own + got[...].astype(F32)
    total = jnp.concatenate([own, cont_ref[...]], axis=0)
    k = total[:, :LANES]
    gk = (k * c_ref[...] - partner(k) * s_ref[...]).astype(BF16)
    gkv = jnp.concatenate([gk, total[:, LANES:].astype(BF16)], axis=1)
    store_grad(sc_ref, split, dot(nt_ref[...], gkv), grads)
    gn_ref[...] += dot_nt(gkv, jnp.concatenate([wk_ref[...], wv_ref[...]], axis=1))

    @pl.when(step == pl.num_programs(0) - 1)
    def _():
        gn = gn_ref[...]
        x = x_ref[...].astype(F32)
        q = lax.rsqrt(jnp.mean(x * x, axis=-1, keepdims=True) + EPS)
        u = gn * gain_ref[...]
        mean = jnp.mean(u * x, axis=-1, keepdims=True)
        gi_ref[...] = gh_ref[...] + q * u - x * (q * q * q * mean)


def kv_back_call(sc, x, low_t, gn, gh, gain, cosine, sine, pack, own, cont, got, split):
    t = x.shape[0]
    r = t // 2
    specs, shapes = grad_outs(split, 2 * D)
    wide = spec((r, 2 * LANES), lambda i: (0, i))
    return pl.pallas_call(
        functools.partial(kv_back_body, split, len(got)),
        grid=(PAIRS,),
        in_specs=[
            SMEM_SPEC, whole((t, D)), whole((D, t)), whole((t, D)), whole((t, D)), whole((1, D)),
            whole((t, LANES)), whole((t, LANES)),
            spec((D, LANES), lambda i: (0, PAIRS + i)),
            spec((D, LANES), lambda i: (0, 2 * PAIRS + i)),
            wide, wide,
        ]
        + [wide] * len(got),
        out_specs=[whole((t, D))] + specs,
        out_shape=[shape((t, D), F32)] + shapes,
        scratch_shapes=[pltpu.VMEM((t, D), F32)],
        name="kv_back",
        **params((8 * t * D * D, 24 * t * D)),
    )(sc, x, low_t, gn, gh, gain, cosine, sine, pack, pack, own, cont, *got)


def rotation_tables(position):
    half = HEAD_DIM // 2
    frequency = 10000.0 ** (-jnp.arange(half, dtype=F32) / half)
    angles = position[:, None] * frequency[None, :]
    cosine, sine = jnp.cos(angles), jnp.sin(angles)
    return (
        jnp.concatenate([cosine] * 4, axis=1),
        jnp.concatenate([-sine, sine, -sine, sine], axis=1),
    )


def to_rows(array):
    return jnp.transpose(array, (1, 0, 2)).reshape(2 * array.shape[0], array.shape[2])


def from_rows(array):
    r = array.shape[0] // 2
    return jnp.transpose(array.reshape(2, r, array.shape[1]), (1, 0, 2))


RING = (0, 2, 4, 6, 7, 5, 3, 1)


def ring_offsets():
    place = {e: i for i, e in enumerate(RING)}
    return [[RING[(place[e] + k) % 8] for k in range(8)] for e in range(8)]


def along_ring(array, step):
    pairs = [(RING[i], RING[(i + step) % 8]) for i in range(8)]
    return lax.ppermute(array, "expert", pairs)


def tie(*values):
    return lax.optimization_barrier(values)


def swap_core(array):
    return lax.ppermute(array, "dp", [(0, 1), (1, 0), (2, 3), (3, 2)])


def add_and_cross(keep, got):
    across = lax.axis_index("dp") // 2
    keep = keep + got.astype(F32)
    send = lax.dynamic_index_in_dim(keep, 1 - across, 0, keepdims=False).astype(BF16)
    mine = lax.dynamic_index_in_dim(keep, across, 0, keepdims=False)
    return mine, lax.ppermute(send, "dp", [(0, 2), (2, 0), (1, 3), (3, 1)])


def add_and_scatter(keep, got):
    keep = (keep + got.astype(F32)).astype(BF16)
    rows, w = keep.shape
    return lax.all_to_all(
        keep.reshape(8, rows // 8, w), "expert", split_axis=0, concat_axis=0, tiled=True
    )


def add_up(got):
    return jnp.sum(got.astype(F32), axis=0)


def scatter_all(array):
    return lax.psum_scatter(
        array.astype(BF16), ALL_AXES, scatter_dimension=0, tiled=True
    ).astype(F32)


def per_device(
    hidden_in, cotangent, gate_residual, routes, groups, lengths, attn_gain, qkv_weight, out_weight,
    ffn_gain, router_weight, const_proj, const_vec, gate_weight, up_weight, down_weight,
):
    del groups
    r = hidden_in.shape[0]
    t = 2 * r
    capacity = r // 2
    owners = lax.axis_size("expert")
    copies = owners // EXPERTS
    slots = EXPERTS * capacity
    me = lax.axis_index("expert")
    per_cont = max(CONT_LEN // r, 1)

    small = jnp.concatenate(
        [
            router_weight, const_proj, const_vec, attn_gain[:, None], ffn_gain[:, None],
            jnp.zeros((attn_gain.shape[0], LANES - 20), BF16),
        ],
        axis=1,
    )
    pack = lax.all_gather(
        jnp.concatenate([qkv_weight, out_weight, small], axis=1), ALL_AXES, axis=0, tiled=True
    )
    index = jnp.arange(r, dtype=jnp.int32)
    row_ids = me * r + index
    position = jnp.concatenate([row_ids, PROMPT + row_ids % CONT_LEN]).astype(F32)
    cosine, sine = rotation_tables(position)
    cont = (me * r) // CONT_LEN
    length = lax.dynamic_slice(lengths, (cont,), (1,))
    header = jnp.stack([me, (me * r) % CONT_LEN]).astype(jnp.int32)
    header = jnp.concatenate([header, length.astype(jnp.int32)])
    ring = owners == 8
    if ring:
        ids = lax.dynamic_index_in_dim(jnp.asarray(ring_offsets(), jnp.int32), me, 0, keepdims=False)
    else:
        ids = jnp.arange(owners, dtype=jnp.int32)
    sc = jnp.concatenate([header, ids, (lax.axis_index("dp") % 2).astype(jnp.int32)[None]])

    picked = to_rows(routes)
    flat = jnp.transpose(picked).reshape(2 * t)
    hot = flat[:, None] == jnp.arange(EXPERTS, dtype=jnp.int32)[None, :]
    earlier = jnp.arange(2 * t)[:, None] > jnp.arange(2 * t)[None, :]
    before = jnp.dot(earlier.astype(BF16), hot.astype(BF16), preferred_element_type=F32)
    slot_index = jnp.sum(jnp.where(hot, before, 0.0), axis=1).astype(jnp.int32)
    target = jnp.where(flat < EXPERTS, flat * capacity + slot_index, -1)
    target_rows = target.reshape(2, t)
    target_cols = jnp.transpose(target_rows)

    def to_owners(rows):
        w = rows.shape[-1]
        shaped = rows.reshape(EXPERTS, 1, capacity, w)
        return jnp.broadcast_to(shaped, (EXPERTS, copies, capacity, w)).reshape(owners, capacity, w)

    def exchange(rows):
        got = lax.all_to_all(rows, "expert", split_axis=0, concat_axis=0, tiled=True)
        return got.reshape(owners * got.shape[1], got.shape[2])

    def from_owners(rows):
        got = exchange(rows.reshape(owners, capacity, D))
        if copies == 1:
            return got
        got = got.reshape(EXPERTS, copies, capacity, D).astype(F32)
        return jnp.sum(got, axis=1).reshape(slots, D).astype(BF16)

    x = to_rows(hidden_in)
    g = to_rows(cotangent)
    out_w, small_w = pack[:, 3 * D : 4 * D], pack[:, 4 * D :]
    small_rows = jnp.transpose(pack[:, 4 * D + 16 : 4 * D + 24]).astype(F32)
    gain_one = small_rows[2:3]
    rows_two = jnp.concatenate([small_rows[0:2], small_rows[3:4], small_rows[3:8]], axis=0)
    gain_two = small_rows[3:4]

    low_one, q, q_t, kv_prompt, kv_cont = qkv_call(x, gain_one, pack, cosine, sine)
    if not ring:
        kv_all = lax.all_gather(kv_prompt, "expert", axis=0, tiled=True)
    if per_cont == 1:
        kv_own = kv_cont
    else:
        cont_groups = [
            [c * per_cont + i for i in range(per_cont)] for c in range(owners // per_cont)
        ]
        kv_own = lax.all_gather(
            kv_cont, "expert", axis=0, tiled=True, axis_index_groups=cont_groups
        )
    weights = lax.all_gather(
        jnp.stack([gate_weight, up_weight, down_weight]), "dp", axis=0, tiled=False
    )
    if ring:
        right, left = [kv_prompt], [kv_prompt]
        for i in range(3):
            right.append(along_ring(right[i], 1))
            left.append(along_ring(left[i], -1))
            if i == 0:
                st, acc = fwd_local(sc, q_t, kv_prompt, kv_own)
            else:
                st, acc = fwd_remote(sc, q_t, (right[i], left[i]), (8 - i, i), st, acc)
            right[i + 1], left[i + 1], st, out_w, small_w = tie(
                right[i + 1], left[i + 1], st, out_w, small_w
            )
        far = [along_ring(right[3][:, :D], 1), along_ring(left[3][:, D:], -1)]
        st, acc = fwd_remote(sc, q_t, (right[3], left[3]), (5, 3), st, acc)
        st, att_t, att = fwd_remote(sc, q_t, far, (4,), st, acc, halves=True, final=True)
    else:
        st, acc = fwd_local(sc, q_t, kv_prompt, kv_own)
        st, att_t, att = fwd_remote(sc, q_t, (kv_all,), range(owners), st, acc, final=True)

    res = jnp.pad(to_rows(gate_residual), ((0, 0), (0, LANES - EXPERTS - 4)))
    hidden, low_two, pr, x_send = route_call(
        x, att, out_w, small_w, gain_two, res, picked, target_rows, slots
    )
    x_got = exchange(to_owners(x_send))
    g_send = grad_rows_call(g, pr, target_rows, slots)
    low_one_t = turn(low_one)
    x_got, g_send = tie(x_got, g_send)
    g_got = exchange(to_owners(g_send))
    expert_rows, gate_pre, up_pre = expert_fwd(x_got, weights)
    out_back = from_owners(expert_rows)
    grad_in, act, d_gate, d_up = expert_in(gate_pre, up_pre, g_got, weights)
    in_back = from_owners(grad_in)
    output, gn, grad_logits, grad_small = mix_call(
        hidden, g, pr, picked, target_cols, out_back, low_two, small_w, rows_two
    )
    act, gn = tie(act, gn)
    grad_w = expert_weights(x_got, g_got, act, d_gate, d_up, weights.shape)
    grad_expert = lax.psum_scatter(
        grad_w.reshape(-1, grad_w.shape[-1]), "dp", scatter_dimension=0, tiled=True
    )
    per = gate_weight.shape[0]
    grad_expert = [grad_expert[i * per : (i + 1) * per].astype(F32) for i in range(3)]
    gh, d_att, d_att_t, grad_ow, gg_two = norm_back_call(
        hidden, g, gn, target_cols, in_back, rows_two, out_w, att
    )

    early = jnp.concatenate(
        [grad_ow, grad_small[:, :19], jnp.transpose(gg_two[0:1]), jnp.zeros((D, LANES - 20), F32)],
        axis=1,
    )
    back = (sc, q_t, q, d_att_t, d_att)
    if ring:
        parts = early.reshape(2, 2, D // 4, D + LANES)
        core = lax.axis_index("dp") % 2
        early_keep = lax.dynamic_index_in_dim(parts, core, 1, keepdims=False)
        early_got = swap_core(
            lax.dynamic_index_in_dim(parts, 1 - core, 1, keepdims=False).astype(BF16)
        )
        dq_t, send_r, send_l, st = bwd_remote(
            *back, st, att_t, far, (4,), halves=True, first=True, dtype=BF16
        )
        for i in range(3, 0, -1):
            got_r, got_l = along_ring(send_r, 1), along_ring(send_l, -1)
            dq_t, part_r, part_l = bwd_remote(
                *back, st, dq_t, (left[i], right[i]), (i, 8 - i), dtype=BF16
            )
            got_r, got_l, part_r, part_l, dq_t, early_got = tie(
                got_r, got_l, part_r, part_l, dq_t, early_got
            )
            send_r, send_l = ring_add(part_r, got_r, part_l, got_l)
            if i == 3:
                early_keep, early_got = add_and_cross(early_keep, early_got)
        send_r, send_l, dq_t = tie(send_r, send_l, dq_t)
        got_r = along_ring(send_r, 1)
        got_l = along_ring(send_l, -1)
        got = (got_r, got_l)
        dq, dkv_own, dkv_cont = bwd_local(*back, st, dq_t, kv_prompt, kv_own)
    else:
        dq_t, dkv_all, st = bwd_remote(
            *back, st, att_t, (kv_all,), range(owners), first=True, dtype=BF16
        )
        dq, dkv_own, dkv_cont = bwd_local(*back, st, dq_t, kv_prompt, kv_own)
        got = (lax.psum_scatter(dkv_all, "expert", scatter_dimension=0, tiled=True),)
        early = scatter_all(early)
    if per_cont > 1:
        dkv_cont = lax.psum_scatter(
            dkv_cont, "expert", scatter_dimension=0, tiled=True, axis_index_groups=cont_groups
        )
    gn_q, *grad_q = q_back_call(sc, low_one_t, dq, cosine, sine, pack, ring)
    if ring:
        got_q = swap_core(grad_q[0])
        keep_q, got_q = add_and_cross(grad_q[1], got_q)
        keep_q, *got = tie(keep_q, *got)
    grad_input, *grad_kv = kv_back_call(
        sc, x, low_one_t, gn_q, gh, gain_one, cosine, sine, pack, dkv_own, dkv_cont, got, ring
    )
    output, grad_input = from_rows(output), from_rows(grad_input)
    if ring:
        got_kv = swap_core(grad_kv[0])
        keep_kv, got_kv = add_and_cross(grad_kv[1], got_kv)
        keep_kv, got_q, early_got = tie(keep_kv, got_q, early_got)
        got_q = add_and_scatter(
            jnp.concatenate([early_keep, keep_q], axis=1),
            jnp.concatenate([early_got, got_q], axis=1),
        )
        got_kv, output, grad_input, *grad_expert = tie(got_kv, output, grad_input, *grad_expert)
        summed = add_up(got_q)
        early, late_q = summed[:, : D + LANES], summed[:, D + LANES :]
        late_kv = add_up(add_and_scatter(keep_kv, got_kv))
    else:
        late_q, late_kv = scatter_all(grad_q[0]), scatter_all(grad_kv[0])
    per = late_kv.shape[0]
    late_kv = jnp.transpose(late_kv.reshape(per, PAIRS, 2, LANES), (0, 2, 1, 3))
    late = jnp.concatenate([late_q, late_kv.reshape(per, 2 * D)], axis=1)
    grad_gain = jnp.sum(late * qkv_weight.astype(F32), axis=1) / attn_gain.astype(F32)
    tail = early[:, D:]
    return (
        output,
        grad_input,
        from_rows(grad_logits)[:, :, : EXPERTS + 4],
        grad_gain,
        late,
        early[:, :D],
        tail[:, 19],
        tail[:, :12],
        tail[:, 12:16],
        tail[:, 16:18],
        grad_expert[0],
        grad_expert[1],
        grad_expert[2],
    )


def solution(mesh):
    rows = P(ALL_AXES, None, None)
    flat = P(ALL_AXES)
    mat = P(ALL_AXES, None)
    expert = P("dp", "expert")
    in_specs = (
        rows, rows, rows, rows, P("dp"), P("dp"), flat, mat, mat, flat, mat, mat, mat,
        expert, expert, expert,
    )
    out_specs = (
        rows, rows, rows, flat, mat, mat, flat, mat, mat, mat, expert, expert, expert,
    )

    return jax.shard_map(
        per_device, mesh=mesh, in_specs=in_specs, out_specs=out_specs, check_vma=False
    )
```

```python
import functools

import jax
import jax.numpy as jnp
from jax import lax
from jax.experimental import pallas as pl
from jax.experimental.pallas import tpu as pltpu
from jax.sharding import PartitionSpec as P


D = 768
HEAD_DIM = 64
PAIRS = 6
EXPERTS = 8
CONT_LEN = 256
PROMPT = 2048
LANES = 128
EPS = 1e-06
NEG = -1e30
LOG2E = 1.4426950408889634
SCALE = float(HEAD_DIM) ** (-0.5)
LC = SCALE * LOG2E
F32 = jnp.float32
BF16 = jnp.bfloat16
ALL_AXES = ("dp", "expert")
VMEM_LIMIT = 60 * 1024 * 1024


def dot(a, b):
    return jnp.dot(a, b, preferred_element_type=F32)


def dot_nt(a, b):
    return lax.dot_general(a, b, (((1,), (1,)), ((), ())), preferred_element_type=F32)


def split_hi_lo(v):
    hi = v.astype(BF16)
    return hi, (v - hi.astype(F32)).astype(BF16)


def params(cost=None, limit=VMEM_LIMIT):
    return dict(
        compiler_params=pltpu.CompilerParams(vmem_limit_bytes=limit),
        cost_estimate=None if cost is None else pl.CostEstimate(
            flops=int(cost[0]), bytes_accessed=int(cost[1]), transcendentals=0
        ),
    )


def shape(dims, dtype):
    return jax.ShapeDtypeStruct(tuple(dims), dtype)


def spec(block, index):
    return pl.BlockSpec(tuple(block), index)


def whole(dims):
    return pl.BlockSpec(tuple(dims), lambda *_: (0,) * len(dims))


SMEM_SPEC = pl.BlockSpec(memory_space=pltpu.SMEM)


def partner(v):
    lane = lax.broadcasted_iota(jnp.int32, v.shape, 1)
    return jnp.where((lane & 63) < 32, pltpu.roll(v, 96, 1), pltpu.roll(v, 32, 1))


def qkv_body(x_ref, gain_ref, wq_ref, wk_ref, wv_ref, c_ref, s_ref, n_ref, q_ref, qt_ref, kvp_ref, kvc_ref):
    @pl.when(pl.program_id(0) == 0)
    def _():
        x = x_ref[...].astype(F32)
        scale = lax.rsqrt(jnp.mean(x * x, axis=-1, keepdims=True) + EPS)
        n_ref[...] = (x * scale * gain_ref[...]).astype(BF16)

    n = n_ref[...]
    cosine = c_ref[...]
    sine = s_ref[...]
    kv = dot(n, jnp.concatenate([wk_ref[...], wv_ref[...]], axis=1))
    k = kv[:, :LANES]
    k = (k * cosine + partner(k) * sine).astype(BF16)
    v = kv[:, LANES:].astype(BF16)
    r = k.shape[0] // 2
    kvp_ref[:, :LANES] = k[:r]
    kvp_ref[:, LANES:] = v[:r]
    kvc_ref[:, :LANES] = k[r:]
    kvc_ref[:, LANES:] = v[r:]
    q = dot(n, wq_ref[...])
    q = q * cosine + partner(q) * sine
    q = q.astype(BF16)
    q_ref[...] = q
    qt_ref[...] = q.T


def qkv_call(x, gain, pack, cosine, sine):
    t = x.shape[0]
    return pl.pallas_call(
        qkv_body,
        grid=(PAIRS,),
        in_specs=[
            whole((t, D)),
            whole((1, D)),
            spec((D, LANES), lambda i: (0, i)),
            spec((D, LANES), lambda i: (0, PAIRS + i)),
            spec((D, LANES), lambda i: (0, 2 * PAIRS + i)),
            whole((t, LANES)),
            whole((t, LANES)),
        ],
        out_specs=[
            whole((t, D)),
            spec((t, LANES), lambda i: (0, i)),
            spec((LANES, t), lambda i: (i, 0)),
            spec((t // 2, 2 * LANES), lambda i: (0, i)),
            spec((t // 2, 2 * LANES), lambda i: (0, i)),
        ],
        out_shape=[
            shape((t, D), BF16),
            shape((t, D), BF16),
            shape((D, t), BF16),
            shape((t // 2, 2 * D), BF16),
            shape((t // 2, 2 * D), BF16),
        ],
        name="qkv_rope",
        **params((2 * t * D * 3 * D, 6 * D * D)),
    )(x, gain, pack, pack, pack, cosine, sine)


def head_rows(v, h):
    row = lax.broadcasted_iota(jnp.int32, v.shape, 0)
    return jnp.where(row // HEAD_DIM == h, v, jnp.zeros_like(v))


def head_lanes(v, h):
    lane = lax.broadcasted_iota(jnp.int32, v.shape, 1)
    return jnp.where(lane // HEAD_DIM == h, v, jnp.zeros_like(v))


def attend_update(qz, kb, vt, lo, hi, mask, st_ref, a_ref, first):
    for h in range(2):
        s = dot(kb, qz[h][:, lo:hi])
        if mask is not None:
            s = jnp.where(mask, s, NEG)
        top = jnp.max(s, axis=0, keepdims=True)
        rows = slice(h * HEAD_DIM, (h + 1) * HEAD_DIM)
        if first:
            p = jnp.exp2((s - top) * LC)
            st_ref[h : h + 1, lo:hi] = top
            st_ref[2 + h : 3 + h, lo:hi] = jnp.sum(p, axis=0, keepdims=True)
            a_ref[rows, lo:hi] = dot(vt[rows], p.astype(BF16))
        else:
            old = st_ref[h : h + 1, lo:hi]
            new = jnp.maximum(old, top)
            alpha = jnp.exp2((old - new) * LC)
            p = jnp.exp2((s - new) * LC)
            st_ref[h : h + 1, lo:hi] = new
            st_ref[2 + h : 3 + h, lo:hi] = st_ref[2 + h : 3 + h, lo:hi] * alpha + jnp.sum(
                p, axis=0, keepdims=True
            )
            a_ref[rows, lo:hi] = a_ref[rows, lo:hi] * alpha + dot(vt[rows], p.astype(BF16))


def local_masks(sc_ref, r, keys, lo, hi):
    cpos = sc_ref[1]
    length = sc_ref[2]
    col = lo + lax.broadcasted_iota(jnp.int32, (r, hi - lo), 1)
    row = lax.broadcasted_iota(jnp.int32, (r, hi - lo), 0)
    own = (row <= col) | (col >= r)
    col = lo + lax.broadcasted_iota(jnp.int32, (keys, hi - lo), 1)
    row = lax.broadcasted_iota(jnp.int32, (keys, hi - lo), 0)
    cont = (col >= r) & (row <= cpos + col - r) & (row < length)
    return own, cont


def fwd_local_body(sc_ref, qt_ref, kv_ref, kvo_ref, st_ref, a_ref):
    t = qt_ref.shape[1]
    r = t // 2
    keys = kvo_ref.shape[0]
    qt = qt_ref[...]
    qz = [head_rows(qt, h) for h in range(2)]
    kb = kv_ref[:, :LANES]
    vt = kv_ref[:, LANES:].T
    kbo = kvo_ref[:, :LANES]
    vto = kvo_ref[:, LANES:].T
    st_ref[...] = jnp.zeros_like(st_ref)
    own, cont = local_masks(sc_ref, r, keys, 0, t)
    attend_update(qz, kb, vt, 0, t, own, st_ref, a_ref, True)
    if r % LANES == 0:
        attend_update(qz, kbo, vto, r, t, cont[:, r:], st_ref, a_ref, False)
    else:
        attend_update(qz, kbo, vto, 0, t, cont, st_ref, a_ref, False)


def halves_value(a_ref, b_ref):
    return jnp.where(pl.program_id(0) < PAIRS // 2, a_ref[...], b_ref[...])


def fwd_remote_body(offsets, count, halves, final, sc_ref, qt_ref, *refs):
    kv_refs, refs = refs[:count], refs[count:]
    st_in, a_in, st_ref, a_ref = refs[:4]
    t = qt_ref.shape[1]
    r = t // 2
    me = sc_ref[0]
    qt = qt_ref[...]
    qz = [head_rows(qt, h) for h in range(2)]
    st_ref[...] = st_in[...]
    a_ref[...] = a_in[...]
    for j, offset in enumerate(offsets):
        block = sc_ref[3 + offset]

        def go(lo, hi, mask):
            if halves:
                kv = halves_value(*kv_refs)
            elif len(kv_refs) == len(offsets):
                kv = kv_refs[j][...]
            else:
                kv = kv_refs[0][j * r : (j + 1) * r, :]
            attend_update(qz, kv[:, :LANES], kv[:, LANES:].T, lo, hi, mask, st_ref, a_ref, False)

        if r % LANES == 0:

            @pl.when(block < me)
            def _():
                go(0, t, None)

            @pl.when(block > me)
            def _():
                go(r, t, None)

        else:

            @pl.when(block != me)
            def _():
                col = lax.broadcasted_iota(jnp.int32, (r, t), 1)
                go(0, t, (col >= r) | (block < me))

    if final:
        low_ref = refs[4]
        for h in range(2):
            rows = slice(h * HEAD_DIM, (h + 1) * HEAD_DIM)
            total = st_ref[2 + h : 3 + h, :]
            a_ref[rows, :] = a_ref[rows, :] / total
            st_ref[h : h + 1, :] = st_ref[h : h + 1, :] * LC + jnp.log2(total)
        low_ref[...] = a_ref[...].astype(BF16).T


def kv_specs(kvs, halves):
    if halves:
        r = kvs[0].shape[0]
        return [
            spec((r, 2 * LANES), lambda i: (0, jnp.minimum(i, PAIRS // 2 - 1))),
            spec((r, 2 * LANES), lambda i: (0, jnp.maximum(i - PAIRS // 2, 0))),
        ]
    return [spec((kv.shape[0], 2 * LANES), lambda i: (0, i)) for kv in kvs]


def fwd_local(sc, qt, kv_prompt, kv_own):
    t = qt.shape[1]
    keys = kv_own.shape[0]
    return pl.pallas_call(
        fwd_local_body,
        grid=(PAIRS,),
        in_specs=[
            SMEM_SPEC,
            spec((LANES, t), lambda i: (i, 0)),
            spec((t // 2, 2 * LANES), lambda i: (0, i)),
            spec((keys, 2 * LANES), lambda i: (0, i)),
        ],
        out_specs=[spec((8, t), lambda i: (i, 0)), spec((LANES, t), lambda i: (i, 0))],
        out_shape=[shape((8 * PAIRS, t), F32), shape((D, t), F32)],
        name="attend_local",
        **params((4 * 4 * t * keys * D, 4 * D * t)),
    )(sc, qt, kv_prompt, kv_own)


def fwd_remote(sc, qt, kvs, offsets, st, acc, halves=False, final=False):
    t = qt.shape[1]
    rows = len(offsets) * (t // 2)
    out_specs = [spec((8, t), lambda i: (i, 0)), spec((LANES, t), lambda i: (i, 0))]
    out_shape = [shape((8 * PAIRS, t), F32), shape((D, t), F32)]
    if final:
        out_specs.append(spec((t, LANES), lambda i: (0, i)))
        out_shape.append(shape((t, D), BF16))
    return pl.pallas_call(
        functools.partial(fwd_remote_body, tuple(offsets), len(kvs), halves, final),
        grid=(PAIRS,),
        in_specs=[SMEM_SPEC, spec((LANES, t), lambda i: (i, 0))]
        + kv_specs(kvs, halves)
        + [spec((8, t), lambda i: (i, 0)), spec((LANES, t), lambda i: (i, 0))],
        out_specs=out_specs,
        out_shape=out_shape,
        name="attend_remote",
        **params((4 * 4 * t * rows * D, 8 * D * t + 4 * D * rows)),
    )(sc, qt, *kvs, st, acc)


def back_block(ops, kb, vb, kt, lo, hi, mask, dq_ref):
    qz, qn, doz, don, lse, delta = ops
    dk = None
    dv = None
    for h in range(2):
        s = dot(kb, qz[h][:, lo:hi])
        dp = dot(vb, doz[h][:, lo:hi])
        p = jnp.exp2(s * LC - lse[h][:, lo:hi])
        if mask is not None:
            p = jnp.where(mask, p, 0.0)
        ds = (p * (dp - delta[h][:, lo:hi])).astype(BF16)
        dv_h = dot(p.astype(BF16), don[h][lo:hi])
        dk_h = dot(ds, qn[h][lo:hi])
        rows = slice(h * HEAD_DIM, (h + 1) * HEAD_DIM)
        dq_ref[rows, lo:hi] += dot(kt[rows], ds)
        dv = dv_h if dv is None else dv + dv_h
        dk = dk_h if dk is None else dk + dk_h
    return dk, dv


def back_operands(qt_ref, q_ref, dot_ref, do_ref, st_ref):
    qt, q, do_t, do = qt_ref[...], q_ref[...], dot_ref[...], do_ref[...]
    return (
        [head_rows(qt, h) for h in range(2)],
        [head_lanes(q, h) for h in range(2)],
        [head_rows(do_t, h) for h in range(2)],
        [head_lanes(do, h) for h in range(2)],
        [st_ref[h : h + 1, :] for h in range(2)],
        [st_ref[4 + h : 5 + h, :] for h in range(2)],
    )


def bwd_local_body(
    sc_ref, qt_ref, q_ref, dot_ref, do_ref, st_ref, dq_in, kv_ref, kvo_ref,
    out_ref, dkv_ref, dkvo_ref, dq_ref,
):
    t = qt_ref.shape[1]
    r = t // 2
    keys = kvo_ref.shape[0]
    ops = back_operands(qt_ref, q_ref, dot_ref, do_ref, st_ref)
    dq_ref[...] = dq_in[...]
    kb, vb = kv_ref[:, :LANES], kv_ref[:, LANES:]
    kbo, vbo = kvo_ref[:, :LANES], kvo_ref[:, LANES:]
    kt, kto = kb.T, kbo.T
    own, cont = local_masks(sc_ref, r, keys, 0, t)
    dk, dv = back_block(ops, kb, vb, kt, 0, t, own, dq_ref)
    if r % LANES == 0:
        dko, dvo = back_block(ops, kbo, vbo, kto, r, t, cont[:, r:], dq_ref)
    else:
        dko, dvo = back_block(ops, kbo, vbo, kto, 0, t, cont, dq_ref)
    dkv_ref[:, :LANES] = dk * SCALE
    dkv_ref[:, LANES:] = dv
    dkvo_ref[:, :LANES] = dko * SCALE
    dkvo_ref[:, LANES:] = dvo
    out_ref[...] = dq_ref[...].T * SCALE


def bwd_remote_body(
    offsets, count, halves, first, dtype, sc_ref, qt_ref, q_ref, dot_ref, do_ref, st_in, *refs
):
    t = qt_ref.shape[1]
    r = t // 2
    me = sc_ref[0]
    kv_refs, refs = refs[:count], refs[count:]
    src, refs = refs[0], refs[1:]
    dq_ref, refs = refs[0], refs[1:]
    out_refs, refs = refs[:count], refs[count:]
    if first:
        st_ref, refs = refs[0], refs[1:]
        st_ref[...] = st_in[...]
        prod = src[...] * dot_ref[...].astype(F32)
        for h in range(2):
            st_ref[4 + h : 5 + h, :] = jnp.sum(
                prod[h * HEAD_DIM : (h + 1) * HEAD_DIM], axis=0, keepdims=True
            )
        dq_ref[...] = jnp.zeros_like(dq_ref)
    else:
        st_ref = st_in
        dq_ref[...] = src[...]
    ops = back_operands(qt_ref, q_ref, dot_ref, do_ref, st_ref)
    split = len(offsets) != count and not halves

    def store(j, dk, dv):
        if halves:
            for part in range(2):

                @pl.when((pl.program_id(0) < PAIRS // 2) == (part == 0))
                def _():
                    out_refs[part][:, :LANES] = dk
                    out_refs[part][:, LANES:] = dv

        elif split:
            out_refs[0][j * r : (j + 1) * r, :LANES] = dk
            out_refs[0][j * r : (j + 1) * r, LANES:] = dv
        else:
            out_refs[j][:, :LANES] = dk
            out_refs[j][:, LANES:] = dv

    for j, offset in enumerate(offsets):
        block = sc_ref[3 + offset]

        def go(lo, mask):
            if halves:
                kv = halves_value(*kv_refs)
            elif split:
                kv = kv_refs[0][j * r : (j + 1) * r, :]
            else:
                kv = kv_refs[j][...]
            kb = kv[:, :LANES]
            dk, dv = back_block(ops, kb, kv[:, LANES:], kb.T, lo, t, mask, dq_ref)
            store(j, (dk * SCALE).astype(dtype), dv.astype(dtype))

        if split:

            @pl.when(block == me)
            def _():
                zero = jnp.zeros((r, LANES), dtype)
                store(j, zero, zero)

        if r % LANES == 0:

            @pl.when(block < me)
            def _():
                go(0, None)

            @pl.when(block > me)
            def _():
                go(r, None)

        else:

            @pl.when(block != me)
            def _():
                col = lax.broadcasted_iota(jnp.int32, (r, t), 1)
                go(0, (col >= r) | (block < me))


def add_low(a, b):
    return (a.astype(F32) + b.astype(F32)).astype(BF16)


def ring_add_body(half, pr_ref, gr_ref, pl_ref, gl_ref, sr_ref, sl_ref):
    if not half:
        sr_ref[...] = add_low(pr_ref[...], gr_ref[...])
        sl_ref[...] = add_low(pl_ref[...], gl_ref[...])
        return
    sr_ref[:, :D] = add_low(pr_ref[:, :D], gr_ref[...])
    sr_ref[:, D:] = pr_ref[:, D:]
    sl_ref[:, :D] = pl_ref[:, :D]
    sl_ref[:, D:] = add_low(pl_ref[:, D:], gl_ref[...])


def ring_add(part_r, got_r, part_l, got_l):
    r = part_r.shape[0]
    part = r // 2
    half = got_r.shape[1] == D
    wide = spec((part, 2 * D), lambda i: (i, 0))
    got = spec((part, got_r.shape[1]), lambda i: (i, 0))
    return pl.pallas_call(
        functools.partial(ring_add_body, half),
        grid=(2,),
        in_specs=[wide, got, wide, got],
        out_specs=[wide, wide],
        out_shape=[shape((r, 2 * D), BF16)] * 2,
        name="ring_add",
        **params((4 * r * D, 16 * r * D)),
    )(part_r, got_r, part_l, got_l)


def q_specs(t):
    return [
        spec((LANES, t), lambda i: (i, 0)),
        spec((t, LANES), lambda i: (0, i)),
        spec((LANES, t), lambda i: (i, 0)),
        spec((t, LANES), lambda i: (0, i)),
        spec((8, t), lambda i: (i, 0)),
    ]


def bwd_local(sc, qt, q, do_t, do, st, dq, kv_prompt, kv_own):
    t = qt.shape[1]
    keys = kv_own.shape[0]
    return pl.pallas_call(
        bwd_local_body,
        grid=(PAIRS,),
        in_specs=[SMEM_SPEC]
        + q_specs(t)
        + [spec((LANES, t), lambda i: (i, 0))]
        + kv_specs((kv_prompt, kv_own), False),
        out_specs=[spec((t, LANES), lambda i: (0, i))] + kv_specs((kv_prompt, kv_own), False),
        out_shape=[
            shape((t, D), F32),
            shape((t // 2, 2 * D), F32),
            shape((keys, 2 * D), F32),
        ],
        scratch_shapes=[pltpu.VMEM((LANES, t), F32)],
        name="attend_back_local",
        **params((10 * 4 * t * keys * D, 16 * D * t)),
    )(sc, qt, q, do_t, do, st, dq, kv_prompt, kv_own)


def bwd_remote(
    sc, qt, q, do_t, do, st, src, kvs, offsets, halves=False, first=False, dtype=F32
):
    t = qt.shape[1]
    rows = len(offsets) * (t // 2)
    out_specs = [spec((LANES, t), lambda i: (i, 0))] + kv_specs(kvs, halves)
    out_shape = [shape((D, t), F32)] + [shape(kv.shape, dtype) for kv in kvs]
    if first:
        out_specs.append(spec((8, t), lambda i: (i, 0)))
        out_shape.append(shape((8 * PAIRS, t), F32))
    return pl.pallas_call(
        functools.partial(bwd_remote_body, tuple(offsets), len(kvs), halves, first, dtype),
        grid=(PAIRS,),
        in_specs=[SMEM_SPEC]
        + q_specs(t)
        + kv_specs(kvs, halves)
        + [spec((LANES, t), lambda i: (i, 0))],
        out_specs=out_specs,
        out_shape=out_shape,
        name="attend_back_remote",
        **params((10 * 4 * t * rows * D, 16 * D * t + 8 * D * rows)),
    )(sc, qt, q, do_t, do, st, *kvs, src)


def route_body(
    x_ref, att_ref, ow_ref, sw_ref, gain_ref, res_ref, rt_ref, tr_ref,
    h_ref, n_ref, pr_ref, xs_ref,
):
    t = x_ref.shape[0]
    step = pl.program_id(0)

    @pl.when(step == 0)
    def _():
        hidden = x_ref[...].astype(F32) + dot(att_ref[...], ow_ref[...])
        h_ref[...] = hidden
        scale = lax.rsqrt(jnp.mean(hidden * hidden, axis=-1, keepdims=True) + EPS)
        low = (hidden * scale * gain_ref[...]).astype(BF16)
        n_ref[...] = low
        z = dot(low, sw_ref[...])
        lane = lax.broadcasted_iota(jnp.int32, (t, LANES), 1)
        is_route = lane < EXPERTS + 4
        logits = jnp.where(is_route, z + res_ref[...], NEG)
        ex = jnp.exp(logits - jnp.max(logits, axis=-1, keepdims=True))
        probs = ex / jnp.sum(ex, axis=-1, keepdims=True)
        out = probs
        first = EXPERTS + 4
        for k in range(2):
            l0 = z[:, first + 2 * k : first + 2 * k + 1]
            l1 = z[:, first + 2 * k + 1 : first + 2 * k + 2]
            top = jnp.maximum(l0, l1)
            e0 = jnp.exp(l0 - top)
            e1 = jnp.exp(l1 - top)
            den = e0 + e1
            out = jnp.where(lane == first + 2 * k, e0 / den, out)
            out = jnp.where(lane == first + 2 * k + 1, e1 / den, out)
        for j in range(2):
            mix = jnp.sum(jnp.where(lane == rt_ref[:, j : j + 1], probs, 0.0), axis=-1, keepdims=True)
            out = jnp.where(lane == 16 + j, mix, out)
        pr_ref[...] = out

    slots = xs_ref.shape[0]
    base = step * slots
    slot = base + lax.broadcasted_iota(jnp.int32, (slots, t), 0)
    pick = (slot == tr_ref[0:1, :]) | (slot == tr_ref[1:2, :])
    xs_ref[...] = dot(pick.astype(BF16), n_ref[...]).astype(BF16)


def out_w_spec():
    return spec((D, D), lambda *_: (0, 3))


def small_w_spec():
    return spec((D, LANES), lambda *_: (0, 4 * D // LANES))


def grad_rows_body(g_ref, pr_ref, tr_ref, gs_ref, mg_ref):
    t = g_ref.shape[0]
    step = pl.program_id(0)

    @pl.when(step == 0)
    def _():
        g = g_ref[...].astype(F32)
        for j in range(2):
            mg_ref[j * t : (j + 1) * t, :] = (g * pr_ref[:, 16 + j : 17 + j]).astype(BF16)

    slots = gs_ref.shape[0]
    slot = step * slots + lax.broadcasted_iota(jnp.int32, (slots, t), 0)
    picks = [(slot == tr_ref[j : j + 1, :]).astype(BF16) for j in range(2)]
    gs_ref[...] = dot(jnp.concatenate(picks, axis=1), mg_ref[...]).astype(BF16)


def grad_rows_call(g, pr, tr, slots):
    t = g.shape[0]
    part = min(slots, 256)
    return pl.pallas_call(
        grad_rows_body,
        grid=(slots // part,),
        in_specs=[whole((t, D)), whole((t, LANES)), whole((2, t))],
        out_specs=spec((part, D), lambda i: (i, 0)),
        out_shape=shape((slots, D), BF16),
        scratch_shapes=[pltpu.VMEM((2 * t, D), BF16)],
        name="grad_rows",
        **params((4 * slots * t * D, 4 * t * D)),
    )(g, pr, tr)


def route_call(x, att, pack, gain, res, rt, tr, slots):
    t = x.shape[0]
    part = min(slots, 256)
    return pl.pallas_call(
        route_body,
        grid=(slots // part,),
        in_specs=[
            whole((t, D)), whole((t, D)), out_w_spec(), small_w_spec(), whole((1, D)),
            whole((t, LANES)), whole((t, 2)), whole((2, t)),
        ],
        out_specs=[
            whole((t, D)), whole((t, D)), whole((t, LANES)),
            spec((part, D), lambda i: (i, 0)),
        ],
        out_shape=[
            shape((t, D), F32), shape((t, D), BF16), shape((t, LANES), F32),
            shape((slots, D), BF16),
        ],
        name="route_dispatch",
        **params((2 * t * D * D + 2 * slots * t * D, 8 * t * D)),
    )(x, att, pack, pack, gain, res, rt, tr)


def expert_fwd_body(x_ref, w_ref, o_ref, gate_ref, up_ref, acc_ref):
    step = pl.program_id(0)
    x = x_ref[...]
    wide = w_ref.shape[-1]
    wg = w_ref[:, 0].reshape(D, wide)
    wu = w_ref[:, 1].reshape(D, wide)
    wd = w_ref[:, 2].reshape(D, wide)
    gate = dot(x, wg)
    up = dot(x, wu)
    gate_ref[...] = gate
    up_ref[...] = up
    act = (gate / (1.0 + jnp.exp(-gate)) * up).astype(BF16)
    out = dot_nt(act, wd)

    @pl.when(step == 0)
    def _():
        acc_ref[...] = out

    @pl.when(step > 0)
    def _():
        acc_ref[...] += out

    @pl.when(step == pl.num_programs(0) - 1)
    def _():
        o_ref[...] = acc_ref[...].astype(BF16)


def expert_fwd(xr, w):
    rows = xr.shape[0]
    shards, _, per, wide = w.shape
    part = min(wide, 256)
    return pl.pallas_call(
        expert_fwd_body,
        grid=(wide // part,),
        in_specs=[whole((rows, D)), spec((shards, 3, per, part), lambda i: (0, 0, 0, i))],
        out_specs=[whole((rows, D))] + [spec((rows, part), lambda i: (0, i))] * 2,
        out_shape=[shape((rows, D), BF16)] + [shape((rows, wide), F32)] * 2,
        scratch_shapes=[pltpu.VMEM((rows, D), F32)],
        name="expert_forward",
        **params((6 * rows * D * wide, 6 * D * wide)),
    )(xr, w)


def expert_in_body(gate_ref, up_ref, g_ref, w_ref, gi_ref, act_ref, dg_ref, du_ref, acc_ref):
    step = pl.program_id(0)
    wide = w_ref.shape[-1]
    wg = w_ref[:, 0].reshape(D, wide)
    wu = w_ref[:, 1].reshape(D, wide)
    wd = w_ref[:, 2].reshape(D, wide)
    gate = gate_ref[...]
    up = up_ref[...]
    ga = dot(g_ref[...], wd)
    sig = 1.0 / (1.0 + jnp.exp(-gate))
    silu = gate * sig
    act_ref[...] = (silu * up).astype(BF16)
    d_gate = (ga * up * sig * (1.0 + gate * (1.0 - sig))).astype(BF16)
    d_up = (ga * silu).astype(BF16)
    dg_ref[...] = d_gate
    du_ref[...] = d_up
    gi = dot_nt(
        jnp.concatenate([d_gate, d_up], axis=1), jnp.concatenate([wg, wu], axis=1)
    )

    @pl.when(step == 0)
    def _():
        acc_ref[...] = gi

    @pl.when(step > 0)
    def _():
        acc_ref[...] += gi

    @pl.when(step == pl.num_programs(0) - 1)
    def _():
        gi_ref[...] = acc_ref[...].astype(BF16)


def expert_in(gate, up, gr, w):
    rows = gr.shape[0]
    shards, _, per, wide = w.shape
    part = min(wide, 256)
    tile = spec((rows, part), lambda i: (0, i))
    return pl.pallas_call(
        expert_in_body,
        grid=(wide // part,),
        in_specs=[tile, tile, whole((rows, D)), spec((shards, 3, per, part), lambda i: (0, 0, 0, i))],
        out_specs=[whole((rows, D)), tile, tile, tile],
        out_shape=[shape((rows, D), BF16)] + [shape((rows, wide), BF16)] * 3,
        scratch_shapes=[pltpu.VMEM((rows, D), F32)],
        name="expert_back_in",
        **params((6 * rows * D * wide, 12 * D * wide)),
    )(gate, up, gr, w)


def expert_weights_body(x_ref, gl_ref, act_ref, dg_ref, du_ref, dw_ref, xt_ref, gt_ref):
    @pl.when(pl.program_id(0) == 0)
    def _():
        gt_ref[...] = gl_ref[...].T
        xt_ref[...] = x_ref[...].T

    shards, _, per, wide = dw_ref.shape
    xt = xt_ref[...]
    dw_ref[:, 0] = dot(xt, dg_ref[...]).astype(BF16).reshape(shards, per, wide)
    dw_ref[:, 1] = dot(xt, du_ref[...]).astype(BF16).reshape(shards, per, wide)
    dw_ref[:, 2] = dot(gt_ref[...], act_ref[...]).astype(BF16).reshape(shards, per, wide)


def expert_weights(xr, low, act, d_gate, d_up, dims):
    rows = xr.shape[0]
    shards, _, per, wide = dims
    part = min(wide, 256)
    tile = spec((rows, part), lambda i: (0, i))
    return pl.pallas_call(
        expert_weights_body,
        grid=(wide // part,),
        in_specs=[whole((rows, D)), whole((rows, D)), tile, tile, tile],
        out_specs=spec((shards, 3, per, part), lambda i: (0, 0, 0, i)),
        out_shape=shape(dims, BF16),
        scratch_shapes=[pltpu.VMEM((D, rows), BF16), pltpu.VMEM((D, rows), BF16)],
        name="expert_weight_grads",
        **params((6 * rows * D * wide, 12 * D * wide)),
    )(xr, low, act, d_gate, d_up)


def mix_body(
    h_ref, g_ref, pr_ref, rt_ref, tc_ref, ret_ref, n_ref, sw_ref, rows_ref,
    out_ref, gn_ref, gl_ref, gs_ref,
):
    t = h_ref.shape[0]
    slots = ret_ref.shape[0]
    hidden = h_ref[...]
    g16 = g_ref[...]
    g = g16.astype(F32)
    pr = pr_ref[...]
    scale = lax.rsqrt(jnp.mean(hidden * hidden, axis=-1, keepdims=True) + EPS)
    normed = hidden * scale * rows_ref[2:3, :]
    lane = lax.broadcasted_iota(jnp.int32, (t, LANES), 1)
    slot = lax.broadcasted_iota(jnp.int32, (t, slots), 1)
    first = EXPERTS + 4
    ret = ret_ref[...]
    c0 = [pr[:, first + 2 * k : first + 2 * k + 1] for k in range(2)]
    c1 = [pr[:, first + 2 * k + 1 : first + 2 * k + 2] for k in range(2)]
    total = hidden
    s = jnp.zeros((t, LANES), F32)
    coef = jnp.zeros((t, 1), F32)
    weight = [jnp.zeros((t, 1), F32) for _ in range(2)]
    for j in range(2):
        route = rt_ref[:, j : j + 1]
        mix = pr[:, 16 + j : 17 + j]
        branch = dot((slot == tc_ref[:, j : j + 1]).astype(BF16), ret)
        keep = jnp.where(route == EXPERTS + 1, 1.0, 0.0)
        for k in range(2):
            here = jnp.where(route == EXPERTS + 2 + k, 1.0, 0.0)
            keep = keep + here * c0[k]
            weight[k] = weight[k] + here * mix
            branch = branch + (here * c1[k]) * rows_ref[k : k + 1, :]
        branch = branch + keep * normed
        coef = coef + mix * keep
        total = total + mix * branch
        gp = jnp.sum(g * branch, axis=-1, keepdims=True)
        s = s + jnp.where(lane == route, gp, 0.0)
    out_ref[...] = total.astype(BF16)
    probs = jnp.where(lane < first, pr, 0.0)
    d_logits = probs * (s - jnp.sum(probs * s, axis=-1, keepdims=True))
    gl_ref[...] = d_logits
    dz = d_logits
    dvec = jnp.zeros((t, LANES), F32)
    g_dot_n = jnp.sum(g * normed, axis=-1, keepdims=True)
    for k in range(2):
        d0 = weight[k] * g_dot_n
        d1 = weight[k] * jnp.sum(g * rows_ref[k : k + 1, :], axis=-1, keepdims=True)
        mean = c0[k] * d0 + c1[k] * d1
        dz = jnp.where(lane == first + 2 * k, c0[k] * (d0 - mean), dz)
        dz = jnp.where(lane == first + 2 * k + 1, c1[k] * (d1 - mean), dz)
        dvec = jnp.where(lane == 16 + k, weight[k] * c1[k], dvec)
    hi, lo = split_hi_lo(dz)
    sw = sw_ref[...]
    gn_ref[...] = coef * g + (dot_nt(hi, sw) + dot_nt(lo, sw))
    nt = n_ref[...].T
    gt = g16.T
    vhi, vlo = split_hi_lo(dvec)
    gs = dot(nt, hi) + dot(nt, lo) + dot(gt, vhi) + dot(gt, vlo)

    @pl.when(pl.program_id(0) == 0)
    def _():
        gs_ref[...] = gs

    @pl.when(pl.program_id(0) > 0)
    def _():
        gs_ref[...] += gs


def mix_call(hidden, g, pr, rt, tc, ret, low, pack, rows):
    t = hidden.shape[0]
    half = min(t, LANES)
    slots = ret.shape[0]
    tile = spec((half, D), lambda i: (i, 0))
    lane_tile = spec((half, LANES), lambda i: (i, 0))
    pair = spec((half, 2), lambda i: (i, 0))
    return pl.pallas_call(
        mix_body,
        grid=(t // half,),
        in_specs=[
            tile, tile, lane_tile, pair, pair, whole((slots, D)), tile, small_w_spec(),
            whole((8, D)),
        ],
        out_specs=[tile, tile, lane_tile, whole((D, LANES))],
        out_shape=[
            shape((t, D), BF16), shape((t, D), F32), shape((t, LANES), F32), shape((D, LANES), F32),
        ],
        name="mixture",
        **params((4 * t * slots * D, 12 * t * D)),
    )(hidden, g, pr, rt, tc, ret, low, pack, rows)


def norm_back_body(
    h_ref, g_ref, gn_ref, tc_ref, ret_ref, rows_ref, ow_ref, att_ref,
    gh_ref, do_ref, dot_ref, gow_ref, gg_ref,
):
    t = h_ref.shape[0]
    slots = ret_ref.shape[0]
    hidden = h_ref[...]
    slot = lax.broadcasted_iota(jnp.int32, (t, slots), 1)
    pick = (slot == tc_ref[:, 0:1]) | (slot == tc_ref[:, 1:2])
    gn = gn_ref[...] + dot(pick.astype(BF16), ret_ref[...])
    q = lax.rsqrt(jnp.mean(hidden * hidden, axis=-1, keepdims=True) + EPS)
    u = gn * rows_ref[2:3, :]
    mean = jnp.mean(u * hidden, axis=-1, keepdims=True)
    gh = g_ref[...].astype(F32) + q * u - hidden * (q * q * q * mean)
    gh_ref[...] = gh
    gb = gh.astype(BF16)
    d_out = dot_nt(gb, ow_ref[...]).astype(BF16)
    do_ref[...] = d_out
    dot_ref[...] = d_out.T
    gow = dot(att_ref[...].T, gb)
    gain = jnp.sum(gn * hidden * q, axis=0, keepdims=True)

    @pl.when(pl.program_id(0) == 0)
    def _():
        gow_ref[...] = gow
        gg_ref[...] = jnp.broadcast_to(gain, gg_ref.shape)

    @pl.when(pl.program_id(0) > 0)
    def _():
        gow_ref[...] += gow
        gg_ref[...] += jnp.broadcast_to(gain, gg_ref.shape)


def norm_back_call(hidden, g, gn, tc, ret, rows, pack, att):
    t = hidden.shape[0]
    half = t // 2 if (t // 2) % LANES == 0 else t
    slots = ret.shape[0]
    tile = spec((half, D), lambda i: (i, 0))
    return pl.pallas_call(
        norm_back_body,
        grid=(t // half,),
        in_specs=[
            tile, tile, tile, spec((half, 2), lambda i: (i, 0)), whole((slots, D)), whole((8, D)),
            out_w_spec(), tile,
        ],
        out_specs=[tile, tile, spec((D, half), lambda i: (0, i)), whole((D, D)), whole((8, D))],
        out_shape=[
            shape((t, D), F32), shape((t, D), BF16), shape((D, t), BF16), shape((D, D), F32),
            shape((8, D), F32),
        ],
        name="norm_two_back",
        **params((2 * t * slots * D + 4 * t * D * D, 16 * t * D)),
    )(hidden, g, gn, tc, ret, rows, pack, att)


def turn_body(x_ref, o_ref):
    o_ref[...] = x_ref[...].T


def turn(x):
    rows, wide = x.shape
    part = 256
    return pl.pallas_call(
        turn_body,
        grid=(wide // part,),
        in_specs=[spec((rows, part), lambda i: (0, i))],
        out_specs=spec((part, rows), lambda i: (i, 0)),
        out_shape=shape((wide, rows), x.dtype),
        name="turn",
        **params((rows * wide, 4 * rows * wide)),
    )(x)


def store_grad(sc_ref, split, value, refs):
    if not split:
        refs[0][...] = value
        return
    send_ref, keep_ref = refs
    per = value.shape[0] // 4
    for core in range(2):

        @pl.when(sc_ref[11] == core)
        def _():
            for part in range(2):
                mine = (2 * part + core) * per
                other = (2 * part + 1 - core) * per
                send_ref[part] = value[other : other + per].astype(BF16)
                keep_ref[part] = value[mine : mine + per]


def grad_outs(split, width):
    block = 2 * LANES
    if not split:
        return [spec((D, block), lambda i: (0, i))], [shape((D, width), F32)]
    dims = (2, D // 4, width)
    tile = spec((2, D // 4, block), lambda i: (0, 0, i))
    return [tile, tile], [shape(dims, BF16), shape(dims, F32)]


def q_back_body(split, sc_ref, nt_ref, dq_ref, c_ref, s_ref, w_ref, gn_ref, *refs):
    step = pl.program_id(0)
    cosine = c_ref[...]
    sine = s_ref[...]
    v0 = dq_ref[:, :LANES]
    v1 = dq_ref[:, LANES:]
    gq = jnp.concatenate(
        [
            (v0 * cosine - partner(v0) * sine).astype(BF16),
            (v1 * cosine - partner(v1) * sine).astype(BF16),
        ],
        axis=1,
    )
    store_grad(sc_ref, split, dot(nt_ref[...], gq), refs)
    gn = dot_nt(gq, w_ref[...])

    @pl.when(step == 0)
    def _():
        gn_ref[...] = gn

    @pl.when(step > 0)
    def _():
        gn_ref[...] += gn


def q_back_call(sc, low_t, dq, cosine, sine, pack, split):
    t = low_t.shape[1]
    specs, shapes = grad_outs(split, D)
    return pl.pallas_call(
        functools.partial(q_back_body, split),
        grid=(PAIRS // 2,),
        in_specs=[
            SMEM_SPEC, whole((D, t)), spec((t, 2 * LANES), lambda i: (0, i)), whole((t, LANES)),
            whole((t, LANES)), spec((D, 2 * LANES), lambda i: (0, i)),
        ],
        out_specs=[whole((t, D))] + specs,
        out_shape=[shape((t, D), F32)] + shapes,
        name="q_back",
        **params((4 * t * D * D, 12 * t * D)),
    )(sc, low_t, dq, cosine, sine, pack)


def kv_back_body(
    split, count, sc_ref, x_ref, nt_ref, gnq_ref, gh_ref, gain_ref, c_ref, s_ref, wk_ref, wv_ref,
    own_ref, cont_ref, *refs
):
    got_refs, refs = refs[:count], refs[count:]
    gi_ref, grads, gn_ref = refs[0], refs[1:-1], refs[-1]
    step = pl.program_id(0)

    @pl.when(step == 0)
    def _():
        gn_ref[...] = gnq_ref[...]

    own = own_ref[...]
    for got in got_refs:
        own = own + got[...].astype(F32)
    total = jnp.concatenate([own, cont_ref[...]], axis=0)
    k = total[:, :LANES]
    gk = (k * c_ref[...] - partner(k) * s_ref[...]).astype(BF16)
    gkv = jnp.concatenate([gk, total[:, LANES:].astype(BF16)], axis=1)
    store_grad(sc_ref, split, dot(nt_ref[...], gkv), grads)
    gn_ref[...] += dot_nt(gkv, jnp.concatenate([wk_ref[...], wv_ref[...]], axis=1))

    @pl.when(step == pl.num_programs(0) - 1)
    def _():
        gn = gn_ref[...]
        x = x_ref[...].astype(F32)
        q = lax.rsqrt(jnp.mean(x * x, axis=-1, keepdims=True) + EPS)
        u = gn * gain_ref[...]
        mean = jnp.mean(u * x, axis=-1, keepdims=True)
        gi_ref[...] = gh_ref[...] + q * u - x * (q * q * q * mean)


def kv_back_call(sc, x, low_t, gn, gh, gain, cosine, sine, pack, own, cont, got, split):
    t = x.shape[0]
    r = t // 2
    specs, shapes = grad_outs(split, 2 * D)
    wide = spec((r, 2 * LANES), lambda i: (0, i))
    return pl.pallas_call(
        functools.partial(kv_back_body, split, len(got)),
        grid=(PAIRS,),
        in_specs=[
            SMEM_SPEC, whole((t, D)), whole((D, t)), whole((t, D)), whole((t, D)), whole((1, D)),
            whole((t, LANES)), whole((t, LANES)),
            spec((D, LANES), lambda i: (0, PAIRS + i)),
            spec((D, LANES), lambda i: (0, 2 * PAIRS + i)),
            wide, wide,
        ]
        + [wide] * len(got),
        out_specs=[whole((t, D))] + specs,
        out_shape=[shape((t, D), F32)] + shapes,
        scratch_shapes=[pltpu.VMEM((t, D), F32)],
        name="kv_back",
        **params((8 * t * D * D, 24 * t * D)),
    )(sc, x, low_t, gn, gh, gain, cosine, sine, pack, pack, own, cont, *got)


def rotation_tables(position):
    half = HEAD_DIM // 2
    frequency = 10000.0 ** (-jnp.arange(half, dtype=F32) / half)
    angles = position[:, None] * frequency[None, :]
    cosine, sine = jnp.cos(angles), jnp.sin(angles)
    return (
        jnp.concatenate([cosine] * 4, axis=1),
        jnp.concatenate([-sine, sine, -sine, sine], axis=1),
    )


def to_rows(array):
    return jnp.transpose(array, (1, 0, 2)).reshape(2 * array.shape[0], array.shape[2])


def from_rows(array):
    r = array.shape[0] // 2
    return jnp.transpose(array.reshape(2, r, array.shape[1]), (1, 0, 2))


RING = (0, 2, 4, 6, 7, 5, 3, 1)


def ring_offsets():
    place = {e: i for i, e in enumerate(RING)}
    return [[RING[(place[e] + k) % 8] for k in range(8)] for e in range(8)]


def along_ring(array, step):
    pairs = [(RING[i], RING[(i + step) % 8]) for i in range(8)]
    return lax.ppermute(array, "expert", pairs)


def tie(*values):
    return lax.optimization_barrier(values)


def swap_core(array):
    return lax.ppermute(array, "dp", [(0, 1), (1, 0), (2, 3), (3, 2)])


def add_and_cross(keep, got):
    across = lax.axis_index("dp") // 2
    keep = keep + got.astype(F32)
    send = lax.dynamic_index_in_dim(keep, 1 - across, 0, keepdims=False).astype(BF16)
    mine = lax.dynamic_index_in_dim(keep, across, 0, keepdims=False)
    return mine, lax.ppermute(send, "dp", [(0, 2), (2, 0), (1, 3), (3, 1)])


def add_and_scatter(keep, got):
    keep = (keep + got.astype(F32)).astype(BF16)
    rows, w = keep.shape
    return lax.all_to_all(
        keep.reshape(8, rows // 8, w), "expert", split_axis=0, concat_axis=0, tiled=True
    )


def add_up(got):
    return jnp.sum(got.astype(F32), axis=0)


def scatter_all(array):
    return lax.psum_scatter(
        array.astype(BF16), ALL_AXES, scatter_dimension=0, tiled=True
    ).astype(F32)


def per_device(
    hidden_in, cotangent, gate_residual, routes, groups, lengths, attn_gain, qkv_weight, out_weight,
    ffn_gain, router_weight, const_proj, const_vec, gate_weight, up_weight, down_weight,
):
    del groups
    r = hidden_in.shape[0]
    t = 2 * r
    capacity = r // 2
    owners = lax.axis_size("expert")
    copies = owners // EXPERTS
    slots = EXPERTS * capacity
    me = lax.axis_index("expert")
    per_cont = max(CONT_LEN // r, 1)

    small = jnp.concatenate(
        [
            router_weight, const_proj, const_vec, attn_gain[:, None], ffn_gain[:, None],
            jnp.zeros((attn_gain.shape[0], LANES - 20), BF16),
        ],
        axis=1,
    )
    pack = lax.all_gather(
        jnp.concatenate([qkv_weight, out_weight, small], axis=1), ALL_AXES, axis=0, tiled=True
    )
    index = jnp.arange(r, dtype=jnp.int32)
    row_ids = me * r + index
    position = jnp.concatenate([row_ids, PROMPT + row_ids % CONT_LEN]).astype(F32)
    cosine, sine = rotation_tables(position)
    cont = (me * r) // CONT_LEN
    length = lax.dynamic_slice(lengths, (cont,), (1,))
    header = jnp.stack([me, (me * r) % CONT_LEN]).astype(jnp.int32)
    header = jnp.concatenate([header, length.astype(jnp.int32)])
    ring = owners == 8
    if ring:
        ids = lax.dynamic_index_in_dim(jnp.asarray(ring_offsets(), jnp.int32), me, 0, keepdims=False)
    else:
        ids = jnp.arange(owners, dtype=jnp.int32)
    sc = jnp.concatenate([header, ids, (lax.axis_index("dp") % 2).astype(jnp.int32)[None]])

    picked = to_rows(routes)
    flat = jnp.transpose(picked).reshape(2 * t)
    hot = flat[:, None] == jnp.arange(EXPERTS, dtype=jnp.int32)[None, :]
    earlier = jnp.arange(2 * t)[:, None] > jnp.arange(2 * t)[None, :]
    before = jnp.dot(earlier.astype(BF16), hot.astype(BF16), preferred_element_type=F32)
    slot_index = jnp.sum(jnp.where(hot, before, 0.0), axis=1).astype(jnp.int32)
    target = jnp.where(flat < EXPERTS, flat * capacity + slot_index, -1)
    target_rows = target.reshape(2, t)
    target_cols = jnp.transpose(target_rows)

    def to_owners(rows):
        w = rows.shape[-1]
        shaped = rows.reshape(EXPERTS, 1, capacity, w)
        return jnp.broadcast_to(shaped, (EXPERTS, copies, capacity, w)).reshape(owners, capacity, w)

    def exchange(rows):
        got = lax.all_to_all(rows, "expert", split_axis=0, concat_axis=0, tiled=True)
        return got.reshape(owners * got.shape[1], got.shape[2])

    def from_owners(rows):
        got = exchange(rows.reshape(owners, capacity, D))
        if copies == 1:
            return got
        got = got.reshape(EXPERTS, copies, capacity, D).astype(F32)
        return jnp.sum(got, axis=1).reshape(slots, D).astype(BF16)

    x = to_rows(hidden_in)
    g = to_rows(cotangent)
    small_w = pack[:, 4 * D :]
    small_rows = jnp.transpose(small_w[:, 16:24]).astype(F32)
    gain_one = small_rows[2:3]
    rows_two = jnp.concatenate([small_rows[0:2], small_rows[3:4], small_rows[3:8]], axis=0)
    gain_two = small_rows[3:4]

    low_one, q, q_t, kv_prompt, kv_cont = qkv_call(x, gain_one, pack, cosine, sine)
    if not ring:
        kv_all = lax.all_gather(kv_prompt, "expert", axis=0, tiled=True)
    if per_cont == 1:
        kv_own = kv_cont
    else:
        cont_groups = [
            [c * per_cont + i for i in range(per_cont)] for c in range(owners // per_cont)
        ]
        kv_own = lax.all_gather(
            kv_cont, "expert", axis=0, tiled=True, axis_index_groups=cont_groups
        )
    weights = lax.all_gather(
        jnp.stack([gate_weight, up_weight, down_weight]), "dp", axis=0, tiled=False
    )
    if ring:
        right, left = [kv_prompt], [kv_prompt]
        for i in range(3):
            right.append(along_ring(right[i], 1))
            left.append(along_ring(left[i], -1))
            if i == 0:
                st, acc = fwd_local(sc, q_t, kv_prompt, kv_own)
            else:
                st, acc = fwd_remote(sc, q_t, (right[i], left[i]), (8 - i, i), st, acc)
            right[i + 1], left[i + 1], st = tie(right[i + 1], left[i + 1], st)
        far = [along_ring(right[3][:, :D], 1), along_ring(left[3][:, D:], -1)]
        st, acc = fwd_remote(sc, q_t, (right[3], left[3]), (5, 3), st, acc)
        st, att_t, att = fwd_remote(sc, q_t, far, (4,), st, acc, halves=True, final=True)
    else:
        st, acc = fwd_local(sc, q_t, kv_prompt, kv_own)
        st, att_t, att = fwd_remote(sc, q_t, (kv_all,), range(owners), st, acc, final=True)

    res = jnp.pad(to_rows(gate_residual), ((0, 0), (0, LANES - EXPERTS - 4)))
    hidden, low_two, pr, x_send = route_call(
        x, att, pack, gain_two, res, picked, target_rows, slots
    )
    x_got = exchange(to_owners(x_send))
    g_send = grad_rows_call(g, pr, target_rows, slots)
    low_one_t = turn(low_one)
    x_got, g_send = tie(x_got, g_send)
    g_got = exchange(to_owners(g_send))
    expert_rows, gate_pre, up_pre = expert_fwd(x_got, weights)
    out_back = from_owners(expert_rows)
    grad_in, act, d_gate, d_up = expert_in(gate_pre, up_pre, g_got, weights)
    in_back = from_owners(grad_in)
    output, gn, grad_logits, grad_small = mix_call(
        hidden, g, pr, picked, target_cols, out_back, low_two, pack, rows_two
    )
    act, gn = tie(act, gn)
    grad_w = expert_weights(x_got, g_got, act, d_gate, d_up, weights.shape)
    grad_expert = lax.psum_scatter(
        grad_w.reshape(-1, grad_w.shape[-1]), "dp", scatter_dimension=0, tiled=True
    )
    per = gate_weight.shape[0]
    grad_expert = [grad_expert[i * per : (i + 1) * per].astype(F32) for i in range(3)]
    gh, d_att, d_att_t, grad_ow, gg_two = norm_back_call(
        hidden, g, gn, target_cols, in_back, rows_two, pack, att
    )

    def early_rows(grad_ow, grad_small, gg_two):
        return jnp.concatenate(
            [
                grad_ow, grad_small[:, :19], jnp.transpose(gg_two[0:1]),
                jnp.zeros((D, LANES - 20), F32),
            ],
            axis=1,
        )

    early = (grad_ow, grad_small, gg_two)
    back = (sc, q_t, q, d_att_t, d_att)
    if ring:
        dq_t, send_r, send_l, st = bwd_remote(
            *back, st, att_t, far, (4,), halves=True, first=True, dtype=BF16
        )
        for i in range(3, 0, -1):
            got_r, got_l = along_ring(send_r, 1), along_ring(send_l, -1)
            dq_t, part_r, part_l = bwd_remote(
                *back, st, dq_t, (left[i], right[i]), (i, 8 - i), dtype=BF16
            )
            got_r, got_l, part_r, part_l, dq_t, early = tie(
                got_r, got_l, part_r, part_l, dq_t, early
            )
            send_r, send_l = ring_add(part_r, got_r, part_l, got_l)
            if i == 3:
                send_r, early = tie(send_r, early)
                parts = early_rows(*early).reshape(2, 2, D // 4, D + LANES)
                core = lax.axis_index("dp") % 2
                early_keep = lax.dynamic_index_in_dim(parts, core, 1, keepdims=False)
                early_send = lax.dynamic_index_in_dim(parts, 1 - core, 1, keepdims=False)
                dq_t, early_send = tie(dq_t, early_send.astype(BF16))
                early = swap_core(early_send)
            elif i == 2:
                send_r, early = tie(send_r, early)
                early_keep, early_got = add_and_cross(early_keep, early)
                dq_t, early_keep = tie(dq_t, early_keep)
                early = early_got
        early_got = early
        send_r, send_l, dq_t = tie(send_r, send_l, dq_t)
        got_r = along_ring(send_r, 1)
        got_l = along_ring(send_l, -1)
        got = (got_r, got_l)
        dq, dkv_own, dkv_cont = bwd_local(*back, st, dq_t, kv_prompt, kv_own)
    else:
        dq_t, dkv_all, st = bwd_remote(
            *back, st, att_t, (kv_all,), range(owners), first=True, dtype=BF16
        )
        dq, dkv_own, dkv_cont = bwd_local(*back, st, dq_t, kv_prompt, kv_own)
        got = (lax.psum_scatter(dkv_all, "expert", scatter_dimension=0, tiled=True),)
        early = scatter_all(early_rows(*early))
    if per_cont > 1:
        dkv_cont = lax.psum_scatter(
            dkv_cont, "expert", scatter_dimension=0, tiled=True, axis_index_groups=cont_groups
        )
    gn_q, *grad_q = q_back_call(sc, low_one_t, dq, cosine, sine, pack, ring)
    if ring:
        got_q = swap_core(grad_q[0])
    grad_input, *grad_kv = kv_back_call(
        sc, x, low_one_t, gn_q, gh, gain_one, cosine, sine, pack, dkv_own, dkv_cont, got, ring
    )
    output, grad_input = from_rows(output), from_rows(grad_input)
    if ring:
        got_kv = swap_core(grad_kv[0])
        keep_q, got_q = add_and_cross(grad_q[1], got_q)
        keep_kv, got_kv = add_and_cross(grad_kv[1], got_kv)
        keep_kv, got_q, early_got = tie(keep_kv, got_q, early_got)
        got_q = add_and_scatter(
            jnp.concatenate([early_keep, keep_q], axis=1),
            jnp.concatenate([early_got, got_q], axis=1),
        )
        got_kv, output, grad_input, *grad_expert = tie(got_kv, output, grad_input, *grad_expert)
        summed = add_up(got_q)
        early, late_q = summed[:, : D + LANES], summed[:, D + LANES :]
        late_kv = add_up(add_and_scatter(keep_kv, got_kv))
    else:
        late_q, late_kv = scatter_all(grad_q[0]), scatter_all(grad_kv[0])
    per = late_kv.shape[0]
    late_kv = jnp.transpose(late_kv.reshape(per, PAIRS, 2, LANES), (0, 2, 1, 3))
    late = jnp.concatenate([late_q, late_kv.reshape(per, 2 * D)], axis=1)
    grad_gain = jnp.sum(late * qkv_weight.astype(F32), axis=1) / attn_gain.astype(F32)
    tail = early[:, D:]
    return (
        output,
        grad_input,
        from_rows(grad_logits)[:, :, : EXPERTS + 4],
        grad_gain,
        late,
        early[:, :D],
        tail[:, 19],
        tail[:, :12],
        tail[:, 12:16],
        tail[:, 16:18],
        grad_expert[0],
        grad_expert[1],
        grad_expert[2],
    )


def solution(mesh):
    rows = P(ALL_AXES, None, None)
    flat = P(ALL_AXES)
    mat = P(ALL_AXES, None)
    expert = P("dp", "expert")
    in_specs = (
        rows, rows, rows, rows, P("dp"), P("dp"), flat, mat, mat, flat, mat, mat, mat,
        expert, expert, expert,
    )
    out_specs = (
        rows, rows, rows, flat, mat, mat, flat, mat, mat, mat, expert, expert, expert,
    )

    return jax.shard_map(
        per_device, mesh=mesh, in_specs=in_specs, out_specs=out_specs, check_vma=False
    )
```
